32 devices in a mesh: dp: 2 (over x), gr: 4 (over z), gc: 4 (over y, core).
Axes of the slice: x: 2, y: 2, z: 4, core: 2. Of those that a mesh axis runs over, the one named last changes fastest.
Arguments:
- tokens: bfloat16 [16384, 768], P(('dp', 'gr', 'gc')), may hold values from -6 to 6
- teacher: bfloat16 [16384, 768], P(('dp', 'gr', 'gc')), may hold values from -15 to 15
- pass_embed: bfloat16 [768], P('gr'), may hold values from -0.119628906 to 0.119628906
- ln1_gain: bfloat16 [768], P('gr'), may hold values from 0.25 to 1.75
- ln1_bias: bfloat16 [768], P('gr'), may hold values from -0.119628906 to 0.119628906
- qkv_weight: bfloat16 [768, 2304], P('gr', 'gc'), may hold values from -0.21875 to 0.21875
- out_weight: bfloat16 [768, 768], P('gc', 'gr'), may hold values from -1.75 to 1.75
- out_bias: bfloat16 [768], P('gr'), may hold values from -0.8984375 to 0.8984375
- ln2_gain: bfloat16 [768], P('gr'), may hold values from 0.25 to 1.75
- ln2_bias: bfloat16 [768], P('gr'), may hold values from -0.8984375 to 0.8984375
- fc1_weight: bfloat16 [768, 3072], P('gr', 'gc'), may hold values from -0.3125 to 0.3125
- fc1_bias: bfloat16 [3072], P('gc'), may hold values from -2 to 2
- fc2_weight: bfloat16 [768, 3072], P('gr', 'gc'), may hold values from -0.109375 to 0.109375
- fc2_bias: bfloat16 [768], P('gr'), may hold values from -0.8984375 to 0.8984375
- cont_group: int32 [64], P(('dp', 'gr')), may hold values from 0 to 3, as said below
- token_count: int32 [1], replicated, may hold values from 8192 to 16384
Outputs:
- output: bfloat16 [16384, 768], P(('dp', 'gr', 'gc'))
- loss: float32 [1], replicated
- input_grad: float32 [16384, 768], P(('dp', 'gr', 'gc'))
- pass_embed_grad: float32 [768], P('gr')
- ln1_gain_grad: float32 [768], P('gr')
- ln1_bias_grad: float32 [768], P('gr')
- qkv_weight_grad: float32 [768, 2304], P('gr', 'gc')
- out_weight_grad: float32 [768, 768], P('gc', 'gr')
- out_bias_grad: float32 [768], P('gr')
- ln2_gain_grad: float32 [768], P('gr')
- ln2_bias_grad: float32 [768], P('gr')
- fc1_weight_grad: float32 [768, 3072], P('gr', 'gc')
- fc1_bias_grad: float32 [3072], P('gc')
- fc2_weight_grad: float32 [768, 3072], P('gr', 'gc')
- fc2_bias_grad: float32 [768], P('gr')
The draws below stay inside these ranges and needn't reach their ends.
Inputs may be any that keep to these rules, and one draw needn't show every extreme that they name: `cont_group`: continuation k names a group of index k // 32 of dp by its place among that index's 4 groups; each place is named by exactly 8 of that index's continuations.
All inputs are finite; a program needn't handle non-finite values.
Results may differ from the reference program's by a relative error of at most 0.025.
Values may be sent and summed in bfloat16 or wider, within the bound.
A program may use at most 192 MiB of HBM per device.

```python
import math
import jax
import jax.numpy as jnp
from jax import lax

D = 768
HEADS = 12
HD = 64
FF = 3072
P_SIZE = 1024
NC = 8
CL = 128
GPS = 1
GROUPS_DP = 4
GROUPS = 8
SHARD = 2048
TOKENS = 16384
CONTS = 64
N_GR = 4
N_GC = 4


def draw_cont_group(key, part):

    def one_block(block_index):
        order = jax.random.permutation(jax.random.fold_in(key, block_index), GROUPS_DP * NC)
        return (order % GROUPS_DP).astype(jnp.int32)
    blocks = jax.vmap(one_block)(jnp.arange(CONTS // (GROUPS_DP * NC)))
    return blocks.reshape(CONTS)


def levels(stream_key, shape, shards, smallest, largest):
    level = 1.0
    for dim, parts in shards:
        heights = jax.random.uniform(jax.random.fold_in(jax.random.fold_in(stream_key, 6), dim), (parts,), jnp.float32, smallest / len(shards), largest / len(shards))
        level = level * jnp.repeat(jnp.exp(heights), shape[dim] // parts).reshape((-1,) + (1,) * (len(shape) - 1 - dim))
    return level


def centred(stream_key, dims, deviation, most, split=(), kind=jnp.bfloat16):
    result = jax.random.normal(stream_key, dims, jnp.float32) * deviation
    if len(split) > 0:
        result = levels(stream_key, dims, split, -0.22, 0.18) * result
    return jnp.clip(result, min=-most, max=most).astype(kind)


def setup_inputs(seed: int = 0) -> dict:
    key_of = jax.random.split(jax.random.key(seed), 17)
    tokens = centred(key_of[0], (TOKENS, D), 1.0, 6.0, ((0, 32),))
    teacher = centred(key_of[1], (TOKENS, D), 3.0, 15.0, ((0, 32),))
    pass_embed = centred(key_of[2], (D,), 0.02, 0.119628906, ((0, 4),))
    ln1_gain = jnp.clip(1.0 + 0.15 * jax.random.normal(key_of[3], (D,), jnp.float32), 0.25, 1.75).astype(jnp.bfloat16)
    ln1_bias = centred(key_of[4], (D,), 0.02, 0.119628906, ((0, 4),))
    qkv_weight = centred(key_of[5], (D, 3 * D), D ** -0.5, 0.21875, ((0, 4), (1, 4)))
    out_weight = centred(key_of[6], (D, D), (D // 64) ** -0.5, 1.75, ((0, 4), (1, 4)))
    out_bias = centred(key_of[7], (D,), 0.15, 0.8984375, ((0, 4),))
    ln2_gain = jnp.clip(1.0 + 0.15 * jax.random.normal(key_of[8], (D,), jnp.float32), 0.25, 1.75).astype(jnp.bfloat16)
    ln2_bias = centred(key_of[9], (D,), 0.15, 0.8984375, ((0, 4),))
    fc1_weight = centred(key_of[10], (D, FF), (D // 2) ** -0.5, 0.3125, ((0, 4), (1, 4)))
    fc1_bias = centred(key_of[11], (FF,), 0.3, 2.0, ((0, 4),))
    fc2_weight = centred(key_of[12], (D, FF), FF ** -0.5, 0.109375, ((0, 4), (1, 4)))
    fc2_bias = centred(key_of[13], (D,), 0.15, 0.8984375, ((0, 4),))
    cont_group = draw_cont_group(jax.random.fold_in(key_of[16], 71), 0)
    token_count = jax.random.randint(key_of[15], (1,), TOKENS // 2, TOKENS + 1).astype(jnp.int32)
    return {"tokens": tokens, "teacher": teacher, "pass_embed": pass_embed, "ln1_gain": ln1_gain, "ln1_bias": ln1_bias, "qkv_weight": qkv_weight, "out_weight": out_weight, "out_bias": out_bias, "ln2_gain": ln2_gain, "ln2_bias": ln2_bias, "fc1_weight": fc1_weight, "fc1_bias": fc1_bias, "fc2_weight": fc2_weight, "fc2_bias": fc2_bias, "cont_group": cont_group, "token_count": token_count}


eps = 1e-05
negative = -1e+30

@jax.custom_vjp
def low(v):
    return lax.optimization_barrier(v.astype(jnp.bfloat16)).astype(jnp.float32)

@jax.custom_vjp
def low_back(v):
    return v

def low_keep(v):
    return (low(v), None)

def low_pass(kept, grad):
    return (grad,)

def back_keep(v):
    return (v, None)

def back_low(kept, grad):
    return (low(grad),)
low.defvjp(low_keep, low_pass)
low_back.defvjp(back_keep, back_low)

def grid_product(values, weight, split_in, split_out):
    row_count = values.shape[0]
    width_in = weight.shape[0]
    width_out = weight.shape[1]
    pieces = values.reshape(row_count, split_in, width_in // split_in)
    copies = low_back(jnp.broadcast_to(pieces[None], (split_out, row_count, split_in, width_in // split_in)))
    blocks = weight.reshape(split_in, width_in // split_in, split_out, width_out // split_out)
    partial_sums = jnp.einsum('ctgk,gkcf->gtcf', copies, blocks, precision=lax.Precision.HIGHEST)
    return lax.optimization_barrier(jnp.sum(low(partial_sums), axis=0)).reshape(row_count, width_out)

def layer_norm(hidden, gain, shift):
    center = lax.optimization_barrier(jnp.mean(hidden, axis=1, keepdims=True))
    offset = hidden - center
    spread = lax.optimization_barrier(jnp.mean(offset * offset, axis=1, keepdims=True))
    return offset * lax.rsqrt(spread + eps) * gain + shift

def causal_mask(size):
    positions = jnp.arange(size)
    return positions[None, :] <= positions[:, None]

def attention(qkv):
    score_scale = 1.0 / math.sqrt(HD)
    highest = lax.Precision.HIGHEST
    head_cols = qkv.reshape(qkv.shape[0], HEADS, 3, HD)
    queries = head_cols[:, :, 0]
    key_rows = head_cols[:, :, 1]
    value_rows = head_cols[:, :, 2]
    prompt_raw = low_back(jnp.einsum('qhd,khd->hqk', queries[:P_SIZE], key_rows[:P_SIZE], precision=highest))
    prompt_scores = jnp.where(causal_mask(P_SIZE)[None], prompt_raw * score_scale, negative)
    prompt_prob = low(jax.nn.softmax(prompt_scores, axis=2))
    prompt_mix = jnp.einsum('hqk,khd->qhd', prompt_prob, value_rows[:P_SIZE], precision=highest)
    cont_queries = queries[P_SIZE:].reshape(NC, CL, HEADS, HD)
    cont_keys = key_rows[P_SIZE:].reshape(NC, CL, HEADS, HD)
    cont_values = value_rows[P_SIZE:].reshape(NC, CL, HEADS, HD)
    far_raw = low_back(jnp.einsum('nqhd,khd->nhqk', cont_queries, key_rows[:P_SIZE], precision=highest))
    near_raw = low_back(jnp.einsum('nqhd,nkhd->nhqk', cont_queries, cont_keys, precision=highest))
    near_scores = jnp.where(causal_mask(CL)[None, None], near_raw * score_scale, negative)
    joint = jnp.concatenate([far_raw * score_scale, near_scores], axis=3)
    cont_prob = low(jax.nn.softmax(joint, axis=3))
    cont_mix = jnp.einsum('nhqk,khd->nqhd', cont_prob[..., :P_SIZE], value_rows[:P_SIZE], precision=highest)
    cont_mix = cont_mix + jnp.einsum('nhqk,nkhd->nqhd', cont_prob[..., P_SIZE:], cont_values, precision=highest)
    return jnp.concatenate([prompt_mix.reshape(P_SIZE, HEADS * HD), cont_mix.reshape(NC * CL, HEADS * HD)], axis=0)

def group_loss(params, inputs, goal):
    pass_vec, gain_one, shift_one, w_qkv, w_out, b_out, gain_two, shift_two, w_up, b_up, w_down, b_down = params
    hidden = inputs + pass_vec
    normed = low(layer_norm(hidden, gain_one, shift_one))
    qkv = low(low_back(grid_product(normed, w_qkv, N_GR, N_GC)))
    mixed = low(low_back(attention(qkv)))
    hidden = hidden + low_back(grid_product(mixed, w_out, N_GC, N_GR) + b_out)
    normed = low(layer_norm(hidden, gain_two, shift_two))
    pre_act = low_back(grid_product(normed, w_up, N_GR, N_GC) + b_up)
    active = low(jax.nn.gelu(pre_act, approximate=True))
    final = hidden + low_back(grid_product(active, w_down.T, N_GC, N_GR) + b_down)
    diff = final - goal
    return (final, 0.5 * jnp.sum(diff * diff))

def place_rows(shard, local):
    quarter = SHARD // N_GR
    return (shard // N_GC * N_GR + local // quarter) * (N_GC * quarter) + shard % N_GC * quarter + local % quarter

def reference(tokens, teacher, pass_embed, ln1_gain, ln1_bias, qkv_weight, out_weight, out_bias, ln2_gain, ln2_bias, fc1_weight, fc1_bias, fc2_weight, fc2_bias, cont_group, token_count):
    params = tuple((a.astype(jnp.float32) for a in (pass_embed, ln1_gain, ln1_bias, qkv_weight, out_weight, out_bias, ln2_gain, ln2_bias, fc1_weight, fc1_bias, fc2_weight, fc2_bias)))
    inputs_all = tokens.astype(jnp.float32)
    goal_all = teacher.astype(jnp.float32)
    cont_index = jnp.arange(CONTS).astype(jnp.int32)
    owners = cont_group.astype(jnp.int32) + cont_index // (GROUPS_DP * NC) * GROUPS_DP
    members = jnp.argsort(owners, stable=True).astype(jnp.int32).reshape(GROUPS, NC)
    cont_shard = (cont_index // (GPS * NC)).astype(jnp.int32)
    cont_local = (GPS * P_SIZE + cont_index % (GPS * NC) * CL).astype(jnp.int32)
    group_index = jnp.arange(GROUPS).astype(jnp.int32)

    def step(carried, group):
        grads, grad_rows, finals, total = carried
        prompt_local = group % GPS * P_SIZE + jnp.arange(P_SIZE).astype(jnp.int32)
        prompt_rows = place_rows(group // GPS, prompt_local)
        chosen = members[group]
        local_rows = cont_local[chosen][:, None] + jnp.arange(CL).astype(jnp.int32)[None, :]
        cont_rows = place_rows(cont_shard[chosen][:, None], local_rows).reshape(NC * CL)
        row_index = jnp.concatenate([prompt_rows, cont_rows]).astype(jnp.int32)
        goal = goal_all[row_index]
        (final, half), back = jax.vjp(lambda prm, inp: group_loss(prm, inp, goal), params, inputs_all[row_index])
        grad_params, grad_inputs = back((jnp.zeros_like(final), jnp.ones_like(half)))
        grads = jax.tree.map(lambda a, b: a + b, grads, grad_params)
        grad_rows = grad_rows.at[row_index].set(grad_inputs)
        finals = finals.at[row_index].set(final)
        return ((grads, grad_rows, finals, total + half), None)
    start = (jax.tree.map(jnp.zeros_like, params), jnp.zeros_like(inputs_all), jnp.zeros_like(inputs_all), jnp.zeros((), jnp.float32))
    (grads, grad_rows, finals, total), _ = lax.scan(step, start, group_index)
    loss = (2.0 * total / (D * token_count[0].astype(jnp.float32))).reshape(1)
    return (finals.astype(jnp.bfloat16), loss, grad_rows, grads[0], grads[1], grads[2], grads[3], grads[4], grads[5], grads[6], grads[7], grads[8], grads[9], grads[10], grads[11])
```

```python
from functools import partial

import jax
import jax.numpy as jnp
from jax import lax
from jax.experimental import pallas as pl
from jax.experimental.pallas import tpu as pltpu
from jax.sharding import PartitionSpec as P

D = 768
HD = 64
FF = 3072
P_SIZE = 1024
CL = 128
QROWS = 512
eps = 1e-05
negative = -1e30
BF = jnp.bfloat16
F32 = jnp.float32


def nt(a, b):
    return lax.dot_general(a, b, (((1,), (1,)), ((), ())), preferred_element_type=F32)


def nn(a, b):
    return lax.dot_general(a, b, (((1,), (0,)), ((), ())), preferred_element_type=F32)


def tn(a, b):
    return lax.dot_general(a, b, (((0,), (0,)), ((), ())), preferred_element_type=F32)


def att_fwd_kernel(grp_ref, z_ref, q_ref, kvo_ref, kvp_ref, o_ref, lse_ref):
    j = pl.program_id(1)
    row0 = pl.multiple_of(grp_ref[j] * P_SIZE, P_SIZE)
    z = z_ref[0]
    lane = lax.broadcasted_iota(jnp.int32, (CL, 128), 1)
    low = lane < 64
    zero = jnp.zeros((CL, 128), BF)
    q = q_ref[...]
    q_parts = (jnp.where(low, zero, q), jnp.where(low, q, zero))

    @pl.when(z >= 2)
    def _():
        row = lax.broadcasted_iota(jnp.int32, (CL, CL), 0)
        near_ok = lax.broadcasted_iota(jnp.int32, (CL, CL), 1) <= row
        mixes, sums = [], []
        for h in range(2):
            cols = slice(128 * h, 128 * h + 128)
            kv = kvp_ref[pl.ds(row0, P_SIZE), cols]
            kvo = kvo_ref[:, cols]
            far = nt(q_parts[h], kv)
            near = jnp.where(near_ok, nt(q_parts[h], kvo), negative)
            top = jnp.maximum(
                jnp.max(far, axis=1, keepdims=True), jnp.max(near, axis=1, keepdims=True)
            )
            far = jnp.exp(far - top)
            near = jnp.exp(near - top)
            total = jnp.sum(far, axis=1, keepdims=True) + jnp.sum(near, axis=1, keepdims=True)
            mix = nn(far.astype(BF), kv) + nn(near.astype(BF), kvo)
            mixes.append(mix / total)
            sums.append(jnp.broadcast_to(top + jnp.log(total), (CL, 128)))
        o_ref[...] = jnp.where(low, mixes[0], mixes[1]).astype(BF)
        lse_ref[...] = jnp.where(low, sums[0], sums[1])

    @pl.when(z < 2)
    def _():
        limit = z * QROWS + (j % (QROWS // CL)) * CL
        row = lax.broadcasted_iota(jnp.int32, (CL, P_SIZE), 0)
        key = lax.broadcasted_iota(jnp.int32, (CL, P_SIZE), 1)
        allowed = key - row <= limit
        mixes, sums = [], []
        for h in range(2):
            cols = slice(128 * h, 128 * h + 128)
            kv = kvp_ref[pl.ds(row0, P_SIZE), cols]
            far = jnp.where(allowed, nt(q_parts[h], kv), negative)
            top = jnp.max(far, axis=1, keepdims=True)
            far = jnp.exp(far - top)
            total = jnp.sum(far, axis=1, keepdims=True)
            mix = nn(far.astype(BF), kv)
            mixes.append(mix / total)
            sums.append(jnp.broadcast_to(top + jnp.log(total), (CL, 128)))
        o_ref[...] = jnp.where(low, mixes[0], mixes[1]).astype(BF)
        lse_ref[...] = jnp.where(low, sums[0], sums[1])


def attend(grp, z, q, kvo, kvp):
    rows = q.shape[0]
    pairs = q.shape[1] // 128
    groups_rows = kvp.shape[0]
    return pl.pallas_call(
        att_fwd_kernel,
        name="att_fwd",
        grid_spec=pltpu.PrefetchScalarGridSpec(
            num_scalar_prefetch=2,
            grid=(pairs, rows // CL),
            in_specs=[
                pl.BlockSpec((CL, 128), lambda p, j, *_: (j, p)),
                pl.BlockSpec((CL, 256), lambda p, j, *_: (j, p)),
                pl.BlockSpec((groups_rows, 256), lambda p, j, *_: (0, p)),
            ],
            out_specs=[
                pl.BlockSpec((CL, 128), lambda p, j, *_: (j, p)),
                pl.BlockSpec((CL, 128), lambda p, j, *_: (j, p)),
            ],
        ),
        out_shape=[
            jax.ShapeDtypeStruct((rows, pairs * 128), BF),
            jax.ShapeDtypeStruct((rows, pairs * 128), F32),
        ],
        compiler_params=pltpu.CompilerParams(vmem_limit_bytes=40 << 20),
        cost_estimate=pl.CostEstimate(
            flops=4 * rows * P_SIZE * 128 * pairs * 2,
            bytes_accessed=groups_rows * 512 * pairs,
            transcendentals=rows * P_SIZE * pairs * 2,
        ),
    )(grp, z, q, kvo, kvp)


def att_bwd_kernel(
    grp_ref, z_ref, q_ref, gm_ref, lse_ref, kvo_ref, kvp_ref, dq_ref, dkvo_ref, dkvp_ref, acc
):
    j = pl.program_id(1)
    row0 = pl.multiple_of(grp_ref[j] * P_SIZE, P_SIZE)
    z = z_ref[0]
    low = lax.broadcasted_iota(jnp.int32, (CL, 128), 1) < 64
    zero = jnp.zeros((CL, 128), BF)
    q = q_ref[...]
    gm = gm_ref[...]
    stacks = (
        jnp.concatenate([jnp.where(low, zero, q), jnp.where(low, gm, zero)], axis=0),
        jnp.concatenate([jnp.where(low, q, zero), jnp.where(low, zero, gm)], axis=0),
    )

    @pl.when(j == 0)
    def _():
        acc[...] = jnp.zeros_like(acc)

    @pl.when(z >= 2)
    def _():
        row = lax.broadcasted_iota(jnp.int32, (CL, CL), 0)
        near_ok = row <= lax.broadcasted_iota(jnp.int32, (CL, CL), 1)
        dqs = []
        for h in range(2):
            cols = slice(128 * h, 128 * h + 128)
            kv = kvp_ref[pl.ds(row0, P_SIZE), cols]
            kvo = kvo_ref[:, cols]
            lse = lse_ref[0, 0, h : h + 1, :]
            far = nt(kv, stacks[h])
            near = nt(kvo, stacks[h])
            pf = jnp.exp(far[:, :CL] - lse)
            pn = jnp.where(near_ok, jnp.exp(near[:, :CL] - lse), 0.0)
            df = far[:, CL:]
            dn = near[:, CL:]
            inner = jnp.sum(pf * df, axis=0, keepdims=True) + jnp.sum(
                pn * dn, axis=0, keepdims=True
            )
            sf = (pf * (df - inner)).astype(BF)
            sn = (pn * (dn - inner)).astype(BF)
            acc[pl.ds(row0, P_SIZE), cols] += nn(
                jnp.concatenate([sf, pf.astype(BF)], axis=1), stacks[h]
            )
            dkvo_ref[:, cols] = nn(
                jnp.concatenate([sn, pn.astype(BF)], axis=1), stacks[h]
            ).astype(BF)
            dqs.append(tn(sf, kv) + tn(sn, kvo))
        dq_ref[...] = (jnp.where(low, dqs[1], dqs[0]) * 0.125).astype(BF)

    @pl.when(z < 2)
    def _():
        limit = z * QROWS + (j % (QROWS // CL)) * CL
        key = lax.broadcasted_iota(jnp.int32, (P_SIZE, CL), 0)
        row = lax.broadcasted_iota(jnp.int32, (P_SIZE, CL), 1)
        allowed = key - row <= limit
        dqs = []
        for h in range(2):
            cols = slice(128 * h, 128 * h + 128)
            kv = kvp_ref[pl.ds(row0, P_SIZE), cols]
            lse = lse_ref[0, 0, h : h + 1, :]
            far = nt(kv, stacks[h])
            pf = jnp.where(allowed, jnp.exp(far[:, :CL] - lse), 0.0)
            df = far[:, CL:]
            inner = jnp.sum(pf * df, axis=0, keepdims=True)
            sf = (pf * (df - inner)).astype(BF)
            acc[pl.ds(row0, P_SIZE), cols] += nn(
                jnp.concatenate([sf, pf.astype(BF)], axis=1), stacks[h]
            )
            dqs.append(tn(sf, kv))
        dkvo_ref[...] = jnp.zeros_like(dkvo_ref)
        dq_ref[...] = (jnp.where(low, dqs[1], dqs[0]) * 0.125).astype(BF)

    @pl.when(j == pl.num_programs(1) - 1)
    def _():
        dkvp_ref[...] = acc[...].astype(BF)


def attend_back(grp, z, q, gm, lse, kvo, kvp):
    rows = q.shape[0]
    pairs = q.shape[1] // 128
    groups_rows = kvp.shape[0]
    return pl.pallas_call(
        att_bwd_kernel,
        name="att_bwd",
        grid_spec=pltpu.PrefetchScalarGridSpec(
            num_scalar_prefetch=2,
            grid=(pairs, rows // CL),
            in_specs=[
                pl.BlockSpec((CL, 128), lambda p, j, *_: (j, p)),
                pl.BlockSpec((CL, 128), lambda p, j, *_: (j, p)),
                pl.BlockSpec((1, 1, 2, 128), lambda p, j, *_: (p, j, 0, 0)),
                pl.BlockSpec((CL, 256), lambda p, j, *_: (j, p)),
                pl.BlockSpec((groups_rows, 256), lambda p, j, *_: (0, p)),
            ],
            out_specs=[
                pl.BlockSpec((CL, 128), lambda p, j, *_: (j, p)),
                pl.BlockSpec((CL, 256), lambda p, j, *_: (j, p)),
                pl.BlockSpec((groups_rows, 256), lambda p, j, *_: (0, p)),
            ],
            scratch_shapes=[pltpu.VMEM((groups_rows, 256), F32)],
        ),
        out_shape=[
            jax.ShapeDtypeStruct((rows, pairs * 128), BF),
            jax.ShapeDtypeStruct((rows, pairs * 256), BF),
            jax.ShapeDtypeStruct((groups_rows, pairs * 256), BF),
        ],
        compiler_params=pltpu.CompilerParams(vmem_limit_bytes=48 << 20),
        cost_estimate=pl.CostEstimate(
            flops=10 * rows * P_SIZE * 128 * pairs * 2,
            bytes_accessed=groups_rows * 1024 * pairs,
            transcendentals=rows * P_SIZE * pairs * 2,
        ),
    )(grp, z, q, gm, lse, kvo, kvp)


def norm(hidden, gain, shift):
    center = jnp.mean(hidden, axis=1, keepdims=True)
    offset = hidden - center
    factor = lax.rsqrt(jnp.mean(offset * offset, axis=1, keepdims=True) + eps)
    unit = offset * factor
    return unit * gain + shift, unit, factor


def norm_back(grad, gain, unit, factor):
    grad_unit = grad * gain
    first = jnp.mean(grad_unit, axis=1, keepdims=True)
    second = jnp.mean(grad_unit * unit, axis=1, keepdims=True)
    grad_in = factor * (grad_unit - first - unit * second)
    return grad_in, jnp.sum(grad * unit, axis=0), jnp.sum(grad, axis=0)


def head_layout(blocks):
    chunks = blocks.transpose(1, 0, 2).reshape(D, 6, 3, HD)
    q_list, kv_list = [], []
    for pair in range(3):
        a, b = 2 * pair, 2 * pair + 1
        q_list += [chunks[:, b, 0], chunks[:, a, 0]]
        kv_list += [chunks[:, a, 2], chunks[:, a, 1], chunks[:, b, 1], chunks[:, b, 2]]
    return jnp.concatenate(q_list, axis=1), jnp.concatenate(kv_list, axis=1)


def head_layout_back(grad_q, grad_kv):
    qc = grad_q.reshape(D, 3, 2, HD)
    kc = grad_kv.reshape(D, 3, 4, HD)
    pieces = []
    for pair in range(3):
        pieces += [qc[:, pair, 1], kc[:, pair, 1], kc[:, pair, 0]]
        pieces += [qc[:, pair, 0], kc[:, pair, 2], kc[:, pair, 3]]
    whole = jnp.concatenate(pieces, axis=1)
    return whole.reshape(D, 2, 576).transpose(1, 0, 2)


def on_device(
    tokens,
    teacher,
    pass_embed,
    ln1_gain,
    ln1_bias,
    qkv_weight,
    out_weight,
    out_bias,
    ln2_gain,
    ln2_bias,
    fc1_weight,
    fc1_bias,
    fc2_weight,
    fc2_bias,
    cont_group,
    token_count,
):
    n_gr = lax.axis_size("gr")
    n_gc = lax.axis_size("gc")
    z = lax.axis_index("gr")
    g = lax.axis_index("gc")
    c = g % 2
    y = g // 2
    swap_core = [(i, i ^ 1) for i in range(n_gc)]
    swap_y = [(i, i ^ 2) for i in range(n_gc)]

    vectors = jnp.stack(
        [pass_embed, ln1_gain, ln1_bias, out_bias, ln2_gain, ln2_bias, fc2_bias]
    )
    vectors = lax.all_gather(vectors, "gr", axis=1, tiled=True).astype(F32)
    embed, gain1, shift1, b_out, gain2, shift2, b_down = [vectors[i] for i in range(7)]
    b_up = lax.all_gather(fc1_bias, "gc", axis=0, tiled=True).astype(F32)
    owners = lax.all_gather(cont_group, "gr", axis=0, tiled=True)
    owners = owners.reshape(n_gc, 2, 4)
    mine = lax.dynamic_slice(owners, (2 * y, jnp.maximum(z - 2, 0), 0), (2, 1, 4)).reshape(8)
    own_groups = jnp.repeat(2 * y + jnp.arange(2), 4)
    grp = jnp.where(z < 2, own_groups, mine).astype(jnp.int32)
    z_arr = z.astype(jnp.int32).reshape(1)

    hidden = tokens.astype(F32) + embed
    normed1, unit1, factor1 = norm(hidden, gain1, shift1)
    n1 = normed1.astype(BF)

    w_other = lax.ppermute(qkv_weight, "gc", swap_y)
    w_pair = jnp.where(y == 0, jnp.stack([qkv_weight, w_other]), jnp.stack([w_other, qkv_weight]))
    w_qkv = lax.all_gather(w_pair, "gr", axis=1, tiled=True)
    w_q, w_kv = head_layout(w_qkv)

    n1_other = lax.ppermute(n1, "gc", swap_core)
    n1_chip = jnp.where(
        c == 0, jnp.concatenate([n1, n1_other]), jnp.concatenate([n1_other, n1])
    )
    n1_col = lax.all_gather(n1, "gr", axis=0, tiled=True)[:P_SIZE]
    n1_prompt = lax.all_gather(n1_col, "gc", axis=0, tiled=True)

    w_out = lax.all_gather(out_weight, ("gc", "gr"))
    w_up = lax.all_gather(fc1_weight, ("gc", "gr")).reshape(n_gc, D, FF // n_gc)
    w_down = lax.all_gather(fc2_weight, ("gc", "gr")).reshape(n_gc, D, FF // n_gc)
    w_out = w_out.reshape(n_gc, n_gr, 192, 192).transpose(0, 2, 1, 3).reshape(D, D)

    kvp = nn(n1_prompt, w_kv).astype(BF)
    kvo = nn(n1_chip, w_kv).astype(BF)
    q = (nn(n1_chip, w_q) * 0.125).astype(BF)
    mixed_heads, lse = attend(grp, z_arr, q, kvo, kvp)
    lse_rows = lse[:, ::64].reshape(8, CL, 3, 2).transpose(2, 0, 3, 1)

    halves = mixed_heads.reshape(2, QROWS, 2, 192)
    keep = lax.dynamic_index_in_dim(halves, c, 0, keepdims=False)
    give = lax.dynamic_index_in_dim(halves, 1 - c, 0, keepdims=False)
    take = lax.ppermute(give, "gc", swap_core)
    mixed = jnp.where(c == 0, jnp.stack([keep, take], axis=2), jnp.stack([take, keep], axis=2))
    mixed = mixed.reshape(QROWS, D)

    hidden2 = hidden + nn(mixed, w_out) + b_out
    normed2, unit2, factor2 = norm(hidden2, gain2, shift2)
    n2 = normed2.astype(BF)
    pre = lax.dot_general(n2, w_up, (((1,), (1,)), ((), ())), preferred_element_type=F32)
    pre = pre.reshape(QROWS, FF) + b_up
    active, gelu_back = jax.vjp(partial(jax.nn.gelu, approximate=True), pre)
    act = active.astype(BF)
    act_blocks = act.reshape(QROWS, n_gc, FF // n_gc)
    final = (
        hidden2
        + lax.dot_general(
            act_blocks, w_down, (((1, 2), (0, 2)), ((), ())), preferred_element_type=F32
        )
        + b_down
    )
    grad_final = final - teacher.astype(F32)
    squared = jnp.sum(grad_final * grad_final)
    gb = grad_final.astype(BF)
    grad_b_down = jnp.sum(gb, axis=0, dtype=F32)
    grad_active = lax.dot_general(
        gb, w_down, (((1,), (1,)), ((), ())), preferred_element_type=F32
    ).reshape(QROWS, FF)
    grad_w_down = jnp.einsum("td,tgf->gdf", gb, act_blocks, preferred_element_type=F32)
    (grad_pre,) = gelu_back(grad_active)
    gp = grad_pre.astype(BF)
    gp_blocks = gp.reshape(QROWS, n_gc, FF // n_gc)
    grad_b_up = jnp.sum(gp, axis=0, dtype=F32)
    grad_w_up = jnp.einsum("td,tgf->gdf", n2, gp_blocks, preferred_element_type=F32)
    grad_n2 = lax.dot_general(
        gp_blocks, w_up, (((1, 2), (0, 2)), ((), ())), preferred_element_type=F32
    )
    back2, grad_gain2, grad_shift2 = norm_back(grad_n2, gain2, unit2, factor2)
    grad_h2 = grad_final + back2
    ga = grad_h2.astype(BF)
    grad_b_out = jnp.sum(ga, axis=0, dtype=F32)
    grad_w_out = tn(mixed, ga)
    gm = nt(ga, w_out).astype(BF)

    gm_blocks = gm.reshape(QROWS, 2, 2, 192)
    gm_keep = lax.dynamic_index_in_dim(gm_blocks, c, 2, keepdims=False)
    gm_give = lax.dynamic_index_in_dim(gm_blocks, 1 - c, 2, keepdims=False)
    gm_take = lax.ppermute(gm_give, "gc", swap_core)
    gm_chip = jnp.where(c == 0, jnp.stack([gm_keep, gm_take]), jnp.stack([gm_take, gm_keep]))
    gm_chip = gm_chip.reshape(2 * QROWS, 384)

    def scatter16(blocks):
        part = lax.psum_scatter(
            blocks.astype(BF), ("gc", "gr"), scatter_dimension=0, tiled=True
        )
        return lax.psum(part, "dp").astype(F32)

    out_w_down = scatter16(grad_w_down.reshape(n_gc * n_gr * 192, 768))
    out_w_up = scatter16(grad_w_up.reshape(n_gc * n_gr * 192, 768))
    out_w_out = scatter16(
        grad_w_out.reshape(n_gc, 192, n_gr, 192).transpose(0, 2, 1, 3).reshape(-1, 192)
    )

    dq, dkvo, dkvp = attend_back(grp, z_arr, q, gm_chip, lse_rows, kvo, kvp)

    part_prompt = nt(dkvp, w_kv).astype(BF)
    back_prompt = lax.psum_scatter(part_prompt, "gc", scatter_dimension=0, tiled=True)
    back_prompt = lax.psum_scatter(
        jnp.concatenate([back_prompt, jnp.zeros_like(back_prompt)]),
        "gr",
        scatter_dimension=0,
        tiled=True,
    ).astype(F32)
    part_chip = (nt(dq, w_q) + nt(dkvo, w_kv)).reshape(2, QROWS, D)
    part_keep = lax.dynamic_index_in_dim(part_chip, c, 0, keepdims=False)
    part_give = lax.dynamic_index_in_dim(part_chip, 1 - c, 0, keepdims=False)
    part_take = lax.ppermute(part_give.astype(BF), "gc", swap_core).astype(F32)
    grad_n1 = part_keep + part_take + back_prompt

    grad_kv = tn(n1_prompt, dkvp) + tn(n1_chip, dkvo)
    grad_q = tn(n1_chip, dq)
    grad_qkv = head_layout_back(grad_q, grad_kv)
    qkv_keep = lax.dynamic_index_in_dim(grad_qkv, y, 0, keepdims=False)
    qkv_give = lax.dynamic_index_in_dim(grad_qkv, 1 - y, 0, keepdims=False)
    qkv_take = lax.ppermute(qkv_give.astype(BF), "gc", swap_y).astype(F32)
    out_w_qkv = lax.psum_scatter(
        (qkv_keep + qkv_take).astype(BF), "gr", scatter_dimension=0, tiled=True
    )
    out_w_qkv = lax.psum(out_w_qkv, "dp").astype(F32)

    back1, grad_gain1, grad_shift1 = norm_back(grad_n1, gain1, unit1, factor1)
    input_grad = grad_h2 + back1
    sums = jnp.concatenate(
        [
            jnp.sum(input_grad, axis=0),
            grad_gain1,
            grad_shift1,
            grad_gain2,
            grad_shift2,
            grad_b_out,
            grad_b_down,
            grad_b_up,
            jnp.broadcast_to(squared, (128,)),
        ]
    )
    sums = lax.psum(sums, ("dp", "gr", "gc"))
    loss = (sums[-1] / (D * token_count[0].astype(F32))).reshape(1)
    rows = sums[: 7 * D].reshape(7, n_gr, D // n_gr)
    rows = lax.dynamic_index_in_dim(rows, z, 1, keepdims=False)
    up = lax.dynamic_index_in_dim(
        sums[7 * D : 7 * D + FF].reshape(n_gc, FF // n_gc), g, 0, keepdims=False
    )
    return (
        final.astype(BF),
        loss,
        input_grad,
        rows[0],
        rows[1],
        rows[2],
        out_w_qkv,
        out_w_out,
        rows[5],
        rows[3],
        rows[4],
        out_w_up,
        up,
        out_w_down,
        rows[6],
    )


def solution(mesh):
    rows = P(("dp", "gr", "gc"), None)
    in_specs = (
        rows,
        rows,
        P("gr"),
        P("gr"),
        P("gr"),
        P("gr", "gc"),
        P("gc", "gr"),
        P("gr"),
        P("gr"),
        P("gr"),
        P("gr", "gc"),
        P("gc"),
        P("gr", "gc"),
        P("gr"),
        P(("dp", "gr")),
        P(),
    )
    out_specs = (
        rows,
        P(),
        rows,
        P("gr"),
        P("gr"),
        P("gr"),
        P("gr", "gc"),
        P("gc", "gr"),
        P("gr"),
        P("gr"),
        P("gr"),
        P("gr", "gc"),
        P("gc"),
        P("gr", "gc"),
        P("gr"),
    )
    return jax.shard_map(
        on_device, mesh=mesh, in_specs=in_specs, out_specs=out_specs, check_vma=False
    )
```

```python
from functools import partial

import jax
import jax.numpy as jnp
from jax import lax
from jax.experimental import pallas as pl
from jax.experimental.pallas import tpu as pltpu
from jax.sharding import PartitionSpec as P

D = 768
HD = 64
FF = 3072
P_SIZE = 1024
CL = 128
QROWS = 512
eps = 1e-05
negative = -1e30
BF = jnp.bfloat16
F32 = jnp.float32


def nt(a, b):
    return lax.dot_general(a, b, (((1,), (1,)), ((), ())), preferred_element_type=F32)


def nn(a, b):
    return lax.dot_general(a, b, (((1,), (0,)), ((), ())), preferred_element_type=F32)


def tn(a, b):
    return lax.dot_general(a, b, (((0,), (0,)), ((), ())), preferred_element_type=F32)


def att_fwd_kernel(grp_ref, z_ref, q_ref, kvo_ref, kvp_ref, o_ref, lse_ref):
    j = pl.program_id(1)
    row0 = pl.multiple_of(grp_ref[j] * P_SIZE, P_SIZE)
    z = z_ref[0]
    lane = lax.broadcasted_iota(jnp.int32, (CL, 128), 1)
    low = lane < 64
    zero = jnp.zeros((CL, 128), BF)
    q = q_ref[...]
    q_parts = (jnp.where(low, zero, q), jnp.where(low, q, zero))

    @pl.when(z >= 2)
    def _():
        row = lax.broadcasted_iota(jnp.int32, (CL, CL), 0)
        near_ok = lax.broadcasted_iota(jnp.int32, (CL, CL), 1) <= row
        mixes, sums = [], []
        for h in range(2):
            cols = slice(128 * h, 128 * h + 128)
            kv = kvp_ref[pl.ds(row0, P_SIZE), cols]
            kvo = kvo_ref[:, cols]
            far = nt(q_parts[h], kv)
            near = jnp.where(near_ok, nt(q_parts[h], kvo), negative)
            top = jnp.maximum(
                jnp.max(far, axis=1, keepdims=True), jnp.max(near, axis=1, keepdims=True)
            )
            far = jnp.exp(far - top)
            near = jnp.exp(near - top)
            total = jnp.sum(far, axis=1, keepdims=True) + jnp.sum(near, axis=1, keepdims=True)
            mix = nn(far.astype(BF), kv) + nn(near.astype(BF), kvo)
            mixes.append(mix / total)
            sums.append(jnp.broadcast_to(top + jnp.log(total), (CL, 128)))
        o_ref[...] = jnp.where(low, mixes[0], mixes[1]).astype(BF)
        lse_ref[...] = jnp.where(low, sums[0], sums[1])

    @pl.when(z < 2)
    def _():
        limit = z * QROWS + (j % (QROWS // CL)) * CL
        row = lax.broadcasted_iota(jnp.int32, (CL, P_SIZE), 0)
        key = lax.broadcasted_iota(jnp.int32, (CL, P_SIZE), 1)
        allowed = key - row <= limit
        mixes, sums = [], []
        for h in range(2):
            cols = slice(128 * h, 128 * h + 128)
            kv = kvp_ref[pl.ds(row0, P_SIZE), cols]
            far = jnp.where(allowed, nt(q_parts[h], kv), negative)
            top = jnp.max(far, axis=1, keepdims=True)
            far = jnp.exp(far - top)
            total = jnp.sum(far, axis=1, keepdims=True)
            mix = nn(far.astype(BF), kv)
            mixes.append(mix / total)
            sums.append(jnp.broadcast_to(top + jnp.log(total), (CL, 128)))
        o_ref[...] = jnp.where(low, mixes[0], mixes[1]).astype(BF)
        lse_ref[...] = jnp.where(low, sums[0], sums[1])


def attend(grp, z, q, kvo, kvp):
    rows = q.shape[0]
    pairs = q.shape[1] // 128
    groups_rows = kvp.shape[0]
    return pl.pallas_call(
        att_fwd_kernel,
        name="att_fwd",
        grid_spec=pltpu.PrefetchScalarGridSpec(
            num_scalar_prefetch=2,
            grid=(pairs, rows // CL),
            in_specs=[
                pl.BlockSpec((CL, 128), lambda p, j, *_: (j, p)),
                pl.BlockSpec((CL, 256), lambda p, j, *_: (j, p)),
                pl.BlockSpec((groups_rows, 256), lambda p, j, *_: (0, p)),
            ],
            out_specs=[
                pl.BlockSpec((CL, 128), lambda p, j, *_: (j, p)),
                pl.BlockSpec((CL, 128), lambda p, j, *_: (j, p)),
            ],
        ),
        out_shape=[
            jax.ShapeDtypeStruct((rows, pairs * 128), BF),
            jax.ShapeDtypeStruct((rows, pairs * 128), F32),
        ],
        compiler_params=pltpu.CompilerParams(vmem_limit_bytes=40 << 20),
        cost_estimate=pl.CostEstimate(
            flops=4 * rows * P_SIZE * 128 * pairs * 2,
            bytes_accessed=groups_rows * 512 * pairs,
            transcendentals=rows * P_SIZE * pairs * 2,
        ),
    )(grp, z, q, kvo, kvp)


def att_bwd_kernel(
    grp_ref, z_ref, q_ref, gm_ref, lse_ref, kvo_ref, kvp_ref, dq_ref, dkvo_ref, dkvp_ref, acc
):
    j = pl.program_id(1)
    row0 = pl.multiple_of(grp_ref[j] * P_SIZE, P_SIZE)
    z = z_ref[0]
    low = lax.broadcasted_iota(jnp.int32, (CL, 128), 1) < 64
    zero = jnp.zeros((CL, 128), BF)
    q = q_ref[...]
    gm = gm_ref[...]
    stacks = (
        jnp.concatenate([jnp.where(low, zero, q), jnp.where(low, gm, zero)], axis=0),
        jnp.concatenate([jnp.where(low, q, zero), jnp.where(low, zero, gm)], axis=0),
    )

    @pl.when(j == 0)
    def _():
        acc[...] = jnp.zeros_like(acc)

    @pl.when(z >= 2)
    def _():
        row = lax.broadcasted_iota(jnp.int32, (CL, CL), 0)
        near_ok = row <= lax.broadcasted_iota(jnp.int32, (CL, CL), 1)
        dqs = []
        for h in range(2):
            cols = slice(128 * h, 128 * h + 128)
            kv = kvp_ref[pl.ds(row0, P_SIZE), cols]
            kvo = kvo_ref[:, cols]
            lse = lse_ref[0, 0, h : h + 1, :]
            far = nt(kv, stacks[h])
            near = nt(kvo, stacks[h])
            pf = jnp.exp(far[:, :CL] - lse)
            pn = jnp.where(near_ok, jnp.exp(near[:, :CL] - lse), 0.0)
            df = far[:, CL:]
            dn = near[:, CL:]
            inner = jnp.sum(pf * df, axis=0, keepdims=True) + jnp.sum(
                pn * dn, axis=0, keepdims=True
            )
            sf = (pf * (df - inner)).astype(BF)
            sn = (pn * (dn - inner)).astype(BF)
            acc[pl.ds(row0, P_SIZE), cols] += nn(
                jnp.concatenate([sf, pf.astype(BF)], axis=1), stacks[h]
            )
            dkvo_ref[:, cols] = nn(
                jnp.concatenate([sn, pn.astype(BF)], axis=1), stacks[h]
            ).astype(BF)
            dqs.append(tn(sf, kv) + tn(sn, kvo))
        dq_ref[...] = (jnp.where(low, dqs[1], dqs[0]) * 0.125).astype(BF)

    @pl.when(z < 2)
    def _():
        limit = z * QROWS + (j % (QROWS // CL)) * CL
        key = lax.broadcasted_iota(jnp.int32, (P_SIZE, CL), 0)
        row = lax.broadcasted_iota(jnp.int32, (P_SIZE, CL), 1)
        allowed = key - row <= limit
        dqs = []
        for h in range(2):
            cols = slice(128 * h, 128 * h + 128)
            kv = kvp_ref[pl.ds(row0, P_SIZE), cols]
            lse = lse_ref[0, 0, h : h + 1, :]
            far = nt(kv, stacks[h])
            pf = jnp.where(allowed, jnp.exp(far[:, :CL] - lse), 0.0)
            df = far[:, CL:]
            inner = jnp.sum(pf * df, axis=0, keepdims=True)
            sf = (pf * (df - inner)).astype(BF)
            acc[pl.ds(row0, P_SIZE), cols] += nn(
                jnp.concatenate([sf, pf.astype(BF)], axis=1), stacks[h]
            )
            dqs.append(tn(sf, kv))
        dkvo_ref[...] = jnp.zeros_like(dkvo_ref)
        dq_ref[...] = (jnp.where(low, dqs[1], dqs[0]) * 0.125).astype(BF)

    @pl.when(j == pl.num_programs(1) - 1)
    def _():
        dkvp_ref[...] = acc[...].astype(BF)


def attend_back(grp, z, q, gm, lse, kvo, kvp):
    rows = q.shape[0]
    pairs = q.shape[1] // 128
    groups_rows = kvp.shape[0]
    return pl.pallas_call(
        att_bwd_kernel,
        name="att_bwd",
        grid_spec=pltpu.PrefetchScalarGridSpec(
            num_scalar_prefetch=2,
            grid=(pairs, rows // CL),
            in_specs=[
                pl.BlockSpec((CL, 128), lambda p, j, *_: (j, p)),
                pl.BlockSpec((CL, 128), lambda p, j, *_: (j, p)),
                pl.BlockSpec((1, 1, 2, 128), lambda p, j, *_: (p, j, 0, 0)),
                pl.BlockSpec((CL, 256), lambda p, j, *_: (j, p)),
                pl.BlockSpec((groups_rows, 256), lambda p, j, *_: (0, p)),
            ],
            out_specs=[
                pl.BlockSpec((CL, 128), lambda p, j, *_: (j, p)),
                pl.BlockSpec((CL, 256), lambda p, j, *_: (j, p)),
                pl.BlockSpec((groups_rows, 256), lambda p, j, *_: (0, p)),
            ],
            scratch_shapes=[pltpu.VMEM((groups_rows, 256), F32)],
        ),
        out_shape=[
            jax.ShapeDtypeStruct((rows, pairs * 128), BF),
            jax.ShapeDtypeStruct((rows, pairs * 256), BF),
            jax.ShapeDtypeStruct((groups_rows, pairs * 256), BF),
        ],
        compiler_params=pltpu.CompilerParams(vmem_limit_bytes=48 << 20),
        cost_estimate=pl.CostEstimate(
            flops=10 * rows * P_SIZE * 128 * pairs * 2,
            bytes_accessed=groups_rows * 1024 * pairs,
            transcendentals=rows * P_SIZE * pairs * 2,
        ),
    )(grp, z, q, gm, lse, kvo, kvp)


MESH = pl.DeviceIdType.MESH


def places():
    x = lax.axis_index("dp")
    z = lax.axis_index("gr")
    g = lax.axis_index("gc")
    return x, z, g, g // 2, g % 2


def greet(partners):
    barrier = pltpu.get_barrier_semaphore()
    for partner in partners:
        pl.semaphore_signal(barrier, inc=1, device_id=partner, device_id_type=MESH)
    pl.semaphore_wait(barrier, len(partners))


def all_partners():
    x, z, g, y, c = places()
    by_z = [{"gr": lax.rem(z + step, 4)} for step in (1, 2, 3)]
    return [{"gc": g ^ 1}, {"gc": g ^ 2}, {"dp": x ^ 1}] + by_z


def send(src, dst, sems, slot, target):
    return pltpu.make_async_remote_copy(
        src_ref=src,
        dst_ref=dst,
        send_sem=sems[0].at[slot],
        recv_sem=sems[1].at[slot],
        device_id=target,
        device_id_type=MESH,
    )


def add_into(dst, left, right):
    dst[...] = (left[...].astype(F32) + right[...].astype(F32)).astype(dst.dtype)


RS_SLOTS = 10


def rs_steps(grads, outs, bufs, sems, sem_own, base):
    own, ra, rb0, rb1, rc0, rc1, sc, rd, re = bufs
    x, z, g, y, c = places()
    sib, over_y, over_x = {"gc": g ^ 1}, {"gc": g ^ 2}, {"dp": x ^ 1}
    rows = grads.shape[2]
    q = rows // 4
    mine0 = pl.ds(pl.multiple_of(q * x, 16), q)
    other0 = pl.ds(pl.multiple_of(q * (1 - x), 16), q)
    mine1 = pl.ds(pl.multiple_of(2 * q + q * x, 16), q)
    other1 = pl.ds(pl.multiple_of(2 * q + q * (1 - x), 16), q)
    first = pl.ds(0, 2 * q)

    def slot(i):
        return base * RS_SLOTS + i

    loads = [
        pltpu.make_async_copy(grads.at[2 * i + c], own.at[i], sem_own.at[2 * base + i])
        for i in range(2)
    ]
    hop_a = [send(grads.at[2 * i + 1 - c], ra.at[i], sems, slot(i), sib) for i in range(2)]
    hop_b0 = send(own.at[1 - y, :, first], rb0, sems, slot(2), over_y)
    hop_b1 = send(own.at[:, :, other1], rb1, sems, slot(3), over_x)
    hop_c0 = send(own.at[y, :, other0], rc0, sems, slot(4), over_x)
    hop_c1 = send(own.at[1 - y, :, mine1], rc1, sems, slot(5), over_y)
    hop_z = [
        send(
            sc.at[lax.rem(z + step, 4)],
            rd.at[step - 1],
            sems,
            slot(5 + step),
            {"gr": lax.rem(z + step, 4)},
        )
        for step in (1, 2, 3)
    ]
    hop_d = send(sc.at[z], re, sems, slot(9), over_x)

    def start():
        for copy in loads + hop_a:
            copy.start()

    def after_a():
        for copy in loads + hop_a:
            copy.wait()

        @pl.loop(0, 8)
        def _(i):
            add_into(own.at[i // 4, i % 4], own.at[i // 4, i % 4], ra.at[i // 4, i % 4])

        hop_b0.start()
        hop_b1.start()

    def after_b():
        hop_b0.wait()
        hop_b1.wait()

        @pl.loop(0, 4)
        def _(i):
            add_into(own.at[y, i, first], own.at[y, i, first], rb0.at[i])
            add_into(own.at[0, i, mine1], own.at[0, i, mine1], rb1.at[0, i])
            add_into(own.at[1, i, mine1], own.at[1, i, mine1], rb1.at[1, i])

        hop_c0.start()
        hop_c1.start()

    def after_c():
        hop_c0.wait()
        hop_c1.wait()

        @pl.loop(0, 4)
        def _(i):
            add_into(sc.at[i, pl.ds(0, q)], own.at[y, i, mine0], rc0.at[i])
            add_into(sc.at[i, pl.ds(q, q)], own.at[y, i, mine1], rc1.at[i])

        for copy in hop_z:
            copy.start()

    def after_z():
        for copy in hop_z:
            copy.wait()
        total = sc[z].astype(F32)
        for i in range(3):
            total = total + rd[i].astype(F32)
        sc[z] = total.astype(BF)
        hop_d.start()

    def finish():
        hop_d.wait()
        outs[mine0] = sc[z, pl.ds(0, q)].astype(F32)
        outs[mine1] = sc[z, pl.ds(q, q)].astype(F32)
        outs[other0] = re[pl.ds(0, q)].astype(F32)
        outs[other1] = re[pl.ds(q, q)].astype(F32)

    return [start, after_a, after_b, after_c, after_z, finish]


def rs_scratch(shape):
    _, n_gr, rows, cols = shape
    q = rows // 4
    return [
        pltpu.VMEM((2, n_gr, rows, cols), BF),
        pltpu.VMEM((2, n_gr, rows, cols), BF),
        pltpu.VMEM((n_gr, 2 * q, cols), BF),
        pltpu.VMEM((2, n_gr, q, cols), BF),
        pltpu.VMEM((n_gr, q, cols), BF),
        pltpu.VMEM((n_gr, q, cols), BF),
        pltpu.VMEM((n_gr, 2 * q, cols), BF),
        pltpu.VMEM((3, 2 * q, cols), BF),
        pltpu.VMEM((2 * q, cols), BF),
    ]


def scatter_kernel(count, *refs):
    grads, outs = refs[:count], refs[count : 2 * count]
    bufs = refs[2 * count : 2 * count + 9 * count]
    send_sem, recv_sem, sem_own = refs[11 * count :]
    greet(all_partners())
    steps = [
        rs_steps(grads[k], outs[k], bufs[9 * k : 9 * k + 9], (send_sem, recv_sem), sem_own, k)
        for k in range(count)
    ]
    for stage in range(len(steps[0])):
        for k in range(count):
            steps[k][stage]()


def scatter_grads(grads, collective_id):
    count = len(grads)
    scratch = []
    for grad in grads:
        scratch += rs_scratch(grad.shape)
    return pl.pallas_call(
        partial(scatter_kernel, count),
        name="scatter_grads",
        in_specs=[pl.BlockSpec(memory_space=pl.ANY)] * count,
        out_specs=[pl.BlockSpec(memory_space=pltpu.VMEM)] * count,
        out_shape=[jax.ShapeDtypeStruct(grad.shape[2:], F32) for grad in grads],
        scratch_shapes=scratch
        + [
            pltpu.SemaphoreType.DMA((RS_SLOTS * count,)),
            pltpu.SemaphoreType.DMA((RS_SLOTS * count,)),
            pltpu.SemaphoreType.DMA((2 * count,)),
        ],
        compiler_params=pltpu.CompilerParams(
            collective_id=collective_id, has_side_effects=True, vmem_limit_bytes=50 << 20
        ),
    )(*grads)


def norm(hidden, gain, shift):
    center = jnp.mean(hidden, axis=1, keepdims=True)
    offset = hidden - center
    factor = lax.rsqrt(jnp.mean(offset * offset, axis=1, keepdims=True) + eps)
    unit = offset * factor
    return unit * gain + shift, unit, factor


def norm_back(grad, gain, unit, factor):
    grad_unit = grad * gain
    first = jnp.mean(grad_unit, axis=1, keepdims=True)
    second = jnp.mean(grad_unit * unit, axis=1, keepdims=True)
    grad_in = factor * (grad_unit - first - unit * second)
    return grad_in, jnp.sum(grad * unit, axis=0), jnp.sum(grad, axis=0)


def head_layout(blocks):
    chunks = blocks.transpose(1, 0, 2).reshape(D, 6, 3, HD)
    q_list, kv_list = [], []
    for pair in range(3):
        a, b = 2 * pair, 2 * pair + 1
        q_list += [chunks[:, b, 0], chunks[:, a, 0]]
        kv_list += [chunks[:, a, 2], chunks[:, a, 1], chunks[:, b, 1], chunks[:, b, 2]]
    return jnp.concatenate(q_list, axis=1), jnp.concatenate(kv_list, axis=1)


def head_layout_back(grad_q, grad_kv):
    qc = grad_q.reshape(D, 3, 2, HD)
    kc = grad_kv.reshape(D, 3, 4, HD)
    pieces = []
    for pair in range(3):
        pieces += [qc[:, pair, 1], kc[:, pair, 1], kc[:, pair, 0]]
        pieces += [qc[:, pair, 0], kc[:, pair, 2], kc[:, pair, 3]]
    whole = jnp.concatenate(pieces, axis=1)
    return whole.reshape(D, 2, 576).transpose(1, 0, 2)


def on_device(
    tokens,
    teacher,
    pass_embed,
    ln1_gain,
    ln1_bias,
    qkv_weight,
    out_weight,
    out_bias,
    ln2_gain,
    ln2_bias,
    fc1_weight,
    fc1_bias,
    fc2_weight,
    fc2_bias,
    cont_group,
    token_count,
):
    n_dp = lax.axis_size("dp")
    n_gr = lax.axis_size("gr")
    n_gc = lax.axis_size("gc")
    z = lax.axis_index("gr")
    g = lax.axis_index("gc")
    c = g % 2
    y = g // 2
    swap_core = [(i, i ^ 1) for i in range(n_gc)]
    swap_y = [(i, i ^ 2) for i in range(n_gc)]

    vectors = jnp.stack(
        [pass_embed, ln1_gain, ln1_bias, out_bias, ln2_gain, ln2_bias, fc2_bias]
    )
    vectors = lax.all_gather(vectors, "gr", axis=1, tiled=True).astype(F32)
    embed, gain1, shift1, b_out, gain2, shift2, b_down = [vectors[i] for i in range(7)]
    b_up = lax.all_gather(fc1_bias, "gc", axis=0, tiled=True).astype(F32)
    owners = lax.all_gather(cont_group, "gr", axis=0, tiled=True)
    owners = owners.reshape(n_gc, 2, 4)
    mine = lax.dynamic_slice(owners, (2 * y, jnp.maximum(z - 2, 0), 0), (2, 1, 4)).reshape(8)
    own_groups = jnp.repeat(2 * y + jnp.arange(2), 4)
    grp = jnp.where(z < 2, own_groups, mine).astype(jnp.int32)
    z_arr = z.astype(jnp.int32).reshape(1)

    hidden = tokens.astype(F32) + embed
    normed1, unit1, factor1 = norm(hidden, gain1, shift1)
    n1 = normed1.astype(BF)

    w_other = lax.ppermute(qkv_weight, "gc", swap_y)
    w_pair = jnp.where(y == 0, jnp.stack([qkv_weight, w_other]), jnp.stack([w_other, qkv_weight]))
    w_qkv = lax.all_gather(w_pair, "gr", axis=1, tiled=True)
    w_q, w_kv = head_layout(w_qkv)

    n1_other = lax.ppermute(n1, "gc", swap_core)
    n1_chip = jnp.where(
        c == 0, jnp.concatenate([n1, n1_other]), jnp.concatenate([n1_other, n1])
    )
    n1_col = lax.all_gather(n1, "gr", axis=0, tiled=True)[:P_SIZE]
    n1_prompt = lax.all_gather(n1_col, "gc", axis=0, tiled=True)

    w_out = lax.all_gather(out_weight, ("gc", "gr"))
    w_up = lax.all_gather(fc1_weight, ("gc", "gr")).reshape(n_gc, D, FF // n_gc)
    w_down = lax.all_gather(fc2_weight, ("gc", "gr")).reshape(n_gc, D, FF // n_gc)
    w_out = w_out.reshape(n_gc, n_gr, 192, 192).transpose(0, 2, 1, 3).reshape(D, D)

    kvp = nn(n1_prompt, w_kv).astype(BF)
    kvo = nn(n1_chip, w_kv).astype(BF)
    q = (nn(n1_chip, w_q) * 0.125).astype(BF)
    mixed_heads, lse = attend(grp, z_arr, q, kvo, kvp)
    lse_rows = lse[:, ::64].reshape(8, CL, 3, 2).transpose(2, 0, 3, 1)

    halves = mixed_heads.reshape(2, QROWS, 2, 192)
    keep = lax.dynamic_index_in_dim(halves, c, 0, keepdims=False)
    give = lax.dynamic_index_in_dim(halves, 1 - c, 0, keepdims=False)
    take = lax.ppermute(give, "gc", swap_core)
    mixed = jnp.where(c == 0, jnp.stack([keep, take], axis=2), jnp.stack([take, keep], axis=2))
    mixed = mixed.reshape(QROWS, D)

    hidden2 = hidden + nn(mixed, w_out) + b_out
    normed2, unit2, factor2 = norm(hidden2, gain2, shift2)
    n2 = normed2.astype(BF)
    pre = lax.dot_general(n2, w_up, (((1,), (1,)), ((), ())), preferred_element_type=F32)
    pre = pre.reshape(QROWS, FF) + b_up
    active, gelu_back = jax.vjp(partial(jax.nn.gelu, approximate=True), pre)
    act = active.astype(BF)
    act_blocks = act.reshape(QROWS, n_gc, FF // n_gc)
    final = (
        hidden2
        + lax.dot_general(
            act_blocks, w_down, (((1, 2), (0, 2)), ((), ())), preferred_element_type=F32
        )
        + b_down
    )
    grad_final = final - teacher.astype(F32)
    squared = jnp.sum(grad_final * grad_final)
    gb = grad_final.astype(BF)
    grad_b_down = jnp.sum(gb, axis=0, dtype=F32)
    grad_active = lax.dot_general(
        gb, w_down, (((1,), (1,)), ((), ())), preferred_element_type=F32
    ).reshape(QROWS, FF)
    grad_w_down = jnp.einsum("td,tgf->gdf", gb, act_blocks, preferred_element_type=F32)
    (grad_pre,) = gelu_back(grad_active)
    gp = grad_pre.astype(BF)
    gp_blocks = gp.reshape(QROWS, n_gc, FF // n_gc)
    grad_b_up = jnp.sum(gp, axis=0, dtype=F32)
    grad_w_up = jnp.einsum("td,tgf->gdf", n2, gp_blocks, preferred_element_type=F32)
    grad_n2 = lax.dot_general(
        gp_blocks, w_up, (((1, 2), (0, 2)), ((), ())), preferred_element_type=F32
    )
    back2, grad_gain2, grad_shift2 = norm_back(grad_n2, gain2, unit2, factor2)
    grad_h2 = grad_final + back2
    ga = grad_h2.astype(BF)
    grad_b_out = jnp.sum(ga, axis=0, dtype=F32)
    grad_w_out = tn(mixed, ga)
    gm = nt(ga, w_out).astype(BF)

    gm_blocks = gm.reshape(QROWS, 2, 2, 192)
    gm_keep = lax.dynamic_index_in_dim(gm_blocks, c, 2, keepdims=False)
    gm_give = lax.dynamic_index_in_dim(gm_blocks, 1 - c, 2, keepdims=False)
    gm_take = lax.ppermute(gm_give, "gc", swap_core)
    gm_chip = jnp.where(c == 0, jnp.stack([gm_keep, gm_take]), jnp.stack([gm_take, gm_keep]))
    gm_chip = gm_chip.reshape(2 * QROWS, 384)

    def scatter16(blocks):
        part = lax.psum_scatter(
            blocks.astype(BF).reshape(n_gc * n_gr * blocks.shape[2], -1),
            ("gc", "gr"),
            scatter_dimension=0,
            tiled=True,
        )
        return lax.psum(part, "dp").astype(F32)

    weight_grads = [
        grad_w_down.astype(BF).reshape(n_gc, n_gr, 192, 768),
        grad_w_up.astype(BF).reshape(n_gc, n_gr, 192, 768),
        grad_w_out.astype(BF).reshape(n_gc, 192, n_gr, 192).transpose(0, 2, 1, 3),
    ]
    if n_dp == 2:
        out_w_down, out_w_up, out_w_out = scatter_grads(weight_grads, 3)
    else:
        out_w_down, out_w_up, out_w_out = [scatter16(grad) for grad in weight_grads]

    dq, dkvo, dkvp = attend_back(grp, z_arr, q, gm_chip, lse_rows, kvo, kvp)

    part_prompt = nt(dkvp, w_kv).astype(BF)
    back_prompt = lax.psum_scatter(part_prompt, "gc", scatter_dimension=0, tiled=True)
    back_prompt = lax.psum_scatter(
        jnp.concatenate([back_prompt, jnp.zeros_like(back_prompt)]),
        "gr",
        scatter_dimension=0,
        tiled=True,
    ).astype(F32)
    part_chip = (nt(dq, w_q) + nt(dkvo, w_kv)).reshape(2, QROWS, D)
    part_keep = lax.dynamic_index_in_dim(part_chip, c, 0, keepdims=False)
    part_give = lax.dynamic_index_in_dim(part_chip, 1 - c, 0, keepdims=False)
    part_take = lax.ppermute(part_give.astype(BF), "gc", swap_core).astype(F32)
    grad_n1 = part_keep + part_take + back_prompt

    grad_kv = tn(n1_prompt, dkvp) + tn(n1_chip, dkvo)
    grad_q = tn(n1_chip, dq)
    grad_qkv = head_layout_back(grad_q, grad_kv)
    qkv_keep = lax.dynamic_index_in_dim(grad_qkv, y, 0, keepdims=False)
    qkv_give = lax.dynamic_index_in_dim(grad_qkv, 1 - y, 0, keepdims=False)
    qkv_take = lax.ppermute(qkv_give.astype(BF), "gc", swap_y).astype(F32)
    out_w_qkv = lax.psum_scatter(
        (qkv_keep + qkv_take).astype(BF), "gr", scatter_dimension=0, tiled=True
    )
    out_w_qkv = lax.psum(out_w_qkv, "dp").astype(F32)

    back1, grad_gain1, grad_shift1 = norm_back(grad_n1, gain1, unit1, factor1)
    input_grad = grad_h2 + back1
    sums = jnp.concatenate(
        [
            jnp.sum(input_grad, axis=0),
            grad_gain1,
            grad_shift1,
            grad_gain2,
            grad_shift2,
            grad_b_out,
            grad_b_down,
            grad_b_up,
            jnp.broadcast_to(squared, (128,)),
        ]
    )
    sums = lax.psum(sums, ("dp", "gr", "gc"))
    loss = (sums[-1] / (D * token_count[0].astype(F32))).reshape(1)
    rows = sums[: 7 * D].reshape(7, n_gr, D // n_gr)
    rows = lax.dynamic_index_in_dim(rows, z, 1, keepdims=False)
    up = lax.dynamic_index_in_dim(
        sums[7 * D : 7 * D + FF].reshape(n_gc, FF // n_gc), g, 0, keepdims=False
    )
    return (
        final.astype(BF),
        loss,
        input_grad,
        rows[0],
        rows[1],
        rows[2],
        out_w_qkv,
        out_w_out,
        rows[5],
        rows[3],
        rows[4],
        out_w_up,
        up,
        out_w_down,
        rows[6],
    )


def solution(mesh):
    rows = P(("dp", "gr", "gc"), None)
    in_specs = (
        rows,
        rows,
        P("gr"),
        P("gr"),
        P("gr"),
        P("gr", "gc"),
        P("gc", "gr"),
        P("gr"),
        P("gr"),
        P("gr"),
        P("gr", "gc"),
        P("gc"),
        P("gr", "gc"),
        P("gr"),
        P(("dp", "gr")),
        P(),
    )
    out_specs = (
        rows,
        P(),
        rows,
        P("gr"),
        P("gr"),
        P("gr"),
        P("gr", "gc"),
        P("gc", "gr"),
        P("gr"),
        P("gr"),
        P("gr"),
        P("gr", "gc"),
        P("gc"),
        P("gr", "gc"),
        P("gr"),
    )
    return jax.shard_map(
        on_device, mesh=mesh, in_specs=in_specs, out_specs=out_specs, check_vma=False
    )
```

```python
from functools import partial

import jax
import jax.numpy as jnp
from jax import lax
from jax.experimental import pallas as pl
from jax.experimental.pallas import tpu as pltpu
from jax.sharding import PartitionSpec as P

D = 768
HD = 64
FF = 3072
P_SIZE = 1024
CL = 128
QROWS = 512
eps = 1e-05
negative = -1e30
BF = jnp.bfloat16
F32 = jnp.float32


def nt(a, b):
    return lax.dot_general(a, b, (((1,), (1,)), ((), ())), preferred_element_type=F32)


def nn(a, b):
    return lax.dot_general(a, b, (((1,), (0,)), ((), ())), preferred_element_type=F32)


def tn(a, b):
    return lax.dot_general(a, b, (((0,), (0,)), ((), ())), preferred_element_type=F32)


def att_fwd_kernel(grp_ref, z_ref, q_ref, kvo_ref, kvp_ref, o_ref, lse_ref):
    j = pl.program_id(1)
    row0 = pl.multiple_of(grp_ref[j] * P_SIZE, P_SIZE)
    z = z_ref[0]
    lane = lax.broadcasted_iota(jnp.int32, (CL, 128), 1)
    low = lane < 64
    zero = jnp.zeros((CL, 128), BF)
    q = q_ref[...]
    q_parts = (jnp.where(low, zero, q), jnp.where(low, q, zero))

    @pl.when(z >= 2)
    def _():
        row = lax.broadcasted_iota(jnp.int32, (CL, CL), 0)
        near_ok = lax.broadcasted_iota(jnp.int32, (CL, CL), 1) <= row
        mixes, sums = [], []
        for h in range(2):
            cols = slice(128 * h, 128 * h + 128)
            kv = kvp_ref[pl.ds(row0, P_SIZE), cols]
            kvo = kvo_ref[:, cols]
            far = nt(q_parts[h], kv)
            near = jnp.where(near_ok, nt(q_parts[h], kvo), negative)
            top = jnp.maximum(
                jnp.max(far, axis=1, keepdims=True), jnp.max(near, axis=1, keepdims=True)
            )
            far = jnp.exp(far - top)
            near = jnp.exp(near - top)
            total = jnp.sum(far, axis=1, keepdims=True) + jnp.sum(near, axis=1, keepdims=True)
            mix = nn(far.astype(BF), kv) + nn(near.astype(BF), kvo)
            mixes.append(mix / total)
            sums.append(jnp.broadcast_to(top + jnp.log(total), (CL, 128)))
        o_ref[...] = jnp.where(low, mixes[0], mixes[1]).astype(BF)
        lse_ref[...] = jnp.where(low, sums[0], sums[1])

    @pl.when(z < 2)
    def _():
        limit = z * QROWS + (j % (QROWS // CL)) * CL
        row = lax.broadcasted_iota(jnp.int32, (CL, P_SIZE), 0)
        key = lax.broadcasted_iota(jnp.int32, (CL, P_SIZE), 1)
        allowed = key - row <= limit
        mixes, sums = [], []
        for h in range(2):
            cols = slice(128 * h, 128 * h + 128)
            kv = kvp_ref[pl.ds(row0, P_SIZE), cols]
            far = jnp.where(allowed, nt(q_parts[h], kv), negative)
            top = jnp.max(far, axis=1, keepdims=True)
            far = jnp.exp(far - top)
            total = jnp.sum(far, axis=1, keepdims=True)
            mix = nn(far.astype(BF), kv)
            mixes.append(mix / total)
            sums.append(jnp.broadcast_to(top + jnp.log(total), (CL, 128)))
        o_ref[...] = jnp.where(low, mixes[0], mixes[1]).astype(BF)
        lse_ref[...] = jnp.where(low, sums[0], sums[1])


def attend(grp, z, q, kvo, kvp):
    rows = q.shape[0]
    pairs = q.shape[1] // 128
    groups_rows = kvp.shape[0]
    return pl.pallas_call(
        att_fwd_kernel,
        name="att_fwd",
        grid_spec=pltpu.PrefetchScalarGridSpec(
            num_scalar_prefetch=2,
            grid=(pairs, rows // CL),
            in_specs=[
                pl.BlockSpec((CL, 128), lambda p, j, *_: (j, p)),
                pl.BlockSpec((CL, 256), lambda p, j, *_: (j, p)),
                pl.BlockSpec((groups_rows, 256), lambda p, j, *_: (0, p)),
            ],
            out_specs=[
                pl.BlockSpec((CL, 128), lambda p, j, *_: (j, p)),
                pl.BlockSpec((CL, 128), lambda p, j, *_: (j, p)),
            ],
        ),
        out_shape=[
            jax.ShapeDtypeStruct((rows, pairs * 128), BF),
            jax.ShapeDtypeStruct((rows, pairs * 128), F32),
        ],
        compiler_params=pltpu.CompilerParams(vmem_limit_bytes=40 << 20),
        cost_estimate=pl.CostEstimate(
            flops=4 * rows * P_SIZE * 128 * pairs * 2,
            bytes_accessed=groups_rows * 512 * pairs,
            transcendentals=rows * P_SIZE * pairs * 2,
        ),
    )(grp, z, q, kvo, kvp)


def att_bwd_kernel(
    grp_ref, z_ref, q_ref, gm_ref, lse_ref, kvo_ref, kvp_ref, dq_ref, dkvo_ref, dkvp_ref, acc
):
    j = pl.program_id(1)
    row0 = pl.multiple_of(grp_ref[j] * P_SIZE, P_SIZE)
    z = z_ref[0]
    low = lax.broadcasted_iota(jnp.int32, (CL, 128), 1) < 64
    zero = jnp.zeros((CL, 128), BF)
    q = q_ref[...]
    gm = gm_ref[...]
    stacks = (
        jnp.concatenate([jnp.where(low, zero, q), jnp.where(low, gm, zero)], axis=0),
        jnp.concatenate([jnp.where(low, q, zero), jnp.where(low, zero, gm)], axis=0),
    )

    @pl.when(j == 0)
    def _():
        acc[...] = jnp.zeros_like(acc)

    @pl.when(z >= 2)
    def _():
        row = lax.broadcasted_iota(jnp.int32, (CL, CL), 0)
        near_ok = row <= lax.broadcasted_iota(jnp.int32, (CL, CL), 1)
        dqs = []
        for h in range(2):
            cols = slice(128 * h, 128 * h + 128)
            kv = kvp_ref[pl.ds(row0, P_SIZE), cols]
            kvo = kvo_ref[:, cols]
            lse = lse_ref[0, 0, h : h + 1, :]
            far = nt(kv, stacks[h])
            near = nt(kvo, stacks[h])
            pf = jnp.exp(far[:, :CL] - lse)
            pn = jnp.where(near_ok, jnp.exp(near[:, :CL] - lse), 0.0)
            df = far[:, CL:]
            dn = near[:, CL:]
            inner = jnp.sum(pf * df, axis=0, keepdims=True) + jnp.sum(
                pn * dn, axis=0, keepdims=True
            )
            sf = (pf * (df - inner)).astype(BF)
            sn = (pn * (dn - inner)).astype(BF)
            acc[pl.ds(row0, P_SIZE), cols] += nn(
                jnp.concatenate([sf, pf.astype(BF)], axis=1), stacks[h]
            )
            dkvo_ref[:, cols] = nn(
                jnp.concatenate([sn, pn.astype(BF)], axis=1), stacks[h]
            ).astype(BF)
            dqs.append(tn(sf, kv) + tn(sn, kvo))
        dq_ref[...] = (jnp.where(low, dqs[1], dqs[0]) * 0.125).astype(BF)

    @pl.when(z < 2)
    def _():
        limit = z * QROWS + (j % (QROWS // CL)) * CL
        key = lax.broadcasted_iota(jnp.int32, (P_SIZE, CL), 0)
        row = lax.broadcasted_iota(jnp.int32, (P_SIZE, CL), 1)
        allowed = key - row <= limit
        dqs = []
        for h in range(2):
            cols = slice(128 * h, 128 * h + 128)
            kv = kvp_ref[pl.ds(row0, P_SIZE), cols]
            lse = lse_ref[0, 0, h : h + 1, :]
            far = nt(kv, stacks[h])
            pf = jnp.where(allowed, jnp.exp(far[:, :CL] - lse), 0.0)
            df = far[:, CL:]
            inner = jnp.sum(pf * df, axis=0, keepdims=True)
            sf = (pf * (df - inner)).astype(BF)
            acc[pl.ds(row0, P_SIZE), cols] += nn(
                jnp.concatenate([sf, pf.astype(BF)], axis=1), stacks[h]
            )
            dqs.append(tn(sf, kv))
        dkvo_ref[...] = jnp.zeros_like(dkvo_ref)
        dq_ref[...] = (jnp.where(low, dqs[1], dqs[0]) * 0.125).astype(BF)

    @pl.when(j == pl.num_programs(1) - 1)
    def _():
        dkvp_ref[...] = acc[...].astype(BF)


def attend_back(grp, z, q, gm, lse, kvo, kvp):
    rows = q.shape[0]
    pairs = q.shape[1] // 128
    groups_rows = kvp.shape[0]
    return pl.pallas_call(
        att_bwd_kernel,
        name="att_bwd",
        grid_spec=pltpu.PrefetchScalarGridSpec(
            num_scalar_prefetch=2,
            grid=(pairs, rows // CL),
            in_specs=[
                pl.BlockSpec((CL, 128), lambda p, j, *_: (j, p)),
                pl.BlockSpec((CL, 128), lambda p, j, *_: (j, p)),
                pl.BlockSpec((1, 1, 2, 128), lambda p, j, *_: (p, j, 0, 0)),
                pl.BlockSpec((CL, 256), lambda p, j, *_: (j, p)),
                pl.BlockSpec((groups_rows, 256), lambda p, j, *_: (0, p)),
            ],
            out_specs=[
                pl.BlockSpec((CL, 128), lambda p, j, *_: (j, p)),
                pl.BlockSpec((CL, 256), lambda p, j, *_: (j, p)),
                pl.BlockSpec((groups_rows, 256), lambda p, j, *_: (0, p)),
            ],
            scratch_shapes=[pltpu.VMEM((groups_rows, 256), F32)],
        ),
        out_shape=[
            jax.ShapeDtypeStruct((rows, pairs * 128), BF),
            jax.ShapeDtypeStruct((rows, pairs * 256), BF),
            jax.ShapeDtypeStruct((groups_rows, pairs * 256), BF),
        ],
        compiler_params=pltpu.CompilerParams(vmem_limit_bytes=48 << 20),
        cost_estimate=pl.CostEstimate(
            flops=10 * rows * P_SIZE * 128 * pairs * 2,
            bytes_accessed=groups_rows * 1024 * pairs,
            transcendentals=rows * P_SIZE * pairs * 2,
        ),
    )(grp, z, q, gm, lse, kvo, kvp)


MESH = pl.DeviceIdType.MESH


def places():
    x = lax.axis_index("dp")
    z = lax.axis_index("gr")
    g = lax.axis_index("gc")
    return x, z, g, g // 2, g % 2


def greet(partners):
    barrier = pltpu.get_barrier_semaphore()
    for partner in partners:
        pl.semaphore_signal(barrier, inc=1, device_id=partner, device_id_type=MESH)
    pl.semaphore_wait(barrier, len(partners))


def all_partners():
    x, z, g, y, c = places()
    by_z = [{"gr": z ^ step} for step in (1, 2, 3)]
    return [{"gc": g ^ 1}, {"gc": g ^ 2}, {"dp": x ^ 1}] + by_z


def send(src, dst, sems, slot, target, send_slot=None):
    return pltpu.make_async_remote_copy(
        src_ref=src,
        dst_ref=dst,
        send_sem=sems[0].at[slot if send_slot is None else send_slot],
        recv_sem=sems[1].at[slot],
        device_id=target,
        device_id_type=MESH,
    )


def add_into(dst, left, right):
    dst[...] = (left[...].astype(F32) + right[...].astype(F32)).astype(dst.dtype)


RS_SLOTS = 10


def rs_steps(grads, outs, bufs, sems, sem_own, base):
    own, ra, rb0, rb1, rc0, rc1, sc, rd, re = bufs
    x, z, g, y, c = places()
    sib, over_y, over_x = {"gc": g ^ 1}, {"gc": g ^ 2}, {"dp": x ^ 1}
    rows = grads.shape[2]
    q = rows // 4
    mine0 = pl.ds(pl.multiple_of(q * x, 16), q)
    other0 = pl.ds(pl.multiple_of(q * (1 - x), 16), q)
    mine1 = pl.ds(pl.multiple_of(2 * q + q * x, 16), q)
    other1 = pl.ds(pl.multiple_of(2 * q + q * (1 - x), 16), q)
    first = pl.ds(0, 2 * q)

    def slot(i):
        return base * RS_SLOTS + i

    loads = [
        pltpu.make_async_copy(grads.at[2 * i + c], own.at[i], sem_own.at[2 * base + i])
        for i in range(2)
    ]
    hop_a = [send(grads.at[2 * i + 1 - c], ra.at[i], sems, slot(i), sib) for i in range(2)]
    hop_b0 = send(own.at[1 - y, :, first], rb0, sems, slot(2), over_y)
    hop_b1 = send(own.at[:, :, other1], rb1, sems, slot(3), over_x)
    hop_c0 = send(own.at[y, :, other0], rc0, sems, slot(4), over_x)
    hop_c1 = send(own.at[1 - y, :, mine1], rc1, sems, slot(5), over_y)
    hop_z = [
        send(
            sc.at[z ^ step],
            rd.at[step - 1],
            sems,
            slot(5 + step),
            {"gr": z ^ step},
        )
        for step in (1, 2, 3)
    ]
    hop_d = send(sc.at[z], re, sems, slot(9), over_x)

    def start():
        for copy in loads + hop_a:
            copy.start()

    def after_a():
        for copy in loads + hop_a:
            copy.wait()

        @pl.loop(0, 8)
        def _(i):
            add_into(own.at[i // 4, i % 4], own.at[i // 4, i % 4], ra.at[i // 4, i % 4])

        hop_b0.start()
        hop_b1.start()

    def after_b():
        hop_b0.wait()
        hop_b1.wait()

        @pl.loop(0, 4)
        def _(i):
            add_into(own.at[y, i, first], own.at[y, i, first], rb0.at[i])
            add_into(own.at[0, i, mine1], own.at[0, i, mine1], rb1.at[0, i])
            add_into(own.at[1, i, mine1], own.at[1, i, mine1], rb1.at[1, i])

        hop_c0.start()
        hop_c1.start()

    def after_c():
        hop_c0.wait()
        hop_c1.wait()

        @pl.loop(0, 4)
        def _(i):
            add_into(sc.at[i, pl.ds(0, q)], own.at[y, i, mine0], rc0.at[i])
            add_into(sc.at[i, pl.ds(q, q)], own.at[y, i, mine1], rc1.at[i])

        for copy in hop_z:
            copy.start()

    def after_z():
        for copy in hop_z:
            copy.wait()
        total = sc[z].astype(F32)
        for i in range(3):
            total = total + rd[i].astype(F32)
        sc[z] = total.astype(BF)
        hop_d.start()

    def finish():
        hop_d.wait()
        outs[mine0] = sc[z, pl.ds(0, q)].astype(F32)
        outs[mine1] = sc[z, pl.ds(q, q)].astype(F32)
        outs[other0] = re[pl.ds(0, q)].astype(F32)
        outs[other1] = re[pl.ds(q, q)].astype(F32)

    return [start, after_a, after_b, after_c, after_z, finish]


def rs_scratch(shape):
    _, n_gr, rows, cols = shape
    q = rows // 4
    return [
        pltpu.VMEM((2, n_gr, rows, cols), BF),
        pltpu.VMEM((2, n_gr, rows, cols), BF),
        pltpu.VMEM((n_gr, 2 * q, cols), BF),
        pltpu.VMEM((2, n_gr, q, cols), BF),
        pltpu.VMEM((n_gr, q, cols), BF),
        pltpu.VMEM((n_gr, q, cols), BF),
        pltpu.VMEM((n_gr, 2 * q, cols), BF),
        pltpu.VMEM((3, 2 * q, cols), BF),
        pltpu.VMEM((2 * q, cols), BF),
    ]


def scatter_kernel(count, *refs):
    grads, outs = refs[:count], refs[count : 2 * count]
    bufs = refs[2 * count : 2 * count + 9 * count]
    send_sem, recv_sem, sem_own = refs[11 * count :]
    greet(all_partners())
    steps = [
        rs_steps(grads[k], outs[k], bufs[9 * k : 9 * k + 9], (send_sem, recv_sem), sem_own, k)
        for k in range(count)
    ]
    for stage in range(len(steps[0])):
        for k in range(count):
            steps[k][stage]()


def scatter_grads(grads, collective_id):
    count = len(grads)
    scratch = []
    for grad in grads:
        scratch += rs_scratch(grad.shape)
    return pl.pallas_call(
        partial(scatter_kernel, count),
        name="scatter_grads",
        in_specs=[pl.BlockSpec(memory_space=pl.ANY)] * count,
        out_specs=[pl.BlockSpec(memory_space=pltpu.VMEM)] * count,
        out_shape=[jax.ShapeDtypeStruct(grad.shape[2:], F32) for grad in grads],
        scratch_shapes=scratch
        + [
            pltpu.SemaphoreType.DMA((RS_SLOTS * count,)),
            pltpu.SemaphoreType.DMA((RS_SLOTS * count,)),
            pltpu.SemaphoreType.DMA((2 * count,)),
        ],
        compiler_params=pltpu.CompilerParams(
            collective_id=collective_id, has_side_effects=True, vmem_limit_bytes=50 << 20
        ),
    )(*grads)


def norm_rows(hidden, gain, shift):
    center = jnp.mean(hidden, axis=1, keepdims=True)
    offset = hidden - center
    factor = lax.rsqrt(jnp.mean(offset * offset, axis=1, keepdims=True) + eps)
    return offset * factor * gain + shift


CHUNKS = 4


def start_kernel(
    tokens,
    vec,
    bup,
    own,
    wq,
    prompts,
    chip,
    wpair,
    vec_out,
    bup_out,
    own_out,
    n1,
    vec_in,
    z_sems,
    y_sems,
    d_sems,
    w_sems,
    s_sems,
    l_sems,
):
    x, z, g, y, c = places()
    sib, over_y, over_x = {"gc": g ^ 1}, {"gc": g ^ 2}, {"dp": x ^ 1}
    greet(all_partners() + [{"gc": g ^ 3}])
    half_rows = wq.shape[0] // 2
    my_half = pl.ds(pl.multiple_of(x * half_rows, 16), half_rows)

    small = []
    for s in (1, 2, 3):
        to = {"gr": z ^ s}
        small.append(send(vec, vec_in.at[s], s_sems, s, to))
        small.append(send(own, own_out.at[z], s_sems, 3 + s, to))
        small.append(send(bup, bup_out.at[g], s_sems, 6 + s, {"gc": g ^ s}))
    for copy in small:
        copy.start()
    own_out[z] = own[...]
    bup_out[g] = bup[...]

    w_local = pltpu.make_async_copy(wq.at[my_half], wpair.at[y, z, my_half], l_sems.at[0])
    w_local.start()
    w_gr = [
        send(wq.at[my_half], wpair.at[y, z, my_half], w_sems, s, {"gr": z ^ s}) for s in (1, 2, 3)
    ]
    for copy in w_gr:
        copy.start()

    def w_step(s):
        block = z ^ s
        piece = wpair.at[y, block, my_half]
        across = wpair.at[1 - y, block, my_half]
        return (
            send(piece, piece, w_sems, 4 + s, over_y),
            send(piece, piece, w_sems, 8 + s, over_x),
            send(across, across, w_sems, 12 + s, over_x),
        )

    for copy in small[0::3]:
        copy.wait_recv()
    total = vec[...]
    for s in (1, 2, 3):
        total = total + vec_in[s]
    vec_out[...] = total

    @pl.loop(0, QROWS // 128)
    def _(i):
        rows = pl.ds(pl.multiple_of(i * 128, 128), 128)
        hidden = tokens[rows].astype(F32) + vec_out[0:1]
        n1[rows] = norm_rows(hidden, vec_out[1:2], vec_out[2:3]).astype(BF)

    to_chip = pltpu.make_async_copy(n1, chip.at[c], l_sems.at[1])
    to_chip.start()
    chip_send = send(n1, chip.at[c], s_sems, 10, sib)
    chip_send.start()
    is_prompt = z < 2

    @pl.when(is_prompt)
    def _():
        local = pltpu.make_async_copy(n1, prompts.at[g, z], l_sems.at[2])
        local.start()
        local.wait()

    w_local.wait()
    for copy in w_step(0)[:2]:
        copy.start()

    rows = QROWS // CHUNKS

    def item(column, half, k):
        return prompts.at[column, half, pl.ds(k * rows, rows)]

    def copies(half, k):
        mine = item(g, half, k)
        across = item(g ^ 2, half, k)
        n = half * CHUNKS + k
        return {
            "up": send(mine, mine, z_sems, n, {"gr": jnp.minimum(z + 1, 3)}),
            "down": send(
                mine, mine, z_sems, n, {"gr": jnp.maximum(z - 1, 0)}, 2 * CHUNKS + k
            ),
            "y": send(mine, mine, y_sems, n, over_y),
            "core": send(mine, mine, d_sems, n, sib),
            "core2": send(across, across, d_sems, 2 * CHUNKS + n, sib),
        }

    first = jnp.where(z == 0, 0, 1)

    def forward(step):
        half = first if step < CHUNKS else 1 - first
        k = step % CHUNKS
        moves = copies(half, k)

        @pl.when(half != z)
        def _():
            moves["up"].wait_recv()

        @pl.when(jnp.logical_and(z < 3, half <= z))
        def _():
            moves["up"].start()

        @pl.when(jnp.logical_and(z == 1, half == 1))
        def _():
            moves["down"].start()

        moves["y"].start()
        moves["core"].start()

    def across(step):
        half = first if step < CHUNKS else 1 - first
        moves = copies(half, step % CHUNKS)
        moves["y"].wait_recv()
        moves["core2"].start()

    for step in range(2 * CHUNKS):
        forward(step)
        if step >= 2:
            across(step - 2)
        if step in (1, 2, 3):
            w_gr[step - 1].wait_recv()
            one, two, _ = w_step(step)
            one.start()
            two.start()
        if step in (4, 5, 6, 7):
            one, _, three = w_step(step - 4)
            one.wait_recv()
            three.start()
    across(2 * CHUNKS - 2)
    across(2 * CHUNKS - 1)

    for step in range(2 * CHUNKS):
        half = first if step < CHUNKS else 1 - first
        moves = copies(half, step % CHUNKS)
        moves["core"].wait_recv()
        moves["core2"].wait_recv()
        moves["y"].wait_send()
        moves["core"].wait_send()
        moves["core2"].wait_send()

        @pl.when(jnp.logical_and(z < 3, half <= z))
        def _():
            moves["up"].wait_send()

        @pl.when(jnp.logical_and(z == 1, half == 1))
        def _():
            moves["down"].wait_send()

    for copy in w_gr:
        copy.wait_send()
    for s in range(4):
        one, two, three = w_step(s)
        one.wait_send()
        two.wait()
        three.wait()
    for i, copy in enumerate(small):
        if i % 3 == 0:
            copy.wait_send()
        else:
            copy.wait()
    to_chip.wait()
    chip_send.wait()


def start_exchange(tokens, vec, bup, own, wq, collective_id):
    any_space = pl.BlockSpec(memory_space=pl.ANY)
    vmem = pl.BlockSpec(memory_space=pltpu.VMEM)

    def dma(count):
        return pltpu.SemaphoreType.DMA((count,))

    def pair(count, extra=0):
        return dma(count + extra), dma(count)

    z_pair, y_pair, d_pair = pair(2 * CHUNKS, CHUNKS), pair(2 * CHUNKS), pair(4 * CHUNKS)
    w_pair, s_pair = pair(16), pair(11)

    def body(*refs):
        main, sems = refs[:13], refs[13:]
        start_kernel(*main, sems[0:2], sems[2:4], sems[4:6], sems[6:8], sems[8:10], sems[10])

    return pl.pallas_call(
        body,
        name="start_exchange",
        in_specs=[vmem, vmem, vmem, vmem, any_space],
        out_specs=[any_space, any_space, any_space, vmem, vmem, vmem],
        out_shape=[
            jax.ShapeDtypeStruct((4, 2, QROWS, D), BF),
            jax.ShapeDtypeStruct((2, QROWS, D), BF),
            jax.ShapeDtypeStruct((2, 4) + wq.shape, BF),
            jax.ShapeDtypeStruct(vec.shape, F32),
            jax.ShapeDtypeStruct((4,) + bup.shape, F32),
            jax.ShapeDtypeStruct((4,) + own.shape, jnp.int32),
        ],
        scratch_shapes=[pltpu.VMEM((QROWS, D), BF), pltpu.VMEM((4,) + vec.shape, F32)]
        + [*z_pair, *y_pair, *d_pair, *w_pair, *s_pair, dma(3)],
        compiler_params=pltpu.CompilerParams(
            collective_id=collective_id, has_side_effects=True, vmem_limit_bytes=32 << 20
        ),
    )(tokens, vec, bup, own, wq)


GATHER_SLOTS = 36


def gather_steps(blocks, wholes, sems, l_sems):
    x, z, g, y, c = places()
    sib, over_y, over_x = {"gc": g ^ 1}, {"gc": g ^ 2}, {"dp": x ^ 1}
    steps = []

    def plan(a):
        block, whole = blocks[a], wholes[a]
        rows = block.shape[0]
        q = rows // 4
        half = pl.ds(pl.multiple_of(x * 2 * q, 16), 2 * q)
        qa = pl.ds(pl.multiple_of(x * 2 * q, 16), q)
        qb = pl.ds(pl.multiple_of(x * 2 * q + q, 16), q)
        base = a * GATHER_SLOTS
        local = pltpu.make_async_copy(block.at[half], whole.at[g, z, half], l_sems.at[a])
        by_gr = [
            send(block.at[half], whole.at[g, z, half], sems, base + s, {"gr": z ^ s})
            for s in (1, 2, 3)
        ]

        def moves(s):
            o = base + 4 + 8 * s
            mine, far = whole.at[g, z ^ s], whole.at[g ^ 2, z ^ s]
            return {
                "ay": send(mine.at[qa], mine.at[qa], sems, o, over_y),
                "ax": send(mine.at[qa], mine.at[qa], sems, o + 1, over_x),
                "afx": send(far.at[qa], far.at[qa], sems, o + 2, over_x),
                "bx": send(mine.at[qb], mine.at[qb], sems, o + 3, over_x),
                "by": send(mine.at[qb], mine.at[qb], sems, o + 4, over_y),
                "bfy": send(
                    mine.at[pl.ds(pl.multiple_of((1 - x) * 2 * q + q, 16), q)],
                    mine.at[pl.ds(pl.multiple_of((1 - x) * 2 * q + q, 16), q)],
                    sems,
                    o + 5,
                    over_y,
                ),
                "c1": send(mine, mine, sems, o + 6, sib),
                "c2": send(far, far, sems, o + 7, sib),
            }

        return local, by_gr, moves

    plans = [plan(a) for a in range(len(blocks))]

    def begin():
        for local, by_gr, _ in plans:
            local.start()
            for copy in by_gr:
                copy.start()
        for local, _, _ in plans:
            local.wait()

    def first(a, s):
        def run():
            _, by_gr, moves = plans[a]
            if s:
                by_gr[s - 1].wait_recv()
            m = moves(s)
            for name in ("ay", "bx", "ax", "by"):
                m[name].start()

        return run

    def second(a, s):
        def run():
            m = plans[a][2](s)
            m["ay"].wait_recv()
            m["afx"].start()
            m["bx"].wait_recv()
            m["bfy"].start()

        return run

    def third(a, s):
        def run():
            m = plans[a][2](s)
            for name in ("ax", "afx", "by", "bfy"):
                m[name].wait_recv()
            m["c1"].start()
            m["c2"].start()

        return run

    def finish():
        for _, by_gr, moves in plans:
            for copy in by_gr:
                copy.wait_send()
            for s in range(4):
                m = moves(s)
                m["c1"].wait_recv()
                m["c2"].wait_recv()
                for copy in m.values():
                    copy.wait_send()

    order = [(a, s) for a in range(len(blocks)) for s in range(4)]
    steps = [begin]
    n = len(order)
    for i in range(n + 4):
        part = []
        if i < n:
            part.append(first(*order[i]))
        if 2 <= i < n + 2:
            part.append(second(*order[i - 2]))
        if i >= 4:
            part.append(third(*order[i - 4]))
        steps.append(partial(lambda fs: [f() for f in fs], part))
    steps.append(finish)
    return steps


def att_gather_kernel(count, grp_ref, q_ref, kvo_ref, kvp_ref, *refs):
    blocks = refs[:count]
    mixed, lse_ref = refs[count : count + 2]
    wholes = refs[count + 2 : 2 * count + 2]
    mix, sems_s, sems_r, l_sems, m_send, m_recv, m_local = refs[2 * count + 2 :]
    p, j = pl.program_id(0), pl.program_id(1)
    step = p * pl.num_programs(1) + j
    x, z, g, y, c = places()

    hooks = gather_steps(blocks, wholes, (sems_s, sems_r), l_sems)

    @pl.when(step == 0)
    def _():
        greet(all_partners())

    last = len(hooks) - 1
    for i, hook in enumerate(hooks):
        when = i * 23 // last
        if i == last:
            continue

        @pl.when(step == when)
        def _():
            hook()

    group = grp_ref[j]
    low = lax.broadcasted_iota(jnp.int32, (CL, 128), 1) < 64
    zero = jnp.zeros((CL, 128), BF)
    q = q_ref[...]
    q_parts = (jnp.where(low, zero, q), jnp.where(low, q, zero))

    def store(mixes, sums):
        mix[p, j // 4, pl.ds(pl.multiple_of((j % 4) * CL, CL), CL)] = jnp.where(
            low, mixes[0], mixes[1]
        ).astype(BF)
        flat = jnp.where(low, sums[0], sums[1]).T
        lse_ref[0, 0, 0:1] = flat[0:1]
        lse_ref[0, 0, 1:2] = flat[64:65]

    @pl.when(z >= 2)
    def _():
        row = lax.broadcasted_iota(jnp.int32, (CL, CL), 0)
        near_ok = lax.broadcasted_iota(jnp.int32, (CL, CL), 1) <= row
        mixes, sums = [], []
        for h in range(2):
            cols = slice(128 * h, 128 * h + 128)
            kv = kvp_ref[group, :, cols]
            kvo = kvo_ref[:, cols]
            far = nt(q_parts[h], kv)
            near = jnp.where(near_ok, nt(q_parts[h], kvo), negative)
            top = jnp.maximum(
                jnp.max(far, axis=1, keepdims=True), jnp.max(near, axis=1, keepdims=True)
            )
            far = jnp.exp(far - top)
            near = jnp.exp(near - top)
            total = jnp.sum(far, axis=1, keepdims=True) + jnp.sum(near, axis=1, keepdims=True)
            mixes.append((nn(far.astype(BF), kv) + nn(near.astype(BF), kvo)) / total)
            sums.append(jnp.broadcast_to(top + jnp.log(total), (CL, 128)))
        store(mixes, sums)

    @pl.when(z < 2)
    def _():
        limit = z * QROWS + (j % (QROWS // CL)) * CL
        row = lax.broadcasted_iota(jnp.int32, (CL, P_SIZE), 0)
        key = lax.broadcasted_iota(jnp.int32, (CL, P_SIZE), 1)
        allowed = key - row <= limit
        mixes, sums = [], []
        for h in range(2):
            cols = slice(128 * h, 128 * h + 128)
            kv = kvp_ref[group, :, cols]
            far = jnp.where(allowed, nt(q_parts[h], kv), negative)
            top = jnp.max(far, axis=1, keepdims=True)
            far = jnp.exp(far - top)
            total = jnp.sum(far, axis=1, keepdims=True)
            mixes.append(nn(far.astype(BF), kv) / total)
            sums.append(jnp.broadcast_to(top + jnp.log(total), (CL, 128)))
        store(mixes, sums)

    def exchange(i):
        cols = pl.ds(128 * i, 128)
        return (
            pltpu.make_async_copy(mix.at[i, c], mixed.at[c, :, cols], m_local.at[i]),
            send(mix.at[i, 1 - c], mixed.at[c, :, cols], (m_send, m_recv), i, {"gc": g ^ 1}),
        )

    for i in range(3):

        @pl.when(step == 8 * i + 7)
        def _():
            for copy in exchange(i):
                copy.start()

    @pl.when(step == 23)
    def _():
        hooks[last]()
        for i in range(3):
            for copy in exchange(i):
                copy.wait()


def attend_gather(grp, q, kvo, kvp, blocks, collective_id):
    rows = q.shape[0]
    count = len(blocks)
    any_space = pl.BlockSpec(memory_space=pl.ANY)
    slots = GATHER_SLOTS * count
    return pl.pallas_call(
        partial(att_gather_kernel, count),
        name="attend_gather",
        grid_spec=pltpu.PrefetchScalarGridSpec(
            num_scalar_prefetch=1,
            grid=(3, rows // CL),
            in_specs=[
                pl.BlockSpec((CL, 128), lambda p, j, *_: (j, p)),
                pl.BlockSpec((CL, 256), lambda p, j, *_: (j, p)),
                pl.BlockSpec((4, P_SIZE, 256), lambda p, j, *_: (0, 0, p)),
            ]
            + [any_space] * count,
            out_specs=[any_space, pl.BlockSpec((1, 1, 2, 128), lambda p, j, *_: (p, j, 0, 0))]
            + [any_space] * count,
            scratch_shapes=[
                pltpu.VMEM((3, 2, QROWS, 128), BF),
                pltpu.SemaphoreType.DMA((slots,)),
                pltpu.SemaphoreType.DMA((slots,)),
                pltpu.SemaphoreType.DMA((count,)),
                pltpu.SemaphoreType.DMA((3,)),
                pltpu.SemaphoreType.DMA((3,)),
                pltpu.SemaphoreType.DMA((3,)),
            ],
        ),
        out_shape=[
            jax.ShapeDtypeStruct((2, QROWS, 384), BF),
            jax.ShapeDtypeStruct((3, rows // CL, 2, 128), F32),
        ]
        + [jax.ShapeDtypeStruct((4, 4) + block.shape, BF) for block in blocks],
        compiler_params=pltpu.CompilerParams(
            collective_id=collective_id, has_side_effects=True, vmem_limit_bytes=40 << 20
        ),
    )(grp, q, kvo, kvp.reshape(4, P_SIZE, kvp.shape[1]), *blocks)


def norm(hidden, gain, shift):
    center = jnp.mean(hidden, axis=1, keepdims=True)
    offset = hidden - center
    factor = lax.rsqrt(jnp.mean(offset * offset, axis=1, keepdims=True) + eps)
    unit = offset * factor
    return unit * gain + shift, unit, factor


def norm_back(grad, gain, unit, factor):
    grad_unit = grad * gain
    first = jnp.mean(grad_unit, axis=1, keepdims=True)
    second = jnp.mean(grad_unit * unit, axis=1, keepdims=True)
    grad_in = factor * (grad_unit - first - unit * second)
    return grad_in, jnp.sum(grad * unit, axis=0), jnp.sum(grad, axis=0)


def head_layout(blocks):
    chunks = blocks.transpose(1, 0, 2).reshape(D, 6, 3, HD)
    q_list, kv_list = [], []
    for pair in range(3):
        a, b = 2 * pair, 2 * pair + 1
        q_list += [chunks[:, b, 0], chunks[:, a, 0]]
        kv_list += [chunks[:, a, 2], chunks[:, a, 1], chunks[:, b, 1], chunks[:, b, 2]]
    return jnp.concatenate(q_list, axis=1), jnp.concatenate(kv_list, axis=1)


def head_layout_back(grad_q, grad_kv):
    qc = grad_q.reshape(D, 3, 2, HD)
    kc = grad_kv.reshape(D, 3, 4, HD)
    pieces = []
    for pair in range(3):
        pieces += [qc[:, pair, 1], kc[:, pair, 1], kc[:, pair, 0]]
        pieces += [qc[:, pair, 0], kc[:, pair, 2], kc[:, pair, 3]]
    whole = jnp.concatenate(pieces, axis=1)
    return whole.reshape(D, 2, 576).transpose(1, 0, 2)


def on_device(
    tokens,
    teacher,
    pass_embed,
    ln1_gain,
    ln1_bias,
    qkv_weight,
    out_weight,
    out_bias,
    ln2_gain,
    ln2_bias,
    fc1_weight,
    fc1_bias,
    fc2_weight,
    fc2_bias,
    cont_group,
    token_count,
):
    n_dp = lax.axis_size("dp")
    n_gr = lax.axis_size("gr")
    n_gc = lax.axis_size("gc")
    z = lax.axis_index("gr")
    g = lax.axis_index("gc")
    c = g % 2
    y = g // 2
    swap_core = [(i, i ^ 1) for i in range(n_gc)]
    swap_y = [(i, i ^ 2) for i in range(n_gc)]

    packed = jnp.stack(
        [pass_embed, ln1_gain, ln1_bias, out_bias, ln2_gain, ln2_bias, fc2_bias, fc2_bias]
    ).astype(F32)
    if n_dp == 2:
        vec = lax.dynamic_update_slice(jnp.zeros((8, D), F32), packed, (0, z * packed.shape[1]))
        bup = jnp.broadcast_to(fc1_bias.astype(F32), (8, fc1_bias.shape[0]))
        own = jnp.broadcast_to(jnp.pad(cont_group, (0, 120)), (8, 128))
        n1_prompt, n1_chip, w_pair, vectors, b_up, owners = start_exchange(
            tokens, vec, bup, own, qkv_weight, 1
        )
        n1_prompt = n1_prompt.reshape(4 * P_SIZE, D)
        n1_chip = n1_chip.reshape(2 * QROWS, D)
        w_qkv = w_pair.reshape(2, D, 576)
        b_up = b_up[:, 0].reshape(FF)
        owners = owners[:, 0, :8]
    else:
        vectors = lax.all_gather(packed, "gr", axis=1, tiled=True)
        b_up = lax.all_gather(fc1_bias, "gc", axis=0, tiled=True).astype(F32)
        owners = lax.all_gather(cont_group, "gr", axis=0, tiled=True)
    embed, gain1, shift1, b_out, gain2, shift2, b_down = [vectors[i] for i in range(7)]
    owners = owners.reshape(4, 2, 4)
    mine = lax.dynamic_slice(owners, (2 * y, jnp.maximum(z - 2, 0), 0), (2, 1, 4)).reshape(8)
    own_groups = jnp.repeat(2 * y + jnp.arange(2), 4)
    grp = jnp.where(z < 2, own_groups, mine).astype(jnp.int32)
    z_arr = z.astype(jnp.int32).reshape(1)

    hidden = tokens.astype(F32) + embed
    normed1, unit1, factor1 = norm(hidden, gain1, shift1)
    n1 = normed1.astype(BF)

    if n_dp != 2:
        w_other = lax.ppermute(qkv_weight, "gc", swap_y)
        w_pair = jnp.where(
            y == 0, jnp.stack([qkv_weight, w_other]), jnp.stack([w_other, qkv_weight])
        )
        w_qkv = lax.all_gather(w_pair, "gr", axis=1, tiled=True)
        n1_other = lax.ppermute(n1, "gc", swap_core)
        n1_chip = jnp.where(
            c == 0, jnp.concatenate([n1, n1_other]), jnp.concatenate([n1_other, n1])
        )
        n1_col = lax.all_gather(n1, "gr", axis=0, tiled=True)[:P_SIZE]
        n1_prompt = lax.all_gather(n1_col, "gc", axis=0, tiled=True)
    w_q, w_kv = head_layout(w_qkv)

    kvp = nn(n1_prompt, w_kv).astype(BF)
    kvo = nn(n1_chip, w_kv).astype(BF)
    q = (nn(n1_chip, w_q) * 0.125).astype(BF)
    if n_dp == 2:
        mixed, lse_rows, w_out, w_up, w_down = attend_gather(
            grp, q, kvo, kvp, [out_weight, fc1_weight, fc2_weight], 2
        )
    else:
        w_out = lax.all_gather(out_weight, ("gc", "gr"))
        w_up = lax.all_gather(fc1_weight, ("gc", "gr"))
        w_down = lax.all_gather(fc2_weight, ("gc", "gr"))
        mixed_heads, lse = attend(grp, z_arr, q, kvo, kvp)
        lse_rows = lse[:, ::64].reshape(8, CL, 3, 2).transpose(2, 0, 3, 1)
        halves = mixed_heads.reshape(2, QROWS, 384)
        keep = lax.dynamic_index_in_dim(halves, c, 0, keepdims=False)
        give = lax.dynamic_index_in_dim(halves, 1 - c, 0, keepdims=False)
        take = lax.ppermute(give, "gc", swap_core)
        mixed = jnp.where(c == 0, jnp.stack([keep, take]), jnp.stack([take, keep]))
    w_up = w_up.reshape(n_gc, D, FF // n_gc)
    w_down = w_down.reshape(n_gc, D, FF // n_gc)
    w_out = w_out.reshape(2, 2, n_gr, 192, 192).transpose(1, 0, 3, 2, 4).reshape(2, 384, D)

    attended = lax.dot_general(
        mixed, w_out, (((0, 2), (0, 1)), ((), ())), preferred_element_type=F32
    )
    hidden2 = hidden + attended + b_out
    normed2, unit2, factor2 = norm(hidden2, gain2, shift2)
    n2 = normed2.astype(BF)
    pre = lax.dot_general(n2, w_up, (((1,), (1,)), ((), ())), preferred_element_type=F32)
    pre = pre.reshape(QROWS, FF) + b_up
    active, gelu_back = jax.vjp(partial(jax.nn.gelu, approximate=True), pre)
    act = active.astype(BF)
    act_blocks = act.reshape(QROWS, n_gc, FF // n_gc)
    final = (
        hidden2
        + lax.dot_general(
            act_blocks, w_down, (((1, 2), (0, 2)), ((), ())), preferred_element_type=F32
        )
        + b_down
    )
    grad_final = final - teacher.astype(F32)
    squared = jnp.sum(grad_final * grad_final)
    gb = grad_final.astype(BF)
    grad_b_down = jnp.sum(gb, axis=0, dtype=F32)
    grad_active = lax.dot_general(
        gb, w_down, (((1,), (1,)), ((), ())), preferred_element_type=F32
    ).reshape(QROWS, FF)
    grad_w_down = jnp.einsum("td,tgf->gdf", gb, act_blocks, preferred_element_type=F32)
    (grad_pre,) = gelu_back(grad_active)
    gp = grad_pre.astype(BF)
    gp_blocks = gp.reshape(QROWS, n_gc, FF // n_gc)
    grad_b_up = jnp.sum(gp, axis=0, dtype=F32)
    grad_w_up = jnp.einsum("td,tgf->gdf", n2, gp_blocks, preferred_element_type=F32)
    grad_n2 = lax.dot_general(
        gp_blocks, w_up, (((1, 2), (0, 2)), ((), ())), preferred_element_type=F32
    )
    back2, grad_gain2, grad_shift2 = norm_back(grad_n2, gain2, unit2, factor2)
    grad_h2 = grad_final + back2
    ga = grad_h2.astype(BF)
    grad_b_out = jnp.sum(ga, axis=0, dtype=F32)
    grad_w_out = jnp.einsum("ctk,tn->ckn", mixed, ga, preferred_element_type=F32)
    gm = jnp.einsum("tn,ckn->ctk", ga, w_out, preferred_element_type=F32).astype(BF)

    gm_keep = lax.dynamic_index_in_dim(gm, c, 0, keepdims=False)
    gm_give = lax.dynamic_index_in_dim(gm, 1 - c, 0, keepdims=False)
    gm_take = lax.ppermute(gm_give, "gc", swap_core)
    gm_chip = jnp.where(c == 0, jnp.stack([gm_keep, gm_take]), jnp.stack([gm_take, gm_keep]))
    gm_chip = gm_chip.reshape(2 * QROWS, 384)

    def scatter16(blocks):
        part = lax.psum_scatter(
            blocks.astype(BF).reshape(n_gc * n_gr * blocks.shape[2], -1),
            ("gc", "gr"),
            scatter_dimension=0,
            tiled=True,
        )
        return lax.psum(part, "dp").astype(F32)

    weight_grads = [
        grad_w_down.astype(BF).reshape(n_gc, n_gr, 192, 768),
        grad_w_up.astype(BF).reshape(n_gc, n_gr, 192, 768),
        grad_w_out.astype(BF)
        .reshape(2, 2, 192, n_gr, 192)
        .transpose(1, 0, 3, 2, 4)
        .reshape(n_gc, n_gr, 192, 192),
    ]
    if n_dp == 2:
        out_w_down, out_w_up, out_w_out = scatter_grads(weight_grads, 3)
    else:
        out_w_down, out_w_up, out_w_out = [scatter16(grad) for grad in weight_grads]

    dq, dkvo, dkvp = attend_back(grp, z_arr, q, gm_chip, lse_rows, kvo, kvp)

    part_prompt = nt(dkvp, w_kv).astype(BF)
    back_prompt = lax.psum_scatter(part_prompt, "gc", scatter_dimension=0, tiled=True)
    back_prompt = lax.psum_scatter(
        jnp.concatenate([back_prompt, jnp.zeros_like(back_prompt)]),
        "gr",
        scatter_dimension=0,
        tiled=True,
    ).astype(F32)
    part_chip = (nt(dq, w_q) + nt(dkvo, w_kv)).reshape(2, QROWS, D)
    part_keep = lax.dynamic_index_in_dim(part_chip, c, 0, keepdims=False)
    part_give = lax.dynamic_index_in_dim(part_chip, 1 - c, 0, keepdims=False)
    part_take = lax.ppermute(part_give.astype(BF), "gc", swap_core).astype(F32)
    grad_n1 = part_keep + part_take + back_prompt

    grad_kv = tn(n1_prompt, dkvp) + tn(n1_chip, dkvo)
    grad_q = tn(n1_chip, dq)
    grad_qkv = head_layout_back(grad_q, grad_kv)
    qkv_keep = lax.dynamic_index_in_dim(grad_qkv, y, 0, keepdims=False)
    qkv_give = lax.dynamic_index_in_dim(grad_qkv, 1 - y, 0, keepdims=False)
    qkv_take = lax.ppermute(qkv_give.astype(BF), "gc", swap_y).astype(F32)
    out_w_qkv = lax.psum_scatter(
        (qkv_keep + qkv_take).astype(BF), "gr", scatter_dimension=0, tiled=True
    )
    out_w_qkv = lax.psum(out_w_qkv, "dp").astype(F32)

    back1, grad_gain1, grad_shift1 = norm_back(grad_n1, gain1, unit1, factor1)
    input_grad = grad_h2 + back1
    sums = jnp.concatenate(
        [
            jnp.sum(input_grad, axis=0),
            grad_gain1,
            grad_shift1,
            grad_gain2,
            grad_shift2,
            grad_b_out,
            grad_b_down,
            grad_b_up,
            jnp.broadcast_to(squared, (128,)),
        ]
    )
    sums = lax.psum(sums, ("dp", "gr", "gc"))
    loss = (sums[-1] / (D * token_count[0].astype(F32))).reshape(1)
    rows = sums[: 7 * D].reshape(7, n_gr, D // n_gr)
    rows = lax.dynamic_index_in_dim(rows, z, 1, keepdims=False)
    up = lax.dynamic_index_in_dim(
        sums[7 * D : 7 * D + FF].reshape(n_gc, FF // n_gc), g, 0, keepdims=False
    )
    return (
        final.astype(BF),
        loss,
        input_grad,
        rows[0],
        rows[1],
        rows[2],
        out_w_qkv,
        out_w_out,
        rows[5],
        rows[3],
        rows[4],
        out_w_up,
        up,
        out_w_down,
        rows[6],
    )


def solution(mesh):
    rows = P(("dp", "gr", "gc"), None)
    in_specs = (
        rows,
        rows,
        P("gr"),
        P("gr"),
        P("gr"),
        P("gr", "gc"),
        P("gc", "gr"),
        P("gr"),
        P("gr"),
        P("gr"),
        P("gr", "gc"),
        P("gc"),
        P("gr", "gc"),
        P("gr"),
        P(("dp", "gr")),
        P(),
    )
    out_specs = (
        rows,
        P(),
        rows,
        P("gr"),
        P("gr"),
        P("gr"),
        P("gr", "gc"),
        P("gc", "gr"),
        P("gr"),
        P("gr"),
        P("gr"),
        P("gr", "gc"),
        P("gc"),
        P("gr", "gc"),
        P("gr"),
    )
    return jax.shard_map(
        on_device, mesh=mesh, in_specs=in_specs, out_specs=out_specs, check_vma=False
    )
```

```python
from functools import partial

import jax
import jax.numpy as jnp
from jax import lax
from jax.experimental import pallas as pl
from jax.experimental.pallas import tpu as pltpu
from jax.sharding import PartitionSpec as P

D = 768
HD = 64
FF = 3072
P_SIZE = 1024
CL = 128
QROWS = 512
eps = 1e-05
negative = -1e30
BF = jnp.bfloat16
F32 = jnp.float32


def nt(a, b):
    return lax.dot_general(a, b, (((1,), (1,)), ((), ())), preferred_element_type=F32)


def nn(a, b):
    return lax.dot_general(a, b, (((1,), (0,)), ((), ())), preferred_element_type=F32)


def tn(a, b):
    return lax.dot_general(a, b, (((0,), (0,)), ((), ())), preferred_element_type=F32)


def att_fwd_kernel(grp_ref, z_ref, q_ref, kvo_ref, kvp_ref, o_ref, lse_ref):
    j = pl.program_id(1)
    row0 = pl.multiple_of(grp_ref[j] * P_SIZE, P_SIZE)
    z = z_ref[0]
    lane = lax.broadcasted_iota(jnp.int32, (CL, 128), 1)
    low = lane < 64
    zero = jnp.zeros((CL, 128), BF)
    q = q_ref[...]
    q_parts = (jnp.where(low, zero, q), jnp.where(low, q, zero))

    @pl.when(z >= 2)
    def _():
        row = lax.broadcasted_iota(jnp.int32, (CL, CL), 0)
        near_ok = lax.broadcasted_iota(jnp.int32, (CL, CL), 1) <= row
        mixes, sums = [], []
        for h in range(2):
            cols = slice(128 * h, 128 * h + 128)
            kv = kvp_ref[pl.ds(row0, P_SIZE), cols]
            kvo = kvo_ref[:, cols]
            far = nt(q_parts[h], kv)
            near = jnp.where(near_ok, nt(q_parts[h], kvo), negative)
            top = jnp.maximum(
                jnp.max(far, axis=1, keepdims=True), jnp.max(near, axis=1, keepdims=True)
            )
            far = jnp.exp(far - top)
            near = jnp.exp(near - top)
            total = jnp.sum(far, axis=1, keepdims=True) + jnp.sum(near, axis=1, keepdims=True)
            mix = nn(far.astype(BF), kv) + nn(near.astype(BF), kvo)
            mixes.append(mix / total)
            sums.append(jnp.broadcast_to(top + jnp.log(total), (CL, 128)))
        o_ref[...] = jnp.where(low, mixes[0], mixes[1]).astype(BF)
        lse_ref[...] = jnp.where(low, sums[0], sums[1])

    @pl.when(z < 2)
    def _():
        limit = z * QROWS + (j % (QROWS // CL)) * CL
        row = lax.broadcasted_iota(jnp.int32, (CL, P_SIZE), 0)
        key = lax.broadcasted_iota(jnp.int32, (CL, P_SIZE), 1)
        allowed = key - row <= limit
        mixes, sums = [], []
        for h in range(2):
            cols = slice(128 * h, 128 * h + 128)
            kv = kvp_ref[pl.ds(row0, P_SIZE), cols]
            far = jnp.where(allowed, nt(q_parts[h], kv), negative)
            top = jnp.max(far, axis=1, keepdims=True)
            far = jnp.exp(far - top)
            total = jnp.sum(far, axis=1, keepdims=True)
            mix = nn(far.astype(BF), kv)
            mixes.append(mix / total)
            sums.append(jnp.broadcast_to(top + jnp.log(total), (CL, 128)))
        o_ref[...] = jnp.where(low, mixes[0], mixes[1]).astype(BF)
        lse_ref[...] = jnp.where(low, sums[0], sums[1])


def attend(grp, z, q, kvo, kvp):
    rows = q.shape[0]
    pairs = q.shape[1] // 128
    groups_rows = kvp.shape[0]
    return pl.pallas_call(
        att_fwd_kernel,
        name="att_fwd",
        grid_spec=pltpu.PrefetchScalarGridSpec(
            num_scalar_prefetch=2,
            grid=(pairs, rows // CL),
            in_specs=[
                pl.BlockSpec((CL, 128), lambda p, j, *_: (j, p)),
                pl.BlockSpec((CL, 256), lambda p, j, *_: (j, p)),
                pl.BlockSpec((groups_rows, 256), lambda p, j, *_: (0, p)),
            ],
            out_specs=[
                pl.BlockSpec((CL, 128), lambda p, j, *_: (j, p)),
                pl.BlockSpec((CL, 128), lambda p, j, *_: (j, p)),
            ],
        ),
        out_shape=[
            jax.ShapeDtypeStruct((rows, pairs * 128), BF),
            jax.ShapeDtypeStruct((rows, pairs * 128), F32),
        ],
        compiler_params=pltpu.CompilerParams(vmem_limit_bytes=40 << 20),
        cost_estimate=pl.CostEstimate(
            flops=4 * rows * P_SIZE * 128 * pairs * 2,
            bytes_accessed=groups_rows * 512 * pairs,
            transcendentals=rows * P_SIZE * pairs * 2,
        ),
    )(grp, z, q, kvo, kvp)


def att_bwd_kernel(
    grp_ref, z_ref, q_ref, gm_ref, lse_ref, kvo_ref, kvp_ref, dq_ref, dkvo_ref, dkvp_ref, acc
):
    j = pl.program_id(1)
    row0 = pl.multiple_of(grp_ref[j] * P_SIZE, P_SIZE)
    z = z_ref[0]
    low = lax.broadcasted_iota(jnp.int32, (CL, 128), 1) < 64
    zero = jnp.zeros((CL, 128), BF)
    q = q_ref[...]
    gm = gm_ref[...]
    stacks = (
        jnp.concatenate([jnp.where(low, zero, q), jnp.where(low, gm, zero)], axis=0),
        jnp.concatenate([jnp.where(low, q, zero), jnp.where(low, zero, gm)], axis=0),
    )

    @pl.when(j == 0)
    def _():
        acc[...] = jnp.zeros_like(acc)

    @pl.when(z >= 2)
    def _():
        row = lax.broadcasted_iota(jnp.int32, (CL, CL), 0)
        near_ok = row <= lax.broadcasted_iota(jnp.int32, (CL, CL), 1)
        dqs = []
        for h in range(2):
            cols = slice(128 * h, 128 * h + 128)
            kv = kvp_ref[pl.ds(row0, P_SIZE), cols]
            kvo = kvo_ref[:, cols]
            lse = lse_ref[0, 0, h : h + 1, :]
            far = nt(kv, stacks[h])
            near = nt(kvo, stacks[h])
            pf = jnp.exp(far[:, :CL] - lse)
            pn = jnp.where(near_ok, jnp.exp(near[:, :CL] - lse), 0.0)
            df = far[:, CL:]
            dn = near[:, CL:]
            inner = jnp.sum(pf * df, axis=0, keepdims=True) + jnp.sum(
                pn * dn, axis=0, keepdims=True
            )
            sf = (pf * (df - inner)).astype(BF)
            sn = (pn * (dn - inner)).astype(BF)
            acc[pl.ds(row0, P_SIZE), cols] += nn(
                jnp.concatenate([sf, pf.astype(BF)], axis=1), stacks[h]
            )
            dkvo_ref[:, cols] = nn(
                jnp.concatenate([sn, pn.astype(BF)], axis=1), stacks[h]
            ).astype(BF)
            dqs.append(tn(sf, kv) + tn(sn, kvo))
        dq_ref[...] = (jnp.where(low, dqs[1], dqs[0]) * 0.125).astype(BF)

    @pl.when(z < 2)
    def _():
        limit = z * QROWS + (j % (QROWS // CL)) * CL
        key = lax.broadcasted_iota(jnp.int32, (P_SIZE, CL), 0)
        row = lax.broadcasted_iota(jnp.int32, (P_SIZE, CL), 1)
        allowed = key - row <= limit
        dqs = []
        for h in range(2):
            cols = slice(128 * h, 128 * h + 128)
            kv = kvp_ref[pl.ds(row0, P_SIZE), cols]
            lse = lse_ref[0, 0, h : h + 1, :]
            far = nt(kv, stacks[h])
            pf = jnp.where(allowed, jnp.exp(far[:, :CL] - lse), 0.0)
            df = far[:, CL:]
            inner = jnp.sum(pf * df, axis=0, keepdims=True)
            sf = (pf * (df - inner)).astype(BF)
            acc[pl.ds(row0, P_SIZE), cols] += nn(
                jnp.concatenate([sf, pf.astype(BF)], axis=1), stacks[h]
            )
            dqs.append(tn(sf, kv))
        dkvo_ref[...] = jnp.zeros_like(dkvo_ref)
        dq_ref[...] = (jnp.where(low, dqs[1], dqs[0]) * 0.125).astype(BF)

    @pl.when(j == pl.num_programs(1) - 1)
    def _():
        dkvp_ref[...] = acc[...].astype(BF)


def attend_back(grp, z, q, gm, lse, kvo, kvp):
    rows = q.shape[0]
    pairs = q.shape[1] // 128
    groups_rows = kvp.shape[0]
    return pl.pallas_call(
        att_bwd_kernel,
        name="att_bwd",
        grid_spec=pltpu.PrefetchScalarGridSpec(
            num_scalar_prefetch=2,
            grid=(pairs, rows // CL),
            in_specs=[
                pl.BlockSpec((CL, 128), lambda p, j, *_: (j, p)),
                pl.BlockSpec((CL, 128), lambda p, j, *_: (j, p)),
                pl.BlockSpec((1, 1, 2, 128), lambda p, j, *_: (p, j, 0, 0)),
                pl.BlockSpec((CL, 256), lambda p, j, *_: (j, p)),
                pl.BlockSpec((groups_rows, 256), lambda p, j, *_: (0, p)),
            ],
            out_specs=[
                pl.BlockSpec((CL, 128), lambda p, j, *_: (j, p)),
                pl.BlockSpec((CL, 256), lambda p, j, *_: (j, p)),
                pl.BlockSpec((groups_rows, 256), lambda p, j, *_: (0, p)),
            ],
            scratch_shapes=[pltpu.VMEM((groups_rows, 256), F32)],
        ),
        out_shape=[
            jax.ShapeDtypeStruct((rows, pairs * 128), BF),
            jax.ShapeDtypeStruct((rows, pairs * 256), BF),
            jax.ShapeDtypeStruct((groups_rows, pairs * 256), BF),
        ],
        compiler_params=pltpu.CompilerParams(vmem_limit_bytes=48 << 20),
        cost_estimate=pl.CostEstimate(
            flops=10 * rows * P_SIZE * 128 * pairs * 2,
            bytes_accessed=groups_rows * 1024 * pairs,
            transcendentals=rows * P_SIZE * pairs * 2,
        ),
    )(grp, z, q, gm, lse, kvo, kvp)


MESH = pl.DeviceIdType.MESH


def places():
    x = lax.axis_index("dp")
    z = lax.axis_index("gr")
    g = lax.axis_index("gc")
    return x, z, g, g // 2, g % 2


def greet(partners):
    barrier = pltpu.get_barrier_semaphore()
    for partner in partners:
        pl.semaphore_signal(barrier, inc=1, device_id=partner, device_id_type=MESH)
    pl.semaphore_wait(barrier, len(partners))


def all_partners():
    x, z, g, y, c = places()
    by_z = [{"gr": z ^ step} for step in (1, 2, 3)]
    return [{"gc": g ^ 1}, {"gc": g ^ 2}, {"dp": x ^ 1}] + by_z


def send(src, dst, sems, slot, target, send_slot=None):
    return pltpu.make_async_remote_copy(
        src_ref=src,
        dst_ref=dst,
        send_sem=sems[0].at[slot if send_slot is None else send_slot],
        recv_sem=sems[1].at[slot],
        device_id=target,
        device_id_type=MESH,
    )


def add_into(dst, left, right):
    dst[...] = (left[...].astype(F32) + right[...].astype(F32)).astype(dst.dtype)


RS_SLOTS = 28
RS_ORDER = (3, 2, 1, 0)


def rs_plan(grads, outs, bufs, sems, l_sems, base, paired):
    own, ra, rb0, rb1, rc0, rc1, sc, rd, re = bufs
    x, z, g, y, c = places()
    sib, over_y, over_x = {"gc": g ^ 1}, {"gc": g ^ 2}, {"dp": x ^ 1}
    rows = grads.shape[2]
    q = rows // 4
    mine0 = pl.ds(pl.multiple_of(q * x, 16), q)
    other0 = pl.ds(pl.multiple_of(q * (1 - x), 16), q)
    mine1 = pl.ds(pl.multiple_of(2 * q + q * x, 16), q)
    other1 = pl.ds(pl.multiple_of(2 * q + q * (1 - x), 16), q)
    first = pl.ds(0, 2 * q)
    slot = base * RS_SLOTS

    def load(i, s):
        source = grads.at[2 * i + c, z ^ s] if paired else grads.at[i, z ^ s]
        return pltpu.make_async_copy(source, own.at[i, s], l_sems.at[8 * base + 2 * s + i])

    def hop_a(i, s):
        return send(grads.at[2 * i + 1 - c, z ^ s], ra.at[i, s], sems, slot + 6 * s + i, sib)

    def hop_b0(s):
        return send(own.at[1 - y, s, first], rb0.at[s], sems, slot + 6 * s + 2, over_y)

    def hop_b1(s):
        return send(own.at[:, s, other1], rb1.at[s], sems, slot + 6 * s + 3, over_x)

    def hop_c0(s):
        return send(own.at[y, s, other0], rc0.at[s], sems, slot + 6 * s + 4, over_x)

    def hop_c1(s):
        return send(own.at[1 - y, s, mine1], rc1.at[s], sems, slot + 6 * s + 5, over_y)

    def hop_z(s):
        return send(sc.at[s], rd.at[s - 1], sems, slot + 23 + s, {"gr": z ^ s})

    def hop_d():
        return send(sc.at[0], re, sems, slot + 27, over_x)

    def begin(s):
        for i in range(2):
            load(i, s).start()
            if paired:
                hop_a(i, s).start()

    def after_a(s):
        for i in range(2):
            load(i, s).wait()
            if paired:
                hop_a(i, s).wait()
                add_into(own.at[i, s], own.at[i, s], ra.at[i, s])
        hop_b0(s).start()
        hop_b1(s).start()

    def after_b(s):
        hop_b0(s).wait()
        hop_b1(s).wait()
        add_into(own.at[y, s, first], own.at[y, s, first], rb0.at[s])
        for i in range(2):
            add_into(own.at[i, s, mine1], own.at[i, s, mine1], rb1.at[s, i])
        hop_c0(s).start()
        hop_c1(s).start()

    def after_c(s):
        hop_c0(s).wait()
        hop_c1(s).wait()
        add_into(sc.at[s, pl.ds(0, q)], own.at[y, s, mine0], rc0.at[s])
        add_into(sc.at[s, pl.ds(q, q)], own.at[y, s, mine1], rc1.at[s])
        if s:
            hop_z(s).start()

    def total():
        for s in (1, 2, 3):
            hop_z(s).wait()
        whole = sc[0].astype(F32)
        for i in range(3):
            whole = whole + rd[i].astype(F32)
        sc[0] = whole.astype(BF)
        hop_d().start()

    def finish():
        hop_d().wait()
        outs[mine0] = sc[0, pl.ds(0, q)].astype(F32)
        outs[mine1] = sc[0, pl.ds(q, q)].astype(F32)
        outs[other0] = re[pl.ds(0, q)].astype(F32)
        outs[other1] = re[pl.ds(q, q)].astype(F32)

    return begin, after_a, after_b, after_c, total, finish


def rs_steps(plans):
    order = [(plan, s) for plan in plans for s in RS_ORDER]
    n = len(order)
    steps = [[partial(plan[0], s) for plan, s in order]]
    for i in range(n + 10):
        part = []
        if i < n:
            part.append(partial(order[i][0][1], order[i][1]))
        if 2 <= i < n + 2:
            part.append(partial(order[i - 2][0][2], order[i - 2][1]))
        if 4 <= i < n + 4:
            part.append(partial(order[i - 4][0][3], order[i - 4][1]))
        if 7 <= i < n + 7 and (i - 7) % 4 == 3:
            part.append(plans[(i - 7) // 4][4])
        if 9 <= i < n + 9 and (i - 9) % 4 == 3:
            part.append(plans[(i - 9) // 4][5])
        if part:
            steps.append(part)
    return steps


def rs_scratch(rows, cols, paired):
    q = rows // 4
    return [
        pltpu.VMEM((2, 4, rows, cols), BF),
        pltpu.VMEM((2, 4, rows, cols) if paired else (16, 128), BF),
        pltpu.VMEM((4, 2 * q, cols), BF),
        pltpu.VMEM((4, 2, q, cols), BF),
        pltpu.VMEM((4, q, cols), BF),
        pltpu.VMEM((4, q, cols), BF),
        pltpu.VMEM((4, 2 * q, cols), BF),
        pltpu.VMEM((3, 2 * q, cols), BF),
        pltpu.VMEM((2 * q, cols), BF),
    ]


def att_scatter_kernel(count, grp_ref, q_ref, lse_ref, kvo_ref, kvp_ref, gm, *refs):
    grads = refs[:count]
    dq_ref, dkvo_ref, dkv_ref = refs[count : count + 3]
    outs = refs[count + 3 : 2 * count + 3]
    rest = refs[2 * count + 3 :]
    bufs, (gmx, sem_s, sem_r, l_sems, m_send, m_recv, m_local) = rest[: 9 * count], rest[9 * count :]
    p, j = pl.program_id(0), pl.program_id(1)
    step = p * pl.num_programs(1) + j
    x, z, g, y, c = places()
    hooks = rs_steps(
        [
            rs_plan(grads[k], outs[k], bufs[9 * k : 9 * k + 9], (sem_s, sem_r), l_sems, k, True)
            for k in range(count)
        ]
    )

    def exchange(i):
        cols = pl.ds(128 * i, 128)
        return (
            pltpu.make_async_copy(gm.at[c, :, cols], gmx.at[i, c], m_local.at[i]),
            send(gm.at[1 - c, :, cols], gmx.at[i, c], (m_send, m_recv), i, {"gc": g ^ 1}),
        )

    @pl.when(step == 0)
    def _():
        greet(all_partners())
        for i in range(3):
            for copy in exchange(i):
                copy.start()
        for hook in hooks[0]:
            hook()
        for copy in exchange(0):
            copy.wait()

    for i in (1, 2):

        @pl.when(step == 8 * i)
        def _():
            for copy in exchange(i):
                copy.wait()

    last = len(hooks) - 1
    for when in range(1, 23):
        parts = [h for i in range(1, last) if i * 22 // (last - 1) == when for h in hooks[i]]
        if parts:

            @pl.when(step == when)
            def _():
                for hook in parts:
                    hook()

    group = grp_ref[j]
    low = lax.broadcasted_iota(jnp.int32, (CL, 128), 1) < 64
    zero = jnp.zeros((CL, 128), BF)
    q = q_ref[...]
    gmix = gmx[p, j // 4, pl.ds(pl.multiple_of((j % 4) * CL, CL), CL)]
    stacks = (
        jnp.concatenate([jnp.where(low, zero, q), jnp.where(low, gmix, zero)], axis=0),
        jnp.concatenate([jnp.where(low, q, zero), jnp.where(low, zero, gmix)], axis=0),
    )

    @pl.when(z >= 2)
    def _():
        row = lax.broadcasted_iota(jnp.int32, (CL, CL), 0)
        near_ok = row <= lax.broadcasted_iota(jnp.int32, (CL, CL), 1)
        dqs = []
        for h in range(2):
            cols = slice(128 * h, 128 * h + 128)
            kv = kvp_ref[group, :, cols]
            kvo = kvo_ref[:, cols]
            lse = lse_ref[0, 0, h : h + 1, :]
            far = nt(kv, stacks[h])
            near = nt(kvo, stacks[h])
            pf = jnp.exp(far[:, :CL] - lse)
            pn = jnp.where(near_ok, jnp.exp(near[:, :CL] - lse), 0.0)
            df = far[:, CL:]
            dn = near[:, CL:]
            inner = jnp.sum(pf * df, axis=0, keepdims=True) + jnp.sum(
                pn * dn, axis=0, keepdims=True
            )
            sf = (pf * (df - inner)).astype(BF)
            sn = (pn * (dn - inner)).astype(BF)
            dkv_ref[0, :, cols] = nn(
                jnp.concatenate([sf, pf.astype(BF)], axis=1), stacks[h]
            ).astype(BF)
            dkvo_ref[:, cols] = nn(
                jnp.concatenate([sn, pn.astype(BF)], axis=1), stacks[h]
            ).astype(BF)
            dqs.append(tn(sf, kv) + tn(sn, kvo))
        dq_ref[...] = (jnp.where(low, dqs[1], dqs[0]) * 0.125).astype(BF)

    @pl.when(z < 2)
    def _():
        limit = z * QROWS + (j % (QROWS // CL)) * CL
        key = lax.broadcasted_iota(jnp.int32, (P_SIZE, CL), 0)
        row = lax.broadcasted_iota(jnp.int32, (P_SIZE, CL), 1)
        allowed = key - row <= limit
        dqs = []
        for h in range(2):
            cols = slice(128 * h, 128 * h + 128)
            kv = kvp_ref[group, :, cols]
            lse = lse_ref[0, 0, h : h + 1, :]
            far = nt(kv, stacks[h])
            pf = jnp.where(allowed, jnp.exp(far[:, :CL] - lse), 0.0)
            df = far[:, CL:]
            inner = jnp.sum(pf * df, axis=0, keepdims=True)
            sf = (pf * (df - inner)).astype(BF)
            dkv_ref[0, :, cols] = nn(
                jnp.concatenate([sf, pf.astype(BF)], axis=1), stacks[h]
            ).astype(BF)
            dqs.append(tn(sf, kv))
        dkvo_ref[...] = jnp.zeros_like(dkvo_ref)
        dq_ref[...] = (jnp.where(low, dqs[1], dqs[0]) * 0.125).astype(BF)

    @pl.when(step == 23)
    def _():
        for hook in hooks[last]:
            hook()


def attend_back_scatter(grp, q, lse, kvo, kvp, gm, grads, collective_id):
    rows = q.shape[0]
    count = len(grads)
    any_space = pl.BlockSpec(memory_space=pl.ANY)
    scratch = []
    for grad in grads:
        scratch += rs_scratch(grad.shape[2], grad.shape[3], True)
    slots = RS_SLOTS * count
    return pl.pallas_call(
        partial(att_scatter_kernel, count),
        name="attend_back_scatter",
        grid_spec=pltpu.PrefetchScalarGridSpec(
            num_scalar_prefetch=1,
            grid=(3, rows // CL),
            in_specs=[
                pl.BlockSpec((CL, 128), lambda p, j, *_: (j, p)),
                pl.BlockSpec((1, 1, 2, 128), lambda p, j, *_: (p, j, 0, 0)),
                pl.BlockSpec((CL, 256), lambda p, j, *_: (j, p)),
                pl.BlockSpec((4, P_SIZE, 256), lambda p, j, *_: (0, 0, p)),
            ]
            + [any_space] * (count + 1),
            out_specs=[
                pl.BlockSpec((CL, 128), lambda p, j, *_: (j, p)),
                pl.BlockSpec((CL, 256), lambda p, j, *_: (j, p)),
                pl.BlockSpec((1, P_SIZE, 256), lambda p, j, *_: (j, 0, p)),
            ]
            + [pl.BlockSpec(grad.shape[2:], lambda p, j, *_: (0, 0)) for grad in grads],
            scratch_shapes=scratch
            + [
                pltpu.VMEM((3, 2, QROWS, 128), BF),
                pltpu.SemaphoreType.DMA((slots,)),
                pltpu.SemaphoreType.DMA((slots,)),
                pltpu.SemaphoreType.DMA((8 * count,)),
                pltpu.SemaphoreType.DMA((3,)),
                pltpu.SemaphoreType.DMA((3,)),
                pltpu.SemaphoreType.DMA((3,)),
            ],
        ),
        out_shape=[
            jax.ShapeDtypeStruct((rows, 384), BF),
            jax.ShapeDtypeStruct((rows, 768), BF),
            jax.ShapeDtypeStruct((8, P_SIZE, 768), BF),
        ]
        + [jax.ShapeDtypeStruct(grad.shape[2:], F32) for grad in grads],
        compiler_params=pltpu.CompilerParams(
            collective_id=collective_id, has_side_effects=True, vmem_limit_bytes=56 << 20
        ),
    )(grp, q, lse, kvo, kvp.reshape(4, P_SIZE, kvp.shape[1]), gm, *grads)


def fold_kernel(grp_ref, dkv_ref, w_ref, dkvp_ref, part_ref, acc):
    acc[...] = jnp.zeros_like(acc)
    for j in range(8):
        acc[grp_ref[j]] += dkv_ref[j].astype(F32)
    for k in range(4):
        low = acc[k].astype(BF)
        dkvp_ref[k] = low
        part_ref[k] = nt(low, w_ref[...]).astype(BF)


def fold_prompts(grp, dkv, w_kv):
    tile = 128
    block = pl.BlockSpec((4, tile, D), lambda i, *_: (0, i, 0))
    shape = jax.ShapeDtypeStruct((4, P_SIZE, D), BF)
    return pl.pallas_call(
        fold_kernel,
        name="fold_prompts",
        grid_spec=pltpu.PrefetchScalarGridSpec(
            num_scalar_prefetch=1,
            grid=(P_SIZE // tile,),
            in_specs=[
                pl.BlockSpec((8, tile, D), lambda i, *_: (0, i, 0)),
                pl.BlockSpec((D, D), lambda i, *_: (0, 0)),
            ],
            out_specs=[block, block],
            scratch_shapes=[pltpu.VMEM((4, tile, D), F32)],
        ),
        out_shape=[shape, shape],
        compiler_params=pltpu.CompilerParams(vmem_limit_bytes=40 << 20),
    )(grp, dkv, w_kv)


def norm_rows(hidden, gain, shift):
    center = jnp.mean(hidden, axis=1, keepdims=True)
    offset = hidden - center
    factor = lax.rsqrt(jnp.mean(offset * offset, axis=1, keepdims=True) + eps)
    return offset * factor * gain + shift


CHUNKS = 4


def start_kernel(
    tokens,
    vec,
    bup,
    own,
    wq,
    prompts,
    chip,
    wpair,
    vec_out,
    bup_out,
    own_out,
    n1,
    vec_in,
    z_sems,
    y_sems,
    d_sems,
    w_sems,
    s_sems,
    l_sems,
):
    x, z, g, y, c = places()
    sib, over_y, over_x = {"gc": g ^ 1}, {"gc": g ^ 2}, {"dp": x ^ 1}
    greet(all_partners() + [{"gc": g ^ 3}])
    half_rows = wq.shape[0] // 2
    my_half = pl.ds(pl.multiple_of(x * half_rows, 16), half_rows)

    small = []
    for s in (1, 2, 3):
        to = {"gr": z ^ s}
        small.append(send(vec, vec_in.at[s], s_sems, s, to))
        small.append(send(own, own_out.at[z], s_sems, 3 + s, to))
        small.append(send(bup, bup_out.at[g], s_sems, 6 + s, {"gc": g ^ s}))
    for copy in small:
        copy.start()
    own_out[z] = own[...]
    bup_out[g] = bup[...]

    w_local = pltpu.make_async_copy(wq.at[my_half], wpair.at[y, z, my_half], l_sems.at[0])
    w_local.start()
    w_gr = [
        send(wq.at[my_half], wpair.at[y, z, my_half], w_sems, s, {"gr": z ^ s}) for s in (1, 2, 3)
    ]
    for copy in w_gr:
        copy.start()

    def w_step(s):
        block = z ^ s
        piece = wpair.at[y, block, my_half]
        across = wpair.at[1 - y, block, my_half]
        return (
            send(piece, piece, w_sems, 4 + s, over_y),
            send(piece, piece, w_sems, 8 + s, over_x),
            send(across, across, w_sems, 12 + s, over_x),
        )

    for copy in small[0::3]:
        copy.wait_recv()
    total = vec[...]
    for s in (1, 2, 3):
        total = total + vec_in[s]
    vec_out[...] = total

    @pl.loop(0, QROWS // 128)
    def _(i):
        rows = pl.ds(pl.multiple_of(i * 128, 128), 128)
        hidden = tokens[rows].astype(F32) + vec_out[0:1]
        n1[rows] = norm_rows(hidden, vec_out[1:2], vec_out[2:3]).astype(BF)

    to_chip = pltpu.make_async_copy(n1, chip.at[c], l_sems.at[1])
    to_chip.start()
    chip_send = send(n1, chip.at[c], s_sems, 10, sib)
    chip_send.start()
    is_prompt = z < 2

    @pl.when(is_prompt)
    def _():
        local = pltpu.make_async_copy(n1, prompts.at[g, z], l_sems.at[2])
        local.start()
        local.wait()

    w_local.wait()
    for copy in w_step(0)[:2]:
        copy.start()

    rows = QROWS // CHUNKS

    def item(column, half, k):
        return prompts.at[column, half, pl.ds(k * rows, rows)]

    def copies(half, k):
        mine = item(g, half, k)
        across = item(g ^ 2, half, k)
        n = half * CHUNKS + k
        return {
            "up": send(mine, mine, z_sems, n, {"gr": jnp.minimum(z + 1, 3)}),
            "down": send(
                mine, mine, z_sems, n, {"gr": jnp.maximum(z - 1, 0)}, 2 * CHUNKS + k
            ),
            "y": send(mine, mine, y_sems, n, over_y),
            "core": send(mine, mine, d_sems, n, sib),
            "core2": send(across, across, d_sems, 2 * CHUNKS + n, sib),
        }

    first = jnp.where(z == 0, 0, 1)

    def forward(step):
        half = first if step < CHUNKS else 1 - first
        k = step % CHUNKS
        moves = copies(half, k)

        @pl.when(half != z)
        def _():
            moves["up"].wait_recv()

        @pl.when(jnp.logical_and(z < 3, half <= z))
        def _():
            moves["up"].start()

        @pl.when(jnp.logical_and(z == 1, half == 1))
        def _():
            moves["down"].start()

        moves["y"].start()
        moves["core"].start()

    def across(step):
        half = first if step < CHUNKS else 1 - first
        moves = copies(half, step % CHUNKS)
        moves["y"].wait_recv()
        moves["core2"].start()

    for step in range(2 * CHUNKS):
        forward(step)
        if step >= 2:
            across(step - 2)
        if step in (1, 2, 3):
            w_gr[step - 1].wait_recv()
            one, two, _ = w_step(step)
            one.start()
            two.start()
        if step in (4, 5, 6, 7):
            one, _, three = w_step(step - 4)
            one.wait_recv()
            three.start()
    across(2 * CHUNKS - 2)
    across(2 * CHUNKS - 1)

    for step in range(2 * CHUNKS):
        half = first if step < CHUNKS else 1 - first
        moves = copies(half, step % CHUNKS)
        moves["core"].wait_recv()
        moves["core2"].wait_recv()
        moves["y"].wait_send()
        moves["core"].wait_send()
        moves["core2"].wait_send()

        @pl.when(jnp.logical_and(z < 3, half <= z))
        def _():
            moves["up"].wait_send()

        @pl.when(jnp.logical_and(z == 1, half == 1))
        def _():
            moves["down"].wait_send()

    for copy in w_gr:
        copy.wait_send()
    for s in range(4):
        one, two, three = w_step(s)
        one.wait_send()
        two.wait()
        three.wait()
    for i, copy in enumerate(small):
        if i % 3 == 0:
            copy.wait_send()
        else:
            copy.wait()
    to_chip.wait()
    chip_send.wait()


def start_exchange(tokens, vec, bup, own, wq, collective_id):
    any_space = pl.BlockSpec(memory_space=pl.ANY)
    vmem = pl.BlockSpec(memory_space=pltpu.VMEM)

    def dma(count):
        return pltpu.SemaphoreType.DMA((count,))

    def pair(count, extra=0):
        return dma(count + extra), dma(count)

    z_pair, y_pair, d_pair = pair(2 * CHUNKS, CHUNKS), pair(2 * CHUNKS), pair(4 * CHUNKS)
    w_pair, s_pair = pair(16), pair(11)

    def body(*refs):
        main, sems = refs[:13], refs[13:]
        start_kernel(*main, sems[0:2], sems[2:4], sems[4:6], sems[6:8], sems[8:10], sems[10])

    return pl.pallas_call(
        body,
        name="start_exchange",
        in_specs=[vmem, vmem, vmem, vmem, any_space],
        out_specs=[any_space, any_space, any_space, vmem, vmem, vmem],
        out_shape=[
            jax.ShapeDtypeStruct((4, 2, QROWS, D), BF),
            jax.ShapeDtypeStruct((2, QROWS, D), BF),
            jax.ShapeDtypeStruct((2, 4) + wq.shape, BF),
            jax.ShapeDtypeStruct(vec.shape, F32),
            jax.ShapeDtypeStruct((4,) + bup.shape, F32),
            jax.ShapeDtypeStruct((4,) + own.shape, jnp.int32),
        ],
        scratch_shapes=[pltpu.VMEM((QROWS, D), BF), pltpu.VMEM((4,) + vec.shape, F32)]
        + [*z_pair, *y_pair, *d_pair, *w_pair, *s_pair, dma(3)],
        compiler_params=pltpu.CompilerParams(
            collective_id=collective_id, has_side_effects=True, vmem_limit_bytes=32 << 20
        ),
    )(tokens, vec, bup, own, wq)


GATHER_SLOTS = 36


def gather_steps(blocks, wholes, sems, l_sems):
    x, z, g, y, c = places()
    sib, over_y, over_x = {"gc": g ^ 1}, {"gc": g ^ 2}, {"dp": x ^ 1}
    steps = []

    def plan(a):
        block, whole = blocks[a], wholes[a]
        rows = block.shape[0]
        q = rows // 4
        half = pl.ds(pl.multiple_of(x * 2 * q, 16), 2 * q)
        qa = pl.ds(pl.multiple_of(x * 2 * q, 16), q)
        qb = pl.ds(pl.multiple_of(x * 2 * q + q, 16), q)
        base = a * GATHER_SLOTS
        local = pltpu.make_async_copy(block.at[half], whole.at[g, z, half], l_sems.at[a])
        by_gr = [
            send(block.at[half], whole.at[g, z, half], sems, base + s, {"gr": z ^ s})
            for s in (1, 2, 3)
        ]

        def moves(s):
            o = base + 4 + 8 * s
            mine, far = whole.at[g, z ^ s], whole.at[g ^ 2, z ^ s]
            return {
                "ay": send(mine.at[qa], mine.at[qa], sems, o, over_y),
                "ax": send(mine.at[qa], mine.at[qa], sems, o + 1, over_x),
                "afx": send(far.at[qa], far.at[qa], sems, o + 2, over_x),
                "bx": send(mine.at[qb], mine.at[qb], sems, o + 3, over_x),
                "by": send(mine.at[qb], mine.at[qb], sems, o + 4, over_y),
                "bfy": send(
                    mine.at[pl.ds(pl.multiple_of((1 - x) * 2 * q + q, 16), q)],
                    mine.at[pl.ds(pl.multiple_of((1 - x) * 2 * q + q, 16), q)],
                    sems,
                    o + 5,
                    over_y,
                ),
                "c1": send(mine, mine, sems, o + 6, sib),
                "c2": send(far, far, sems, o + 7, sib),
            }

        return local, by_gr, moves

    plans = [plan(a) for a in range(len(blocks))]

    def begin():
        for local, by_gr, _ in plans:
            local.start()
            for copy in by_gr:
                copy.start()
        for local, _, _ in plans:
            local.wait()

    def first(a, s):
        def run():
            _, by_gr, moves = plans[a]
            if s:
                by_gr[s - 1].wait_recv()
            m = moves(s)
            for name in ("ay", "bx", "ax", "by"):
                m[name].start()

        return run

    def second(a, s):
        def run():
            m = plans[a][2](s)
            m["ay"].wait_recv()
            m["afx"].start()
            m["bx"].wait_recv()
            m["bfy"].start()

        return run

    def third(a, s):
        def run():
            m = plans[a][2](s)
            for name in ("ax", "afx", "by", "bfy"):
                m[name].wait_recv()
            m["c1"].start()
            m["c2"].start()

        return run

    def finish():
        for _, by_gr, moves in plans:
            for copy in by_gr:
                copy.wait_send()
            for s in range(4):
                m = moves(s)
                m["c1"].wait_recv()
                m["c2"].wait_recv()
                for copy in m.values():
                    copy.wait_send()

    order = [(a, s) for a in range(len(blocks)) for s in range(4)]
    steps = [begin]
    n = len(order)
    for i in range(n + 4):
        part = []
        if i < n:
            part.append(first(*order[i]))
        if 2 <= i < n + 2:
            part.append(second(*order[i - 2]))
        if i >= 4:
            part.append(third(*order[i - 4]))
        steps.append(partial(lambda fs: [f() for f in fs], part))
    steps.append(finish)
    return steps


def att_gather_kernel(count, grp_ref, q_ref, kvo_ref, kvp_ref, *refs):
    blocks = refs[:count]
    mixed, lse_ref = refs[count : count + 2]
    wholes = refs[count + 2 : 2 * count + 2]
    mix, sems_s, sems_r, l_sems, m_send, m_recv, m_local = refs[2 * count + 2 :]
    p, j = pl.program_id(0), pl.program_id(1)
    step = p * pl.num_programs(1) + j
    x, z, g, y, c = places()

    hooks = gather_steps(blocks, wholes, (sems_s, sems_r), l_sems)

    @pl.when(step == 0)
    def _():
        greet(all_partners())

    last = len(hooks) - 1
    for i, hook in enumerate(hooks):
        when = i * 23 // last
        if i == last:
            continue

        @pl.when(step == when)
        def _():
            hook()

    group = grp_ref[j]
    low = lax.broadcasted_iota(jnp.int32, (CL, 128), 1) < 64
    zero = jnp.zeros((CL, 128), BF)
    q = q_ref[...]
    q_parts = (jnp.where(low, zero, q), jnp.where(low, q, zero))

    def store(mixes, sums):
        mix[p, j // 4, pl.ds(pl.multiple_of((j % 4) * CL, CL), CL)] = jnp.where(
            low, mixes[0], mixes[1]
        ).astype(BF)
        flat = jnp.where(low, sums[0], sums[1]).T
        lse_ref[0, 0, 0:1] = flat[0:1]
        lse_ref[0, 0, 1:2] = flat[64:65]

    @pl.when(z >= 2)
    def _():
        row = lax.broadcasted_iota(jnp.int32, (CL, CL), 0)
        near_ok = lax.broadcasted_iota(jnp.int32, (CL, CL), 1) <= row
        mixes, sums = [], []
        for h in range(2):
            cols = slice(128 * h, 128 * h + 128)
            kv = kvp_ref[group, :, cols]
            kvo = kvo_ref[:, cols]
            far = nt(q_parts[h], kv)
            near = jnp.where(near_ok, nt(q_parts[h], kvo), negative)
            top = jnp.maximum(
                jnp.max(far, axis=1, keepdims=True), jnp.max(near, axis=1, keepdims=True)
            )
            far = jnp.exp(far - top)
            near = jnp.exp(near - top)
            total = jnp.sum(far, axis=1, keepdims=True) + jnp.sum(near, axis=1, keepdims=True)
            mixes.append((nn(far.astype(BF), kv) + nn(near.astype(BF), kvo)) / total)
            sums.append(jnp.broadcast_to(top + jnp.log(total), (CL, 128)))
        store(mixes, sums)

    @pl.when(z < 2)
    def _():
        limit = z * QROWS + (j % (QROWS // CL)) * CL
        row = lax.broadcasted_iota(jnp.int32, (CL, P_SIZE), 0)
        key = lax.broadcasted_iota(jnp.int32, (CL, P_SIZE), 1)
        allowed = key - row <= limit
        mixes, sums = [], []
        for h in range(2):
            cols = slice(128 * h, 128 * h + 128)
            kv = kvp_ref[group, :, cols]
            far = jnp.where(allowed, nt(q_parts[h], kv), negative)
            top = jnp.max(far, axis=1, keepdims=True)
            far = jnp.exp(far - top)
            total = jnp.sum(far, axis=1, keepdims=True)
            mixes.append(nn(far.astype(BF), kv) / total)
            sums.append(jnp.broadcast_to(top + jnp.log(total), (CL, 128)))
        store(mixes, sums)

    def exchange(i):
        cols = pl.ds(128 * i, 128)
        return (
            pltpu.make_async_copy(mix.at[i, c], mixed.at[c, :, cols], m_local.at[i]),
            send(mix.at[i, 1 - c], mixed.at[c, :, cols], (m_send, m_recv), i, {"gc": g ^ 1}),
        )

    for i in range(3):

        @pl.when(step == 8 * i + 7)
        def _():
            for copy in exchange(i):
                copy.start()

    @pl.when(step == 23)
    def _():
        hooks[last]()
        for i in range(3):
            for copy in exchange(i):
                copy.wait()


def attend_gather(grp, q, kvo, kvp, blocks, collective_id):
    rows = q.shape[0]
    count = len(blocks)
    any_space = pl.BlockSpec(memory_space=pl.ANY)
    slots = GATHER_SLOTS * count
    return pl.pallas_call(
        partial(att_gather_kernel, count),
        name="attend_gather",
        grid_spec=pltpu.PrefetchScalarGridSpec(
            num_scalar_prefetch=1,
            grid=(3, rows // CL),
            in_specs=[
                pl.BlockSpec((CL, 128), lambda p, j, *_: (j, p)),
                pl.BlockSpec((CL, 256), lambda p, j, *_: (j, p)),
                pl.BlockSpec((4, P_SIZE, 256), lambda p, j, *_: (0, 0, p)),
            ]
            + [any_space] * count,
            out_specs=[any_space, pl.BlockSpec((1, 1, 2, 128), lambda p, j, *_: (p, j, 0, 0))]
            + [any_space] * count,
            scratch_shapes=[
                pltpu.VMEM((3, 2, QROWS, 128), BF),
                pltpu.SemaphoreType.DMA((slots,)),
                pltpu.SemaphoreType.DMA((slots,)),
                pltpu.SemaphoreType.DMA((count,)),
                pltpu.SemaphoreType.DMA((3,)),
                pltpu.SemaphoreType.DMA((3,)),
                pltpu.SemaphoreType.DMA((3,)),
            ],
        ),
        out_shape=[
            jax.ShapeDtypeStruct((2, QROWS, 384), BF),
            jax.ShapeDtypeStruct((3, rows // CL, 2, 128), F32),
        ]
        + [jax.ShapeDtypeStruct((4, 4) + block.shape, BF) for block in blocks],
        compiler_params=pltpu.CompilerParams(
            collective_id=collective_id, has_side_effects=True, vmem_limit_bytes=40 << 20
        ),
    )(grp, q, kvo, kvp.reshape(4, P_SIZE, kvp.shape[1]), *blocks)


def tail_kernel(
    part,
    chip,
    dw,
    grad_h2,
    tokens,
    vec,
    sums,
    out,
    sums_out,
    dw_out,
    own,
    ra,
    rb,
    rz,
    keep,
    take,
    gsum,
    cur,
    sb,
    *rest,
):
    bufs, (sem_s, sem_r, l_sems, w_s, w_r, w_l) = rest[:9], rest[9:]
    sems = (sem_s, sem_r)
    x, z, g, y, c = places()
    sib, over_y, over_x = {"gc": g ^ 1}, {"gc": g ^ 2}, {"dp": x ^ 1}
    down = {"gr": jnp.maximum(z - 1, 0)}
    far = z >= 2
    greet(all_partners())
    hooks = rs_steps([rs_plan(dw, dw_out, bufs, (w_s, w_r), w_l, 0, False)])
    size = QROWS // CHUNKS
    chunks = [(h, k) for h in range(2) for k in range(CHUNKS)]

    def rows(k):
        return pl.ds(k * size, size)

    def index(side):
        return 1 - y if side == 0 else y

    def load(side, h, k):
        i = index(side)
        return pltpu.make_async_copy(
            part.at[2 * i + c, h, rows(k)],
            own.at[i, h, rows(k)],
            l_sems.at[8 * side + CHUNKS * h + k],
        )

    def hop_a(side, h, k):
        i = index(side)
        return send(
            part.at[2 * i + 1 - c, h, rows(k)],
            ra.at[i, h, rows(k)],
            sems,
            8 * side + CHUNKS * h + k,
            sib,
        )

    def hop_y(h, k):
        return send(
            own.at[1 - y, h, rows(k)], rb.at[h, rows(k)], sems, 16 + CHUNKS * h + k, over_y
        )

    def hop_z(h, k):
        return send(own.at[y, h, rows(k)], rz.at[h, rows(k)], sems, 24 + CHUNKS * h + k, down)

    hop_chip = send(chip.at[1 - c], take, sems, 32, sib)
    load_chip = pltpu.make_async_copy(chip.at[c], keep, l_sems.at[16])

    def fold(h, k, other):
        add_into(own.at[y, h, rows(k)], own.at[y, h, rows(k)], other.at[rows(k)])

    for h, k in chunks:

        @pl.when(far)
        def _():
            load(0, h, k).start()
            hop_a(0, h, k).start()

        load(1, h, k).start()
        hop_a(1, h, k).start()
    hop_chip.start()
    load_chip.start()
    for hook in hooks[0]:
        hook()

    def stage1(h, k):
        @pl.when(far)
        def _():
            load(0, h, k).wait()
            hop_a(0, h, k).wait()
            add_into(
                own.at[1 - y, h, rows(k)], own.at[1 - y, h, rows(k)], ra.at[1 - y, h, rows(k)]
            )
            hop_y(h, k).start()

        load(1, h, k).wait()
        hop_a(1, h, k).wait()
        fold(h, k, ra.at[y, h])

    def stage2(h, k):
        @pl.when(far)
        def _():
            hop_y(h, k).wait()
            fold(h, k, rb.at[h])

        @pl.when(z == 3)
        def _():
            hop_z(h, k).start()

    def stage3(h, k):
        @pl.when(z == 2)
        def _():
            hop_z(h, k).wait_recv()
            fold(h, k, rz.at[h])
            hop_z(h, k).start()

    def stage4(h, k):
        @pl.when(z == 1)
        def _():
            hop_z(h, k).wait_recv()
            fold(h, k, rz.at[h])
            if h == 0:
                hop_z(h, k).start()

    def stage5(h, k):
        if h == 0:

            @pl.when(z == 0)
            def _():
                hop_z(h, k).wait_recv()
                fold(h, k, rz.at[h])

    n = len(chunks)
    stages = (stage1, stage2, stage3, stage4, stage5)
    for i in range(max(n + 4, len(hooks) - 1)):
        for lag, stage in enumerate(stages):
            if 0 <= i - lag < n:
                stage(*chunks[i - lag])
        if i + 1 < len(hooks):
            for hook in hooks[i + 1]:
                hook()
    for h, k in chunks:

        @pl.when(z >= 2 if h else z >= 1)
        def _():
            hop_z(h, k).wait_send()

    load_chip.wait()
    hop_chip.wait()

    @pl.loop(0, CHUNKS)
    def _(k):
        r = pl.ds(pl.multiple_of(k * size, size), size)
        gsum[r] = keep[r].astype(F32) + take[r].astype(F32)

    @pl.when(z < 2)
    def _():
        place = jnp.minimum(z, 1)

        @pl.loop(0, CHUNKS)
        def _(k):
            r = pl.ds(pl.multiple_of(k * size, size), size)
            gsum[r] += own[y, place, r].astype(F32)

    cur[...] = sums[...]

    @pl.loop(0, CHUNKS)
    def _(k):
        r = pl.ds(pl.multiple_of(k * size, size), size)
        hidden = tokens[r].astype(F32) + vec[0:1]
        center = jnp.mean(hidden, axis=1, keepdims=True)
        offset = hidden - center
        factor = lax.rsqrt(jnp.mean(offset * offset, axis=1, keepdims=True) + eps)
        unit = offset * factor
        grad = gsum[r]
        scaled = grad * vec[1:2]
        first = jnp.mean(scaled, axis=1, keepdims=True)
        second = jnp.mean(scaled * unit, axis=1, keepdims=True)
        total = grad_h2[r] + factor * (scaled - first - unit * second)
        out[r] = total
        cur[0:1] += jnp.sum(total, axis=0, keepdims=True)
        cur[1:2] += jnp.sum(grad * unit, axis=0, keepdims=True)
        cur[2:3] += jnp.sum(grad, axis=0, keepdims=True)

    for i, target in enumerate((sib, over_y, over_x)):
        hop = send(cur, sb.at[i], sems, 33 + i, target)
        hop.start()
        hop.wait()
        cur[...] += sb[i]
    hops = [send(cur, sb.at[2 + s], sems, 35 + s, {"gr": z ^ s}) for s in (1, 2, 3)]
    for hop in hops:
        hop.start()
    for hop in hops:
        hop.wait()
    sums_out[...] = (cur[...] + sb[3]) + (sb[4] + sb[5])


def tail_exchange(part, chip, dw, grad_h2, tokens, vec, sums, collective_id):
    any_space = pl.BlockSpec(memory_space=pl.ANY)
    vmem = pl.BlockSpec(memory_space=pltpu.VMEM)
    return pl.pallas_call(
        tail_kernel,
        name="tail_exchange",
        in_specs=[any_space, any_space, any_space, vmem, vmem, vmem, vmem],
        out_specs=[vmem, vmem, vmem],
        out_shape=[
            jax.ShapeDtypeStruct((QROWS, D), F32),
            jax.ShapeDtypeStruct(sums.shape, F32),
            jax.ShapeDtypeStruct(dw.shape[2:], F32),
        ],
        scratch_shapes=[
            pltpu.VMEM((2, 2, QROWS, D), BF),
            pltpu.VMEM((2, 2, QROWS, D), BF),
            pltpu.VMEM((2, QROWS, D), BF),
            pltpu.VMEM((2, QROWS, D), BF),
            pltpu.VMEM((QROWS, D), BF),
            pltpu.VMEM((QROWS, D), BF),
            pltpu.VMEM((QROWS, D), F32),
            pltpu.VMEM(sums.shape, F32),
            pltpu.VMEM((6,) + sums.shape, F32),
        ]
        + rs_scratch(dw.shape[2], dw.shape[3], False)
        + [
            pltpu.SemaphoreType.DMA((39,)),
            pltpu.SemaphoreType.DMA((39,)),
            pltpu.SemaphoreType.DMA((17,)),
            pltpu.SemaphoreType.DMA((RS_SLOTS,)),
            pltpu.SemaphoreType.DMA((RS_SLOTS,)),
            pltpu.SemaphoreType.DMA((8,)),
        ],
        compiler_params=pltpu.CompilerParams(
            collective_id=collective_id, has_side_effects=True, vmem_limit_bytes=48 << 20
        ),
    )(part, chip, dw, grad_h2, tokens, vec, sums)


def norm(hidden, gain, shift):
    center = jnp.mean(hidden, axis=1, keepdims=True)
    offset = hidden - center
    factor = lax.rsqrt(jnp.mean(offset * offset, axis=1, keepdims=True) + eps)
    unit = offset * factor
    return unit * gain + shift, unit, factor


def norm_back(grad, gain, unit, factor):
    grad_unit = grad * gain
    first = jnp.mean(grad_unit, axis=1, keepdims=True)
    second = jnp.mean(grad_unit * unit, axis=1, keepdims=True)
    grad_in = factor * (grad_unit - first - unit * second)
    return grad_in, jnp.sum(grad * unit, axis=0), jnp.sum(grad, axis=0)


def head_layout(blocks):
    chunks = blocks.transpose(1, 0, 2).reshape(D, 6, 3, HD)
    q_list, kv_list = [], []
    for pair in range(3):
        a, b = 2 * pair, 2 * pair + 1
        q_list += [chunks[:, b, 0], chunks[:, a, 0]]
        kv_list += [chunks[:, a, 2], chunks[:, a, 1], chunks[:, b, 1], chunks[:, b, 2]]
    return jnp.concatenate(q_list, axis=1), jnp.concatenate(kv_list, axis=1)


def head_layout_back(grad_q, grad_kv):
    qc = grad_q.reshape(D, 3, 2, HD)
    kc = grad_kv.reshape(D, 3, 4, HD)
    pieces = []
    for pair in range(3):
        pieces += [qc[:, pair, 1], kc[:, pair, 1], kc[:, pair, 0]]
        pieces += [qc[:, pair, 0], kc[:, pair, 2], kc[:, pair, 3]]
    whole = jnp.concatenate(pieces, axis=1)
    return whole.reshape(D, 2, 576).transpose(1, 0, 2)


def on_device(
    tokens,
    teacher,
    pass_embed,
    ln1_gain,
    ln1_bias,
    qkv_weight,
    out_weight,
    out_bias,
    ln2_gain,
    ln2_bias,
    fc1_weight,
    fc1_bias,
    fc2_weight,
    fc2_bias,
    cont_group,
    token_count,
):
    n_dp = lax.axis_size("dp")
    n_gr = lax.axis_size("gr")
    n_gc = lax.axis_size("gc")
    z = lax.axis_index("gr")
    g = lax.axis_index("gc")
    c = g % 2
    y = g // 2
    swap_core = [(i, i ^ 1) for i in range(n_gc)]
    swap_y = [(i, i ^ 2) for i in range(n_gc)]

    packed = jnp.stack(
        [pass_embed, ln1_gain, ln1_bias, out_bias, ln2_gain, ln2_bias, fc2_bias, fc2_bias]
    ).astype(F32)
    if n_dp == 2:
        vec = lax.dynamic_update_slice(jnp.zeros((8, D), F32), packed, (0, z * packed.shape[1]))
        bup = jnp.broadcast_to(fc1_bias.astype(F32), (8, fc1_bias.shape[0]))
        own = jnp.broadcast_to(jnp.pad(cont_group, (0, 120)), (8, 128))
        n1_prompt, n1_chip, w_pair, vectors, b_up, owners = start_exchange(
            tokens, vec, bup, own, qkv_weight, 1
        )
        n1_prompt = n1_prompt.reshape(4 * P_SIZE, D)
        n1_chip = n1_chip.reshape(2 * QROWS, D)
        w_qkv = w_pair.reshape(2, D, 576)
        b_up = b_up[:, 0].reshape(FF)
        owners = owners[:, 0, :8]
    else:
        vectors = lax.all_gather(packed, "gr", axis=1, tiled=True)
        b_up = lax.all_gather(fc1_bias, "gc", axis=0, tiled=True).astype(F32)
        owners = lax.all_gather(cont_group, "gr", axis=0, tiled=True)
    embed, gain1, shift1, b_out, gain2, shift2, b_down = [vectors[i] for i in range(7)]
    owners = owners.reshape(4, 2, 4)
    mine = lax.dynamic_slice(owners, (2 * y, jnp.maximum(z - 2, 0), 0), (2, 1, 4)).reshape(8)
    own_groups = jnp.repeat(2 * y + jnp.arange(2), 4)
    grp = jnp.where(z < 2, own_groups, mine).astype(jnp.int32)
    z_arr = z.astype(jnp.int32).reshape(1)

    hidden = tokens.astype(F32) + embed
    normed1, unit1, factor1 = norm(hidden, gain1, shift1)
    n1 = normed1.astype(BF)

    if n_dp != 2:
        w_other = lax.ppermute(qkv_weight, "gc", swap_y)
        w_pair = jnp.where(
            y == 0, jnp.stack([qkv_weight, w_other]), jnp.stack([w_other, qkv_weight])
        )
        w_qkv = lax.all_gather(w_pair, "gr", axis=1, tiled=True)
        n1_other = lax.ppermute(n1, "gc", swap_core)
        n1_chip = jnp.where(
            c == 0, jnp.concatenate([n1, n1_other]), jnp.concatenate([n1_other, n1])
        )
        n1_col = lax.all_gather(n1, "gr", axis=0, tiled=True)[:P_SIZE]
        n1_prompt = lax.all_gather(n1_col, "gc", axis=0, tiled=True)
    w_q, w_kv = head_layout(w_qkv)

    kvp = nn(n1_prompt, w_kv).astype(BF)
    kvo = nn(n1_chip, w_kv).astype(BF)
    q = (nn(n1_chip, w_q) * 0.125).astype(BF)
    if n_dp == 2:
        mixed, lse_rows, w_out, w_up, w_down = attend_gather(
            grp, q, kvo, kvp, [out_weight, fc1_weight, fc2_weight], 2
        )
    else:
        w_out = lax.all_gather(out_weight, ("gc", "gr"))
        w_up = lax.all_gather(fc1_weight, ("gc", "gr"))
        w_down = lax.all_gather(fc2_weight, ("gc", "gr"))
        mixed_heads, lse = attend(grp, z_arr, q, kvo, kvp)
        lse_rows = lse[:, ::64].reshape(8, CL, 3, 2).transpose(2, 0, 3, 1)
        halves = mixed_heads.reshape(2, QROWS, 384)
        keep = lax.dynamic_index_in_dim(halves, c, 0, keepdims=False)
        give = lax.dynamic_index_in_dim(halves, 1 - c, 0, keepdims=False)
        take = lax.ppermute(give, "gc", swap_core)
        mixed = jnp.where(c == 0, jnp.stack([keep, take]), jnp.stack([take, keep]))
    w_up = w_up.reshape(n_gc, D, FF // n_gc)
    w_down = w_down.reshape(n_gc, D, FF // n_gc)
    w_out = w_out.reshape(2, 2, n_gr, 192, 192).transpose(1, 0, 3, 2, 4).reshape(2, 384, D)

    attended = lax.dot_general(
        mixed, w_out, (((0, 2), (0, 1)), ((), ())), preferred_element_type=F32
    )
    hidden2 = hidden + attended + b_out
    normed2, unit2, factor2 = norm(hidden2, gain2, shift2)
    n2 = normed2.astype(BF)
    pre = lax.dot_general(n2, w_up, (((1,), (1,)), ((), ())), preferred_element_type=F32)
    pre = pre.reshape(QROWS, FF) + b_up
    active, gelu_back = jax.vjp(partial(jax.nn.gelu, approximate=True), pre)
    act = active.astype(BF)
    act_blocks = act.reshape(QROWS, n_gc, FF // n_gc)
    final = (
        hidden2
        + lax.dot_general(
            act_blocks, w_down, (((1, 2), (0, 2)), ((), ())), preferred_element_type=F32
        )
        + b_down
    )
    grad_final = final - teacher.astype(F32)
    squared = jnp.sum(grad_final * grad_final)
    gb = grad_final.astype(BF)
    grad_b_down = jnp.sum(gb, axis=0, dtype=F32)
    grad_active = lax.dot_general(
        gb, w_down, (((1,), (1,)), ((), ())), preferred_element_type=F32
    ).reshape(QROWS, FF)
    grad_w_down = jnp.einsum("td,tgf->gdf", gb, act_blocks, preferred_element_type=F32)
    (grad_pre,) = gelu_back(grad_active)
    gp = grad_pre.astype(BF)
    gp_blocks = gp.reshape(QROWS, n_gc, FF // n_gc)
    grad_b_up = jnp.sum(gp, axis=0, dtype=F32)
    grad_w_up = jnp.einsum("td,tgf->gdf", n2, gp_blocks, preferred_element_type=F32)
    grad_n2 = lax.dot_general(
        gp_blocks, w_up, (((1, 2), (0, 2)), ((), ())), preferred_element_type=F32
    )
    back2, grad_gain2, grad_shift2 = norm_back(grad_n2, gain2, unit2, factor2)
    grad_h2 = grad_final + back2
    ga = grad_h2.astype(BF)
    grad_b_out = jnp.sum(ga, axis=0, dtype=F32)
    grad_w_out = jnp.einsum("ctk,tn->ckn", mixed, ga, preferred_element_type=F32)
    gm = jnp.einsum("tn,ckn->ctk", ga, w_out, preferred_element_type=F32).astype(BF)

    weight_grads = [
        grad_w_down.astype(BF).reshape(n_gc, n_gr, 192, 768),
        grad_w_up.astype(BF).reshape(n_gc, n_gr, 192, 768),
        grad_w_out.astype(BF)
        .reshape(2, 2, 192, n_gr, 192)
        .transpose(1, 0, 3, 2, 4)
        .reshape(n_gc, n_gr, 192, 192),
    ]
    if n_dp == 2:
        dq, dkvo, dkv, out_w_down, out_w_up, out_w_out = attend_back_scatter(
            grp, q, lse_rows, kvo, kvp, gm, weight_grads, 3
        )
        dkvp, part_prompt = fold_prompts(grp, dkv, w_kv)
        dkvp = dkvp.reshape(4 * P_SIZE, D)
        part_prompt = part_prompt.reshape(4 * P_SIZE, D)
    else:
        gm_keep = lax.dynamic_index_in_dim(gm, c, 0, keepdims=False)
        gm_give = lax.dynamic_index_in_dim(gm, 1 - c, 0, keepdims=False)
        gm_take = lax.ppermute(gm_give, "gc", swap_core)
        gm_chip = jnp.where(c == 0, jnp.stack([gm_keep, gm_take]), jnp.stack([gm_take, gm_keep]))
        gm_chip = gm_chip.reshape(2 * QROWS, 384)

        def scatter16(blocks):
            part = lax.psum_scatter(
                blocks.reshape(n_gc * n_gr * blocks.shape[2], -1),
                ("gc", "gr"),
                scatter_dimension=0,
                tiled=True,
            )
            return lax.psum(part, "dp").astype(F32)

        out_w_down, out_w_up, out_w_out = [scatter16(grad) for grad in weight_grads]
        dq, dkvo, dkvp = attend_back(grp, z_arr, q, gm_chip, lse_rows, kvo, kvp)
        part_prompt = nt(dkvp, w_kv).astype(BF)

    part_chip = (nt(dq, w_q) + nt(dkvo, w_kv)).reshape(2, QROWS, D)
    grad_kv = tn(n1_prompt, dkvp) + tn(n1_chip, dkvo)
    grad_q = tn(n1_chip, dq)
    grad_qkv = head_layout_back(grad_q, grad_kv)
    later_sums = jnp.concatenate(
        [
            grad_gain2[None],
            grad_shift2[None],
            grad_b_out[None],
            grad_b_down[None],
            grad_b_up.reshape(4, D),
            jnp.broadcast_to(squared, (1, D)),
            jnp.zeros((4, D), F32),
        ]
    )
    if n_dp == 2:
        input_grad, sums, out_w_qkv = tail_exchange(
            part_prompt.reshape(4, 2, QROWS, D),
            part_chip.astype(BF),
            grad_qkv.astype(BF).reshape(2, 4, 192, 576),
            grad_h2,
            tokens,
            vectors,
            jnp.concatenate([jnp.zeros((3, D), F32), later_sums]),
            4,
        )
    else:
        back_prompt = lax.psum_scatter(part_prompt, "gc", scatter_dimension=0, tiled=True)
        back_prompt = lax.psum_scatter(
            jnp.concatenate([back_prompt, jnp.zeros_like(back_prompt)]),
            "gr",
            scatter_dimension=0,
            tiled=True,
        ).astype(F32)
        part_keep = lax.dynamic_index_in_dim(part_chip, c, 0, keepdims=False)
        part_give = lax.dynamic_index_in_dim(part_chip, 1 - c, 0, keepdims=False)
        part_take = lax.ppermute(part_give.astype(BF), "gc", swap_core).astype(F32)
        grad_n1 = part_keep + part_take + back_prompt
        qkv_keep = lax.dynamic_index_in_dim(grad_qkv, y, 0, keepdims=False)
        qkv_give = lax.dynamic_index_in_dim(grad_qkv, 1 - y, 0, keepdims=False)
        qkv_take = lax.ppermute(qkv_give.astype(BF), "gc", swap_y).astype(F32)
        out_w_qkv = lax.psum_scatter(
            (qkv_keep + qkv_take).astype(BF), "gr", scatter_dimension=0, tiled=True
        )
        out_w_qkv = lax.psum(out_w_qkv, "dp").astype(F32)
        back1, grad_gain1, grad_shift1 = norm_back(grad_n1, gain1, unit1, factor1)
        input_grad = grad_h2 + back1
        first_sums = jnp.stack([jnp.sum(input_grad, axis=0), grad_gain1, grad_shift1])
        sums = lax.psum(jnp.concatenate([first_sums, later_sums]), ("dp", "gr", "gc"))
    sums = sums[:12].reshape(12 * D)
    loss = (sums[-1] / (D * token_count[0].astype(F32))).reshape(1)
    rows = sums[: 7 * D].reshape(7, n_gr, D // n_gr)
    rows = lax.dynamic_index_in_dim(rows, z, 1, keepdims=False)
    up = lax.dynamic_index_in_dim(
        sums[7 * D : 7 * D + FF].reshape(n_gc, FF // n_gc), g, 0, keepdims=False
    )
    return (
        final.astype(BF),
        loss,
        input_grad,
        rows[0],
        rows[1],
        rows[2],
        out_w_qkv,
        out_w_out,
        rows[5],
        rows[3],
        rows[4],
        out_w_up,
        up,
        out_w_down,
        rows[6],
    )


def solution(mesh):
    rows = P(("dp", "gr", "gc"), None)
    in_specs = (
        rows,
        rows,
        P("gr"),
        P("gr"),
        P("gr"),
        P("gr", "gc"),
        P("gc", "gr"),
        P("gr"),
        P("gr"),
        P("gr"),
        P("gr", "gc"),
        P("gc"),
        P("gr", "gc"),
        P("gr"),
        P(("dp", "gr")),
        P(),
    )
    out_specs = (
        rows,
        P(),
        rows,
        P("gr"),
        P("gr"),
        P("gr"),
        P("gr", "gc"),
        P("gc", "gr"),
        P("gr"),
        P("gr"),
        P("gr"),
        P("gr", "gc"),
        P("gc"),
        P("gr", "gc"),
        P("gr"),
    )
    return jax.shard_map(
        on_device, mesh=mesh, in_specs=in_specs, out_specs=out_specs, check_vma=False
    )
```

```python
from functools import partial
import math

import jax
import jax.numpy as jnp
from jax import lax
from jax.experimental import pallas as pl
from jax.experimental.pallas import tpu as pltpu
from jax.sharding import PartitionSpec as P

D = 768
HD = 64
FF = 3072
P_SIZE = 1024
CL = 128
QROWS = 512
eps = 1e-05
negative = -1e30
BF = jnp.bfloat16
F32 = jnp.float32


def nt(a, b):
    return lax.dot_general(a, b, (((1,), (1,)), ((), ())), preferred_element_type=F32)


def nn(a, b):
    return lax.dot_general(a, b, (((1,), (0,)), ((), ())), preferred_element_type=F32)


def tn(a, b):
    return lax.dot_general(a, b, (((0,), (0,)), ((), ())), preferred_element_type=F32)


def att_fwd_kernel(grp_ref, z_ref, q_ref, kvo_ref, kvp_ref, o_ref, lse_ref):
    j = pl.program_id(1)
    row0 = pl.multiple_of(grp_ref[j] * P_SIZE, P_SIZE)
    z = z_ref[0]
    lane = lax.broadcasted_iota(jnp.int32, (CL, 128), 1)
    low = lane < 64
    zero = jnp.zeros((CL, 128), BF)
    q = q_ref[...]
    q_parts = (jnp.where(low, zero, q), jnp.where(low, q, zero))

    @pl.when(z >= 2)
    def _():
        row = lax.broadcasted_iota(jnp.int32, (CL, CL), 0)
        near_ok = lax.broadcasted_iota(jnp.int32, (CL, CL), 1) <= row
        mixes, sums = [], []
        for h in range(2):
            cols = slice(128 * h, 128 * h + 128)
            kv = kvp_ref[pl.ds(row0, P_SIZE), cols]
            kvo = kvo_ref[:, cols]
            far = nt(q_parts[h], kv)
            near = jnp.where(near_ok, nt(q_parts[h], kvo), negative)
            top = jnp.maximum(
                jnp.max(far, axis=1, keepdims=True), jnp.max(near, axis=1, keepdims=True)
            )
            far = jnp.exp(far - top)
            near = jnp.exp(near - top)
            total = jnp.sum(far, axis=1, keepdims=True) + jnp.sum(near, axis=1, keepdims=True)
            mix = nn(far.astype(BF), kv) + nn(near.astype(BF), kvo)
            mixes.append(mix / total)
            sums.append(jnp.broadcast_to(top + jnp.log(total), (CL, 128)))
        o_ref[...] = jnp.where(low, mixes[0], mixes[1]).astype(BF)
        lse_ref[...] = jnp.where(low, sums[0], sums[1])

    @pl.when(z < 2)
    def _():
        limit = z * QROWS + (j % (QROWS // CL)) * CL
        row = lax.broadcasted_iota(jnp.int32, (CL, P_SIZE), 0)
        key = lax.broadcasted_iota(jnp.int32, (CL, P_SIZE), 1)
        allowed = key - row <= limit
        mixes, sums = [], []
        for h in range(2):
            cols = slice(128 * h, 128 * h + 128)
            kv = kvp_ref[pl.ds(row0, P_SIZE), cols]
            far = jnp.where(allowed, nt(q_parts[h], kv), negative)
            top = jnp.max(far, axis=1, keepdims=True)
            far = jnp.exp(far - top)
            total = jnp.sum(far, axis=1, keepdims=True)
            mix = nn(far.astype(BF), kv)
            mixes.append(mix / total)
            sums.append(jnp.broadcast_to(top + jnp.log(total), (CL, 128)))
        o_ref[...] = jnp.where(low, mixes[0], mixes[1]).astype(BF)
        lse_ref[...] = jnp.where(low, sums[0], sums[1])


def attend(grp, z, q, kvo, kvp):
    rows = q.shape[0]
    pairs = q.shape[1] // 128
    groups_rows = kvp.shape[0]
    return pl.pallas_call(
        att_fwd_kernel,
        name="att_fwd",
        grid_spec=pltpu.PrefetchScalarGridSpec(
            num_scalar_prefetch=2,
            grid=(pairs, rows // CL),
            in_specs=[
                pl.BlockSpec((CL, 128), lambda p, j, *_: (j, p)),
                pl.BlockSpec((CL, 256), lambda p, j, *_: (j, p)),
                pl.BlockSpec((groups_rows, 256), lambda p, j, *_: (0, p)),
            ],
            out_specs=[
                pl.BlockSpec((CL, 128), lambda p, j, *_: (j, p)),
                pl.BlockSpec((CL, 128), lambda p, j, *_: (j, p)),
            ],
        ),
        out_shape=[
            jax.ShapeDtypeStruct((rows, pairs * 128), BF),
            jax.ShapeDtypeStruct((rows, pairs * 128), F32),
        ],
        compiler_params=pltpu.CompilerParams(vmem_limit_bytes=40 << 20),
        cost_estimate=pl.CostEstimate(
            flops=4 * rows * P_SIZE * 128 * pairs * 2,
            bytes_accessed=groups_rows * 512 * pairs,
            transcendentals=rows * P_SIZE * pairs * 2,
        ),
    )(grp, z, q, kvo, kvp)


def att_bwd_kernel(
    grp_ref, z_ref, q_ref, gm_ref, lse_ref, kvo_ref, kvp_ref, dq_ref, dkvo_ref, dkvp_ref, acc
):
    j = pl.program_id(1)
    row0 = pl.multiple_of(grp_ref[j] * P_SIZE, P_SIZE)
    z = z_ref[0]
    low = lax.broadcasted_iota(jnp.int32, (CL, 128), 1) < 64
    zero = jnp.zeros((CL, 128), BF)
    q = q_ref[...]
    gm = gm_ref[...]
    stacks = (
        jnp.concatenate([jnp.where(low, zero, q), jnp.where(low, gm, zero)], axis=0),
        jnp.concatenate([jnp.where(low, q, zero), jnp.where(low, zero, gm)], axis=0),
    )

    @pl.when(j == 0)
    def _():
        acc[...] = jnp.zeros_like(acc)

    @pl.when(z >= 2)
    def _():
        row = lax.broadcasted_iota(jnp.int32, (CL, CL), 0)
        near_ok = row <= lax.broadcasted_iota(jnp.int32, (CL, CL), 1)
        dqs = []
        for h in range(2):
            cols = slice(128 * h, 128 * h + 128)
            kv = kvp_ref[pl.ds(row0, P_SIZE), cols]
            kvo = kvo_ref[:, cols]
            lse = lse_ref[0, 0, h : h + 1, :]
            far = nt(kv, stacks[h])
            near = nt(kvo, stacks[h])
            pf = jnp.exp(far[:, :CL] - lse)
            pn = jnp.where(near_ok, jnp.exp(near[:, :CL] - lse), 0.0)
            df = far[:, CL:]
            dn = near[:, CL:]
            inner = jnp.sum(pf * df, axis=0, keepdims=True) + jnp.sum(
                pn * dn, axis=0, keepdims=True
            )
            sf = (pf * (df - inner)).astype(BF)
            sn = (pn * (dn - inner)).astype(BF)
            acc[pl.ds(row0, P_SIZE), cols] += nn(
                jnp.concatenate([sf, pf.astype(BF)], axis=1), stacks[h]
            )
            dkvo_ref[:, cols] = nn(
                jnp.concatenate([sn, pn.astype(BF)], axis=1), stacks[h]
            ).astype(BF)
            dqs.append(tn(sf, kv) + tn(sn, kvo))
        dq_ref[...] = (jnp.where(low, dqs[1], dqs[0]) * 0.125).astype(BF)

    @pl.when(z < 2)
    def _():
        limit = z * QROWS + (j % (QROWS // CL)) * CL
        key = lax.broadcasted_iota(jnp.int32, (P_SIZE, CL), 0)
        row = lax.broadcasted_iota(jnp.int32, (P_SIZE, CL), 1)
        allowed = key - row <= limit
        dqs = []
        for h in range(2):
            cols = slice(128 * h, 128 * h + 128)
            kv = kvp_ref[pl.ds(row0, P_SIZE), cols]
            lse = lse_ref[0, 0, h : h + 1, :]
            far = nt(kv, stacks[h])
            pf = jnp.where(allowed, jnp.exp(far[:, :CL] - lse), 0.0)
            df = far[:, CL:]
            inner = jnp.sum(pf * df, axis=0, keepdims=True)
            sf = (pf * (df - inner)).astype(BF)
            acc[pl.ds(row0, P_SIZE), cols] += nn(
                jnp.concatenate([sf, pf.astype(BF)], axis=1), stacks[h]
            )
            dqs.append(tn(sf, kv))
        dkvo_ref[...] = jnp.zeros_like(dkvo_ref)
        dq_ref[...] = (jnp.where(low, dqs[1], dqs[0]) * 0.125).astype(BF)

    @pl.when(j == pl.num_programs(1) - 1)
    def _():
        dkvp_ref[...] = acc[...].astype(BF)


def attend_back(grp, z, q, gm, lse, kvo, kvp):
    rows = q.shape[0]
    pairs = q.shape[1] // 128
    groups_rows = kvp.shape[0]
    return pl.pallas_call(
        att_bwd_kernel,
        name="att_bwd",
        grid_spec=pltpu.PrefetchScalarGridSpec(
            num_scalar_prefetch=2,
            grid=(pairs, rows // CL),
            in_specs=[
                pl.BlockSpec((CL, 128), lambda p, j, *_: (j, p)),
                pl.BlockSpec((CL, 128), lambda p, j, *_: (j, p)),
                pl.BlockSpec((1, 1, 2, 128), lambda p, j, *_: (p, j, 0, 0)),
                pl.BlockSpec((CL, 256), lambda p, j, *_: (j, p)),
                pl.BlockSpec((groups_rows, 256), lambda p, j, *_: (0, p)),
            ],
            out_specs=[
                pl.BlockSpec((CL, 128), lambda p, j, *_: (j, p)),
                pl.BlockSpec((CL, 256), lambda p, j, *_: (j, p)),
                pl.BlockSpec((groups_rows, 256), lambda p, j, *_: (0, p)),
            ],
            scratch_shapes=[pltpu.VMEM((groups_rows, 256), F32)],
        ),
        out_shape=[
            jax.ShapeDtypeStruct((rows, pairs * 128), BF),
            jax.ShapeDtypeStruct((rows, pairs * 256), BF),
            jax.ShapeDtypeStruct((groups_rows, pairs * 256), BF),
        ],
        compiler_params=pltpu.CompilerParams(vmem_limit_bytes=48 << 20),
        cost_estimate=pl.CostEstimate(
            flops=10 * rows * P_SIZE * 128 * pairs * 2,
            bytes_accessed=groups_rows * 1024 * pairs,
            transcendentals=rows * P_SIZE * pairs * 2,
        ),
    )(grp, z, q, gm, lse, kvo, kvp)


MESH = pl.DeviceIdType.MESH


def places():
    x = lax.axis_index("dp")
    z = lax.axis_index("gr")
    g = lax.axis_index("gc")
    return x, z, g, g // 2, g % 2


def greet(partners):
    barrier = pltpu.get_barrier_semaphore()
    for partner in partners:
        pl.semaphore_signal(barrier, inc=1, device_id=partner, device_id_type=MESH)
    pl.semaphore_wait(barrier, len(partners))


def all_partners():
    x, z, g, y, c = places()
    by_z = [{"gr": z ^ step} for step in (1, 2, 3)]
    return [{"gc": g ^ 1}, {"gc": g ^ 2}, {"dp": x ^ 1}] + by_z


def send(src, dst, sems, slot, target, send_slot=None):
    return pltpu.make_async_remote_copy(
        src_ref=src,
        dst_ref=dst,
        send_sem=sems[0].at[slot if send_slot is None else send_slot],
        recv_sem=sems[1].at[slot],
        device_id=target,
        device_id_type=MESH,
    )


def add_into(dst, left, right):
    dst[...] = (left[...].astype(F32) + right[...].astype(F32)).astype(dst.dtype)


RS_SLOTS = 28
RS_ORDER = (3, 2, 1, 0)


def rs_plan(grads, outs, bufs, sems, l_sems, base, paired):
    own, ra, rb0, rb1, rc0, rc1, sc, rd, re = bufs
    x, z, g, y, c = places()
    sib, over_y, over_x = {"gc": g ^ 1}, {"gc": g ^ 2}, {"dp": x ^ 1}
    rows = grads.shape[2]
    q = rows // 4
    mine0 = pl.ds(pl.multiple_of(q * x, 16), q)
    other0 = pl.ds(pl.multiple_of(q * (1 - x), 16), q)
    mine1 = pl.ds(pl.multiple_of(2 * q + q * x, 16), q)
    other1 = pl.ds(pl.multiple_of(2 * q + q * (1 - x), 16), q)
    first = pl.ds(0, 2 * q)
    slot = base * RS_SLOTS

    def load(i, s):
        source = grads.at[2 * i + c, z ^ s] if paired else grads.at[i, z ^ s]
        return pltpu.make_async_copy(source, own.at[i, s], l_sems.at[8 * base + 2 * s + i])

    def hop_a(i, s):
        return send(grads.at[2 * i + 1 - c, z ^ s], ra.at[i, s], sems, slot + 6 * s + i, sib)

    def hop_b0(s):
        return send(own.at[1 - y, s, first], rb0.at[s], sems, slot + 6 * s + 2, over_y)

    def hop_b1(s):
        return send(own.at[:, s, other1], rb1.at[s], sems, slot + 6 * s + 3, over_x)

    def hop_c0(s):
        return send(own.at[y, s, other0], rc0.at[s], sems, slot + 6 * s + 4, over_x)

    def hop_c1(s):
        return send(own.at[1 - y, s, mine1], rc1.at[s], sems, slot + 6 * s + 5, over_y)

    def hop_z(s):
        return send(sc.at[s], rd.at[s - 1], sems, slot + 23 + s, {"gr": z ^ s})

    def hop_d():
        return send(sc.at[0], re, sems, slot + 27, over_x)

    def begin(s):
        for i in range(2):
            load(i, s).start()
            if paired:
                hop_a(i, s).start()

    def after_a(s):
        for i in range(2):
            load(i, s).wait()
            if paired:
                hop_a(i, s).wait()
                add_into(own.at[i, s], own.at[i, s], ra.at[i, s])
        hop_b0(s).start()
        hop_b1(s).start()

    def after_b(s):
        hop_b0(s).wait()
        hop_b1(s).wait()
        add_into(own.at[y, s, first], own.at[y, s, first], rb0.at[s])
        for i in range(2):
            add_into(own.at[i, s, mine1], own.at[i, s, mine1], rb1.at[s, i])
        hop_c0(s).start()
        hop_c1(s).start()

    def after_c(s):
        hop_c0(s).wait()
        hop_c1(s).wait()
        add_into(sc.at[s, pl.ds(0, q)], own.at[y, s, mine0], rc0.at[s])
        add_into(sc.at[s, pl.ds(q, q)], own.at[y, s, mine1], rc1.at[s])
        if s:
            hop_z(s).start()

    def total():
        for s in (1, 2, 3):
            hop_z(s).wait()
        whole = sc[0].astype(F32)
        for i in range(3):
            whole = whole + rd[i].astype(F32)
        sc[0] = whole.astype(BF)
        hop_d().start()

    def finish():
        hop_d().wait()
        outs[mine0] = sc[0, pl.ds(0, q)].astype(F32)
        outs[mine1] = sc[0, pl.ds(q, q)].astype(F32)
        outs[other0] = re[pl.ds(0, q)].astype(F32)
        outs[other1] = re[pl.ds(q, q)].astype(F32)

    return begin, after_a, after_b, after_c, total, finish


def rs_steps(plans):
    order = [(plan, s) for plan in plans for s in RS_ORDER]
    n = len(order)
    steps = [[partial(plan[0], s) for plan, s in order]]
    for i in range(n + 10):
        part = []
        if i < n:
            part.append(partial(order[i][0][1], order[i][1]))
        if 2 <= i < n + 2:
            part.append(partial(order[i - 2][0][2], order[i - 2][1]))
        if 4 <= i < n + 4:
            part.append(partial(order[i - 4][0][3], order[i - 4][1]))
        if 7 <= i < n + 7 and (i - 7) % 4 == 3:
            part.append(plans[(i - 7) // 4][4])
        if 9 <= i < n + 9 and (i - 9) % 4 == 3:
            part.append(plans[(i - 9) // 4][5])
        if part:
            steps.append(part)
    return steps


def rs_scratch(rows, cols, paired):
    q = rows // 4
    return [
        pltpu.VMEM((2, 4, rows, cols), BF),
        pltpu.VMEM((2, 4, rows, cols) if paired else (16, 128), BF),
        pltpu.VMEM((4, 2 * q, cols), BF),
        pltpu.VMEM((4, 2, q, cols), BF),
        pltpu.VMEM((4, q, cols), BF),
        pltpu.VMEM((4, q, cols), BF),
        pltpu.VMEM((4, 2 * q, cols), BF),
        pltpu.VMEM((3, 2 * q, cols), BF),
        pltpu.VMEM((2 * q, cols), BF),
    ]


def att_scatter_kernel(count, grp_ref, q_ref, lse_ref, kvo_ref, kvp_ref, gm, *refs):
    grads = refs[:count]
    dq_ref, dkvo_ref, dkv_ref = refs[count : count + 3]
    outs = refs[count + 3 : 2 * count + 3]
    rest = refs[2 * count + 3 :]
    bufs, (gmx, sem_s, sem_r, l_sems, m_send, m_recv, m_local) = rest[: 9 * count], rest[9 * count :]
    p, j = pl.program_id(0), pl.program_id(1)
    step = p * pl.num_programs(1) + j
    x, z, g, y, c = places()
    hooks = rs_steps(
        [
            rs_plan(grads[k], outs[k], bufs[9 * k : 9 * k + 9], (sem_s, sem_r), l_sems, k, True)
            for k in range(count)
        ]
    )

    def exchange(i):
        cols = pl.ds(128 * i, 128)
        return (
            pltpu.make_async_copy(gm.at[c, :, cols], gmx.at[i, c], m_local.at[i]),
            send(gm.at[1 - c, :, cols], gmx.at[i, c], (m_send, m_recv), i, {"gc": g ^ 1}),
        )

    @pl.when(step == 0)
    def _():
        greet(all_partners())
        for i in range(3):
            for copy in exchange(i):
                copy.start()
        for hook in hooks[0]:
            hook()
        for copy in exchange(0):
            copy.wait()

    for i in (1, 2):

        @pl.when(step == 8 * i)
        def _():
            for copy in exchange(i):
                copy.wait()

    last = len(hooks) - 1
    for when in range(1, 23):
        parts = [h for i in range(1, last) if i * 22 // (last - 1) == when for h in hooks[i]]
        if parts:

            @pl.when(step == when)
            def _():
                for hook in parts:
                    hook()

    group = grp_ref[j]
    low = lax.broadcasted_iota(jnp.int32, (CL, 128), 1) < 64
    zero = jnp.zeros((CL, 128), BF)
    q = q_ref[...]
    gmix = gmx[p, j // 4, pl.ds(pl.multiple_of((j % 4) * CL, CL), CL)]
    stacks = (
        jnp.concatenate([jnp.where(low, zero, q), jnp.where(low, gmix, zero)], axis=0),
        jnp.concatenate([jnp.where(low, q, zero), jnp.where(low, zero, gmix)], axis=0),
    )

    @pl.when(z >= 2)
    def _():
        row = lax.broadcasted_iota(jnp.int32, (CL, CL), 0)
        near_ok = row <= lax.broadcasted_iota(jnp.int32, (CL, CL), 1)
        dqs = []
        for h in range(2):
            cols = slice(128 * h, 128 * h + 128)
            kv = kvp_ref[group, :, cols]
            kvo = kvo_ref[:, cols]
            lse = lse_ref[0, 0, h : h + 1, :]
            far = nt(kv, stacks[h])
            near = nt(kvo, stacks[h])
            pf = jnp.exp(far[:, :CL] - lse)
            pn = jnp.where(near_ok, jnp.exp(near[:, :CL] - lse), 0.0)
            df = far[:, CL:]
            dn = near[:, CL:]
            inner = jnp.sum(pf * df, axis=0, keepdims=True) + jnp.sum(
                pn * dn, axis=0, keepdims=True
            )
            sf = (pf * (df - inner)).astype(BF)
            sn = (pn * (dn - inner)).astype(BF)
            dkv_ref[0, :, cols] = nn(
                jnp.concatenate([sf, pf.astype(BF)], axis=1), stacks[h]
            ).astype(BF)
            dkvo_ref[:, cols] = nn(
                jnp.concatenate([sn, pn.astype(BF)], axis=1), stacks[h]
            ).astype(BF)
            dqs.append(tn(sf, kv) + tn(sn, kvo))
        dq_ref[...] = (jnp.where(low, dqs[1], dqs[0]) * 0.125).astype(BF)

    @pl.when(z < 2)
    def _():
        limit = z * QROWS + (j % (QROWS // CL)) * CL
        key = lax.broadcasted_iota(jnp.int32, (P_SIZE, CL), 0)
        row = lax.broadcasted_iota(jnp.int32, (P_SIZE, CL), 1)
        allowed = key - row <= limit
        dqs = []
        for h in range(2):
            cols = slice(128 * h, 128 * h + 128)
            kv = kvp_ref[group, :, cols]
            lse = lse_ref[0, 0, h : h + 1, :]
            far = nt(kv, stacks[h])
            pf = jnp.where(allowed, jnp.exp(far[:, :CL] - lse), 0.0)
            df = far[:, CL:]
            inner = jnp.sum(pf * df, axis=0, keepdims=True)
            sf = (pf * (df - inner)).astype(BF)
            dkv_ref[0, :, cols] = nn(
                jnp.concatenate([sf, pf.astype(BF)], axis=1), stacks[h]
            ).astype(BF)
            dqs.append(tn(sf, kv))
        dkvo_ref[...] = jnp.zeros_like(dkvo_ref)
        dq_ref[...] = (jnp.where(low, dqs[1], dqs[0]) * 0.125).astype(BF)

    @pl.when(step == 23)
    def _():
        for hook in hooks[last]:
            hook()


def attend_back_scatter(grp, q, lse, kvo, kvp, gm, grads, collective_id):
    rows = q.shape[0]
    count = len(grads)
    any_space = pl.BlockSpec(memory_space=pl.ANY)
    scratch = []
    for grad in grads:
        scratch += rs_scratch(grad.shape[2], grad.shape[3], True)
    slots = RS_SLOTS * count
    return pl.pallas_call(
        partial(att_scatter_kernel, count),
        name="attend_back_scatter",
        grid_spec=pltpu.PrefetchScalarGridSpec(
            num_scalar_prefetch=1,
            grid=(3, rows // CL),
            in_specs=[
                pl.BlockSpec((CL, 128), lambda p, j, *_: (j, p)),
                pl.BlockSpec((1, 1, 2, 128), lambda p, j, *_: (p, j, 0, 0)),
                pl.BlockSpec((CL, 256), lambda p, j, *_: (j, p)),
                pl.BlockSpec((4, P_SIZE, 256), lambda p, j, *_: (0, 0, p)),
            ]
            + [any_space] * (count + 1),
            out_specs=[
                pl.BlockSpec((CL, 128), lambda p, j, *_: (j, p)),
                pl.BlockSpec((CL, 256), lambda p, j, *_: (j, p)),
                pl.BlockSpec((1, P_SIZE, 256), lambda p, j, *_: (j, 0, p)),
            ]
            + [pl.BlockSpec(grad.shape[2:], lambda p, j, *_: (0, 0)) for grad in grads],
            scratch_shapes=scratch
            + [
                pltpu.VMEM((3, 2, QROWS, 128), BF),
                pltpu.SemaphoreType.DMA((slots,)),
                pltpu.SemaphoreType.DMA((slots,)),
                pltpu.SemaphoreType.DMA((8 * count,)),
                pltpu.SemaphoreType.DMA((3,)),
                pltpu.SemaphoreType.DMA((3,)),
                pltpu.SemaphoreType.DMA((3,)),
            ],
        ),
        out_shape=[
            jax.ShapeDtypeStruct((rows, 384), BF),
            jax.ShapeDtypeStruct((rows, 768), BF),
            jax.ShapeDtypeStruct((8, P_SIZE, 768), BF),
        ]
        + [jax.ShapeDtypeStruct(grad.shape[2:], F32) for grad in grads],
        compiler_params=pltpu.CompilerParams(
            collective_id=collective_id, has_side_effects=True, vmem_limit_bytes=56 << 20
        ),
    )(grp, q, lse, kvo, kvp.reshape(4, P_SIZE, kvp.shape[1]), gm, *grads)


def fold_kernel(
    grp_ref,
    dkv_ref,
    dkvo_ref,
    dq_ref,
    n1p_ref,
    n1c_ref,
    w_q,
    w_kv,
    part_ref,
    chip_ref,
    dw_ref,
    acc,
    wkt,
    wqt,
    dkvw,
    dqw,
):
    t = pl.program_id(0)

    @pl.when(t == 0)
    def _():
        wkt[...] = w_kv[...].T
        wqt[...] = w_q[...].T
        dkvw[...] = jnp.zeros_like(dkvw)
        dqw[...] = jnp.zeros_like(dqw)

    acc[...] = jnp.zeros_like(acc)
    for j in range(8):
        acc[grp_ref[j]] += dkv_ref[j].astype(F32)
    low = acc[...].astype(BF).reshape(512, D)
    part_ref[...] = nn(low, wkt[...]).astype(BF).reshape(4, CL, D)
    dkvo = dkvo_ref[...]
    dq = dq_ref[...]
    chip_ref[...] = (nn(dq, wqt[...]) + nn(dkvo, wkt[...])).astype(BF)
    n1c = n1c_ref[...]
    rows = jnp.concatenate([n1p_ref[...].reshape(512, D), n1c], axis=0)
    dkvw[...] += tn(rows, jnp.concatenate([low, dkvo], axis=0))
    dqw[...] += tn(n1c, dq)

    @pl.when(t == pl.num_programs(0) - 1)
    def _():
        for head in range(6):
            p, b = head // 2, head % 2
            at_q = 128 * p + (0 if b else 64)
            at_k = 256 * p + (128 if b else 64)
            at_v = 256 * p + (192 if b else 0)
            pieces = (
                dqw[:, at_q : at_q + HD],
                dkvw[:, at_k : at_k + HD],
                dkvw[:, at_v : at_v + HD],
            )
            for i, piece in enumerate(pieces):
                at = (head % 3) * 192 + HD * i
                dw_ref[head // 3, :, at : at + HD] = piece.astype(BF)


def fold_prompts(grp, dkv, dkvo, dq, n1_prompt, n1_chip, w_q, w_kv):
    tile = CL
    groups = pl.BlockSpec((4, tile, D), lambda i, *_: (0, i, 0))
    return pl.pallas_call(
        fold_kernel,
        name="fold_prompts",
        grid_spec=pltpu.PrefetchScalarGridSpec(
            num_scalar_prefetch=1,
            grid=(P_SIZE // tile,),
            in_specs=[
                pl.BlockSpec((8, tile, D), lambda i, *_: (0, i, 0)),
                pl.BlockSpec((tile, D), lambda i, *_: (i, 0)),
                pl.BlockSpec((tile, 384), lambda i, *_: (i, 0)),
                groups,
                pl.BlockSpec((tile, D), lambda i, *_: (i, 0)),
                pl.BlockSpec((D, 384), lambda i, *_: (0, 0)),
                pl.BlockSpec((D, D), lambda i, *_: (0, 0)),
            ],
            out_specs=[
                groups,
                pl.BlockSpec((tile, D), lambda i, *_: (i, 0)),
                pl.BlockSpec((2, D, 576), lambda i, *_: (0, 0, 0)),
            ],
            scratch_shapes=[
                pltpu.VMEM((4, tile, D), F32),
                pltpu.VMEM((D, D), BF),
                pltpu.VMEM((384, D), BF),
                pltpu.VMEM((D, D), F32),
                pltpu.VMEM((D, 384), F32),
            ],
        ),
        out_shape=[
            jax.ShapeDtypeStruct((4, P_SIZE, D), BF),
            jax.ShapeDtypeStruct((2 * QROWS, D), BF),
            jax.ShapeDtypeStruct((2, D, 576), BF),
        ],
        compiler_params=pltpu.CompilerParams(vmem_limit_bytes=48 << 20),
    )(grp, dkv, dkvo, dq, n1_prompt.reshape(4, P_SIZE, D), n1_chip, w_q, w_kv)


def norm_rows(hidden, gain, shift):
    center = jnp.mean(hidden, axis=1, keepdims=True)
    offset = hidden - center
    factor = lax.rsqrt(jnp.mean(offset * offset, axis=1, keepdims=True) + eps)
    return offset * factor * gain + shift


CHUNKS = 4


def start_kernel(
    tokens,
    vec,
    bup,
    own,
    wq,
    prompts,
    chip,
    wpair,
    vec_out,
    bup_out,
    own_out,
    n1,
    vec_in,
    z_sems,
    y_sems,
    d_sems,
    w_sems,
    s_sems,
    l_sems,
):
    x, z, g, y, c = places()
    sib, over_y, over_x = {"gc": g ^ 1}, {"gc": g ^ 2}, {"dp": x ^ 1}
    greet(all_partners() + [{"gc": g ^ 3}])
    half_rows = wq.shape[0] // 2
    my_half = pl.ds(pl.multiple_of(x * half_rows, 16), half_rows)

    small = []
    for s in (1, 2, 3):
        to = {"gr": z ^ s}
        small.append(send(vec, vec_in.at[s], s_sems, s, to))
        small.append(send(own, own_out.at[z], s_sems, 3 + s, to))
        small.append(send(bup, bup_out.at[g], s_sems, 6 + s, {"gc": g ^ s}))
    for copy in small:
        copy.start()
    own_out[z] = own[...]
    bup_out[g] = bup[...]

    w_local = pltpu.make_async_copy(wq.at[my_half], wpair.at[y, z, my_half], l_sems.at[0])
    w_local.start()
    w_gr = [
        send(wq.at[my_half], wpair.at[y, z, my_half], w_sems, s, {"gr": z ^ s}) for s in (1, 2, 3)
    ]
    for copy in w_gr:
        copy.start()

    def w_step(s):
        block = z ^ s
        piece = wpair.at[y, block, my_half]
        across = wpair.at[1 - y, block, my_half]
        return (
            send(piece, piece, w_sems, 4 + s, over_y),
            send(piece, piece, w_sems, 8 + s, over_x),
            send(across, across, w_sems, 12 + s, over_x),
        )

    for copy in small[0::3]:
        copy.wait_recv()
    total = vec[...]
    for s in (1, 2, 3):
        total = total + vec_in[s]
    vec_out[...] = total

    @pl.loop(0, QROWS // 128)
    def _(i):
        rows = pl.ds(pl.multiple_of(i * 128, 128), 128)
        hidden = tokens[rows].astype(F32) + vec_out[0:1]
        n1[rows] = norm_rows(hidden, vec_out[1:2], vec_out[2:3]).astype(BF)

    to_chip = pltpu.make_async_copy(n1, chip.at[c], l_sems.at[1])
    to_chip.start()
    chip_send = send(n1, chip.at[c], s_sems, 10, sib)
    chip_send.start()
    is_prompt = z < 2

    @pl.when(is_prompt)
    def _():
        local = pltpu.make_async_copy(n1, prompts.at[g, z], l_sems.at[2])
        local.start()
        local.wait()

    w_local.wait()
    for copy in w_step(0)[:2]:
        copy.start()

    rows = QROWS // CHUNKS

    def item(column, half, k):
        return prompts.at[column, half, pl.ds(k * rows, rows)]

    def copies(half, k):
        mine = item(g, half, k)
        across = item(g ^ 2, half, k)
        n = half * CHUNKS + k
        return {
            "up": send(mine, mine, z_sems, n, {"gr": jnp.minimum(z + 1, 3)}),
            "down": send(
                mine, mine, z_sems, n, {"gr": jnp.maximum(z - 1, 0)}, 2 * CHUNKS + k
            ),
            "y": send(mine, mine, y_sems, n, over_y),
            "core": send(mine, mine, d_sems, n, sib),
            "core2": send(across, across, d_sems, 2 * CHUNKS + n, sib),
        }

    first = jnp.where(z == 0, 0, 1)

    def forward(step):
        half = first if step < CHUNKS else 1 - first
        k = step % CHUNKS
        moves = copies(half, k)

        @pl.when(half != z)
        def _():
            moves["up"].wait_recv()

        @pl.when(jnp.logical_and(z < 3, half <= z))
        def _():
            moves["up"].start()

        @pl.when(jnp.logical_and(z == 1, half == 1))
        def _():
            moves["down"].start()

        moves["y"].start()
        moves["core"].start()

    def across(step):
        half = first if step < CHUNKS else 1 - first
        moves = copies(half, step % CHUNKS)
        moves["y"].wait_recv()
        moves["core2"].start()

    for step in range(2 * CHUNKS):
        forward(step)
        if step >= 2:
            across(step - 2)
        if step in (1, 2, 3):
            w_gr[step - 1].wait_recv()
            one, two, _ = w_step(step)
            one.start()
            two.start()
        if step in (4, 5, 6, 7):
            one, _, three = w_step(step - 4)
            one.wait_recv()
            three.start()
    across(2 * CHUNKS - 2)
    across(2 * CHUNKS - 1)

    for step in range(2 * CHUNKS):
        half = first if step < CHUNKS else 1 - first
        moves = copies(half, step % CHUNKS)
        moves["core"].wait_recv()
        moves["core2"].wait_recv()
        moves["y"].wait_send()
        moves["core"].wait_send()
        moves["core2"].wait_send()

        @pl.when(jnp.logical_and(z < 3, half <= z))
        def _():
            moves["up"].wait_send()

        @pl.when(jnp.logical_and(z == 1, half == 1))
        def _():
            moves["down"].wait_send()

    for copy in w_gr:
        copy.wait_send()
    for s in range(4):
        one, two, three = w_step(s)
        one.wait_send()
        two.wait()
        three.wait()
    for i, copy in enumerate(small):
        if i % 3 == 0:
            copy.wait_send()
        else:
            copy.wait()
    to_chip.wait()
    chip_send.wait()


def start_exchange(tokens, vec, bup, own, wq, collective_id):
    any_space = pl.BlockSpec(memory_space=pl.ANY)
    vmem = pl.BlockSpec(memory_space=pltpu.VMEM)

    def dma(count):
        return pltpu.SemaphoreType.DMA((count,))

    def pair(count, extra=0):
        return dma(count + extra), dma(count)

    z_pair, y_pair, d_pair = pair(2 * CHUNKS, CHUNKS), pair(2 * CHUNKS), pair(4 * CHUNKS)
    w_pair, s_pair = pair(16), pair(11)

    def body(*refs):
        main, sems = refs[:13], refs[13:]
        start_kernel(*main, sems[0:2], sems[2:4], sems[4:6], sems[6:8], sems[8:10], sems[10])

    return pl.pallas_call(
        body,
        name="start_exchange",
        in_specs=[vmem, vmem, vmem, vmem, any_space],
        out_specs=[any_space, any_space, any_space, vmem, vmem, vmem],
        out_shape=[
            jax.ShapeDtypeStruct((4, 2, QROWS, D), BF),
            jax.ShapeDtypeStruct((2, QROWS, D), BF),
            jax.ShapeDtypeStruct((2, 4) + wq.shape, BF),
            jax.ShapeDtypeStruct(vec.shape, F32),
            jax.ShapeDtypeStruct((4,) + bup.shape, F32),
            jax.ShapeDtypeStruct((4,) + own.shape, jnp.int32),
        ],
        scratch_shapes=[pltpu.VMEM((QROWS, D), BF), pltpu.VMEM((4,) + vec.shape, F32)]
        + [*z_pair, *y_pair, *d_pair, *w_pair, *s_pair, dma(3)],
        compiler_params=pltpu.CompilerParams(
            collective_id=collective_id, has_side_effects=True, vmem_limit_bytes=32 << 20
        ),
    )(tokens, vec, bup, own, wq)


GATHER_SLOTS = 36


def gather_steps(blocks, wholes, sems, l_sems):
    x, z, g, y, c = places()
    sib, over_y, over_x = {"gc": g ^ 1}, {"gc": g ^ 2}, {"dp": x ^ 1}
    steps = []

    def plan(a):
        block, whole = blocks[a], wholes[a]
        rows = block.shape[0]
        q = rows // 4
        half = pl.ds(pl.multiple_of(x * 2 * q, 16), 2 * q)
        qa = pl.ds(pl.multiple_of(x * 2 * q, 16), q)
        qb = pl.ds(pl.multiple_of(x * 2 * q + q, 16), q)
        base = a * GATHER_SLOTS
        local = pltpu.make_async_copy(block.at[half], whole.at[g, z, half], l_sems.at[a])
        by_gr = [
            send(block.at[half], whole.at[g, z, half], sems, base + s, {"gr": z ^ s})
            for s in (1, 2, 3)
        ]

        def moves(s):
            o = base + 4 + 8 * s
            mine, far = whole.at[g, z ^ s], whole.at[g ^ 2, z ^ s]
            return {
                "ay": send(mine.at[qa], mine.at[qa], sems, o, over_y),
                "ax": send(mine.at[qa], mine.at[qa], sems, o + 1, over_x),
                "afx": send(far.at[qa], far.at[qa], sems, o + 2, over_x),
                "bx": send(mine.at[qb], mine.at[qb], sems, o + 3, over_x),
                "by": send(mine.at[qb], mine.at[qb], sems, o + 4, over_y),
                "bfy": send(
                    mine.at[pl.ds(pl.multiple_of((1 - x) * 2 * q + q, 16), q)],
                    mine.at[pl.ds(pl.multiple_of((1 - x) * 2 * q + q, 16), q)],
                    sems,
                    o + 5,
                    over_y,
                ),
                "c1": send(mine, mine, sems, o + 6, sib),
                "c2": send(far, far, sems, o + 7, sib),
            }

        return local, by_gr, moves

    plans = [plan(a) for a in range(len(blocks))]

    def begin():
        for local, by_gr, _ in plans:
            local.start()
            for copy in by_gr:
                copy.start()
        for local, _, _ in plans:
            local.wait()

    def first(a, s):
        def run():
            _, by_gr, moves = plans[a]
            if s:
                by_gr[s - 1].wait_recv()
            m = moves(s)
            for name in ("ay", "bx", "ax", "by"):
                m[name].start()

        return run

    def second(a, s):
        def run():
            m = plans[a][2](s)
            m["ay"].wait_recv()
            m["afx"].start()
            m["bx"].wait_recv()
            m["bfy"].start()

        return run

    def third(a, s):
        def run():
            m = plans[a][2](s)
            for name in ("ax", "afx", "by", "bfy"):
                m[name].wait_recv()
            m["c1"].start()
            m["c2"].start()

        return run

    def finish():
        for _, by_gr, moves in plans:
            for copy in by_gr:
                copy.wait_send()
            for s in range(4):
                m = moves(s)
                m["c1"].wait_recv()
                m["c2"].wait_recv()
                for copy in m.values():
                    copy.wait_send()

    order = [(a, s) for a in range(len(blocks)) for s in range(4)]
    steps = [begin]
    n = len(order)
    for i in range(n + 4):
        part = []
        if i < n:
            part.append(first(*order[i]))
        if 2 <= i < n + 2:
            part.append(second(*order[i - 2]))
        if i >= 4:
            part.append(third(*order[i - 4]))
        steps.append(partial(lambda fs: [f() for f in fs], part))
    steps.append(finish)
    return steps


def att_gather_kernel(count, grp_ref, q_ref, kvo_ref, kvp_ref, *refs):
    blocks = refs[:count]
    mixed, lse_ref = refs[count : count + 2]
    wholes = refs[count + 2 : 2 * count + 2]
    mix, sems_s, sems_r, l_sems, m_send, m_recv, m_local = refs[2 * count + 2 :]
    p, j = pl.program_id(0), pl.program_id(1)
    step = p * pl.num_programs(1) + j
    x, z, g, y, c = places()

    hooks = gather_steps(blocks, wholes, (sems_s, sems_r), l_sems)

    @pl.when(step == 0)
    def _():
        greet(all_partners())

    last = len(hooks) - 1
    for i, hook in enumerate(hooks):
        when = i * 23 // last
        if i == last:
            continue

        @pl.when(step == when)
        def _():
            hook()

    group = grp_ref[j]
    low = lax.broadcasted_iota(jnp.int32, (CL, 128), 1) < 64
    zero = jnp.zeros((CL, 128), BF)
    q = q_ref[...]
    q_parts = (jnp.where(low, zero, q), jnp.where(low, q, zero))

    def store(mixes, sums):
        mix[p, j // 4, pl.ds(pl.multiple_of((j % 4) * CL, CL), CL)] = jnp.where(
            low, mixes[0], mixes[1]
        ).astype(BF)
        flat = jnp.where(low, sums[0], sums[1]).T
        lse_ref[0, 0, 0:1] = flat[0:1]
        lse_ref[0, 0, 1:2] = flat[64:65]

    @pl.when(z >= 2)
    def _():
        row = lax.broadcasted_iota(jnp.int32, (CL, CL), 0)
        near_ok = lax.broadcasted_iota(jnp.int32, (CL, CL), 1) <= row
        mixes, sums = [], []
        for h in range(2):
            cols = slice(128 * h, 128 * h + 128)
            kv = kvp_ref[group, :, cols]
            kvo = kvo_ref[:, cols]
            far = nt(q_parts[h], kv)
            near = jnp.where(near_ok, nt(q_parts[h], kvo), negative)
            top = jnp.maximum(
                jnp.max(far, axis=1, keepdims=True), jnp.max(near, axis=1, keepdims=True)
            )
            far = jnp.exp(far - top)
            near = jnp.exp(near - top)
            total = jnp.sum(far, axis=1, keepdims=True) + jnp.sum(near, axis=1, keepdims=True)
            mixes.append((nn(far.astype(BF), kv) + nn(near.astype(BF), kvo)) / total)
            sums.append(jnp.broadcast_to(top + jnp.log(total), (CL, 128)))
        store(mixes, sums)

    @pl.when(z < 2)
    def _():
        limit = z * QROWS + (j % (QROWS // CL)) * CL
        row = lax.broadcasted_iota(jnp.int32, (CL, P_SIZE), 0)
        key = lax.broadcasted_iota(jnp.int32, (CL, P_SIZE), 1)
        allowed = key - row <= limit
        mixes, sums = [], []
        for h in range(2):
            cols = slice(128 * h, 128 * h + 128)
            kv = kvp_ref[group, :, cols]
            far = jnp.where(allowed, nt(q_parts[h], kv), negative)
            top = jnp.max(far, axis=1, keepdims=True)
            far = jnp.exp(far - top)
            total = jnp.sum(far, axis=1, keepdims=True)
            mixes.append(nn(far.astype(BF), kv) / total)
            sums.append(jnp.broadcast_to(top + jnp.log(total), (CL, 128)))
        store(mixes, sums)

    def exchange(i):
        cols = pl.ds(128 * i, 128)
        return (
            pltpu.make_async_copy(mix.at[i, c], mixed.at[c, :, cols], m_local.at[i]),
            send(mix.at[i, 1 - c], mixed.at[c, :, cols], (m_send, m_recv), i, {"gc": g ^ 1}),
        )

    for i in range(3):

        @pl.when(step == 8 * i + 7)
        def _():
            for copy in exchange(i):
                copy.start()

    @pl.when(step == 23)
    def _():
        hooks[last]()
        for i in range(3):
            for copy in exchange(i):
                copy.wait()


def attend_gather(grp, q, kvo, kvp, blocks, collective_id):
    rows = q.shape[0]
    count = len(blocks)
    any_space = pl.BlockSpec(memory_space=pl.ANY)
    slots = GATHER_SLOTS * count
    return pl.pallas_call(
        partial(att_gather_kernel, count),
        name="attend_gather",
        grid_spec=pltpu.PrefetchScalarGridSpec(
            num_scalar_prefetch=1,
            grid=(3, rows // CL),
            in_specs=[
                pl.BlockSpec((CL, 128), lambda p, j, *_: (j, p)),
                pl.BlockSpec((CL, 256), lambda p, j, *_: (j, p)),
                pl.BlockSpec((4, P_SIZE, 256), lambda p, j, *_: (0, 0, p)),
            ]
            + [any_space] * count,
            out_specs=[any_space, pl.BlockSpec((1, 1, 2, 128), lambda p, j, *_: (p, j, 0, 0))]
            + [any_space] * count,
            scratch_shapes=[
                pltpu.VMEM((3, 2, QROWS, 128), BF),
                pltpu.SemaphoreType.DMA((slots,)),
                pltpu.SemaphoreType.DMA((slots,)),
                pltpu.SemaphoreType.DMA((count,)),
                pltpu.SemaphoreType.DMA((3,)),
                pltpu.SemaphoreType.DMA((3,)),
                pltpu.SemaphoreType.DMA((3,)),
            ],
        ),
        out_shape=[
            jax.ShapeDtypeStruct((2, QROWS, 384), BF),
            jax.ShapeDtypeStruct((3, rows // CL, 2, 128), F32),
        ]
        + [jax.ShapeDtypeStruct((4, 4) + block.shape, BF) for block in blocks],
        compiler_params=pltpu.CompilerParams(
            collective_id=collective_id, has_side_effects=True, vmem_limit_bytes=40 << 20
        ),
    )(grp, q, kvo, kvp.reshape(4, P_SIZE, kvp.shape[1]), *blocks)


def tail_kernel(
    part,
    chip,
    dw,
    grad_h2,
    tokens,
    vec,
    sums,
    out,
    sums_out,
    dw_out,
    own,
    ra,
    rb,
    rz,
    keep,
    take,
    gsum,
    cur,
    sb,
    *rest,
):
    bufs, (sem_s, sem_r, l_sems, w_s, w_r, w_l) = rest[:9], rest[9:]
    sems = (sem_s, sem_r)
    x, z, g, y, c = places()
    sib, over_y, over_x = {"gc": g ^ 1}, {"gc": g ^ 2}, {"dp": x ^ 1}
    down = {"gr": jnp.maximum(z - 1, 0)}
    far = z >= 2
    greet(all_partners())
    hooks = rs_steps([rs_plan(dw, dw_out, bufs, (w_s, w_r), w_l, 0, False)])
    size = QROWS // CHUNKS
    chunks = [(h, k) for h in range(2) for k in range(CHUNKS)]

    def rows(k):
        return pl.ds(k * size, size)

    def index(side):
        return 1 - y if side == 0 else y

    def load(side, h, k):
        i = index(side)
        return pltpu.make_async_copy(
            part.at[2 * i + c, h, rows(k)],
            own.at[i, h, rows(k)],
            l_sems.at[8 * side + CHUNKS * h + k],
        )

    def hop_a(side, h, k):
        i = index(side)
        return send(
            part.at[2 * i + 1 - c, h, rows(k)],
            ra.at[i, h, rows(k)],
            sems,
            8 * side + CHUNKS * h + k,
            sib,
        )

    def hop_y(h, k):
        return send(
            own.at[1 - y, h, rows(k)], rb.at[h, rows(k)], sems, 16 + CHUNKS * h + k, over_y
        )

    def hop_z(h, k):
        return send(own.at[y, h, rows(k)], rz.at[h, rows(k)], sems, 24 + CHUNKS * h + k, down)

    hop_chip = send(chip.at[1 - c], take, sems, 32, sib)
    load_chip = pltpu.make_async_copy(chip.at[c], keep, l_sems.at[16])

    def fold(h, k, other):
        add_into(own.at[y, h, rows(k)], own.at[y, h, rows(k)], other.at[rows(k)])

    for h, k in chunks:

        @pl.when(far)
        def _():
            load(0, h, k).start()
            hop_a(0, h, k).start()

        load(1, h, k).start()
        hop_a(1, h, k).start()
    hop_chip.start()
    load_chip.start()
    for hook in hooks[0]:
        hook()

    def stage1(h, k):
        @pl.when(far)
        def _():
            load(0, h, k).wait()
            hop_a(0, h, k).wait()
            add_into(
                own.at[1 - y, h, rows(k)], own.at[1 - y, h, rows(k)], ra.at[1 - y, h, rows(k)]
            )
            hop_y(h, k).start()

        load(1, h, k).wait()
        hop_a(1, h, k).wait()
        fold(h, k, ra.at[y, h])

    def stage2(h, k):
        @pl.when(far)
        def _():
            hop_y(h, k).wait()
            fold(h, k, rb.at[h])

        @pl.when(z == 3)
        def _():
            hop_z(h, k).start()

    def stage3(h, k):
        @pl.when(z == 2)
        def _():
            hop_z(h, k).wait_recv()
            fold(h, k, rz.at[h])
            hop_z(h, k).start()

    def stage4(h, k):
        @pl.when(z == 1)
        def _():
            hop_z(h, k).wait_recv()
            fold(h, k, rz.at[h])
            if h == 0:
                hop_z(h, k).start()

    def stage5(h, k):
        if h == 0:

            @pl.when(z == 0)
            def _():
                hop_z(h, k).wait_recv()
                fold(h, k, rz.at[h])

    n = len(chunks)
    stages = (stage1, stage2, stage3, stage4, stage5)
    for i in range(max(n + 4, len(hooks) - 1)):
        for lag, stage in enumerate(stages):
            if 0 <= i - lag < n:
                stage(*chunks[i - lag])
        if i + 1 < len(hooks):
            for hook in hooks[i + 1]:
                hook()
    for h, k in chunks:

        @pl.when(z >= 2 if h else z >= 1)
        def _():
            hop_z(h, k).wait_send()

    load_chip.wait()
    hop_chip.wait()

    @pl.loop(0, CHUNKS)
    def _(k):
        r = pl.ds(pl.multiple_of(k * size, size), size)
        gsum[r] = keep[r].astype(F32) + take[r].astype(F32)

    @pl.when(z < 2)
    def _():
        place = jnp.minimum(z, 1)

        @pl.loop(0, CHUNKS)
        def _(k):
            r = pl.ds(pl.multiple_of(k * size, size), size)
            gsum[r] += own[y, place, r].astype(F32)

    cur[...] = sums[...]

    @pl.loop(0, CHUNKS)
    def _(k):
        r = pl.ds(pl.multiple_of(k * size, size), size)
        hidden = tokens[r].astype(F32) + vec[0:1]
        center = jnp.mean(hidden, axis=1, keepdims=True)
        offset = hidden - center
        factor = lax.rsqrt(jnp.mean(offset * offset, axis=1, keepdims=True) + eps)
        unit = offset * factor
        grad = gsum[r]
        scaled = grad * vec[1:2]
        first = jnp.mean(scaled, axis=1, keepdims=True)
        second = jnp.mean(scaled * unit, axis=1, keepdims=True)
        total = grad_h2[r] + factor * (scaled - first - unit * second)
        out[r] = total
        cur[0:1] += jnp.sum(total, axis=0, keepdims=True)
        cur[1:2] += jnp.sum(grad * unit, axis=0, keepdims=True)
        cur[2:3] += jnp.sum(grad, axis=0, keepdims=True)

    for i, target in enumerate((sib, over_y, over_x)):
        hop = send(cur, sb.at[i], sems, 33 + i, target)
        hop.start()
        hop.wait()
        cur[...] += sb[i]
    hops = [send(cur, sb.at[2 + s], sems, 35 + s, {"gr": z ^ s}) for s in (1, 2, 3)]
    for hop in hops:
        hop.start()
    for hop in hops:
        hop.wait()
    sums_out[...] = (cur[...] + sb[3]) + (sb[4] + sb[5])


def tail_exchange(part, chip, dw, grad_h2, tokens, vec, sums, collective_id):
    any_space = pl.BlockSpec(memory_space=pl.ANY)
    vmem = pl.BlockSpec(memory_space=pltpu.VMEM)
    return pl.pallas_call(
        tail_kernel,
        name="tail_exchange",
        in_specs=[any_space, any_space, any_space, vmem, vmem, vmem, vmem],
        out_specs=[vmem, vmem, vmem],
        out_shape=[
            jax.ShapeDtypeStruct((QROWS, D), F32),
            jax.ShapeDtypeStruct(sums.shape, F32),
            jax.ShapeDtypeStruct(dw.shape[2:], F32),
        ],
        scratch_shapes=[
            pltpu.VMEM((2, 2, QROWS, D), BF),
            pltpu.VMEM((2, 2, QROWS, D), BF),
            pltpu.VMEM((2, QROWS, D), BF),
            pltpu.VMEM((2, QROWS, D), BF),
            pltpu.VMEM((QROWS, D), BF),
            pltpu.VMEM((QROWS, D), BF),
            pltpu.VMEM((QROWS, D), F32),
            pltpu.VMEM(sums.shape, F32),
            pltpu.VMEM((6,) + sums.shape, F32),
        ]
        + rs_scratch(dw.shape[2], dw.shape[3], False)
        + [
            pltpu.SemaphoreType.DMA((39,)),
            pltpu.SemaphoreType.DMA((39,)),
            pltpu.SemaphoreType.DMA((17,)),
            pltpu.SemaphoreType.DMA((RS_SLOTS,)),
            pltpu.SemaphoreType.DMA((RS_SLOTS,)),
            pltpu.SemaphoreType.DMA((8,)),
        ],
        compiler_params=pltpu.CompilerParams(
            collective_id=collective_id, has_side_effects=True, vmem_limit_bytes=48 << 20
        ),
    )(part, chip, dw, grad_h2, tokens, vec, sums)


GELU_IN = math.sqrt(2.0 / math.pi)


def middle_kernel(
    mixed,
    w_out_g,
    w_up,
    w_down,
    tokens,
    teacher,
    vec,
    b_up,
    final_out,
    grad_h2,
    dw_up,
    dw_down,
    dw_out,
    gm,
    sums,
    wo,
    wu,
    wd,
    h2,
    n2,
    n2t,
    act,
    slope,
    gf,
    gb,
    gbt,
    acc,
    du,
    dd,
    l_sems,
    o_sems,
):
    loads_u = [pltpu.make_async_copy(w_up.at[b], wu.at[b], l_sems.at[b]) for b in range(4)]
    loads_d = [pltpu.make_async_copy(w_down.at[b], wd.at[b], l_sems.at[4 + b]) for b in range(4)]
    for b in range(4):
        loads_u[b].start()
        loads_d[b].start()
    for k in range(2):
        for i in range(2):
            for r in range(4):
                wo[k, 192 * i : 192 * i + 192, 192 * r : 192 * r + 192] = w_out_g[2 * i + k, r]

    @pl.loop(0, 2)
    def _(t):
        r = pl.ds(pl.multiple_of(t * 256, 256), 256)
        hidden = tokens[r].astype(F32) + vec[0:1]
        attended = nn(mixed[0, r], wo[0]) + nn(mixed[1, r], wo[1])
        total = hidden + attended + vec[3:4]
        h2[r] = total
        n2[r] = norm_rows(total, vec[4:5], vec[5:6]).astype(BF)

    n2t[...] = n2[...].T
    acc[...] = jnp.zeros_like(acc)
    for copy in loads_u + loads_d:
        copy.wait()

    @pl.loop(0, 4)
    def _(b):
        @pl.loop(0, 2)
        def _(t):
            r = pl.ds(pl.multiple_of(t * 256, 256), 256)
            pre = nn(n2[r], wu[b]) + b_up[b, 0:1]
            square = pre * pre
            tanh = jnp.tanh(GELU_IN * pre * (1.0 + 0.044715 * square))
            half = 0.5 * (1.0 + tanh)
            low = (pre * half).astype(BF)
            act[b, r] = low
            slope[b, r] = half + (0.5 * GELU_IN) * pre * (1.0 - tanh * tanh) * (
                1.0 + (3.0 * 0.044715) * square
            )
            acc[r] += nt(low, wd[b])

    sums[...] = jnp.zeros_like(sums)

    @pl.loop(0, 2)
    def _(t):
        r = pl.ds(pl.multiple_of(t * 256, 256), 256)
        final = h2[r] + acc[r] + vec[6:7]
        final_out[r] = final.astype(BF)
        diff = final - teacher[r].astype(F32)
        gf[r] = diff
        low = diff.astype(BF)
        gb[r] = low
        sums[6:7] += jnp.sum(low.astype(F32), axis=0, keepdims=True)
        sums[11:12] += jnp.sum(diff * diff, axis=0, keepdims=True)

    gbt[...] = gb[...].T
    acc[...] = jnp.zeros_like(acc)

    @pl.loop(0, 4)
    def _(b):
        dd[b] = nn(gbt[...], act[b]).astype(BF)
        pltpu.make_async_copy(dd.at[b], dw_down.at[b], o_sems.at[b]).start()

        @pl.loop(0, 2)
        def _(t):
            r = pl.ds(pl.multiple_of(t * 256, 256), 256)
            low = (nn(gb[r], wd[b]) * slope[b, r]).astype(BF)
            act[b, r] = low
            sums[pl.ds(7 + b, 1)] += jnp.sum(low.astype(F32), axis=0, keepdims=True)
            acc[r] += nt(low, wu[b])

        du[b] = nn(n2t[...], act[b]).astype(BF)
        pltpu.make_async_copy(du.at[b], dw_up.at[b], o_sems.at[4 + b]).start()

    @pl.loop(0, 2)
    def _(t):
        r = pl.ds(pl.multiple_of(t * 256, 256), 256)
        hidden = h2[r]
        center = jnp.mean(hidden, axis=1, keepdims=True)
        offset = hidden - center
        factor = lax.rsqrt(jnp.mean(offset * offset, axis=1, keepdims=True) + eps)
        unit = offset * factor
        grad = acc[r]
        scaled = grad * vec[4:5]
        first = jnp.mean(scaled, axis=1, keepdims=True)
        second = jnp.mean(scaled * unit, axis=1, keepdims=True)
        total = gf[r] + factor * (scaled - first - unit * second)
        grad_h2[r] = total
        low = total.astype(BF)
        gb[r] = low
        sums[3:4] += jnp.sum(grad * unit, axis=0, keepdims=True)
        sums[4:5] += jnp.sum(grad, axis=0, keepdims=True)
        sums[5:6] += jnp.sum(low.astype(F32), axis=0, keepdims=True)
        gm[0, r] = nt(low, wo[0]).astype(BF)
        gm[1, r] = nt(low, wo[1]).astype(BF)

    for k in range(2):
        whole = tn(mixed[k], gb[...]).astype(BF)
        for i in range(2):
            for r in range(4):
                dw_out[2 * i + k, r] = whole[192 * i : 192 * i + 192, 192 * r : 192 * r + 192]
    for b in range(4):
        pltpu.make_async_copy(dd.at[b], dw_down.at[b], o_sems.at[b]).wait()
        pltpu.make_async_copy(du.at[b], dw_up.at[b], o_sems.at[4 + b]).wait()


def middle(mixed, w_out_g, w_up, w_down, tokens, teacher, vec, b_up):
    any_space = pl.BlockSpec(memory_space=pl.ANY)
    vmem = pl.BlockSpec(memory_space=pltpu.VMEM)
    blocks = (4, D, D)
    return pl.pallas_call(
        middle_kernel,
        name="middle",
        in_specs=[vmem, vmem, any_space, any_space, vmem, vmem, vmem, vmem],
        out_specs=[vmem, vmem, any_space, any_space, vmem, vmem, vmem],
        out_shape=[
            jax.ShapeDtypeStruct((QROWS, D), BF),
            jax.ShapeDtypeStruct((QROWS, D), F32),
            jax.ShapeDtypeStruct(blocks, BF),
            jax.ShapeDtypeStruct(blocks, BF),
            jax.ShapeDtypeStruct((4, 4, 192, 192), BF),
            jax.ShapeDtypeStruct((2, QROWS, 384), BF),
            jax.ShapeDtypeStruct((16, D), F32),
        ],
        scratch_shapes=[
            pltpu.VMEM((2, 384, D), BF),
            pltpu.VMEM(blocks, BF),
            pltpu.VMEM(blocks, BF),
            pltpu.VMEM((QROWS, D), F32),
            pltpu.VMEM((QROWS, D), BF),
            pltpu.VMEM((D, QROWS), BF),
            pltpu.VMEM((4, QROWS, D), BF),
            pltpu.VMEM((4, QROWS, D), F32),
            pltpu.VMEM((QROWS, D), F32),
            pltpu.VMEM((QROWS, D), BF),
            pltpu.VMEM((D, QROWS), BF),
            pltpu.VMEM((QROWS, D), F32),
            pltpu.VMEM(blocks, BF),
            pltpu.VMEM(blocks, BF),
            pltpu.SemaphoreType.DMA((8,)),
            pltpu.SemaphoreType.DMA((8,)),
        ],
        compiler_params=pltpu.CompilerParams(vmem_limit_bytes=60 << 20),
    )(mixed, w_out_g, w_up, w_down, tokens, teacher, vec, b_up)


def norm(hidden, gain, shift):
    center = jnp.mean(hidden, axis=1, keepdims=True)
    offset = hidden - center
    factor = lax.rsqrt(jnp.mean(offset * offset, axis=1, keepdims=True) + eps)
    unit = offset * factor
    return unit * gain + shift, unit, factor


def norm_back(grad, gain, unit, factor):
    grad_unit = grad * gain
    first = jnp.mean(grad_unit, axis=1, keepdims=True)
    second = jnp.mean(grad_unit * unit, axis=1, keepdims=True)
    grad_in = factor * (grad_unit - first - unit * second)
    return grad_in, jnp.sum(grad * unit, axis=0), jnp.sum(grad, axis=0)


def head_layout(blocks):
    chunks = blocks.transpose(1, 0, 2).reshape(D, 6, 3, HD)
    q_list, kv_list = [], []
    for pair in range(3):
        a, b = 2 * pair, 2 * pair + 1
        q_list += [chunks[:, b, 0], chunks[:, a, 0]]
        kv_list += [chunks[:, a, 2], chunks[:, a, 1], chunks[:, b, 1], chunks[:, b, 2]]
    return jnp.concatenate(q_list, axis=1), jnp.concatenate(kv_list, axis=1)


def head_layout_back(grad_q, grad_kv):
    qc = grad_q.reshape(D, 3, 2, HD)
    kc = grad_kv.reshape(D, 3, 4, HD)
    pieces = []
    for pair in range(3):
        pieces += [qc[:, pair, 1], kc[:, pair, 1], kc[:, pair, 0]]
        pieces += [qc[:, pair, 0], kc[:, pair, 2], kc[:, pair, 3]]
    whole = jnp.concatenate(pieces, axis=1)
    return whole.reshape(D, 2, 576).transpose(1, 0, 2)


def on_device(
    tokens,
    teacher,
    pass_embed,
    ln1_gain,
    ln1_bias,
    qkv_weight,
    out_weight,
    out_bias,
    ln2_gain,
    ln2_bias,
    fc1_weight,
    fc1_bias,
    fc2_weight,
    fc2_bias,
    cont_group,
    token_count,
):
    n_dp = lax.axis_size("dp")
    n_gr = lax.axis_size("gr")
    n_gc = lax.axis_size("gc")
    z = lax.axis_index("gr")
    g = lax.axis_index("gc")
    c = g % 2
    y = g // 2
    swap_core = [(i, i ^ 1) for i in range(n_gc)]
    swap_y = [(i, i ^ 2) for i in range(n_gc)]

    packed = jnp.stack(
        [pass_embed, ln1_gain, ln1_bias, out_bias, ln2_gain, ln2_bias, fc2_bias, fc2_bias]
    ).astype(F32)
    if n_dp == 2:
        vec = lax.dynamic_update_slice(jnp.zeros((8, D), F32), packed, (0, z * packed.shape[1]))
        bup = jnp.broadcast_to(fc1_bias.astype(F32), (8, fc1_bias.shape[0]))
        own = jnp.broadcast_to(jnp.pad(cont_group, (0, 120)), (8, 128))
        n1_prompt, n1_chip, w_pair, vectors, b_up, owners = start_exchange(
            tokens, vec, bup, own, qkv_weight, 1
        )
        n1_prompt = n1_prompt.reshape(4 * P_SIZE, D)
        n1_chip = n1_chip.reshape(2 * QROWS, D)
        w_qkv = w_pair.reshape(2, D, 576)
        owners = owners[:, 0, :8]
    else:
        vectors = lax.all_gather(packed, "gr", axis=1, tiled=True)
        b_up = lax.all_gather(fc1_bias, "gc", axis=0, tiled=True).astype(F32)
        owners = lax.all_gather(cont_group, "gr", axis=0, tiled=True)
    embed, gain1, shift1, b_out, gain2, shift2, b_down = [vectors[i] for i in range(7)]
    owners = owners.reshape(4, 2, 4)
    mine = lax.dynamic_slice(owners, (2 * y, jnp.maximum(z - 2, 0), 0), (2, 1, 4)).reshape(8)
    own_groups = jnp.repeat(2 * y + jnp.arange(2), 4)
    grp = jnp.where(z < 2, own_groups, mine).astype(jnp.int32)
    z_arr = z.astype(jnp.int32).reshape(1)

    hidden = tokens.astype(F32) + embed
    normed1, unit1, factor1 = norm(hidden, gain1, shift1)
    n1 = normed1.astype(BF)

    if n_dp != 2:
        w_other = lax.ppermute(qkv_weight, "gc", swap_y)
        w_pair = jnp.where(
            y == 0, jnp.stack([qkv_weight, w_other]), jnp.stack([w_other, qkv_weight])
        )
        w_qkv = lax.all_gather(w_pair, "gr", axis=1, tiled=True)
        n1_other = lax.ppermute(n1, "gc", swap_core)
        n1_chip = jnp.where(
            c == 0, jnp.concatenate([n1, n1_other]), jnp.concatenate([n1_other, n1])
        )
        n1_col = lax.all_gather(n1, "gr", axis=0, tiled=True)[:P_SIZE]
        n1_prompt = lax.all_gather(n1_col, "gc", axis=0, tiled=True)
    w_q, w_kv = head_layout(w_qkv)

    kvp = nn(n1_prompt, w_kv).astype(BF)
    kvo = nn(n1_chip, w_kv).astype(BF)
    q = (nn(n1_chip, w_q) * 0.125).astype(BF)
    if n_dp == 2:
        mixed, lse_rows, w_out, w_up, w_down = attend_gather(
            grp, q, kvo, kvp, [out_weight, fc1_weight, fc2_weight], 2
        )
    else:
        w_out = lax.all_gather(out_weight, ("gc", "gr"))
        w_up = lax.all_gather(fc1_weight, ("gc", "gr"))
        w_down = lax.all_gather(fc2_weight, ("gc", "gr"))
        mixed_heads, lse = attend(grp, z_arr, q, kvo, kvp)
        lse_rows = lse[:, ::64].reshape(8, CL, 3, 2).transpose(2, 0, 3, 1)
        halves = mixed_heads.reshape(2, QROWS, 384)
        keep = lax.dynamic_index_in_dim(halves, c, 0, keepdims=False)
        give = lax.dynamic_index_in_dim(halves, 1 - c, 0, keepdims=False)
        take = lax.ppermute(give, "gc", swap_core)
        mixed = jnp.where(c == 0, jnp.stack([keep, take]), jnp.stack([take, keep]))
    w_up = w_up.reshape(n_gc, D, FF // n_gc)
    w_down = w_down.reshape(n_gc, D, FF // n_gc)
    if n_dp == 2:
        final, grad_h2, grad_w_up, grad_w_down, grad_w_out, gm, later_sums = middle(
            mixed, w_out, w_up, w_down, tokens, teacher, vectors, b_up
        )
    else:
        w_out = w_out.reshape(2, 2, n_gr, 192, 192).transpose(1, 0, 3, 2, 4).reshape(2, 384, D)

        attended = lax.dot_general(
            mixed, w_out, (((0, 2), (0, 1)), ((), ())), preferred_element_type=F32
        )
        hidden2 = hidden + attended + b_out
        normed2, unit2, factor2 = norm(hidden2, gain2, shift2)
        n2 = normed2.astype(BF)
        pre = lax.dot_general(n2, w_up, (((1,), (1,)), ((), ())), preferred_element_type=F32)
        pre = pre.reshape(QROWS, FF) + b_up
        active, gelu_back = jax.vjp(partial(jax.nn.gelu, approximate=True), pre)
        act = active.astype(BF)
        act_blocks = act.reshape(QROWS, n_gc, FF // n_gc)
        final = (
            hidden2
            + lax.dot_general(
                act_blocks, w_down, (((1, 2), (0, 2)), ((), ())), preferred_element_type=F32
            )
            + b_down
        )
        grad_final = final - teacher.astype(F32)
        squared = jnp.sum(grad_final * grad_final, axis=0)
        gb = grad_final.astype(BF)
        grad_b_down = jnp.sum(gb, axis=0, dtype=F32)
        grad_active = lax.dot_general(
            gb, w_down, (((1,), (1,)), ((), ())), preferred_element_type=F32
        ).reshape(QROWS, FF)
        grad_w_down = jnp.einsum("td,tgf->gdf", gb, act_blocks, preferred_element_type=F32)
        (grad_pre,) = gelu_back(grad_active)
        gp = grad_pre.astype(BF)
        gp_blocks = gp.reshape(QROWS, n_gc, FF // n_gc)
        grad_b_up = jnp.sum(gp, axis=0, dtype=F32)
        grad_w_up = jnp.einsum("td,tgf->gdf", n2, gp_blocks, preferred_element_type=F32)
        grad_n2 = lax.dot_general(
            gp_blocks, w_up, (((1, 2), (0, 2)), ((), ())), preferred_element_type=F32
        )
        back2, grad_gain2, grad_shift2 = norm_back(grad_n2, gain2, unit2, factor2)
        grad_h2 = grad_final + back2
        ga = grad_h2.astype(BF)
        grad_b_out = jnp.sum(ga, axis=0, dtype=F32)
        grad_w_out = jnp.einsum("ctk,tn->ckn", mixed, ga, preferred_element_type=F32)
        gm = jnp.einsum("tn,ckn->ctk", ga, w_out, preferred_element_type=F32).astype(BF)
        grad_w_up = grad_w_up.astype(BF)
        grad_w_down = grad_w_down.astype(BF)
        grad_w_out = (
            grad_w_out.astype(BF)
            .reshape(2, 2, 192, n_gr, 192)
            .transpose(1, 0, 3, 2, 4)
            .reshape(n_gc, n_gr, 192, 192)
        )
    weight_grads = [
        grad_w_down.reshape(n_gc, n_gr, 192, 768),
        grad_w_up.reshape(n_gc, n_gr, 192, 768),
        grad_w_out,
    ]
    if n_dp == 2:
        dq, dkvo, dkv, out_w_down, out_w_up, out_w_out = attend_back_scatter(
            grp, q, lse_rows, kvo, kvp, gm, weight_grads, 3
        )
        part_prompt, part_chip, grad_qkv = fold_prompts(
            grp, dkv, dkvo, dq, n1_prompt, n1_chip, w_q, w_kv
        )
    else:
        gm_keep = lax.dynamic_index_in_dim(gm, c, 0, keepdims=False)
        gm_give = lax.dynamic_index_in_dim(gm, 1 - c, 0, keepdims=False)
        gm_take = lax.ppermute(gm_give, "gc", swap_core)
        gm_chip = jnp.where(c == 0, jnp.stack([gm_keep, gm_take]), jnp.stack([gm_take, gm_keep]))
        gm_chip = gm_chip.reshape(2 * QROWS, 384)

        def scatter16(blocks):
            part = lax.psum_scatter(
                blocks.reshape(n_gc * n_gr * blocks.shape[2], -1),
                ("gc", "gr"),
                scatter_dimension=0,
                tiled=True,
            )
            return lax.psum(part, "dp").astype(F32)

        out_w_down, out_w_up, out_w_out = [scatter16(grad) for grad in weight_grads]
        dq, dkvo, dkvp = attend_back(grp, z_arr, q, gm_chip, lse_rows, kvo, kvp)
        part_prompt = nt(dkvp, w_kv).astype(BF)

        part_chip = (nt(dq, w_q) + nt(dkvo, w_kv)).reshape(2, QROWS, D)
        grad_kv = tn(n1_prompt, dkvp) + tn(n1_chip, dkvo)
        grad_q = tn(n1_chip, dq)
        grad_qkv = head_layout_back(grad_q, grad_kv)

    if n_dp == 2:
        input_grad, sums, out_w_qkv = tail_exchange(
            part_prompt.reshape(4, 2, QROWS, D),
            part_chip.reshape(2, QROWS, D),
            grad_qkv.reshape(2, 4, 192, 576),
            grad_h2,
            tokens,
            vectors,
            later_sums,
            4,
        )
    else:
        later_sums = jnp.concatenate(
            [
                grad_gain2[None],
                grad_shift2[None],
                grad_b_out[None],
                grad_b_down[None],
                grad_b_up.reshape(4, D),
                squared[None],
                jnp.zeros((4, D), F32),
            ]
        )
        back_prompt = lax.psum_scatter(part_prompt, "gc", scatter_dimension=0, tiled=True)
        back_prompt = lax.psum_scatter(
            jnp.concatenate([back_prompt, jnp.zeros_like(back_prompt)]),
            "gr",
            scatter_dimension=0,
            tiled=True,
        ).astype(F32)
        part_keep = lax.dynamic_index_in_dim(part_chip, c, 0, keepdims=False)
        part_give = lax.dynamic_index_in_dim(part_chip, 1 - c, 0, keepdims=False)
        part_take = lax.ppermute(part_give.astype(BF), "gc", swap_core).astype(F32)
        grad_n1 = part_keep + part_take + back_prompt
        qkv_keep = lax.dynamic_index_in_dim(grad_qkv, y, 0, keepdims=False)
        qkv_give = lax.dynamic_index_in_dim(grad_qkv, 1 - y, 0, keepdims=False)
        qkv_take = lax.ppermute(qkv_give.astype(BF), "gc", swap_y).astype(F32)
        out_w_qkv = lax.psum_scatter(
            (qkv_keep + qkv_take).astype(BF), "gr", scatter_dimension=0, tiled=True
        )
        out_w_qkv = lax.psum(out_w_qkv, "dp").astype(F32)
        back1, grad_gain1, grad_shift1 = norm_back(grad_n1, gain1, unit1, factor1)
        input_grad = grad_h2 + back1
        first_sums = jnp.stack([jnp.sum(input_grad, axis=0), grad_gain1, grad_shift1])
        sums = lax.psum(jnp.concatenate([first_sums, later_sums]), ("dp", "gr", "gc"))
    sums = sums[:12].reshape(12 * D)
    loss = (jnp.sum(sums[11 * D :]) / (D * token_count[0].astype(F32))).reshape(1)
    rows = sums[: 7 * D].reshape(7, n_gr, D // n_gr)
    rows = lax.dynamic_index_in_dim(rows, z, 1, keepdims=False)
    up = lax.dynamic_index_in_dim(
        sums[7 * D : 7 * D + FF].reshape(n_gc, FF // n_gc), g, 0, keepdims=False
    )
    return (
        final.astype(BF),
        loss,
        input_grad,
        rows[0],
        rows[1],
        rows[2],
        out_w_qkv,
        out_w_out,
        rows[5],
        rows[3],
        rows[4],
        out_w_up,
        up,
        out_w_down,
        rows[6],
    )


def solution(mesh):
    rows = P(("dp", "gr", "gc"), None)
    in_specs = (
        rows,
        rows,
        P("gr"),
        P("gr"),
        P("gr"),
        P("gr", "gc"),
        P("gc", "gr"),
        P("gr"),
        P("gr"),
        P("gr"),
        P("gr", "gc"),
        P("gc"),
        P("gr", "gc"),
        P("gr"),
        P(("dp", "gr")),
        P(),
    )
    out_specs = (
        rows,
        P(),
        rows,
        P("gr"),
        P("gr"),
        P("gr"),
        P("gr", "gc"),
        P("gc", "gr"),
        P("gr"),
        P("gr"),
        P("gr"),
        P("gr", "gc"),
        P("gc"),
        P("gr", "gc"),
        P("gr"),
    )
    return jax.shard_map(
        on_device, mesh=mesh, in_specs=in_specs, out_specs=out_specs, check_vma=False
    )
```

```python
from functools import partial
import math

import jax
import jax.numpy as jnp
from jax import lax
from jax.experimental import pallas as pl
from jax.experimental.pallas import tpu as pltpu
from jax.sharding import PartitionSpec as P

D = 768
HD = 64
FF = 3072
P_SIZE = 1024
CL = 128
QROWS = 512
eps = 1e-05
negative = -1e30
BF = jnp.bfloat16
F32 = jnp.float32


def nt(a, b):
    return lax.dot_general(a, b, (((1,), (1,)), ((), ())), preferred_element_type=F32)


def nn(a, b):
    return lax.dot_general(a, b, (((1,), (0,)), ((), ())), preferred_element_type=F32)


def tn(a, b):
    return lax.dot_general(a, b, (((0,), (0,)), ((), ())), preferred_element_type=F32)


def att_fwd_kernel(grp_ref, z_ref, q_ref, kvo_ref, kvp_ref, o_ref, lse_ref):
    j = pl.program_id(1)
    row0 = pl.multiple_of(grp_ref[j] * P_SIZE, P_SIZE)
    z = z_ref[0]
    lane = lax.broadcasted_iota(jnp.int32, (CL, 128), 1)
    low = lane < 64
    zero = jnp.zeros((CL, 128), BF)
    q = q_ref[...]
    q_parts = (jnp.where(low, zero, q), jnp.where(low, q, zero))

    @pl.when(z >= 2)
    def _():
        row = lax.broadcasted_iota(jnp.int32, (CL, CL), 0)
        near_ok = lax.broadcasted_iota(jnp.int32, (CL, CL), 1) <= row
        mixes, sums = [], []
        for h in range(2):
            cols = slice(128 * h, 128 * h + 128)
            kv = kvp_ref[pl.ds(row0, P_SIZE), cols]
            kvo = kvo_ref[:, cols]
            far = nt(q_parts[h], kv)
            near = jnp.where(near_ok, nt(q_parts[h], kvo), negative)
            top = jnp.maximum(
                jnp.max(far, axis=1, keepdims=True), jnp.max(near, axis=1, keepdims=True)
            )
            far = jnp.exp(far - top)
            near = jnp.exp(near - top)
            total = jnp.sum(far, axis=1, keepdims=True) + jnp.sum(near, axis=1, keepdims=True)
            mix = nn(far.astype(BF), kv) + nn(near.astype(BF), kvo)
            mixes.append(mix / total)
            sums.append(jnp.broadcast_to(top + jnp.log(total), (CL, 128)))
        o_ref[...] = jnp.where(low, mixes[0], mixes[1]).astype(BF)
        lse_ref[...] = jnp.where(low, sums[0], sums[1])

    @pl.when(z < 2)
    def _():
        limit = z * QROWS + (j % (QROWS // CL)) * CL
        row = lax.broadcasted_iota(jnp.int32, (CL, P_SIZE), 0)
        key = lax.broadcasted_iota(jnp.int32, (CL, P_SIZE), 1)
        allowed = key - row <= limit
        mixes, sums = [], []
        for h in range(2):
            cols = slice(128 * h, 128 * h + 128)
            kv = kvp_ref[pl.ds(row0, P_SIZE), cols]
            far = jnp.where(allowed, nt(q_parts[h], kv), negative)
            top = jnp.max(far, axis=1, keepdims=True)
            far = jnp.exp(far - top)
            total = jnp.sum(far, axis=1, keepdims=True)
            mix = nn(far.astype(BF), kv)
            mixes.append(mix / total)
            sums.append(jnp.broadcast_to(top + jnp.log(total), (CL, 128)))
        o_ref[...] = jnp.where(low, mixes[0], mixes[1]).astype(BF)
        lse_ref[...] = jnp.where(low, sums[0], sums[1])


def attend(grp, z, q, kvo, kvp):
    rows = q.shape[0]
    pairs = q.shape[1] // 128
    groups_rows = kvp.shape[0]
    return pl.pallas_call(
        att_fwd_kernel,
        name="att_fwd",
        grid_spec=pltpu.PrefetchScalarGridSpec(
            num_scalar_prefetch=2,
            grid=(pairs, rows // CL),
            in_specs=[
                pl.BlockSpec((CL, 128), lambda p, j, *_: (j, p)),
                pl.BlockSpec((CL, 256), lambda p, j, *_: (j, p)),
                pl.BlockSpec((groups_rows, 256), lambda p, j, *_: (0, p)),
            ],
            out_specs=[
                pl.BlockSpec((CL, 128), lambda p, j, *_: (j, p)),
                pl.BlockSpec((CL, 128), lambda p, j, *_: (j, p)),
            ],
        ),
        out_shape=[
            jax.ShapeDtypeStruct((rows, pairs * 128), BF),
            jax.ShapeDtypeStruct((rows, pairs * 128), F32),
        ],
        compiler_params=pltpu.CompilerParams(vmem_limit_bytes=40 << 20),
        cost_estimate=pl.CostEstimate(
            flops=4 * rows * P_SIZE * 128 * pairs * 2,
            bytes_accessed=groups_rows * 512 * pairs,
            transcendentals=rows * P_SIZE * pairs * 2,
        ),
    )(grp, z, q, kvo, kvp)


def att_bwd_kernel(
    grp_ref, z_ref, q_ref, gm_ref, lse_ref, kvo_ref, kvp_ref, dq_ref, dkvo_ref, dkvp_ref, acc
):
    j = pl.program_id(1)
    row0 = pl.multiple_of(grp_ref[j] * P_SIZE, P_SIZE)
    z = z_ref[0]
    low = lax.broadcasted_iota(jnp.int32, (CL, 128), 1) < 64
    zero = jnp.zeros((CL, 128), BF)
    q = q_ref[...]
    gm = gm_ref[...]
    stacks = (
        jnp.concatenate([jnp.where(low, zero, q), jnp.where(low, gm, zero)], axis=0),
        jnp.concatenate([jnp.where(low, q, zero), jnp.where(low, zero, gm)], axis=0),
    )

    @pl.when(j == 0)
    def _():
        acc[...] = jnp.zeros_like(acc)

    @pl.when(z >= 2)
    def _():
        row = lax.broadcasted_iota(jnp.int32, (CL, CL), 0)
        near_ok = row <= lax.broadcasted_iota(jnp.int32, (CL, CL), 1)
        dqs = []
        for h in range(2):
            cols = slice(128 * h, 128 * h + 128)
            kv = kvp_ref[pl.ds(row0, P_SIZE), cols]
            kvo = kvo_ref[:, cols]
            lse = lse_ref[0, 0, h : h + 1, :]
            far = nt(kv, stacks[h])
            near = nt(kvo, stacks[h])
            pf = jnp.exp(far[:, :CL] - lse)
            pn = jnp.where(near_ok, jnp.exp(near[:, :CL] - lse), 0.0)
            df = far[:, CL:]
            dn = near[:, CL:]
            inner = jnp.sum(pf * df, axis=0, keepdims=True) + jnp.sum(
                pn * dn, axis=0, keepdims=True
            )
            sf = (pf * (df - inner)).astype(BF)
            sn = (pn * (dn - inner)).astype(BF)
            acc[pl.ds(row0, P_SIZE), cols] += nn(
                jnp.concatenate([sf, pf.astype(BF)], axis=1), stacks[h]
            )
            dkvo_ref[:, cols] = nn(
                jnp.concatenate([sn, pn.astype(BF)], axis=1), stacks[h]
            ).astype(BF)
            dqs.append(tn(sf, kv) + tn(sn, kvo))
        dq_ref[...] = (jnp.where(low, dqs[1], dqs[0]) * 0.125).astype(BF)

    @pl.when(z < 2)
    def _():
        limit = z * QROWS + (j % (QROWS // CL)) * CL
        key = lax.broadcasted_iota(jnp.int32, (P_SIZE, CL), 0)
        row = lax.broadcasted_iota(jnp.int32, (P_SIZE, CL), 1)
        allowed = key - row <= limit
        dqs = []
        for h in range(2):
            cols = slice(128 * h, 128 * h + 128)
            kv = kvp_ref[pl.ds(row0, P_SIZE), cols]
            lse = lse_ref[0, 0, h : h + 1, :]
            far = nt(kv, stacks[h])
            pf = jnp.where(allowed, jnp.exp(far[:, :CL] - lse), 0.0)
            df = far[:, CL:]
            inner = jnp.sum(pf * df, axis=0, keepdims=True)
            sf = (pf * (df - inner)).astype(BF)
            acc[pl.ds(row0, P_SIZE), cols] += nn(
                jnp.concatenate([sf, pf.astype(BF)], axis=1), stacks[h]
            )
            dqs.append(tn(sf, kv))
        dkvo_ref[...] = jnp.zeros_like(dkvo_ref)
        dq_ref[...] = (jnp.where(low, dqs[1], dqs[0]) * 0.125).astype(BF)

    @pl.when(j == pl.num_programs(1) - 1)
    def _():
        dkvp_ref[...] = acc[...].astype(BF)


def attend_back(grp, z, q, gm, lse, kvo, kvp):
    rows = q.shape[0]
    pairs = q.shape[1] // 128
    groups_rows = kvp.shape[0]
    return pl.pallas_call(
        att_bwd_kernel,
        name="att_bwd",
        grid_spec=pltpu.PrefetchScalarGridSpec(
            num_scalar_prefetch=2,
            grid=(pairs, rows // CL),
            in_specs=[
                pl.BlockSpec((CL, 128), lambda p, j, *_: (j, p)),
                pl.BlockSpec((CL, 128), lambda p, j, *_: (j, p)),
                pl.BlockSpec((1, 1, 2, 128), lambda p, j, *_: (p, j, 0, 0)),
                pl.BlockSpec((CL, 256), lambda p, j, *_: (j, p)),
                pl.BlockSpec((groups_rows, 256), lambda p, j, *_: (0, p)),
            ],
            out_specs=[
                pl.BlockSpec((CL, 128), lambda p, j, *_: (j, p)),
                pl.BlockSpec((CL, 256), lambda p, j, *_: (j, p)),
                pl.BlockSpec((groups_rows, 256), lambda p, j, *_: (0, p)),
            ],
            scratch_shapes=[pltpu.VMEM((groups_rows, 256), F32)],
        ),
        out_shape=[
            jax.ShapeDtypeStruct((rows, pairs * 128), BF),
            jax.ShapeDtypeStruct((rows, pairs * 256), BF),
            jax.ShapeDtypeStruct((groups_rows, pairs * 256), BF),
        ],
        compiler_params=pltpu.CompilerParams(vmem_limit_bytes=48 << 20),
        cost_estimate=pl.CostEstimate(
            flops=10 * rows * P_SIZE * 128 * pairs * 2,
            bytes_accessed=groups_rows * 1024 * pairs,
            transcendentals=rows * P_SIZE * pairs * 2,
        ),
    )(grp, z, q, gm, lse, kvo, kvp)


MESH = pl.DeviceIdType.MESH


def places():
    x = lax.axis_index("dp")
    z = lax.axis_index("gr")
    g = lax.axis_index("gc")
    return x, z, g, g // 2, g % 2


def greet(partners):
    barrier = pltpu.get_barrier_semaphore()
    for partner in partners:
        pl.semaphore_signal(barrier, inc=1, device_id=partner, device_id_type=MESH)
    pl.semaphore_wait(barrier, len(partners))


def all_partners():
    x, z, g, y, c = places()
    by_z = [{"gr": z ^ step} for step in (1, 2, 3)]
    return [{"gc": g ^ 1}, {"gc": g ^ 2}, {"dp": x ^ 1}] + by_z


def send(src, dst, sems, slot, target, send_slot=None):
    return pltpu.make_async_remote_copy(
        src_ref=src,
        dst_ref=dst,
        send_sem=sems[0].at[slot if send_slot is None else send_slot],
        recv_sem=sems[1].at[slot],
        device_id=target,
        device_id_type=MESH,
    )


def add_into(dst, left, right):
    dst[...] = (left[...].astype(F32) + right[...].astype(F32)).astype(dst.dtype)


RS_SLOTS = 28
RS_ORDER = (3, 2, 1, 0)


def rs_plan(grads, outs, bufs, sems, l_sems, base, paired):
    own, ra, rb0, rb1, rc0, rc1, sc, rd, re = bufs
    x, z, g, y, c = places()
    sib, over_y, over_x = {"gc": g ^ 1}, {"gc": g ^ 2}, {"dp": x ^ 1}
    rows = grads.shape[2]
    q = rows // 4
    mine0 = pl.ds(pl.multiple_of(q * x, 16), q)
    other0 = pl.ds(pl.multiple_of(q * (1 - x), 16), q)
    mine1 = pl.ds(pl.multiple_of(2 * q + q * x, 16), q)
    other1 = pl.ds(pl.multiple_of(2 * q + q * (1 - x), 16), q)
    first = pl.ds(0, 2 * q)
    slot = base * RS_SLOTS

    def load(i, s):
        source = grads.at[2 * i + c, z ^ s] if paired else grads.at[i, z ^ s]
        return pltpu.make_async_copy(source, own.at[i, s], l_sems.at[8 * base + 2 * s + i])

    def hop_a(i, s):
        return send(grads.at[2 * i + 1 - c, z ^ s], ra.at[i, s], sems, slot + 6 * s + i, sib)

    def hop_b0(s):
        return send(own.at[1 - y, s, first], rb0.at[s], sems, slot + 6 * s + 2, over_y)

    def hop_b1(s):
        return send(own.at[:, s, other1], rb1.at[s], sems, slot + 6 * s + 3, over_x)

    def hop_c0(s):
        return send(own.at[y, s, other0], rc0.at[s], sems, slot + 6 * s + 4, over_x)

    def hop_c1(s):
        return send(own.at[1 - y, s, mine1], rc1.at[s], sems, slot + 6 * s + 5, over_y)

    def hop_z(s):
        return send(sc.at[s], rd.at[s - 1], sems, slot + 23 + s, {"gr": z ^ s})

    def hop_d():
        return send(sc.at[0], re, sems, slot + 27, over_x)

    def begin(s):
        for i in range(2):
            load(i, s).start()
            if paired:
                hop_a(i, s).start()

    def after_a(s):
        for i in range(2):
            load(i, s).wait()
            if paired:
                hop_a(i, s).wait()
                add_into(own.at[i, s], own.at[i, s], ra.at[i, s])
        hop_b0(s).start()
        hop_b1(s).start()

    def after_b(s):
        hop_b0(s).wait()
        hop_b1(s).wait()
        add_into(own.at[y, s, first], own.at[y, s, first], rb0.at[s])
        for i in range(2):
            add_into(own.at[i, s, mine1], own.at[i, s, mine1], rb1.at[s, i])
        hop_c0(s).start()
        hop_c1(s).start()

    def after_c(s):
        hop_c0(s).wait()
        hop_c1(s).wait()
        add_into(sc.at[s, pl.ds(0, q)], own.at[y, s, mine0], rc0.at[s])
        add_into(sc.at[s, pl.ds(q, q)], own.at[y, s, mine1], rc1.at[s])
        if s:
            hop_z(s).start()

    def total():
        for s in (1, 2, 3):
            hop_z(s).wait()
        whole = sc[0].astype(F32)
        for i in range(3):
            whole = whole + rd[i].astype(F32)
        sc[0] = whole.astype(BF)
        hop_d().start()

    def finish():
        hop_d().wait()
        outs[mine0] = sc[0, pl.ds(0, q)].astype(F32)
        outs[mine1] = sc[0, pl.ds(q, q)].astype(F32)
        outs[other0] = re[pl.ds(0, q)].astype(F32)
        outs[other1] = re[pl.ds(q, q)].astype(F32)

    return begin, after_a, after_b, after_c, total, finish


def rs_steps(plans):
    order = [(plan, s) for plan in plans for s in RS_ORDER]
    n = len(order)
    steps = [[partial(plan[0], s) for plan, s in order]]
    for i in range(n + 10):
        part = []
        if i < n:
            part.append(partial(order[i][0][1], order[i][1]))
        if 2 <= i < n + 2:
            part.append(partial(order[i - 2][0][2], order[i - 2][1]))
        if 4 <= i < n + 4:
            part.append(partial(order[i - 4][0][3], order[i - 4][1]))
        if 7 <= i < n + 7 and (i - 7) % 4 == 3:
            part.append(plans[(i - 7) // 4][4])
        if 9 <= i < n + 9 and (i - 9) % 4 == 3:
            part.append(plans[(i - 9) // 4][5])
        if part:
            steps.append(part)
    return steps


def rs_scratch(rows, cols, paired):
    q = rows // 4
    return [
        pltpu.VMEM((2, 4, rows, cols), BF),
        pltpu.VMEM((2, 4, rows, cols) if paired else (16, 128), BF),
        pltpu.VMEM((4, 2 * q, cols), BF),
        pltpu.VMEM((4, 2, q, cols), BF),
        pltpu.VMEM((4, q, cols), BF),
        pltpu.VMEM((4, q, cols), BF),
        pltpu.VMEM((4, 2 * q, cols), BF),
        pltpu.VMEM((3, 2 * q, cols), BF),
        pltpu.VMEM((2 * q, cols), BF),
    ]


def att_scatter_kernel(count, grp_ref, q_ref, lse_ref, kvo_ref, kvp_ref, gm, *refs):
    grads = refs[:count]
    dq_ref, dkvo_ref, dkv_ref = refs[count : count + 3]
    outs = refs[count + 3 : 2 * count + 3]
    rest = refs[2 * count + 3 :]
    bufs, (gmx, sem_s, sem_r, l_sems, m_send, m_recv, m_local) = rest[: 9 * count], rest[9 * count :]
    p, j = pl.program_id(0), pl.program_id(1)
    step = p * pl.num_programs(1) + j
    x, z, g, y, c = places()
    hooks = rs_steps(
        [
            rs_plan(grads[k], outs[k], bufs[9 * k : 9 * k + 9], (sem_s, sem_r), l_sems, k, True)
            for k in range(count)
        ]
    )

    def exchange(i):
        cols = pl.ds(128 * i, 128)
        return (
            pltpu.make_async_copy(gm.at[c, :, cols], gmx.at[i, c], m_local.at[i]),
            send(gm.at[1 - c, :, cols], gmx.at[i, c], (m_send, m_recv), i, {"gc": g ^ 1}),
        )

    @pl.when(step == 0)
    def _():
        greet(all_partners())
        for i in range(3):
            for copy in exchange(i):
                copy.start()
        for hook in hooks[0]:
            hook()
        for copy in exchange(0):
            copy.wait()

    for i in (1, 2):

        @pl.when(step == 8 * i)
        def _():
            for copy in exchange(i):
                copy.wait()

    last = len(hooks) - 1
    for when in range(1, 23):
        parts = [h for i in range(1, last) if i * 22 // (last - 1) == when for h in hooks[i]]
        if parts:

            @pl.when(step == when)
            def _():
                for hook in parts:
                    hook()

    group = grp_ref[j]
    low = lax.broadcasted_iota(jnp.int32, (CL, 128), 1) < 64
    zero = jnp.zeros((CL, 128), BF)
    q = q_ref[0]
    gmix = gmx[p, j // 4, pl.ds(pl.multiple_of((j % 4) * CL, CL), CL)]
    stacks = (
        jnp.concatenate([jnp.where(low, zero, q), jnp.where(low, gmix, zero)], axis=0),
        jnp.concatenate([jnp.where(low, q, zero), jnp.where(low, zero, gmix)], axis=0),
    )

    @pl.when(z >= 2)
    def _():
        row = lax.broadcasted_iota(jnp.int32, (CL, CL), 0)
        near_ok = row <= lax.broadcasted_iota(jnp.int32, (CL, CL), 1)
        dqs = []
        for h in range(2):
            cols = slice(128 * h, 128 * h + 128)
            kv = kvp_ref[0, group, :, cols]
            kvo = kvo_ref[0, :, cols]
            lse = lse_ref[0, 0, h : h + 1, :]
            far = nt(kv, stacks[h])
            near = nt(kvo, stacks[h])
            pf = jnp.exp(far[:, :CL] - lse)
            pn = jnp.where(near_ok, jnp.exp(near[:, :CL] - lse), 0.0)
            df = far[:, CL:]
            dn = near[:, CL:]
            inner = jnp.sum(pf * df, axis=0, keepdims=True) + jnp.sum(
                pn * dn, axis=0, keepdims=True
            )
            sf = (pf * (df - inner)).astype(BF)
            sn = (pn * (dn - inner)).astype(BF)
            dkv_ref[0, :, cols] = nn(
                jnp.concatenate([sf, pf.astype(BF)], axis=1), stacks[h]
            ).astype(BF)
            dkvo_ref[:, cols] = nn(
                jnp.concatenate([sn, pn.astype(BF)], axis=1), stacks[h]
            ).astype(BF)
            dqs.append(tn(sf, kv) + tn(sn, kvo))
        dq_ref[...] = (jnp.where(low, dqs[1], dqs[0]) * 0.125).astype(BF)

    @pl.when(z < 2)
    def _():
        limit = z * QROWS + (j % (QROWS // CL)) * CL
        key = lax.broadcasted_iota(jnp.int32, (P_SIZE, CL), 0)
        row = lax.broadcasted_iota(jnp.int32, (P_SIZE, CL), 1)
        allowed = key - row <= limit
        dqs = []
        for h in range(2):
            cols = slice(128 * h, 128 * h + 128)
            kv = kvp_ref[0, group, :, cols]
            lse = lse_ref[0, 0, h : h + 1, :]
            far = nt(kv, stacks[h])
            pf = jnp.where(allowed, jnp.exp(far[:, :CL] - lse), 0.0)
            df = far[:, CL:]
            inner = jnp.sum(pf * df, axis=0, keepdims=True)
            sf = (pf * (df - inner)).astype(BF)
            dkv_ref[0, :, cols] = nn(
                jnp.concatenate([sf, pf.astype(BF)], axis=1), stacks[h]
            ).astype(BF)
            dqs.append(tn(sf, kv))
        dkvo_ref[...] = jnp.zeros_like(dkvo_ref)
        dq_ref[...] = (jnp.where(low, dqs[1], dqs[0]) * 0.125).astype(BF)

    @pl.when(step == 23)
    def _():
        for hook in hooks[last]:
            hook()


def attend_back_scatter(grp, q, lse, kvo, kvp, gm, grads, collective_id):
    rows = q.shape[1]
    count = len(grads)
    any_space = pl.BlockSpec(memory_space=pl.ANY)
    scratch = []
    for grad in grads:
        scratch += rs_scratch(grad.shape[2], grad.shape[3], True)
    slots = RS_SLOTS * count
    return pl.pallas_call(
        partial(att_scatter_kernel, count),
        name="attend_back_scatter",
        grid_spec=pltpu.PrefetchScalarGridSpec(
            num_scalar_prefetch=1,
            grid=(3, rows // CL),
            in_specs=[
                pl.BlockSpec((1, CL, 128), lambda p, j, *_: (p, j, 0)),
                pl.BlockSpec((1, 1, 2, 128), lambda p, j, *_: (p, j, 0, 0)),
                pl.BlockSpec((1, CL, 256), lambda p, j, *_: (p, j, 0)),
                pl.BlockSpec((1, 4, P_SIZE, 256), lambda p, j, *_: (p, 0, 0, 0)),
            ]
            + [any_space] * (count + 1),
            out_specs=[
                pl.BlockSpec((CL, 128), lambda p, j, *_: (j, p)),
                pl.BlockSpec((CL, 256), lambda p, j, *_: (j, p)),
                pl.BlockSpec((1, P_SIZE, 256), lambda p, j, *_: (j, 0, p)),
            ]
            + [pl.BlockSpec(grad.shape[2:], lambda p, j, *_: (0, 0)) for grad in grads],
            scratch_shapes=scratch
            + [
                pltpu.VMEM((3, 2, QROWS, 128), BF),
                pltpu.SemaphoreType.DMA((slots,)),
                pltpu.SemaphoreType.DMA((slots,)),
                pltpu.SemaphoreType.DMA((8 * count,)),
                pltpu.SemaphoreType.DMA((3,)),
                pltpu.SemaphoreType.DMA((3,)),
                pltpu.SemaphoreType.DMA((3,)),
            ],
        ),
        out_shape=[
            jax.ShapeDtypeStruct((rows, 384), BF),
            jax.ShapeDtypeStruct((rows, 768), BF),
            jax.ShapeDtypeStruct((8, P_SIZE, 768), BF),
        ]
        + [jax.ShapeDtypeStruct(grad.shape[2:], F32) for grad in grads],
        compiler_params=pltpu.CompilerParams(
            collective_id=collective_id, has_side_effects=True, vmem_limit_bytes=56 << 20
        ),
    )(grp, q, lse, kvo, kvp, gm, *grads)


def fold_kernel(
    grp_ref,
    dkv_ref,
    dkvo_ref,
    dq_ref,
    n1p_ref,
    n1c_ref,
    w_q,
    w_kv,
    part_ref,
    chip_ref,
    dw_ref,
    acc,
    wkt,
    wqt,
    dkvw,
    dqw,
):
    t = pl.program_id(0)

    @pl.when(t == 0)
    def _():
        wkt[...] = w_kv[...].T
        wqt[...] = w_q[...].T
        dkvw[...] = jnp.zeros_like(dkvw)
        dqw[...] = jnp.zeros_like(dqw)

    acc[...] = jnp.zeros_like(acc)
    for j in range(8):
        acc[grp_ref[j]] += dkv_ref[j].astype(F32)
    low = acc[...].astype(BF).reshape(512, D)
    part_ref[...] = nn(low, wkt[...]).astype(BF).reshape(4, CL, D)
    dkvo = dkvo_ref[...]
    dq = dq_ref[...]
    chip_ref[...] = (nn(dq, wqt[...]) + nn(dkvo, wkt[...])).astype(BF)
    n1c = n1c_ref[...]
    rows = jnp.concatenate([n1p_ref[...].reshape(512, D), n1c], axis=0)
    dkvw[...] += tn(rows, jnp.concatenate([low, dkvo], axis=0))
    dqw[...] += tn(n1c, dq)

    @pl.when(t == pl.num_programs(0) - 1)
    def _():
        for head in range(6):
            p, b = head // 2, head % 2
            at_q = 128 * p + (0 if b else 64)
            at_k = 256 * p + (128 if b else 64)
            at_v = 256 * p + (192 if b else 0)
            pieces = (
                dqw[:, at_q : at_q + HD],
                dkvw[:, at_k : at_k + HD],
                dkvw[:, at_v : at_v + HD],
            )
            for i, piece in enumerate(pieces):
                at = (head % 3) * 192 + HD * i
                dw_ref[head // 3, :, at : at + HD] = piece.astype(BF)


def fold_prompts(grp, dkv, dkvo, dq, n1_prompt, n1_chip, w_q, w_kv):
    tile = CL
    groups = pl.BlockSpec((4, tile, D), lambda i, *_: (0, i, 0))
    return pl.pallas_call(
        fold_kernel,
        name="fold_prompts",
        grid_spec=pltpu.PrefetchScalarGridSpec(
            num_scalar_prefetch=1,
            grid=(P_SIZE // tile,),
            in_specs=[
                pl.BlockSpec((8, tile, D), lambda i, *_: (0, i, 0)),
                pl.BlockSpec((tile, D), lambda i, *_: (i, 0)),
                pl.BlockSpec((tile, 384), lambda i, *_: (i, 0)),
                groups,
                pl.BlockSpec((tile, D), lambda i, *_: (i, 0)),
                pl.BlockSpec((D, 384), lambda i, *_: (0, 0)),
                pl.BlockSpec((D, D), lambda i, *_: (0, 0)),
            ],
            out_specs=[
                groups,
                pl.BlockSpec((tile, D), lambda i, *_: (i, 0)),
                pl.BlockSpec((2, D, 576), lambda i, *_: (0, 0, 0)),
            ],
            scratch_shapes=[
                pltpu.VMEM((4, tile, D), F32),
                pltpu.VMEM((D, D), BF),
                pltpu.VMEM((384, D), BF),
                pltpu.VMEM((D, D), F32),
                pltpu.VMEM((D, 384), F32),
            ],
        ),
        out_shape=[
            jax.ShapeDtypeStruct((4, P_SIZE, D), BF),
            jax.ShapeDtypeStruct((2 * QROWS, D), BF),
            jax.ShapeDtypeStruct((2, D, 576), BF),
        ],
        compiler_params=pltpu.CompilerParams(vmem_limit_bytes=48 << 20),
    )(grp, dkv, dkvo, dq, n1_prompt.reshape(4, P_SIZE, D), n1_chip, w_q, w_kv)


def norm_rows(hidden, gain, shift):
    center = jnp.mean(hidden, axis=1, keepdims=True)
    offset = hidden - center
    factor = lax.rsqrt(jnp.mean(offset * offset, axis=1, keepdims=True) + eps)
    return offset * factor * gain + shift


CHUNKS = 4
FRONT = 13
GATHER_SLOTS = 40
SEGMENT = 4


def front_kernel(
    tokens,
    vec,
    bup,
    own,
    wq,
    block0,
    block1,
    block2,
    mixed,
    lse_ref,
    whole0,
    whole1,
    whole2,
    prompts_out,
    chip_out,
    q_out,
    kvo_out,
    kvp_out,
    wq_out,
    wkv_out,
    vec_out,
    bup_out,
    own_out,
    n1,
    vec_in,
    prompts,
    chip,
    wpair,
    q_all,
    kvo_all,
    kvp_all,
    mix,
    own_scalar,
    zs,
    zr,
    ys,
    yr,
    ds,
    dr,
    ws,
    wr,
    ss,
    sr,
    gs,
    gr_,
    ms,
    mr,
    l_sems,
    o_sems,
):
    x, z, g, y, c = places()
    sib, over_y, over_x = {"gc": g ^ 1}, {"gc": g ^ 2}, {"dp": x ^ 1}
    z_sems, y_sems, d_sems, w_sems, s_sems, g_sems = (
        (zs, zr),
        (ys, yr),
        (ds, dr),
        (ws, wr),
        (ss, sr),
        (gs, gr_),
    )
    blocks, wholes = (block0, block1, block2), (whole0, whole1, whole2)
    half_rows = wq.shape[0] // 2
    my_half = pl.ds(pl.multiple_of(x * half_rows, 16), half_rows)
    size = QROWS // CHUNKS
    first_half = jnp.where(z == 0, 0, 1)
    order = (z, z ^ 1, jnp.where(z < 2, 2, 1), jnp.where(z < 2, 3, 0))
    above, below = {"gr": jnp.minimum(z + 1, 3)}, {"gr": jnp.maximum(z - 1, 0)}
    inner = jnp.logical_and(z > 0, z < 3)

    def line(part, sems, base, b):
        return (
            (jnp.logical_and(z < 3, b <= z), send(part, part, sems, base + b, above)),
            (
                jnp.logical_and(z > 0, b >= z),
                send(part, part, sems, base + b, below, base + 4 + b),
            ),
        )

    def pass_on(copies):
        for goes, copy in copies:
            pl.when(goes)(copy.start)

    def passed_on(copies):
        for goes, copy in copies:
            pl.when(goes)(copy.wait_send)

    local_copy = pltpu.make_async_copy

    def small(kind, s):
        if kind == 0:
            return send(vec, vec_in.at[s], s_sems, s, {"gr": z ^ s})
        if kind == 1:
            return send(own, own_out.at[z], s_sems, 3 + s, {"gr": z ^ s})
        return send(bup, bup_out.at[g], s_sems, 6 + s, {"gc": g ^ s})

    def chip_send():
        return send(n1, chip.at[c], s_sems, 10, sib)

    def w_local():
        return local_copy(wq.at[my_half], wpair.at[y, z, my_half], l_sems.at[0])

    def w_line(s):
        return line(wpair.at[y, order[s], my_half], w_sems, 0, order[s])

    def w_gc(s):
        piece = wpair.at[y, order[s], my_half]
        return send(piece, piece, w_sems, 8 + s, over_y)

    def w_dp(s):
        piece = wpair.at[y, order[s], my_half]
        return send(piece, piece, w_sems, 12 + s, over_x)

    def w_dp_far(s):
        piece = wpair.at[1 - y, order[s], my_half]
        return send(piece, piece, w_sems, 16 + s, over_x)

    def chunk(number):
        return (first_half if number < CHUNKS else 1 - first_half), number % CHUNKS

    def item(column, number):
        half, k = chunk(number)
        return prompts.at[column, half, pl.ds(k * size, size)]

    def up(number):
        half, k = chunk(number)
        ref = item(g, number)
        return send(ref, ref, z_sems, half * CHUNKS + k, {"gr": jnp.minimum(z + 1, 3)})

    def down(number):
        half, k = chunk(number)
        ref = item(g, number)
        return send(
            ref,
            ref,
            z_sems,
            half * CHUNKS + k,
            {"gr": jnp.maximum(z - 1, 0)},
            2 * CHUNKS + k,
        )

    def side(number):
        half, k = chunk(number)
        ref = item(g, number)
        return send(ref, ref, y_sems, half * CHUNKS + k, over_y)

    def core(number, far):
        half, k = chunk(number)
        ref = item(g ^ 2 if far else g, number)
        return send(ref, ref, d_sems, far * 2 * CHUNKS + half * CHUNKS + k, sib)

    def goes_up(number):
        return jnp.logical_and(z < 3, chunk(number)[0] <= z)

    def goes_down(number):
        return jnp.logical_and(z == 1, chunk(number)[0] == 1)

    def forward(number):
        @pl.when(chunk(number)[0] != z)
        def _():
            up(number).wait_recv()

        @pl.when(goes_up(number))
        def _():
            up(number).start()

        @pl.when(goes_down(number))
        def _():
            down(number).start()

        side(number).start()
        core(number, 0).start()

    def across(number):
        side(number).wait_recv()
        core(number, 1).start()

    def plan(a, s):
        block, whole = blocks[a], wholes[a]
        q = block.shape[0] // 4
        half = pl.ds(pl.multiple_of(x * 2 * q, 16), 2 * q)
        qa = pl.ds(pl.multiple_of(x * 2 * q, 16), q)
        qb = pl.ds(pl.multiple_of(x * 2 * q + q, 16), q)
        qc = pl.ds(pl.multiple_of((1 - x) * 2 * q + q, 16), q)
        base = a * GATHER_SLOTS
        mine, far = whole.at[g, order[s]], whole.at[g ^ 2, order[s]]
        o = base + 8 + 8 * s

        def same(part, number, target):
            return lambda: send(part, part, g_sems, o + number, target)

        return {
            "line": lambda: line(mine.at[half], g_sems, base, order[s]),
            "ay": same(mine.at[qa], 0, over_y),
            "ax": same(mine.at[qa], 1, over_x),
            "afx": same(far.at[qa], 2, over_x),
            "bx": same(mine.at[qb], 3, over_x),
            "by": same(mine.at[qb], 4, over_y),
            "bfy": same(mine.at[qc], 5, over_y),
            "c1": same(mine, 6, sib),
            "c2": same(far, 7, sib),
        }

    def own_block(a):
        return local_copy(blocks[a], wholes[a].at[g, z], l_sems.at[4 + a])

    def names(s):
        return ("ay", "ax", "afx", "bx", "by", "bfy") if s else ("ay", "afx", "by", "bfy")

    def relay(s):
        @pl.when(inner)
        def _():
            for a in range(3):
                copies = plan(a, s)["line"]()
                copies[0][1].wait_recv()
                pass_on(copies)


    def gather_first(s):
        for a in range(3):
            m = plan(a, s)
            if s:
                pl.when(jnp.logical_not(inner))(m["line"]()[0][1].wait_recv)
                m["bx"]().start()
                m["ax"]().start()
            else:
                m["bfy"]().start()
            m["ay"]().start()
            m["by"]().start()

    def gather_second(s):
        for a in range(3):
            m = plan(a, s)
            m["ay"]().wait_recv()
            m["afx"]().start()
            if s:
                m["bx"]().wait_recv()
                m["bfy"]().start()

    def gather_third(s):
        for a in range(3):
            m = plan(a, s)
            if s:
                m["ax"]().wait_recv()
            for name in ("afx", "by", "bfy"):
                m[name]().wait_recv()
            m["c1"]().start()
            m["c2"]().start()

    def out_copies():
        return [
            local_copy(prompts, prompts_out, o_sems.at[0]),
            local_copy(chip, chip_out, o_sems.at[1]),
            local_copy(q_all, q_out, o_sems.at[2]),
            local_copy(kvo_all, kvo_out, o_sems.at[3]),
            local_copy(kvp_all, kvp_out, o_sems.at[4]),
        ]

    def exchange(i):
        cols = pl.ds(128 * i, 128)
        return (
            local_copy(mix.at[i, c], mixed.at[c, :, cols], l_sems.at[7 + i]),
            send(mix.at[i, 1 - c], mixed.at[c, :, cols], (ms, mr), i, sib),
        )

    hooks = {i: [] for i in range(FRONT)}

    def begin():
        greet(all_partners() + [{"gc": g ^ 3}])
        w_local().start()
        for s in (1, 2, 3):
            for kind in range(3):
                small(kind, s).start()
        w_local().wait()
        pass_on(w_line(0))
        own_out[z] = own[...]
        bup_out[g] = bup[...]
        for s in (1, 2, 3):
            small(0, s).wait_recv()
        vec_out[...] = (vec[...] + vec_in[1]) + (vec_in[2] + vec_in[3])

        @pl.loop(0, CHUNKS)
        def _(i):
            rows = pl.ds(pl.multiple_of(i * size, size), size)
            hidden = tokens[rows].astype(F32) + vec_out[0:1]
            n1[rows] = norm_rows(hidden, vec_out[1:2], vec_out[2:3]).astype(BF)

        @pl.when(z < 2)
        def _():
            to = local_copy(n1, prompts.at[g, jnp.minimum(z, 1)], l_sems.at[2])
            to.start()
            to.wait()

    def begin_chip():
        local_copy(n1, chip.at[c], l_sems.at[1]).start()
        chip_send().start()
        w_gc(0).start()
        w_dp(0).start()

    hooks[0] += [begin, partial(forward, 0), begin_chip]
    for i in range(1, 8):
        hooks[i].append(partial(forward, i))
    for i in range(2, 10):
        hooks[i].append(partial(across, i - 2))

    def w_pass(s):
        copies = w_line(s)
        copies[0][1].wait_recv()
        pass_on(copies)
        w_gc(s).start()
        w_dp(s).start()

    def w_across(s):
        w_gc(s).wait_recv()
        w_dp_far(s).start()

    for s in (1, 2, 3):
        hooks[s].append(partial(w_pass, s))
    hooks[2].append(partial(w_across, 0))
    hooks[3] += [partial(w_across, 1)]
    hooks[4] += [partial(w_across, 2), partial(w_across, 3)]

    def assemble():
        for s in range(4):
            w_dp(s).wait_recv()
            w_dp_far(s).wait_recv()
        local_copy(n1, chip.at[c], l_sems.at[1]).wait()
        chip_send().wait_recv()
        for s in (1, 2, 3):
            small(1, s).wait_recv()
        to = local_copy(own_out, own_scalar, l_sems.at[3])
        to.start()
        for head in range(6):
            p, b = head // 2, head % 2
            at_q = 128 * p + (0 if b else 64)
            at_k = 256 * p + (128 if b else 64)
            at_v = 256 * p + (192 if b else 0)
            start = (head % 3) * 192
            for r in range(4):
                rows = slice(192 * r, 192 * r + 192)
                source = wpair.at[head // 3, r]
                wq_out[rows, at_q : at_q + HD] = source[:, start : start + HD]
                wkv_out[rows, at_k : at_k + HD] = source[:, start + HD : start + 2 * HD]
                wkv_out[rows, at_v : at_v + HD] = source[:, start + 2 * HD : start + 3 * HD]
        to.wait()

    hooks[5].append(assemble)

    def project(number):
        core(number, 0).wait_recv()
        core(number, 1).wait_recv()
        half, k = chunk(number)
        w = wkv_out[...]
        rows = jnp.concatenate(
            [prompts[i, half, pl.ds(k * size, size)] for i in range(4)], axis=0
        )
        kv = nn(rows, w).astype(BF)
        to = pl.ds(pl.multiple_of(half * QROWS + k * size, size), size)
        for i in range(4):
            for p in range(3):
                kvp_all[p, i, to] = kv[size * i : size * i + size, 256 * p : 256 * p + 256]
        mine = chip[number // CHUNKS, pl.ds((number % CHUNKS) * size, size)]
        kvo = nn(mine, w).astype(BF)
        queries = (nn(mine, wq_out[...]) * 0.125).astype(BF)
        to = pl.ds(number * size, size)
        for p in range(3):
            kvo_all[p, to] = kvo[:, 256 * p : 256 * p + 256]
            q_all[p, to] = queries[:, 128 * p : 128 * p + 128]

    for i in range(8):
        hooks[5 + i].append(partial(project, i))

    def begin_gather():
        for a in range(3):
            own_block(a).start()
        for a in range(3):
            own_block(a).wait()
            pass_on(plan(a, 0)["line"]())

    hooks[7].insert(1, begin_gather)
    hooks[8].append(partial(gather_first, 0))
    hooks[10].append(partial(gather_second, 0))
    between = [[] for _ in range(24 // SEGMENT + 1)]
    last = len(between) - 1
    between[0] += [lambda: [copy.start() for copy in out_copies()], partial(gather_third, 0)]
    hooks[11].append(partial(relay, 1))
    for slot, stage, s in (
        (0, relay, 2),
        (1, relay, 3),
        (1, gather_first, 1),
        (2, gather_first, 2),
        (2, gather_second, 1),
        (4, gather_first, 3),
        (4, gather_second, 2),
        (4, gather_third, 1),
        (5, gather_second, 3),
        (5, gather_third, 2),
        (6, gather_third, 3),
    ):
        between[slot].append(partial(stage, s))

    for number in range(FRONT):
        for hook in hooks[number]:
            hook()

    low = lax.broadcasted_iota(jnp.int32, (CL, 128), 1) < 64

    def parts(turn):
        p, j = turn // 8, turn % 8
        shard = 2 * y + j // 4
        group = jnp.where(
            z < 2, shard, own_scalar[shard, 0, jnp.maximum(z - 2, 0) * 4 + j % 4]
        )
        rows_j = pl.ds(pl.multiple_of(j * CL, CL), CL)
        zero = jnp.zeros((CL, 128), BF)
        q = q_all[p, rows_j]
        return p, j, group, rows_j, (jnp.where(low, zero, q), jnp.where(low, q, zero))

    def store(p, j, mixes, sums):
        mix[p, j // 4, pl.ds(pl.multiple_of((j % 4) * CL, CL), CL)] = jnp.where(
            low, mixes[0], mixes[1]
        ).astype(BF)
        flat = jnp.where(low, sums[0], sums[1]).T
        lse_ref[p, j, 0:1] = flat[0:1]
        lse_ref[p, j, 1:2] = flat[64:65]

    def cont_turn(turn, carried):
        p, j, group, rows_j, q_parts = parts(turn)
        row = lax.broadcasted_iota(jnp.int32, (CL, CL), 0)
        near_ok = lax.broadcasted_iota(jnp.int32, (CL, CL), 1) <= row
        mixes, sums = [], []
        for h in range(2):
            cols = slice(128 * h, 128 * h + 128)
            kv = kvp_all[p, group, :, cols]
            kvo = kvo_all[p, rows_j, cols]
            far = nt(q_parts[h], kv)
            near = jnp.where(near_ok, nt(q_parts[h], kvo), negative)
            top = jnp.maximum(
                jnp.max(far, axis=1, keepdims=True), jnp.max(near, axis=1, keepdims=True)
            )
            far = jnp.exp(far - top)
            near = jnp.exp(near - top)
            total = jnp.sum(far, axis=1, keepdims=True) + jnp.sum(near, axis=1, keepdims=True)
            mixes.append((nn(far.astype(BF), kv) + nn(near.astype(BF), kvo)) / total)
            sums.append(jnp.broadcast_to(top + jnp.log(total), (CL, 128)))
        store(p, j, mixes, sums)
        return carried

    def prompt_turn(turn, carried):
        p, j, group, rows_j, q_parts = parts(turn)
        limit = z * QROWS + (j % (QROWS // CL)) * CL
        row = lax.broadcasted_iota(jnp.int32, (CL, P_SIZE), 0)
        key = lax.broadcasted_iota(jnp.int32, (CL, P_SIZE), 1)
        allowed = key - row <= limit
        mixes, sums = [], []
        for h in range(2):
            cols = slice(128 * h, 128 * h + 128)
            kv = kvp_all[p, group, :, cols]
            far = jnp.where(allowed, nt(q_parts[h], kv), negative)
            top = jnp.max(far, axis=1, keepdims=True)
            far = jnp.exp(far - top)
            total = jnp.sum(far, axis=1, keepdims=True)
            mixes.append(nn(far.astype(BF), kv) / total)
            sums.append(jnp.broadcast_to(top + jnp.log(total), (CL, 128)))
        store(p, j, mixes, sums)
        return carried

    for segment in range(last):
        for hook in between[segment]:
            hook()
        turns = (segment * SEGMENT, segment * SEGMENT + SEGMENT)

        @pl.when(z >= 2)
        def _():
            lax.fori_loop(*turns, cont_turn, 0)

        @pl.when(z < 2)
        def _():
            lax.fori_loop(*turns, prompt_turn, 0)

        if turns[1] % 8 == 0:
            for copy in exchange(turns[1] // 8 - 1):
                copy.start()
    for hook in between[last]:
        hook()

    for number in range(8):
        side(number).wait_send()
        core(number, 0).wait_send()
        core(number, 1).wait_send()

        @pl.when(goes_up(number))
        def _():
            up(number).wait_send()

        @pl.when(goes_down(number))
        def _():
            down(number).wait_send()

    for s in range(4):
        if s:
            small(0, s).wait_send()
            small(1, s).wait_send()
            small(2, s).wait()
        passed_on(w_line(s))
        w_gc(s).wait_send()
        w_dp(s).wait_send()
        w_dp_far(s).wait_send()
    chip_send().wait_send()
    for s in range(4):
        for a in range(3):
            m = plan(a, s)
            passed_on(m["line"]())
            for name in names(s):
                m[name]().wait_send()
            m["c1"]().wait()
            m["c2"]().wait()
    for i in range(3):
        for copy in exchange(i):
            copy.wait()
    for copy in out_copies():
        copy.wait()


def front(tokens, vec, bup, own, wq, blocks, collective_id):
    any_space = pl.BlockSpec(memory_space=pl.ANY)
    vmem = pl.BlockSpec(memory_space=pltpu.VMEM)
    rows = 2 * QROWS

    def dma(count):
        return pltpu.SemaphoreType.DMA((count,))

    slots = 3 * GATHER_SLOTS
    heads = [(3, rows, 128), (3, rows, 256), (3, 4, P_SIZE, 256)]
    return pl.pallas_call(
        front_kernel,
        name="front",
        in_specs=[vmem, vmem, vmem, vmem] + [any_space] * 4,
        out_specs=[any_space, vmem]
        + [any_space] * 8
        + [vmem] * 5,
        out_shape=[
            jax.ShapeDtypeStruct((2, QROWS, 384), BF),
            jax.ShapeDtypeStruct((3, rows // CL, 2, 128), F32),
        ]
        + [jax.ShapeDtypeStruct((4, 4) + block.shape, BF) for block in blocks]
        + [
            jax.ShapeDtypeStruct((4, 2, QROWS, D), BF),
            jax.ShapeDtypeStruct((2, QROWS, D), BF),
        ]
        + [jax.ShapeDtypeStruct(shape, BF) for shape in heads]
        + [
            jax.ShapeDtypeStruct((D, 384), BF),
            jax.ShapeDtypeStruct((D, D), BF),
            jax.ShapeDtypeStruct(vec.shape, F32),
            jax.ShapeDtypeStruct((4,) + bup.shape, F32),
            jax.ShapeDtypeStruct((4,) + own.shape, jnp.int32),
        ],
        scratch_shapes=[
            pltpu.VMEM((QROWS, D), BF),
            pltpu.VMEM((4,) + vec.shape, F32),
            pltpu.VMEM((4, 2, QROWS, D), BF),
            pltpu.VMEM((2, QROWS, D), BF),
            pltpu.VMEM((2, 4) + wq.shape, BF),
        ]
        + [pltpu.VMEM(shape, BF) for shape in heads]
        + [
            pltpu.VMEM((3, 2, QROWS, 128), BF),
            pltpu.SMEM((4,) + own.shape, jnp.int32),
            dma(3 * CHUNKS),
            dma(2 * CHUNKS),
            dma(2 * CHUNKS),
            dma(2 * CHUNKS),
            dma(4 * CHUNKS),
            dma(4 * CHUNKS),
            dma(20),
            dma(20),
            dma(11),
            dma(11),
            dma(slots),
            dma(slots),
            dma(3),
            dma(3),
            dma(10),
            dma(5),
        ],
        compiler_params=pltpu.CompilerParams(
            collective_id=collective_id, has_side_effects=True, vmem_limit_bytes=56 << 20
        ),
    )(tokens, vec, bup, own, wq, *blocks)


def tail_kernel(
    part,
    chip,
    dw,
    grad_h2,
    tokens,
    vec,
    sums,
    out,
    sums_out,
    dw_out,
    own,
    ra,
    rb,
    rz,
    keep,
    take,
    gsum,
    cur,
    sb,
    *rest,
):
    bufs, (sem_s, sem_r, l_sems, w_s, w_r, w_l) = rest[:9], rest[9:]
    sems = (sem_s, sem_r)
    x, z, g, y, c = places()
    sib, over_y, over_x = {"gc": g ^ 1}, {"gc": g ^ 2}, {"dp": x ^ 1}
    down = {"gr": jnp.maximum(z - 1, 0)}
    far = z >= 2
    greet(all_partners())
    hooks = rs_steps([rs_plan(dw, dw_out, bufs, (w_s, w_r), w_l, 0, False)])
    size = QROWS // CHUNKS
    chunks = [(h, k) for h in range(2) for k in range(CHUNKS)]

    def rows(k):
        return pl.ds(k * size, size)

    def index(side):
        return 1 - y if side == 0 else y

    def load(side, h, k):
        i = index(side)
        return pltpu.make_async_copy(
            part.at[2 * i + c, h, rows(k)],
            own.at[i, h, rows(k)],
            l_sems.at[8 * side + CHUNKS * h + k],
        )

    def hop_a(side, h, k):
        i = index(side)
        return send(
            part.at[2 * i + 1 - c, h, rows(k)],
            ra.at[i, h, rows(k)],
            sems,
            8 * side + CHUNKS * h + k,
            sib,
        )

    def hop_y(h, k):
        return send(
            own.at[1 - y, h, rows(k)], rb.at[h, rows(k)], sems, 16 + CHUNKS * h + k, over_y
        )

    def hop_z(h, k):
        return send(own.at[y, h, rows(k)], rz.at[h, rows(k)], sems, 24 + CHUNKS * h + k, down)

    hop_chip = send(chip.at[1 - c], take, sems, 32, sib)
    load_chip = pltpu.make_async_copy(chip.at[c], keep, l_sems.at[16])

    def fold(h, k, other):
        add_into(own.at[y, h, rows(k)], own.at[y, h, rows(k)], other.at[rows(k)])

    for h, k in chunks:

        @pl.when(far)
        def _():
            load(0, h, k).start()
            hop_a(0, h, k).start()

        load(1, h, k).start()
        hop_a(1, h, k).start()
    hop_chip.start()
    load_chip.start()
    for hook in hooks[0]:
        hook()

    def stage1(h, k):
        @pl.when(far)
        def _():
            load(0, h, k).wait()
            hop_a(0, h, k).wait()
            add_into(
                own.at[1 - y, h, rows(k)], own.at[1 - y, h, rows(k)], ra.at[1 - y, h, rows(k)]
            )
            hop_y(h, k).start()

        load(1, h, k).wait()
        hop_a(1, h, k).wait()
        fold(h, k, ra.at[y, h])

    def stage2(h, k):
        @pl.when(far)
        def _():
            hop_y(h, k).wait()
            fold(h, k, rb.at[h])

        @pl.when(z == 3)
        def _():
            hop_z(h, k).start()

    def stage3(h, k):
        @pl.when(z == 2)
        def _():
            hop_z(h, k).wait_recv()
            fold(h, k, rz.at[h])
            hop_z(h, k).start()

    def stage4(h, k):
        @pl.when(z == 1)
        def _():
            hop_z(h, k).wait_recv()
            fold(h, k, rz.at[h])
            if h == 0:
                hop_z(h, k).start()

    def stage5(h, k):
        if h == 0:

            @pl.when(z == 0)
            def _():
                hop_z(h, k).wait_recv()
                fold(h, k, rz.at[h])

    n = len(chunks)
    stages = (stage1, stage2, stage3, stage4, stage5)
    for i in range(max(n + 4, len(hooks) - 1)):
        for lag, stage in enumerate(stages):
            if 0 <= i - lag < n:
                stage(*chunks[i - lag])
        if i + 1 < len(hooks):
            for hook in hooks[i + 1]:
                hook()
    for h, k in chunks:

        @pl.when(z >= 2 if h else z >= 1)
        def _():
            hop_z(h, k).wait_send()

    load_chip.wait()
    hop_chip.wait()

    @pl.loop(0, CHUNKS)
    def _(k):
        r = pl.ds(pl.multiple_of(k * size, size), size)
        gsum[r] = keep[r].astype(F32) + take[r].astype(F32)

    @pl.when(z < 2)
    def _():
        place = jnp.minimum(z, 1)

        @pl.loop(0, CHUNKS)
        def _(k):
            r = pl.ds(pl.multiple_of(k * size, size), size)
            gsum[r] += own[y, place, r].astype(F32)

    cur[...] = sums[...]

    @pl.loop(0, CHUNKS)
    def _(k):
        r = pl.ds(pl.multiple_of(k * size, size), size)
        hidden = tokens[r].astype(F32) + vec[0:1]
        center = jnp.mean(hidden, axis=1, keepdims=True)
        offset = hidden - center
        factor = lax.rsqrt(jnp.mean(offset * offset, axis=1, keepdims=True) + eps)
        unit = offset * factor
        grad = gsum[r]
        scaled = grad * vec[1:2]
        first = jnp.mean(scaled, axis=1, keepdims=True)
        second = jnp.mean(scaled * unit, axis=1, keepdims=True)
        total = grad_h2[r] + factor * (scaled - first - unit * second)
        out[r] = total
        cur[0:1] += jnp.sum(total, axis=0, keepdims=True)
        cur[1:2] += jnp.sum(grad * unit, axis=0, keepdims=True)
        cur[2:3] += jnp.sum(grad, axis=0, keepdims=True)

    for i, target in enumerate((sib, over_y, over_x)):
        hop = send(cur, sb.at[i], sems, 33 + i, target)
        hop.start()
        hop.wait()
        cur[...] += sb[i]
    hops = [send(cur, sb.at[2 + s], sems, 35 + s, {"gr": z ^ s}) for s in (1, 2, 3)]
    for hop in hops:
        hop.start()
    for hop in hops:
        hop.wait()
    sums_out[...] = (cur[...] + sb[3]) + (sb[4] + sb[5])


def tail_exchange(part, chip, dw, grad_h2, tokens, vec, sums, collective_id):
    any_space = pl.BlockSpec(memory_space=pl.ANY)
    vmem = pl.BlockSpec(memory_space=pltpu.VMEM)
    return pl.pallas_call(
        tail_kernel,
        name="tail_exchange",
        in_specs=[any_space, any_space, any_space, vmem, vmem, vmem, vmem],
        out_specs=[vmem, vmem, vmem],
        out_shape=[
            jax.ShapeDtypeStruct((QROWS, D), F32),
            jax.ShapeDtypeStruct(sums.shape, F32),
            jax.ShapeDtypeStruct(dw.shape[2:], F32),
        ],
        scratch_shapes=[
            pltpu.VMEM((2, 2, QROWS, D), BF),
            pltpu.VMEM((2, 2, QROWS, D), BF),
            pltpu.VMEM((2, QROWS, D), BF),
            pltpu.VMEM((2, QROWS, D), BF),
            pltpu.VMEM((QROWS, D), BF),
            pltpu.VMEM((QROWS, D), BF),
            pltpu.VMEM((QROWS, D), F32),
            pltpu.VMEM(sums.shape, F32),
            pltpu.VMEM((6,) + sums.shape, F32),
        ]
        + rs_scratch(dw.shape[2], dw.shape[3], False)
        + [
            pltpu.SemaphoreType.DMA((39,)),
            pltpu.SemaphoreType.DMA((39,)),
            pltpu.SemaphoreType.DMA((17,)),
            pltpu.SemaphoreType.DMA((RS_SLOTS,)),
            pltpu.SemaphoreType.DMA((RS_SLOTS,)),
            pltpu.SemaphoreType.DMA((8,)),
        ],
        compiler_params=pltpu.CompilerParams(
            collective_id=collective_id, has_side_effects=True, vmem_limit_bytes=48 << 20
        ),
    )(part, chip, dw, grad_h2, tokens, vec, sums)


GELU_IN = math.sqrt(2.0 / math.pi)


def middle_kernel(
    mixed,
    w_out_g,
    w_up,
    w_down,
    tokens,
    teacher,
    vec,
    b_up,
    final_out,
    grad_h2,
    dw_up,
    dw_down,
    dw_out,
    gm,
    sums,
    wo,
    wu,
    wd,
    h2,
    n2,
    n2t,
    act,
    slope,
    gf,
    gb,
    gbt,
    acc,
    du,
    dd,
    l_sems,
    o_sems,
):
    loads_u = [pltpu.make_async_copy(w_up.at[b], wu.at[b], l_sems.at[b]) for b in range(4)]
    loads_d = [pltpu.make_async_copy(w_down.at[b], wd.at[b], l_sems.at[4 + b]) for b in range(4)]
    for b in range(4):
        loads_u[b].start()
        loads_d[b].start()
    for k in range(2):
        for i in range(2):
            for r in range(4):
                wo[k, 192 * i : 192 * i + 192, 192 * r : 192 * r + 192] = w_out_g[2 * i + k, r]

    @pl.loop(0, 2)
    def _(t):
        r = pl.ds(pl.multiple_of(t * 256, 256), 256)
        hidden = tokens[r].astype(F32) + vec[0:1]
        attended = nn(mixed[0, r], wo[0]) + nn(mixed[1, r], wo[1])
        total = hidden + attended + vec[3:4]
        h2[r] = total
        n2[r] = norm_rows(total, vec[4:5], vec[5:6]).astype(BF)

    n2t[...] = n2[...].T
    acc[...] = jnp.zeros_like(acc)
    for copy in loads_u + loads_d:
        copy.wait()

    @pl.loop(0, 4)
    def _(b):
        @pl.loop(0, 2)
        def _(t):
            r = pl.ds(pl.multiple_of(t * 256, 256), 256)
            pre = nn(n2[r], wu[b]) + b_up[b, 0:1]
            square = pre * pre
            tanh = jnp.tanh(GELU_IN * pre * (1.0 + 0.044715 * square))
            half = 0.5 * (1.0 + tanh)
            low = (pre * half).astype(BF)
            act[b, r] = low
            slope[b, r] = half + (0.5 * GELU_IN) * pre * (1.0 - tanh * tanh) * (
                1.0 + (3.0 * 0.044715) * square
            )
            acc[r] += nt(low, wd[b])

    sums[...] = jnp.zeros_like(sums)

    @pl.loop(0, 2)
    def _(t):
        r = pl.ds(pl.multiple_of(t * 256, 256), 256)
        final = h2[r] + acc[r] + vec[6:7]
        final_out[r] = final.astype(BF)
        diff = final - teacher[r].astype(F32)
        gf[r] = diff
        low = diff.astype(BF)
        gb[r] = low
        sums[6:7] += jnp.sum(low.astype(F32), axis=0, keepdims=True)
        sums[11:12] += jnp.sum(diff * diff, axis=0, keepdims=True)

    gbt[...] = gb[...].T
    acc[...] = jnp.zeros_like(acc)

    @pl.loop(0, 4)
    def _(b):
        dd[b] = nn(gbt[...], act[b]).astype(BF)
        pltpu.make_async_copy(dd.at[b], dw_down.at[b], o_sems.at[b]).start()

        @pl.loop(0, 2)
        def _(t):
            r = pl.ds(pl.multiple_of(t * 256, 256), 256)
            low = (nn(gb[r], wd[b]) * slope[b, r]).astype(BF)
            act[b, r] = low
            sums[pl.ds(7 + b, 1)] += jnp.sum(low.astype(F32), axis=0, keepdims=True)
            acc[r] += nt(low, wu[b])

        du[b] = nn(n2t[...], act[b]).astype(BF)
        pltpu.make_async_copy(du.at[b], dw_up.at[b], o_sems.at[4 + b]).start()

    @pl.loop(0, 2)
    def _(t):
        r = pl.ds(pl.multiple_of(t * 256, 256), 256)
        hidden = h2[r]
        center = jnp.mean(hidden, axis=1, keepdims=True)
        offset = hidden - center
        factor = lax.rsqrt(jnp.mean(offset * offset, axis=1, keepdims=True) + eps)
        unit = offset * factor
        grad = acc[r]
        scaled = grad * vec[4:5]
        first = jnp.mean(scaled, axis=1, keepdims=True)
        second = jnp.mean(scaled * unit, axis=1, keepdims=True)
        total = gf[r] + factor * (scaled - first - unit * second)
        grad_h2[r] = total
        low = total.astype(BF)
        gb[r] = low
        sums[3:4] += jnp.sum(grad * unit, axis=0, keepdims=True)
        sums[4:5] += jnp.sum(grad, axis=0, keepdims=True)
        sums[5:6] += jnp.sum(low.astype(F32), axis=0, keepdims=True)
        gm[0, r] = nt(low, wo[0]).astype(BF)
        gm[1, r] = nt(low, wo[1]).astype(BF)

    for k in range(2):
        whole = tn(mixed[k], gb[...]).astype(BF)
        for i in range(2):
            for r in range(4):
                dw_out[2 * i + k, r] = whole[192 * i : 192 * i + 192, 192 * r : 192 * r + 192]
    for b in range(4):
        pltpu.make_async_copy(dd.at[b], dw_down.at[b], o_sems.at[b]).wait()
        pltpu.make_async_copy(du.at[b], dw_up.at[b], o_sems.at[4 + b]).wait()


def middle(mixed, w_out_g, w_up, w_down, tokens, teacher, vec, b_up):
    any_space = pl.BlockSpec(memory_space=pl.ANY)
    vmem = pl.BlockSpec(memory_space=pltpu.VMEM)
    blocks = (4, D, D)
    return pl.pallas_call(
        middle_kernel,
        name="middle",
        in_specs=[vmem, vmem, any_space, any_space, vmem, vmem, vmem, vmem],
        out_specs=[vmem, vmem, any_space, any_space, vmem, vmem, vmem],
        out_shape=[
            jax.ShapeDtypeStruct((QROWS, D), BF),
            jax.ShapeDtypeStruct((QROWS, D), F32),
            jax.ShapeDtypeStruct(blocks, BF),
            jax.ShapeDtypeStruct(blocks, BF),
            jax.ShapeDtypeStruct((4, 4, 192, 192), BF),
            jax.ShapeDtypeStruct((2, QROWS, 384), BF),
            jax.ShapeDtypeStruct((16, D), F32),
        ],
        scratch_shapes=[
            pltpu.VMEM((2, 384, D), BF),
            pltpu.VMEM(blocks, BF),
            pltpu.VMEM(blocks, BF),
            pltpu.VMEM((QROWS, D), F32),
            pltpu.VMEM((QROWS, D), BF),
            pltpu.VMEM((D, QROWS), BF),
            pltpu.VMEM((4, QROWS, D), BF),
            pltpu.VMEM((4, QROWS, D), F32),
            pltpu.VMEM((QROWS, D), F32),
            pltpu.VMEM((QROWS, D), BF),
            pltpu.VMEM((D, QROWS), BF),
            pltpu.VMEM((QROWS, D), F32),
            pltpu.VMEM(blocks, BF),
            pltpu.VMEM(blocks, BF),
            pltpu.SemaphoreType.DMA((8,)),
            pltpu.SemaphoreType.DMA((8,)),
        ],
        compiler_params=pltpu.CompilerParams(vmem_limit_bytes=60 << 20),
    )(mixed, w_out_g, w_up, w_down, tokens, teacher, vec, b_up)


def norm(hidden, gain, shift):
    center = jnp.mean(hidden, axis=1, keepdims=True)
    offset = hidden - center
    factor = lax.rsqrt(jnp.mean(offset * offset, axis=1, keepdims=True) + eps)
    unit = offset * factor
    return unit * gain + shift, unit, factor


def norm_back(grad, gain, unit, factor):
    grad_unit = grad * gain
    first = jnp.mean(grad_unit, axis=1, keepdims=True)
    second = jnp.mean(grad_unit * unit, axis=1, keepdims=True)
    grad_in = factor * (grad_unit - first - unit * second)
    return grad_in, jnp.sum(grad * unit, axis=0), jnp.sum(grad, axis=0)


def head_layout(blocks):
    chunks = blocks.transpose(1, 0, 2).reshape(D, 6, 3, HD)
    q_list, kv_list = [], []
    for pair in range(3):
        a, b = 2 * pair, 2 * pair + 1
        q_list += [chunks[:, b, 0], chunks[:, a, 0]]
        kv_list += [chunks[:, a, 2], chunks[:, a, 1], chunks[:, b, 1], chunks[:, b, 2]]
    return jnp.concatenate(q_list, axis=1), jnp.concatenate(kv_list, axis=1)


def head_layout_back(grad_q, grad_kv):
    qc = grad_q.reshape(D, 3, 2, HD)
    kc = grad_kv.reshape(D, 3, 4, HD)
    pieces = []
    for pair in range(3):
        pieces += [qc[:, pair, 1], kc[:, pair, 1], kc[:, pair, 0]]
        pieces += [qc[:, pair, 0], kc[:, pair, 2], kc[:, pair, 3]]
    whole = jnp.concatenate(pieces, axis=1)
    return whole.reshape(D, 2, 576).transpose(1, 0, 2)


def on_device(
    tokens,
    teacher,
    pass_embed,
    ln1_gain,
    ln1_bias,
    qkv_weight,
    out_weight,
    out_bias,
    ln2_gain,
    ln2_bias,
    fc1_weight,
    fc1_bias,
    fc2_weight,
    fc2_bias,
    cont_group,
    token_count,
):
    n_dp = lax.axis_size("dp")
    n_gr = lax.axis_size("gr")
    n_gc = lax.axis_size("gc")
    z = lax.axis_index("gr")
    g = lax.axis_index("gc")
    c = g % 2
    y = g // 2
    swap_core = [(i, i ^ 1) for i in range(n_gc)]
    swap_y = [(i, i ^ 2) for i in range(n_gc)]

    packed = jnp.stack(
        [pass_embed, ln1_gain, ln1_bias, out_bias, ln2_gain, ln2_bias, fc2_bias, fc2_bias]
    ).astype(F32)
    if n_dp == 2:
        vec = lax.dynamic_update_slice(jnp.zeros((8, D), F32), packed, (0, z * packed.shape[1]))
        bup = jnp.broadcast_to(fc1_bias.astype(F32), (8, fc1_bias.shape[0]))
        own = jnp.broadcast_to(jnp.pad(cont_group, (0, 120)), (8, 128))
        (
            mixed,
            lse_rows,
            w_out,
            w_up,
            w_down,
            n1_prompt,
            n1_chip,
            q,
            kvo,
            kvp,
            w_q,
            w_kv,
            vectors,
            b_up,
            owners,
        ) = front(
            tokens, vec, bup, own, qkv_weight, [out_weight, fc1_weight, fc2_weight], 1
        )
        n1_chip = n1_chip.reshape(2 * QROWS, D)
        owners = owners[:, 0, :8]
    else:
        vectors = lax.all_gather(packed, "gr", axis=1, tiled=True)
        b_up = lax.all_gather(fc1_bias, "gc", axis=0, tiled=True).astype(F32)
        owners = lax.all_gather(cont_group, "gr", axis=0, tiled=True)
    embed, gain1, shift1, b_out, gain2, shift2, b_down = [vectors[i] for i in range(7)]
    owners = owners.reshape(4, 2, 4)
    mine = lax.dynamic_slice(owners, (2 * y, jnp.maximum(z - 2, 0), 0), (2, 1, 4)).reshape(8)
    own_groups = jnp.repeat(2 * y + jnp.arange(2), 4)
    grp = jnp.where(z < 2, own_groups, mine).astype(jnp.int32)
    z_arr = z.astype(jnp.int32).reshape(1)

    hidden = tokens.astype(F32) + embed
    normed1, unit1, factor1 = norm(hidden, gain1, shift1)
    n1 = normed1.astype(BF)

    if n_dp != 2:
        w_other = lax.ppermute(qkv_weight, "gc", swap_y)
        w_pair = jnp.where(
            y == 0, jnp.stack([qkv_weight, w_other]), jnp.stack([w_other, qkv_weight])
        )
        w_qkv = lax.all_gather(w_pair, "gr", axis=1, tiled=True)
        n1_other = lax.ppermute(n1, "gc", swap_core)
        n1_chip = jnp.where(
            c == 0, jnp.concatenate([n1, n1_other]), jnp.concatenate([n1_other, n1])
        )
        n1_col = lax.all_gather(n1, "gr", axis=0, tiled=True)[:P_SIZE]
        n1_prompt = lax.all_gather(n1_col, "gc", axis=0, tiled=True)
        w_q, w_kv = head_layout(w_qkv)
        kvp = nn(n1_prompt, w_kv).astype(BF)
        kvo = nn(n1_chip, w_kv).astype(BF)
        q = (nn(n1_chip, w_q) * 0.125).astype(BF)
        w_out = lax.all_gather(out_weight, ("gc", "gr"))
        w_up = lax.all_gather(fc1_weight, ("gc", "gr"))
        w_down = lax.all_gather(fc2_weight, ("gc", "gr"))
        mixed_heads, lse = attend(grp, z_arr, q, kvo, kvp)
        lse_rows = lse[:, ::64].reshape(8, CL, 3, 2).transpose(2, 0, 3, 1)
        halves = mixed_heads.reshape(2, QROWS, 384)
        keep = lax.dynamic_index_in_dim(halves, c, 0, keepdims=False)
        give = lax.dynamic_index_in_dim(halves, 1 - c, 0, keepdims=False)
        take = lax.ppermute(give, "gc", swap_core)
        mixed = jnp.where(c == 0, jnp.stack([keep, take]), jnp.stack([take, keep]))
    w_up = w_up.reshape(n_gc, D, FF // n_gc)
    w_down = w_down.reshape(n_gc, D, FF // n_gc)
    if n_dp == 2:
        final, grad_h2, grad_w_up, grad_w_down, grad_w_out, gm, later_sums = middle(
            mixed, w_out, w_up, w_down, tokens, teacher, vectors, b_up
        )
    else:
        w_out = w_out.reshape(2, 2, n_gr, 192, 192).transpose(1, 0, 3, 2, 4).reshape(2, 384, D)

        attended = lax.dot_general(
            mixed, w_out, (((0, 2), (0, 1)), ((), ())), preferred_element_type=F32
        )
        hidden2 = hidden + attended + b_out
        normed2, unit2, factor2 = norm(hidden2, gain2, shift2)
        n2 = normed2.astype(BF)
        pre = lax.dot_general(n2, w_up, (((1,), (1,)), ((), ())), preferred_element_type=F32)
        pre = pre.reshape(QROWS, FF) + b_up
        active, gelu_back = jax.vjp(partial(jax.nn.gelu, approximate=True), pre)
        act = active.astype(BF)
        act_blocks = act.reshape(QROWS, n_gc, FF // n_gc)
        final = (
            hidden2
            + lax.dot_general(
                act_blocks, w_down, (((1, 2), (0, 2)), ((), ())), preferred_element_type=F32
            )
            + b_down
        )
        grad_final = final - teacher.astype(F32)
        squared = jnp.sum(grad_final * grad_final, axis=0)
        gb = grad_final.astype(BF)
        grad_b_down = jnp.sum(gb, axis=0, dtype=F32)
        grad_active = lax.dot_general(
            gb, w_down, (((1,), (1,)), ((), ())), preferred_element_type=F32
        ).reshape(QROWS, FF)
        grad_w_down = jnp.einsum("td,tgf->gdf", gb, act_blocks, preferred_element_type=F32)
        (grad_pre,) = gelu_back(grad_active)
        gp = grad_pre.astype(BF)
        gp_blocks = gp.reshape(QROWS, n_gc, FF // n_gc)
        grad_b_up = jnp.sum(gp, axis=0, dtype=F32)
        grad_w_up = jnp.einsum("td,tgf->gdf", n2, gp_blocks, preferred_element_type=F32)
        grad_n2 = lax.dot_general(
            gp_blocks, w_up, (((1, 2), (0, 2)), ((), ())), preferred_element_type=F32
        )
        back2, grad_gain2, grad_shift2 = norm_back(grad_n2, gain2, unit2, factor2)
        grad_h2 = grad_final + back2
        ga = grad_h2.astype(BF)
        grad_b_out = jnp.sum(ga, axis=0, dtype=F32)
        grad_w_out = jnp.einsum("ctk,tn->ckn", mixed, ga, preferred_element_type=F32)
        gm = jnp.einsum("tn,ckn->ctk", ga, w_out, preferred_element_type=F32).astype(BF)
        grad_w_up = grad_w_up.astype(BF)
        grad_w_down = grad_w_down.astype(BF)
        grad_w_out = (
            grad_w_out.astype(BF)
            .reshape(2, 2, 192, n_gr, 192)
            .transpose(1, 0, 3, 2, 4)
            .reshape(n_gc, n_gr, 192, 192)
        )
    weight_grads = [
        grad_w_down.reshape(n_gc, n_gr, 192, 768),
        grad_w_up.reshape(n_gc, n_gr, 192, 768),
        grad_w_out,
    ]
    if n_dp == 2:
        dq, dkvo, dkv, out_w_down, out_w_up, out_w_out = attend_back_scatter(
            grp, q, lse_rows, kvo, kvp, gm, weight_grads, 3
        )
        part_prompt, part_chip, grad_qkv = fold_prompts(
            grp, dkv, dkvo, dq, n1_prompt, n1_chip, w_q, w_kv
        )
    else:
        gm_keep = lax.dynamic_index_in_dim(gm, c, 0, keepdims=False)
        gm_give = lax.dynamic_index_in_dim(gm, 1 - c, 0, keepdims=False)
        gm_take = lax.ppermute(gm_give, "gc", swap_core)
        gm_chip = jnp.where(c == 0, jnp.stack([gm_keep, gm_take]), jnp.stack([gm_take, gm_keep]))
        gm_chip = gm_chip.reshape(2 * QROWS, 384)

        def scatter16(blocks):
            part = lax.psum_scatter(
                blocks.reshape(n_gc * n_gr * blocks.shape[2], -1),
                ("gc", "gr"),
                scatter_dimension=0,
                tiled=True,
            )
            return lax.psum(part, "dp").astype(F32)

        out_w_down, out_w_up, out_w_out = [scatter16(grad) for grad in weight_grads]
        dq, dkvo, dkvp = attend_back(grp, z_arr, q, gm_chip, lse_rows, kvo, kvp)
        part_prompt = nt(dkvp, w_kv).astype(BF)

        part_chip = (nt(dq, w_q) + nt(dkvo, w_kv)).reshape(2, QROWS, D)
        grad_kv = tn(n1_prompt, dkvp) + tn(n1_chip, dkvo)
        grad_q = tn(n1_chip, dq)
        grad_qkv = head_layout_back(grad_q, grad_kv)

    if n_dp == 2:
        input_grad, sums, out_w_qkv = tail_exchange(
            part_prompt.reshape(4, 2, QROWS, D),
            part_chip.reshape(2, QROWS, D),
            grad_qkv.reshape(2, 4, 192, 576),
            grad_h2,
            tokens,
            vectors,
            later_sums,
            4,
        )
    else:
        later_sums = jnp.concatenate(
            [
                grad_gain2[None],
                grad_shift2[None],
                grad_b_out[None],
                grad_b_down[None],
                grad_b_up.reshape(4, D),
                squared[None],
                jnp.zeros((4, D), F32),
            ]
        )
        back_prompt = lax.psum_scatter(part_prompt, "gc", scatter_dimension=0, tiled=True)
        back_prompt = lax.psum_scatter(
            jnp.concatenate([back_prompt, jnp.zeros_like(back_prompt)]),
            "gr",
            scatter_dimension=0,
            tiled=True,
        ).astype(F32)
        part_keep = lax.dynamic_index_in_dim(part_chip, c, 0, keepdims=False)
        part_give = lax.dynamic_index_in_dim(part_chip, 1 - c, 0, keepdims=False)
        part_take = lax.ppermute(part_give.astype(BF), "gc", swap_core).astype(F32)
        grad_n1 = part_keep + part_take + back_prompt
        qkv_keep = lax.dynamic_index_in_dim(grad_qkv, y, 0, keepdims=False)
        qkv_give = lax.dynamic_index_in_dim(grad_qkv, 1 - y, 0, keepdims=False)
        qkv_take = lax.ppermute(qkv_give.astype(BF), "gc", swap_y).astype(F32)
        out_w_qkv = lax.psum_scatter(
            (qkv_keep + qkv_take).astype(BF), "gr", scatter_dimension=0, tiled=True
        )
        out_w_qkv = lax.psum(out_w_qkv, "dp").astype(F32)
        back1, grad_gain1, grad_shift1 = norm_back(grad_n1, gain1, unit1, factor1)
        input_grad = grad_h2 + back1
        first_sums = jnp.stack([jnp.sum(input_grad, axis=0), grad_gain1, grad_shift1])
        sums = lax.psum(jnp.concatenate([first_sums, later_sums]), ("dp", "gr", "gc"))
    sums = sums[:12].reshape(12 * D)
    loss = (jnp.sum(sums[11 * D :]) / (D * token_count[0].astype(F32))).reshape(1)
    rows = sums[: 7 * D].reshape(7, n_gr, D // n_gr)
    rows = lax.dynamic_index_in_dim(rows, z, 1, keepdims=False)
    up = lax.dynamic_index_in_dim(
        sums[7 * D : 7 * D + FF].reshape(n_gc, FF // n_gc), g, 0, keepdims=False
    )
    return (
        final.astype(BF),
        loss,
        input_grad,
        rows[0],
        rows[1],
        rows[2],
        out_w_qkv,
        out_w_out,
        rows[5],
        rows[3],
        rows[4],
        out_w_up,
        up,
        out_w_down,
        rows[6],
    )


def solution(mesh):
    rows = P(("dp", "gr", "gc"), None)
    in_specs = (
        rows,
        rows,
        P("gr"),
        P("gr"),
        P("gr"),
        P("gr", "gc"),
        P("gc", "gr"),
        P("gr"),
        P("gr"),
        P("gr"),
        P("gr", "gc"),
        P("gc"),
        P("gr", "gc"),
        P("gr"),
        P(("dp", "gr")),
        P(),
    )
    out_specs = (
        rows,
        P(),
        rows,
        P("gr"),
        P("gr"),
        P("gr"),
        P("gr", "gc"),
        P("gc", "gr"),
        P("gr"),
        P("gr"),
        P("gr"),
        P("gr", "gc"),
        P("gc"),
        P("gr", "gc"),
        P("gr"),
    )
    return jax.shard_map(
        on_device, mesh=mesh, in_specs=in_specs, out_specs=out_specs, check_vma=False
    )
```

```python
from functools import partial
import math

import jax
import jax.numpy as jnp
from jax import lax
from jax.experimental import pallas as pl
from jax.experimental.pallas import tpu as pltpu
from jax.sharding import PartitionSpec as P

D = 768
HD = 64
FF = 3072
P_SIZE = 1024
CL = 128
QROWS = 512
eps = 1e-05
negative = -1e30
BF = jnp.bfloat16
F32 = jnp.float32


def nt(a, b):
    return lax.dot_general(a, b, (((1,), (1,)), ((), ())), preferred_element_type=F32)


def nn(a, b):
    return lax.dot_general(a, b, (((1,), (0,)), ((), ())), preferred_element_type=F32)


def tn(a, b):
    return lax.dot_general(a, b, (((0,), (0,)), ((), ())), preferred_element_type=F32)


def att_fwd_kernel(grp_ref, z_ref, q_ref, kvo_ref, kvp_ref, o_ref, lse_ref):
    j = pl.program_id(1)
    row0 = pl.multiple_of(grp_ref[j] * P_SIZE, P_SIZE)
    z = z_ref[0]
    lane = lax.broadcasted_iota(jnp.int32, (CL, 128), 1)
    low = lane < 64
    zero = jnp.zeros((CL, 128), BF)
    q = q_ref[...]
    q_parts = (jnp.where(low, zero, q), jnp.where(low, q, zero))

    @pl.when(z >= 2)
    def _():
        row = lax.broadcasted_iota(jnp.int32, (CL, CL), 0)
        near_ok = lax.broadcasted_iota(jnp.int32, (CL, CL), 1) <= row
        mixes, sums = [], []
        for h in range(2):
            cols = slice(128 * h, 128 * h + 128)
            kv = kvp_ref[pl.ds(row0, P_SIZE), cols]
            kvo = kvo_ref[:, cols]
            far = nt(q_parts[h], kv)
            near = jnp.where(near_ok, nt(q_parts[h], kvo), negative)
            top = jnp.maximum(
                jnp.max(far, axis=1, keepdims=True), jnp.max(near, axis=1, keepdims=True)
            )
            far = jnp.exp(far - top)
            near = jnp.exp(near - top)
            total = jnp.sum(far, axis=1, keepdims=True) + jnp.sum(near, axis=1, keepdims=True)
            mix = nn(far.astype(BF), kv) + nn(near.astype(BF), kvo)
            mixes.append(mix / total)
            sums.append(jnp.broadcast_to(top + jnp.log(total), (CL, 128)))
        o_ref[...] = jnp.where(low, mixes[0], mixes[1]).astype(BF)
        lse_ref[...] = jnp.where(low, sums[0], sums[1])

    @pl.when(z < 2)
    def _():
        limit = z * QROWS + (j % (QROWS // CL)) * CL
        row = lax.broadcasted_iota(jnp.int32, (CL, P_SIZE), 0)
        key = lax.broadcasted_iota(jnp.int32, (CL, P_SIZE), 1)
        allowed = key - row <= limit
        mixes, sums = [], []
        for h in range(2):
            cols = slice(128 * h, 128 * h + 128)
            kv = kvp_ref[pl.ds(row0, P_SIZE), cols]
            far = jnp.where(allowed, nt(q_parts[h], kv), negative)
            top = jnp.max(far, axis=1, keepdims=True)
            far = jnp.exp(far - top)
            total = jnp.sum(far, axis=1, keepdims=True)
            mix = nn(far.astype(BF), kv)
            mixes.append(mix / total)
            sums.append(jnp.broadcast_to(top + jnp.log(total), (CL, 128)))
        o_ref[...] = jnp.where(low, mixes[0], mixes[1]).astype(BF)
        lse_ref[...] = jnp.where(low, sums[0], sums[1])


def attend(grp, z, q, kvo, kvp):
    rows = q.shape[0]
    pairs = q.shape[1] // 128
    groups_rows = kvp.shape[0]
    return pl.pallas_call(
        att_fwd_kernel,
        name="att_fwd",
        grid_spec=pltpu.PrefetchScalarGridSpec(
            num_scalar_prefetch=2,
            grid=(pairs, rows // CL),
            in_specs=[
                pl.BlockSpec((CL, 128), lambda p, j, *_: (j, p)),
                pl.BlockSpec((CL, 256), lambda p, j, *_: (j, p)),
                pl.BlockSpec((groups_rows, 256), lambda p, j, *_: (0, p)),
            ],
            out_specs=[
                pl.BlockSpec((CL, 128), lambda p, j, *_: (j, p)),
                pl.BlockSpec((CL, 128), lambda p, j, *_: (j, p)),
            ],
        ),
        out_shape=[
            jax.ShapeDtypeStruct((rows, pairs * 128), BF),
            jax.ShapeDtypeStruct((rows, pairs * 128), F32),
        ],
        compiler_params=pltpu.CompilerParams(vmem_limit_bytes=40 << 20),
        cost_estimate=pl.CostEstimate(
            flops=4 * rows * P_SIZE * 128 * pairs * 2,
            bytes_accessed=groups_rows * 512 * pairs,
            transcendentals=rows * P_SIZE * pairs * 2,
        ),
    )(grp, z, q, kvo, kvp)


def att_bwd_kernel(
    grp_ref, z_ref, q_ref, gm_ref, lse_ref, kvo_ref, kvp_ref, dq_ref, dkvo_ref, dkvp_ref, acc
):
    j = pl.program_id(1)
    row0 = pl.multiple_of(grp_ref[j] * P_SIZE, P_SIZE)
    z = z_ref[0]
    low = lax.broadcasted_iota(jnp.int32, (CL, 128), 1) < 64
    zero = jnp.zeros((CL, 128), BF)
    q = q_ref[...]
    gm = gm_ref[...]
    stacks = (
        jnp.concatenate([jnp.where(low, zero, q), jnp.where(low, gm, zero)], axis=0),
        jnp.concatenate([jnp.where(low, q, zero), jnp.where(low, zero, gm)], axis=0),
    )

    @pl.when(j == 0)
    def _():
        acc[...] = jnp.zeros_like(acc)

    @pl.when(z >= 2)
    def _():
        row = lax.broadcasted_iota(jnp.int32, (CL, CL), 0)
        near_ok = row <= lax.broadcasted_iota(jnp.int32, (CL, CL), 1)
        dqs = []
        for h in range(2):
            cols = slice(128 * h, 128 * h + 128)
            kv = kvp_ref[pl.ds(row0, P_SIZE), cols]
            kvo = kvo_ref[:, cols]
            lse = lse_ref[0, 0, h : h + 1, :]
            far = nt(kv, stacks[h])
            near = nt(kvo, stacks[h])
            pf = jnp.exp(far[:, :CL] - lse)
            pn = jnp.where(near_ok, jnp.exp(near[:, :CL] - lse), 0.0)
            df = far[:, CL:]
            dn = near[:, CL:]
            inner = jnp.sum(pf * df, axis=0, keepdims=True) + jnp.sum(
                pn * dn, axis=0, keepdims=True
            )
            sf = (pf * (df - inner)).astype(BF)
            sn = (pn * (dn - inner)).astype(BF)
            acc[pl.ds(row0, P_SIZE), cols] += nn(
                jnp.concatenate([sf, pf.astype(BF)], axis=1), stacks[h]
            )
            dkvo_ref[:, cols] = nn(
                jnp.concatenate([sn, pn.astype(BF)], axis=1), stacks[h]
            ).astype(BF)
            dqs.append(tn(sf, kv) + tn(sn, kvo))
        dq_ref[...] = (jnp.where(low, dqs[1], dqs[0]) * 0.125).astype(BF)

    @pl.when(z < 2)
    def _():
        limit = z * QROWS + (j % (QROWS // CL)) * CL
        key = lax.broadcasted_iota(jnp.int32, (P_SIZE, CL), 0)
        row = lax.broadcasted_iota(jnp.int32, (P_SIZE, CL), 1)
        allowed = key - row <= limit
        dqs = []
        for h in range(2):
            cols = slice(128 * h, 128 * h + 128)
            kv = kvp_ref[pl.ds(row0, P_SIZE), cols]
            lse = lse_ref[0, 0, h : h + 1, :]
            far = nt(kv, stacks[h])
            pf = jnp.where(allowed, jnp.exp(far[:, :CL] - lse), 0.0)
            df = far[:, CL:]
            inner = jnp.sum(pf * df, axis=0, keepdims=True)
            sf = (pf * (df - inner)).astype(BF)
            acc[pl.ds(row0, P_SIZE), cols] += nn(
                jnp.concatenate([sf, pf.astype(BF)], axis=1), stacks[h]
            )
            dqs.append(tn(sf, kv))
        dkvo_ref[...] = jnp.zeros_like(dkvo_ref)
        dq_ref[...] = (jnp.where(low, dqs[1], dqs[0]) * 0.125).astype(BF)

    @pl.when(j == pl.num_programs(1) - 1)
    def _():
        dkvp_ref[...] = acc[...].astype(BF)


def attend_back(grp, z, q, gm, lse, kvo, kvp):
    rows = q.shape[0]
    pairs = q.shape[1] // 128
    groups_rows = kvp.shape[0]
    return pl.pallas_call(
        att_bwd_kernel,
        name="att_bwd",
        grid_spec=pltpu.PrefetchScalarGridSpec(
            num_scalar_prefetch=2,
            grid=(pairs, rows // CL),
            in_specs=[
                pl.BlockSpec((CL, 128), lambda p, j, *_: (j, p)),
                pl.BlockSpec((CL, 128), lambda p, j, *_: (j, p)),
                pl.BlockSpec((1, 1, 2, 128), lambda p, j, *_: (p, j, 0, 0)),
                pl.BlockSpec((CL, 256), lambda p, j, *_: (j, p)),
                pl.BlockSpec((groups_rows, 256), lambda p, j, *_: (0, p)),
            ],
            out_specs=[
                pl.BlockSpec((CL, 128), lambda p, j, *_: (j, p)),
                pl.BlockSpec((CL, 256), lambda p, j, *_: (j, p)),
                pl.BlockSpec((groups_rows, 256), lambda p, j, *_: (0, p)),
            ],
            scratch_shapes=[pltpu.VMEM((groups_rows, 256), F32)],
        ),
        out_shape=[
            jax.ShapeDtypeStruct((rows, pairs * 128), BF),
            jax.ShapeDtypeStruct((rows, pairs * 256), BF),
            jax.ShapeDtypeStruct((groups_rows, pairs * 256), BF),
        ],
        compiler_params=pltpu.CompilerParams(vmem_limit_bytes=48 << 20),
        cost_estimate=pl.CostEstimate(
            flops=10 * rows * P_SIZE * 128 * pairs * 2,
            bytes_accessed=groups_rows * 1024 * pairs,
            transcendentals=rows * P_SIZE * pairs * 2,
        ),
    )(grp, z, q, gm, lse, kvo, kvp)


MESH = pl.DeviceIdType.MESH


def places():
    x = lax.axis_index("dp")
    z = lax.axis_index("gr")
    g = lax.axis_index("gc")
    return x, z, g, g // 2, g % 2


def greet(partners):
    barrier = pltpu.get_barrier_semaphore()
    for partner in partners:
        pl.semaphore_signal(barrier, inc=1, device_id=partner, device_id_type=MESH)
    pl.semaphore_wait(barrier, len(partners))


def all_partners():
    x, z, g, y, c = places()
    by_z = [{"gr": z ^ step} for step in (1, 2, 3)]
    return [{"gc": g ^ 1}, {"gc": g ^ 2}, {"dp": x ^ 1}] + by_z


def send(src, dst, sems, slot, target, send_slot=None):
    return pltpu.make_async_remote_copy(
        src_ref=src,
        dst_ref=dst,
        send_sem=sems[0].at[slot if send_slot is None else send_slot],
        recv_sem=sems[1].at[slot],
        device_id=target,
        device_id_type=MESH,
    )


def add_into(dst, left, right):
    dst[...] = (left[...].astype(F32) + right[...].astype(F32)).astype(dst.dtype)


RS_SLOTS = 28
RS_ORDER = (3, 2, 1, 0)


def rs_plan(grads, outs, bufs, sems, l_sems, base, paired):
    own, ra, rb0, rb1, rc0, rc1, sc, rd, re = bufs
    x, z, g, y, c = places()
    sib, over_y, over_x = {"gc": g ^ 1}, {"gc": g ^ 2}, {"dp": x ^ 1}
    rows = grads.shape[2]
    q = rows // 4
    mine0 = pl.ds(pl.multiple_of(q * x, 16), q)
    other0 = pl.ds(pl.multiple_of(q * (1 - x), 16), q)
    mine1 = pl.ds(pl.multiple_of(2 * q + q * x, 16), q)
    other1 = pl.ds(pl.multiple_of(2 * q + q * (1 - x), 16), q)
    first = pl.ds(0, 2 * q)
    slot = base * RS_SLOTS

    def load(i, s):
        source = grads.at[2 * i + c, z ^ s] if paired else grads.at[i, z ^ s]
        return pltpu.make_async_copy(source, own.at[i, s], l_sems.at[8 * base + 2 * s + i])

    def hop_a(i, s):
        return send(grads.at[2 * i + 1 - c, z ^ s], ra.at[i, s], sems, slot + 6 * s + i, sib)

    def hop_b0(s):
        return send(own.at[1 - y, s, first], rb0.at[s], sems, slot + 6 * s + 2, over_y)

    def hop_b1(s):
        return send(own.at[:, s, other1], rb1.at[s], sems, slot + 6 * s + 3, over_x)

    def hop_c0(s):
        return send(own.at[y, s, other0], rc0.at[s], sems, slot + 6 * s + 4, over_x)

    def hop_c1(s):
        return send(own.at[1 - y, s, mine1], rc1.at[s], sems, slot + 6 * s + 5, over_y)

    def hop_z(s):
        return send(sc.at[s], rd.at[s - 1], sems, slot + 23 + s, {"gr": z ^ s})

    def hop_d():
        return send(sc.at[0], re, sems, slot + 27, over_x)

    def begin(s):
        for i in range(2):
            load(i, s).start()
            if paired:
                hop_a(i, s).start()

    def after_a(s):
        for i in range(2):
            load(i, s).wait()
            if paired:
                hop_a(i, s).wait()
                add_into(own.at[i, s], own.at[i, s], ra.at[i, s])
        hop_b0(s).start()
        hop_b1(s).start()

    def after_b(s):
        hop_b0(s).wait()
        hop_b1(s).wait()
        add_into(own.at[y, s, first], own.at[y, s, first], rb0.at[s])
        for i in range(2):
            add_into(own.at[i, s, mine1], own.at[i, s, mine1], rb1.at[s, i])
        hop_c0(s).start()
        hop_c1(s).start()

    def after_c(s):
        hop_c0(s).wait()
        hop_c1(s).wait()
        add_into(sc.at[s, pl.ds(0, q)], own.at[y, s, mine0], rc0.at[s])
        add_into(sc.at[s, pl.ds(q, q)], own.at[y, s, mine1], rc1.at[s])
        if s:
            hop_z(s).start()

    def total():
        for s in (1, 2, 3):
            hop_z(s).wait()
        whole = sc[0].astype(F32)
        for i in range(3):
            whole = whole + rd[i].astype(F32)
        sc[0] = whole.astype(BF)
        hop_d().start()

    def finish():
        hop_d().wait()
        outs[mine0] = sc[0, pl.ds(0, q)].astype(F32)
        outs[mine1] = sc[0, pl.ds(q, q)].astype(F32)
        outs[other0] = re[pl.ds(0, q)].astype(F32)
        outs[other1] = re[pl.ds(q, q)].astype(F32)

    return begin, after_a, after_b, after_c, total, finish


def rs_steps(plans):
    order = [(plan, s) for plan in plans for s in RS_ORDER]
    n = len(order)
    steps = [[partial(plan[0], s) for plan, s in order]]
    for i in range(n + 10):
        part = []
        if i < n:
            part.append(partial(order[i][0][1], order[i][1]))
        if 2 <= i < n + 2:
            part.append(partial(order[i - 2][0][2], order[i - 2][1]))
        if 4 <= i < n + 4:
            part.append(partial(order[i - 4][0][3], order[i - 4][1]))
        if 7 <= i < n + 7 and (i - 7) % 4 == 3:
            part.append(plans[(i - 7) // 4][4])
        if 9 <= i < n + 9 and (i - 9) % 4 == 3:
            part.append(plans[(i - 9) // 4][5])
        if part:
            steps.append(part)
    return steps


def rs_scratch(rows, cols, paired):
    q = rows // 4
    return [
        pltpu.VMEM((2, 4, rows, cols), BF),
        pltpu.VMEM((2, 4, rows, cols) if paired else (16, 128), BF),
        pltpu.VMEM((4, 2 * q, cols), BF),
        pltpu.VMEM((4, 2, q, cols), BF),
        pltpu.VMEM((4, q, cols), BF),
        pltpu.VMEM((4, q, cols), BF),
        pltpu.VMEM((4, 2 * q, cols), BF),
        pltpu.VMEM((3, 2 * q, cols), BF),
        pltpu.VMEM((2 * q, cols), BF),
    ]


def att_scatter_kernel(count, grp_ref, q_ref, lse_ref, kvo_ref, kvp_ref, gm, *refs):
    grads = refs[:count]
    dq_ref, dkvo_ref, dkv_ref = refs[count : count + 3]
    outs = refs[count + 3 : 2 * count + 3]
    rest = refs[2 * count + 3 :]
    bufs, (gmx, sem_s, sem_r, l_sems, m_send, m_recv, m_local) = rest[: 9 * count], rest[9 * count :]
    p, j = pl.program_id(0), pl.program_id(1)
    step = p * pl.num_programs(1) + j
    x, z, g, y, c = places()
    hooks = rs_steps(
        [
            rs_plan(grads[k], outs[k], bufs[9 * k : 9 * k + 9], (sem_s, sem_r), l_sems, k, True)
            for k in range(count)
        ]
    )

    def exchange(i):
        cols = pl.ds(128 * i, 128)
        return (
            pltpu.make_async_copy(gm.at[c, :, cols], gmx.at[i, c], m_local.at[i]),
            send(gm.at[1 - c, :, cols], gmx.at[i, c], (m_send, m_recv), i, {"gc": g ^ 1}),
        )

    @pl.when(step == 0)
    def _():
        greet(all_partners())
        for i in range(3):
            for copy in exchange(i):
                copy.start()
        for hook in hooks[0]:
            hook()
        for copy in exchange(0):
            copy.wait()

    for i in (1, 2):

        @pl.when(step == 8 * i)
        def _():
            for copy in exchange(i):
                copy.wait()

    last = len(hooks) - 1
    for when in range(1, 23):
        parts = [h for i in range(1, last) if i * 22 // (last - 1) == when for h in hooks[i]]
        if parts:

            @pl.when(step == when)
            def _():
                for hook in parts:
                    hook()

    group = grp_ref[j]
    low = lax.broadcasted_iota(jnp.int32, (CL, 128), 1) < 64
    zero = jnp.zeros((CL, 128), BF)
    q = q_ref[0]
    gmix = gmx[p, j // 4, pl.ds(pl.multiple_of((j % 4) * CL, CL), CL)]
    stacks = (
        jnp.concatenate([jnp.where(low, zero, q), jnp.where(low, gmix, zero)], axis=0),
        jnp.concatenate([jnp.where(low, q, zero), jnp.where(low, zero, gmix)], axis=0),
    )

    @pl.when(z >= 2)
    def _():
        row = lax.broadcasted_iota(jnp.int32, (CL, CL), 0)
        near_ok = row <= lax.broadcasted_iota(jnp.int32, (CL, CL), 1)
        dqs = []
        for h in range(2):
            cols = slice(128 * h, 128 * h + 128)
            kv = kvp_ref[0, group, :, cols]
            kvo = kvo_ref[0, :, cols]
            lse = lse_ref[0, 0, h : h + 1, :]
            far = nt(kv, stacks[h])
            near = nt(kvo, stacks[h])
            pf = jnp.exp(far[:, :CL] - lse)
            pn = jnp.where(near_ok, jnp.exp(near[:, :CL] - lse), 0.0)
            df = far[:, CL:]
            dn = near[:, CL:]
            inner = jnp.sum(pf * df, axis=0, keepdims=True) + jnp.sum(
                pn * dn, axis=0, keepdims=True
            )
            sf = (pf * (df - inner)).astype(BF)
            sn = (pn * (dn - inner)).astype(BF)
            dkv_ref[0, :, cols] = nn(
                jnp.concatenate([sf, pf.astype(BF)], axis=1), stacks[h]
            ).astype(BF)
            dkvo_ref[:, cols] = nn(
                jnp.concatenate([sn, pn.astype(BF)], axis=1), stacks[h]
            ).astype(BF)
            dqs.append(tn(sf, kv) + tn(sn, kvo))
        dq_ref[...] = (jnp.where(low, dqs[1], dqs[0]) * 0.125).astype(BF)

    @pl.when(z < 2)
    def _():
        limit = z * QROWS + (j % (QROWS // CL)) * CL
        key = lax.broadcasted_iota(jnp.int32, (P_SIZE, CL), 0)
        row = lax.broadcasted_iota(jnp.int32, (P_SIZE, CL), 1)
        allowed = key - row <= limit
        dqs = []
        for h in range(2):
            cols = slice(128 * h, 128 * h + 128)
            kv = kvp_ref[0, group, :, cols]
            lse = lse_ref[0, 0, h : h + 1, :]
            far = nt(kv, stacks[h])
            pf = jnp.where(allowed, jnp.exp(far[:, :CL] - lse), 0.0)
            df = far[:, CL:]
            inner = jnp.sum(pf * df, axis=0, keepdims=True)
            sf = (pf * (df - inner)).astype(BF)
            dkv_ref[0, :, cols] = nn(
                jnp.concatenate([sf, pf.astype(BF)], axis=1), stacks[h]
            ).astype(BF)
            dqs.append(tn(sf, kv))
        dkvo_ref[...] = jnp.zeros_like(dkvo_ref)
        dq_ref[...] = (jnp.where(low, dqs[1], dqs[0]) * 0.125).astype(BF)

    @pl.when(step == 23)
    def _():
        for hook in hooks[last]:
            hook()


def attend_back_scatter(grp, q, lse, kvo, kvp, gm, grads, collective_id):
    rows = q.shape[1]
    count = len(grads)
    any_space = pl.BlockSpec(memory_space=pl.ANY)
    scratch = []
    for grad in grads:
        scratch += rs_scratch(grad.shape[2], grad.shape[3], True)
    slots = RS_SLOTS * count
    return pl.pallas_call(
        partial(att_scatter_kernel, count),
        name="attend_back_scatter",
        grid_spec=pltpu.PrefetchScalarGridSpec(
            num_scalar_prefetch=1,
            grid=(3, rows // CL),
            in_specs=[
                pl.BlockSpec((1, CL, 128), lambda p, j, *_: (p, j, 0)),
                pl.BlockSpec((1, 1, 2, 128), lambda p, j, *_: (p, j, 0, 0)),
                pl.BlockSpec((1, CL, 256), lambda p, j, *_: (p, j, 0)),
                pl.BlockSpec((1, 4, P_SIZE, 256), lambda p, j, *_: (p, 0, 0, 0)),
            ]
            + [any_space] * (count + 1),
            out_specs=[
                pl.BlockSpec((CL, 128), lambda p, j, *_: (j, p)),
                pl.BlockSpec((CL, 256), lambda p, j, *_: (j, p)),
                pl.BlockSpec((1, P_SIZE, 256), lambda p, j, *_: (j, 0, p)),
            ]
            + [pl.BlockSpec(grad.shape[2:], lambda p, j, *_: (0, 0)) for grad in grads],
            scratch_shapes=scratch
            + [
                pltpu.VMEM((3, 2, QROWS, 128), BF),
                pltpu.SemaphoreType.DMA((slots,)),
                pltpu.SemaphoreType.DMA((slots,)),
                pltpu.SemaphoreType.DMA((8 * count,)),
                pltpu.SemaphoreType.DMA((3,)),
                pltpu.SemaphoreType.DMA((3,)),
                pltpu.SemaphoreType.DMA((3,)),
            ],
        ),
        out_shape=[
            jax.ShapeDtypeStruct((rows, 384), BF),
            jax.ShapeDtypeStruct((rows, 768), BF),
            jax.ShapeDtypeStruct((8, P_SIZE, 768), BF),
        ]
        + [jax.ShapeDtypeStruct(grad.shape[2:], F32) for grad in grads],
        compiler_params=pltpu.CompilerParams(
            collective_id=collective_id, has_side_effects=True, vmem_limit_bytes=56 << 20
        ),
    )(grp, q, lse, kvo, kvp, gm, *grads)


def norm_rows(hidden, gain, shift):
    center = jnp.mean(hidden, axis=1, keepdims=True)
    offset = hidden - center
    factor = lax.rsqrt(jnp.mean(offset * offset, axis=1, keepdims=True) + eps)
    return offset * factor * gain + shift


CHUNKS = 4
FRONT = 13
GATHER_SLOTS = 40
SEGMENT = 4


def front_kernel(
    tokens,
    vec,
    bup,
    own,
    wq,
    block0,
    block1,
    block2,
    mixed,
    lse_ref,
    whole0,
    whole1,
    whole2,
    prompts_out,
    chip_out,
    q_out,
    kvo_out,
    kvp_out,
    wq_out,
    wkv_out,
    vec_out,
    bup_out,
    own_out,
    n1,
    vec_in,
    prompts,
    chip,
    wpair,
    q_all,
    kvo_all,
    kvp_all,
    mix,
    own_scalar,
    zs,
    zr,
    ys,
    yr,
    ds,
    dr,
    ws,
    wr,
    ss,
    sr,
    gs,
    gr_,
    ms,
    mr,
    l_sems,
    o_sems,
):
    x, z, g, y, c = places()
    sib, over_y, over_x = {"gc": g ^ 1}, {"gc": g ^ 2}, {"dp": x ^ 1}
    z_sems, y_sems, d_sems, w_sems, s_sems, g_sems = (
        (zs, zr),
        (ys, yr),
        (ds, dr),
        (ws, wr),
        (ss, sr),
        (gs, gr_),
    )
    blocks, wholes = (block0, block1, block2), (whole0, whole1, whole2)
    half_rows = wq.shape[0] // 2
    my_half = pl.ds(pl.multiple_of(x * half_rows, 16), half_rows)
    size = QROWS // CHUNKS
    first_half = jnp.where(z == 0, 0, 1)
    order = (z, z ^ 1, jnp.where(z < 2, 2, 1), jnp.where(z < 2, 3, 0))
    above, below = {"gr": jnp.minimum(z + 1, 3)}, {"gr": jnp.maximum(z - 1, 0)}
    inner = jnp.logical_and(z > 0, z < 3)

    def line(part, sems, base, b):
        return (
            (jnp.logical_and(z < 3, b <= z), send(part, part, sems, base + b, above)),
            (
                jnp.logical_and(z > 0, b >= z),
                send(part, part, sems, base + b, below, base + 4 + b),
            ),
        )

    def pass_on(copies):
        for goes, copy in copies:
            pl.when(goes)(copy.start)

    def passed_on(copies):
        for goes, copy in copies:
            pl.when(goes)(copy.wait_send)

    local_copy = pltpu.make_async_copy

    def small(kind, s):
        if kind == 0:
            return send(vec, vec_in.at[s], s_sems, s, {"gr": z ^ s})
        if kind == 1:
            return send(own, own_out.at[z], s_sems, 3 + s, {"gr": z ^ s})
        return send(bup, bup_out.at[g], s_sems, 6 + s, {"gc": g ^ s})

    def chip_send():
        return send(n1, chip.at[c], s_sems, 10, sib)

    def w_local():
        return local_copy(wq.at[my_half], wpair.at[y, z, my_half], l_sems.at[0])

    def w_line(s):
        return line(wpair.at[y, order[s], my_half], w_sems, 0, order[s])

    def w_gc(s):
        piece = wpair.at[y, order[s], my_half]
        return send(piece, piece, w_sems, 8 + s, over_y)

    def w_dp(s):
        piece = wpair.at[y, order[s], my_half]
        return send(piece, piece, w_sems, 12 + s, over_x)

    def w_dp_far(s):
        piece = wpair.at[1 - y, order[s], my_half]
        return send(piece, piece, w_sems, 16 + s, over_x)

    def chunk(number):
        return (first_half if number < CHUNKS else 1 - first_half), number % CHUNKS

    def item(column, number):
        half, k = chunk(number)
        return prompts.at[column, half, pl.ds(k * size, size)]

    def up(number):
        half, k = chunk(number)
        ref = item(g, number)
        return send(ref, ref, z_sems, half * CHUNKS + k, {"gr": jnp.minimum(z + 1, 3)})

    def down(number):
        half, k = chunk(number)
        ref = item(g, number)
        return send(
            ref,
            ref,
            z_sems,
            half * CHUNKS + k,
            {"gr": jnp.maximum(z - 1, 0)},
            2 * CHUNKS + k,
        )

    def side(number):
        half, k = chunk(number)
        ref = item(g, number)
        return send(ref, ref, y_sems, half * CHUNKS + k, over_y)

    def core(number, far):
        half, k = chunk(number)
        ref = item(g ^ 2 if far else g, number)
        return send(ref, ref, d_sems, far * 2 * CHUNKS + half * CHUNKS + k, sib)

    def goes_up(number):
        return jnp.logical_and(z < 3, chunk(number)[0] <= z)

    def goes_down(number):
        return jnp.logical_and(z == 1, chunk(number)[0] == 1)

    def forward(number):
        @pl.when(chunk(number)[0] != z)
        def _():
            up(number).wait_recv()

        @pl.when(goes_up(number))
        def _():
            up(number).start()

        @pl.when(goes_down(number))
        def _():
            down(number).start()

        side(number).start()
        core(number, 0).start()

    def across(number):
        side(number).wait_recv()
        core(number, 1).start()

    def plan(a, s):
        block, whole = blocks[a], wholes[a]
        q = block.shape[0] // 4
        half = pl.ds(pl.multiple_of(x * 2 * q, 16), 2 * q)
        qa = pl.ds(pl.multiple_of(x * 2 * q, 16), q)
        qb = pl.ds(pl.multiple_of(x * 2 * q + q, 16), q)
        qc = pl.ds(pl.multiple_of((1 - x) * 2 * q + q, 16), q)
        base = a * GATHER_SLOTS
        mine, far = whole.at[g, order[s]], whole.at[g ^ 2, order[s]]
        o = base + 8 + 8 * s

        def same(part, number, target):
            return lambda: send(part, part, g_sems, o + number, target)

        return {
            "line": lambda: line(mine.at[half], g_sems, base, order[s]),
            "ay": same(mine.at[qa], 0, over_y),
            "ax": same(mine.at[qa], 1, over_x),
            "afx": same(far.at[qa], 2, over_x),
            "bx": same(mine.at[qb], 3, over_x),
            "by": same(mine.at[qb], 4, over_y),
            "bfy": same(mine.at[qc], 5, over_y),
            "bfx": same(far.at[qb], 5, over_x),
            "c1": same(mine, 6, sib),
            "c2": same(far, 7, sib),
        }

    def own_block(a):
        return local_copy(blocks[a], wholes[a].at[g, z], l_sems.at[4 + a])

    def names(s):
        return ("ay", "ax", "afx", "bx", "by", "bfy") if s else ("ay", "afx", "by", "bfx")

    def relay(s):
        @pl.when(inner)
        def _():
            for a in range(3):
                copies = plan(a, s)["line"]()
                copies[0][1].wait_recv()
                pass_on(copies)


    def gather_first(s):
        for a in range(3):
            m = plan(a, s)
            if s:
                pl.when(jnp.logical_not(inner))(m["line"]()[0][1].wait_recv)
                m["bx"]().start()
                m["ax"]().start()
            m["ay"]().start()
            m["by"]().start()

    def gather_second(s):
        for a in range(3):
            m = plan(a, s)
            m["ay"]().wait_recv()
            m["afx"]().start()
            if s:
                m["bx"]().wait_recv()
                m["bfy"]().start()
            else:
                m["by"]().wait_recv()
                m["bfx"]().start()

    def gather_third(s):
        for a in range(3):
            m = plan(a, s)
            for name in ("ax", "afx", "by", "bfy") if s else ("afx", "bfx"):
                m[name]().wait_recv()
            m["c1"]().start()
            m["c2"]().start()

    def out_copies():
        return [
            local_copy(prompts, prompts_out, o_sems.at[0]),
            local_copy(chip, chip_out, o_sems.at[1]),
            local_copy(q_all, q_out, o_sems.at[2]),
            local_copy(kvo_all, kvo_out, o_sems.at[3]),
            local_copy(kvp_all, kvp_out, o_sems.at[4]),
        ]

    def exchange(i):
        cols = pl.ds(128 * i, 128)
        return (
            local_copy(mix.at[i, c], mixed.at[c, :, cols], l_sems.at[7 + i]),
            send(mix.at[i, 1 - c], mixed.at[c, :, cols], (ms, mr), i, sib),
        )

    hooks = {i: [] for i in range(FRONT)}

    def begin():
        greet(all_partners() + [{"gc": g ^ 3}])
        w_local().start()
        for s in (1, 2, 3):
            for kind in range(3):
                small(kind, s).start()
        w_local().wait()
        pass_on(w_line(0))
        own_out[z] = own[...]
        bup_out[g] = bup[...]
        for s in (1, 2, 3):
            small(0, s).wait_recv()
        vec_out[...] = (vec[...] + vec_in[1]) + (vec_in[2] + vec_in[3])

        @pl.loop(0, CHUNKS)
        def _(i):
            rows = pl.ds(pl.multiple_of(i * size, size), size)
            hidden = tokens[rows].astype(F32) + vec_out[0:1]
            n1[rows] = norm_rows(hidden, vec_out[1:2], vec_out[2:3]).astype(BF)

        @pl.when(z < 2)
        def _():
            to = local_copy(n1, prompts.at[g, jnp.minimum(z, 1)], l_sems.at[2])
            to.start()
            to.wait()

    def begin_chip():
        local_copy(n1, chip.at[c], l_sems.at[1]).start()
        chip_send().start()
        w_gc(0).start()
        w_dp(0).start()

    hooks[0] += [begin, partial(forward, 0), begin_chip]
    for i in range(1, 8):
        hooks[i].append(partial(forward, i))
    for i in range(2, 10):
        hooks[i].append(partial(across, i - 2))

    def w_pass(s):
        copies = w_line(s)
        copies[0][1].wait_recv()
        pass_on(copies)
        w_gc(s).start()
        w_dp(s).start()

    def w_across(s):
        w_gc(s).wait_recv()
        w_dp_far(s).start()

    for s in (1, 2, 3):
        hooks[s].append(partial(w_pass, s))
    hooks[2].append(partial(w_across, 0))
    hooks[3] += [partial(w_across, 1)]
    hooks[4] += [partial(w_across, 2), partial(w_across, 3)]

    def assemble():
        for s in range(4):
            w_dp(s).wait_recv()
            w_dp_far(s).wait_recv()
        local_copy(n1, chip.at[c], l_sems.at[1]).wait()
        chip_send().wait_recv()
        for s in (1, 2, 3):
            small(1, s).wait_recv()
        to = local_copy(own_out, own_scalar, l_sems.at[3])
        to.start()
        for head in range(6):
            p, b = head // 2, head % 2
            at_q = 128 * p + (0 if b else 64)
            at_k = 256 * p + (128 if b else 64)
            at_v = 256 * p + (192 if b else 0)
            start = (head % 3) * 192
            for r in range(4):
                rows = slice(192 * r, 192 * r + 192)
                source = wpair.at[head // 3, r]
                wq_out[rows, at_q : at_q + HD] = source[:, start : start + HD]
                wkv_out[rows, at_k : at_k + HD] = source[:, start + HD : start + 2 * HD]
                wkv_out[rows, at_v : at_v + HD] = source[:, start + 2 * HD : start + 3 * HD]
        to.wait()

    hooks[5].append(assemble)

    def project(number):
        core(number, 0).wait_recv()
        core(number, 1).wait_recv()
        half, k = chunk(number)
        w = wkv_out[...]
        rows = jnp.concatenate(
            [prompts[i, half, pl.ds(k * size, size)] for i in range(4)], axis=0
        )
        kv = nn(rows, w).astype(BF)
        to = pl.ds(pl.multiple_of(half * QROWS + k * size, size), size)
        for i in range(4):
            for p in range(3):
                kvp_all[p, i, to] = kv[size * i : size * i + size, 256 * p : 256 * p + 256]
        mine = chip[number // CHUNKS, pl.ds((number % CHUNKS) * size, size)]
        kvo = nn(mine, w).astype(BF)
        queries = (nn(mine, wq_out[...]) * 0.125).astype(BF)
        to = pl.ds(number * size, size)
        for p in range(3):
            kvo_all[p, to] = kvo[:, 256 * p : 256 * p + 256]
            q_all[p, to] = queries[:, 128 * p : 128 * p + 128]

    for i in range(8):
        hooks[5 + i].append(partial(project, i))

    def own_first():
        for a in range(3):
            own_block(a).start()

    def own_down():
        for a in range(3):
            own_block(a).wait()
            goes, copy = plan(a, 0)["line"]()[1]
            pl.when(goes)(copy.start)

    def own_up():
        for a in range(3):
            goes, copy = plan(a, 0)["line"]()[0]
            pl.when(goes)(copy.start)

    hooks[0].append(own_first)
    hooks[1].append(own_down)
    hooks[9].append(own_up)
    hooks[8].append(partial(gather_first, 0))
    hooks[10].append(partial(gather_second, 0))
    between = [[] for _ in range(24 // SEGMENT + 1)]
    last = len(between) - 1
    between[0] += [lambda: [copy.start() for copy in out_copies()], partial(gather_third, 0)]
    hooks[10].append(partial(relay, 1))
    hooks[12].append(partial(relay, 2))
    for slot, stage, s in (
        (0, relay, 3),
        (0, gather_first, 1),
        (1, gather_first, 2),
        (1, gather_second, 1),
        (2, gather_first, 3),
        (2, gather_second, 2),
        (3, gather_third, 1),
        (3, gather_second, 3),
        (4, gather_third, 2),
        (6, gather_third, 3),
    ):
        between[slot].append(partial(stage, s))

    for number in range(FRONT):
        for hook in hooks[number]:
            hook()

    low = lax.broadcasted_iota(jnp.int32, (CL, 128), 1) < 64

    def parts(turn):
        p, j = turn // 8, turn % 8
        shard = 2 * y + j // 4
        group = jnp.where(
            z < 2, shard, own_scalar[shard, 0, jnp.maximum(z - 2, 0) * 4 + j % 4]
        )
        rows_j = pl.ds(pl.multiple_of(j * CL, CL), CL)
        zero = jnp.zeros((CL, 128), BF)
        q = q_all[p, rows_j]
        return p, j, group, rows_j, (jnp.where(low, zero, q), jnp.where(low, q, zero))

    def store(p, j, mixes, sums):
        mix[p, j // 4, pl.ds(pl.multiple_of((j % 4) * CL, CL), CL)] = jnp.where(
            low, mixes[0], mixes[1]
        ).astype(BF)
        flat = jnp.where(low, sums[0], sums[1]).T
        lse_ref[p, j, 0:1] = flat[0:1]
        lse_ref[p, j, 1:2] = flat[64:65]

    def cont_turn(turn, carried):
        p, j, group, rows_j, q_parts = parts(turn)
        row = lax.broadcasted_iota(jnp.int32, (CL, CL), 0)
        near_ok = lax.broadcasted_iota(jnp.int32, (CL, CL), 1) <= row
        mixes, sums = [], []
        for h in range(2):
            cols = slice(128 * h, 128 * h + 128)
            kv = kvp_all[p, group, :, cols]
            kvo = kvo_all[p, rows_j, cols]
            far = nt(q_parts[h], kv)
            near = jnp.where(near_ok, nt(q_parts[h], kvo), negative)
            top = jnp.maximum(
                jnp.max(far, axis=1, keepdims=True), jnp.max(near, axis=1, keepdims=True)
            )
            far = jnp.exp(far - top)
            near = jnp.exp(near - top)
            total = jnp.sum(far, axis=1, keepdims=True) + jnp.sum(near, axis=1, keepdims=True)
            mixes.append((nn(far.astype(BF), kv) + nn(near.astype(BF), kvo)) / total)
            sums.append(jnp.broadcast_to(top + jnp.log(total), (CL, 128)))
        store(p, j, mixes, sums)
        return carried

    def prompt_turn(turn, carried):
        p, j, group, rows_j, q_parts = parts(turn)
        limit = z * QROWS + (j % (QROWS // CL)) * CL
        row = lax.broadcasted_iota(jnp.int32, (CL, P_SIZE), 0)
        key = lax.broadcasted_iota(jnp.int32, (CL, P_SIZE), 1)
        allowed = key - row <= limit
        mixes, sums = [], []
        for h in range(2):
            cols = slice(128 * h, 128 * h + 128)
            kv = kvp_all[p, group, :, cols]
            far = jnp.where(allowed, nt(q_parts[h], kv), negative)
            top = jnp.max(far, axis=1, keepdims=True)
            far = jnp.exp(far - top)
            total = jnp.sum(far, axis=1, keepdims=True)
            mixes.append(nn(far.astype(BF), kv) / total)
            sums.append(jnp.broadcast_to(top + jnp.log(total), (CL, 128)))
        store(p, j, mixes, sums)
        return carried

    def one_turn(turn, carried):
        for segment in range(last):

            @pl.when(turn == segment * SEGMENT)
            def _():
                for hook in between[segment]:
                    hook()

        @pl.when(z >= 2)
        def _():
            cont_turn(turn, 0)

        @pl.when(z < 2)
        def _():
            prompt_turn(turn, 0)

        for i in range(3):

            @pl.when(turn == 8 * i + 7)
            def _():
                for copy in exchange(i):
                    copy.start()

        return carried

    lax.fori_loop(0, 24, one_turn, 0)
    for hook in between[last]:
        hook()

    for number in range(8):
        side(number).wait_send()
        core(number, 0).wait_send()
        core(number, 1).wait_send()

        @pl.when(goes_up(number))
        def _():
            up(number).wait_send()

        @pl.when(goes_down(number))
        def _():
            down(number).wait_send()

    for s in range(4):
        if s:
            small(0, s).wait_send()
            small(1, s).wait_send()
            small(2, s).wait()
        passed_on(w_line(s))
        w_gc(s).wait_send()
        w_dp(s).wait_send()
        w_dp_far(s).wait_send()
    chip_send().wait_send()
    for s in range(4):
        for a in range(3):
            m = plan(a, s)
            passed_on(m["line"]())
            for name in names(s):
                m[name]().wait_send()
            m["c1"]().wait()
            m["c2"]().wait()
    for i in range(3):
        for copy in exchange(i):
            copy.wait()
    for copy in out_copies():
        copy.wait()


def front(tokens, vec, bup, own, wq, blocks, collective_id):
    any_space = pl.BlockSpec(memory_space=pl.ANY)
    vmem = pl.BlockSpec(memory_space=pltpu.VMEM)
    rows = 2 * QROWS

    def dma(count):
        return pltpu.SemaphoreType.DMA((count,))

    slots = 3 * GATHER_SLOTS
    heads = [(3, rows, 128), (3, rows, 256), (3, 4, P_SIZE, 256)]
    return pl.pallas_call(
        front_kernel,
        name="front",
        in_specs=[vmem, vmem, vmem, vmem] + [any_space] * 4,
        out_specs=[any_space, vmem]
        + [any_space] * 8
        + [vmem] * 5,
        out_shape=[
            jax.ShapeDtypeStruct((2, QROWS, 384), BF),
            jax.ShapeDtypeStruct((3, rows // CL, 2, 128), F32),
        ]
        + [jax.ShapeDtypeStruct((4, 4) + block.shape, BF) for block in blocks]
        + [
            jax.ShapeDtypeStruct((4, 2, QROWS, D), BF),
            jax.ShapeDtypeStruct((2, QROWS, D), BF),
        ]
        + [jax.ShapeDtypeStruct(shape, BF) for shape in heads]
        + [
            jax.ShapeDtypeStruct((D, 384), BF),
            jax.ShapeDtypeStruct((D, D), BF),
            jax.ShapeDtypeStruct(vec.shape, F32),
            jax.ShapeDtypeStruct((4,) + bup.shape, F32),
            jax.ShapeDtypeStruct((4,) + own.shape, jnp.int32),
        ],
        scratch_shapes=[
            pltpu.VMEM((QROWS, D), BF),
            pltpu.VMEM((4,) + vec.shape, F32),
            pltpu.VMEM((4, 2, QROWS, D), BF),
            pltpu.VMEM((2, QROWS, D), BF),
            pltpu.VMEM((2, 4) + wq.shape, BF),
        ]
        + [pltpu.VMEM(shape, BF) for shape in heads]
        + [
            pltpu.VMEM((3, 2, QROWS, 128), BF),
            pltpu.SMEM((4,) + own.shape, jnp.int32),
            dma(3 * CHUNKS),
            dma(2 * CHUNKS),
            dma(2 * CHUNKS),
            dma(2 * CHUNKS),
            dma(4 * CHUNKS),
            dma(4 * CHUNKS),
            dma(20),
            dma(20),
            dma(11),
            dma(11),
            dma(slots),
            dma(slots),
            dma(3),
            dma(3),
            dma(10),
            dma(5),
        ],
        compiler_params=pltpu.CompilerParams(
            collective_id=collective_id, has_side_effects=True, vmem_limit_bytes=56 << 20
        ),
    )(tokens, vec, bup, own, wq, *blocks)


def tail_kernel(
    grp,
    dkv,
    n1p,
    n1c,
    dkvo,
    dq,
    w_q,
    w_kv,
    grad_h2,
    tokens,
    vec,
    sums,
    out,
    sums_out,
    dw_out,
    part,
    chip,
    tiles,
    rows_p,
    low,
    wkt,
    wqt,
    dkvw,
    dqw,
    dw,
    ra,
    rb,
    rz,
    take,
    gsum,
    cur,
    sb,
    *rest,
):
    bufs, (sem_s, sem_r, l_sems, w_s, w_r, w_l) = rest[:9], rest[9:]
    sems = (sem_s, sem_r)
    x, z, g, y, c = places()
    sib, over_y, over_x = {"gc": g ^ 1}, {"gc": g ^ 2}, {"dp": x ^ 1}
    down = {"gr": jnp.maximum(z - 1, 0)}
    far = z >= 2
    size = QROWS // CHUNKS
    count = 2 * CHUNKS

    def fetch(t):
        rows = pl.ds(pl.multiple_of(t * size, size), size)
        h, r = t // CHUNKS, pl.ds(pl.multiple_of((t % CHUNKS) * size, size), size)
        slot = t % 2
        return (
            pltpu.make_async_copy(dkv.at[:, rows], tiles.at[slot], l_sems.at[slot]),
            pltpu.make_async_copy(n1p.at[:, h, r], rows_p.at[slot], l_sems.at[2 + slot]),
        )

    for copy in fetch(0):
        copy.start()
    greet(all_partners())
    wkt[...] = w_kv[...].T
    wqt[...] = w_q[...].T
    dkvw[...] = jnp.zeros_like(dkvw)
    dqw[...] = jnp.zeros_like(dqw)

    def at(t):
        return t // CHUNKS, pl.ds(pl.multiple_of((t % CHUNKS) * size, size), size)

    def mine(side, t):
        h, r = at(t)
        return part.at[2 * (1 - y if side == 0 else y) + c, h, r]

    def hop_a(side, t):
        h, r = at(t)
        i = 1 - y if side == 0 else y
        return send(part.at[2 * i + 1 - c, h, r], ra.at[i, h, r], sems, 8 * side + t, sib)

    def hop_y(t):
        h, r = at(t)
        return send(mine(0, t), rb.at[h, r], sems, 16 + t, over_y)

    def hop_z(t):
        h, r = at(t)
        return send(mine(1, t), rz.at[h, r], sems, 24 + t, down)

    hop_chip = send(chip.at[1 - c], take, sems, 32, sib)

    def fold(t, other):
        h, r = at(t)
        add_into(mine(1, t), mine(1, t), other.at[r])

    def stage0(t):
        slot = t % 2
        for copy in fetch(t):
            copy.wait()

        @pl.when(t + 1 < count)
        def _():
            for copy in fetch(t + 1):
                copy.start()

        weights = [
            [jnp.where(grp[j] == i, 1.0, 0.0).astype(F32) for j in range(8)] for i in range(4)
        ]

        @pl.loop(0, size // 16)
        def _(q):
            r = pl.ds(pl.multiple_of(q * 16, 16), 16)
            pieces = [tiles[slot, j, r].astype(F32) for j in range(8)]
            for i in range(4):
                total = weights[i][0] * pieces[0]
                for j in range(1, 8):
                    total = total + weights[i][j] * pieces[j]
                low[i, r] = total.astype(BF)

        whole = low[...].reshape(4 * size, D)
        grads = nn(whole, wkt[...]).astype(BF)
        h, r = at(t)
        for i in range(4):
            part[i, h, r] = grads[size * i : size * i + size]

        @pl.when(far)
        def _():
            hop_a(0, t).start()

        hop_a(1, t).start()
        own = pl.ds(pl.multiple_of(t * size, size), size)
        near, grad_q, rows_c = dkvo[own], dq[own], n1c[own]
        chip[h, r] = (nn(grad_q, wqt[...]) + nn(near, wkt[...])).astype(BF)
        rows = jnp.concatenate([rows_p[slot].reshape(4 * size, D), rows_c], axis=0)
        dkvw[...] += tn(rows, jnp.concatenate([whole, near], axis=0))
        dqw[...] += tn(rows_c, grad_q)

    def stage1(t):
        h, r = at(t)

        @pl.when(far)
        def _():
            hop_a(0, t).wait()
            add_into(mine(0, t), mine(0, t), ra.at[1 - y, h, r])
            hop_y(t).start()

        hop_a(1, t).wait()
        fold(t, ra.at[y, h])

    def stage2(t):
        @pl.when(far)
        def _():
            hop_y(t).wait()
            fold(t, rb.at[t // CHUNKS])

        @pl.when(z == 3)
        def _():
            hop_z(t).start()

    def stage3(t):
        @pl.when(z == 2)
        def _():
            hop_z(t).wait_recv()
            fold(t, rz.at[t // CHUNKS])
            hop_z(t).start()

    def stage4(t):
        @pl.when(z == 1)
        def _():
            hop_z(t).wait_recv()
            fold(t, rz.at[t // CHUNKS])

            @pl.when(t < CHUNKS)
            def _():
                hop_z(t).start()

    def stage5(t):
        @pl.when(jnp.logical_and(z == 0, t < CHUNKS))
        def _():
            hop_z(t).wait_recv()
            fold(t, rz.at[0])

    def stages(t, carried):
        for lag, stage in zip(
            (0, 1, 3, 5, 7, 9), (stage0, stage1, stage2, stage3, stage4, stage5)
        ):

            @pl.when(jnp.logical_and(t >= lag, t < count + lag))
            def _():
                stage(t - lag)

        return carried

    lax.fori_loop(0, count, stages, 0)
    hop_chip.start()

    for head in range(6):
        p, b = head // 2, head % 2
        places_in = (
            dqw[:, 128 * p + (0 if b else 64) : 128 * p + (64 if b else 128)],
            dkvw[:, 256 * p + (128 if b else 64) : 256 * p + (192 if b else 128)],
            dkvw[:, 256 * p + (192 if b else 0) : 256 * p + (256 if b else 64)],
        )
        for i, piece in enumerate(places_in):
            at_col = (head % 3) * 192 + HD * i
            for r in range(4):
                dw[head // 3, r, :, at_col : at_col + HD] = piece[192 * r : 192 * r + 192].astype(
                    BF
                )
    begin, after_a, after_b, after_c, total, finish = rs_plan(
        dw, dw_out, bufs, (w_s, w_r), w_l, 0, False
    )
    for s in RS_ORDER:
        begin(s)
    for s in RS_ORDER:
        after_a(s)
    lax.fori_loop(count, count + 3, stages, 0)
    for s in RS_ORDER:
        after_b(s)
    lax.fori_loop(count + 3, count + 9, stages, 0)
    for s in RS_ORDER:
        after_c(s)

    @pl.loop(0, count)
    def _(t):
        @pl.when(jnp.logical_or(z >= 2, jnp.logical_and(z == 1, t < CHUNKS)))
        def _():
            hop_z(t).wait_send()

    hop_chip.wait()

    cur[...] = sums[...]

    @pl.loop(0, CHUNKS)
    def _(k):
        r = pl.ds(pl.multiple_of(k * size, size), size)
        gsum[r] = chip[c, r].astype(F32) + take[r].astype(F32)

        @pl.when(z < 2)
        def _():
            gsum[r] += part[2 * y + c, jnp.minimum(z, 1), r].astype(F32)

        hidden = tokens[r].astype(F32) + vec[0:1]
        center = jnp.mean(hidden, axis=1, keepdims=True)
        offset = hidden - center
        factor = lax.rsqrt(jnp.mean(offset * offset, axis=1, keepdims=True) + eps)
        unit = offset * factor
        grad = gsum[r]
        scaled = grad * vec[1:2]
        first = jnp.mean(scaled, axis=1, keepdims=True)
        second = jnp.mean(scaled * unit, axis=1, keepdims=True)
        result = grad_h2[r] + factor * (scaled - first - unit * second)
        out[r] = result
        cur[0:1] += jnp.sum(result, axis=0, keepdims=True)
        cur[1:2] += jnp.sum(grad * unit, axis=0, keepdims=True)
        cur[2:3] += jnp.sum(grad, axis=0, keepdims=True)

    for i, target in enumerate((sib, over_y, over_x)):
        hop = send(cur, sb.at[i], sems, 33 + i, target)
        hop.start()
        hop.wait()
        cur[...] += sb[i]
        if i == 1:
            total()
    hops = [send(cur, sb.at[2 + s], sems, 35 + s, {"gr": z ^ s}) for s in (1, 2, 3)]
    for hop in hops:
        hop.start()
    finish()
    for hop in hops:
        hop.wait()
    sums_out[...] = (cur[...] + sb[3]) + (sb[4] + sb[5])


def tail_exchange(
    grp, dkv, n1p, n1c, dkvo, dq, w_q, w_kv, grad_h2, tokens, vec, sums, collective_id
):
    any_space = pl.BlockSpec(memory_space=pl.ANY)
    vmem = pl.BlockSpec(memory_space=pltpu.VMEM)
    block = (2, 4, 192, 576)
    return pl.pallas_call(
        tail_kernel,
        name="tail_exchange",
        in_specs=[pl.BlockSpec(memory_space=pltpu.SMEM), any_space, any_space] + [vmem] * 9,
        out_specs=[vmem, vmem, vmem],
        out_shape=[
            jax.ShapeDtypeStruct((QROWS, D), F32),
            jax.ShapeDtypeStruct(sums.shape, F32),
            jax.ShapeDtypeStruct(block[2:], F32),
        ],
        scratch_shapes=[
            pltpu.VMEM((4, 2, QROWS, D), BF),
            pltpu.VMEM((2, QROWS, D), BF),
            pltpu.VMEM((2, 8, CL, D), BF),
            pltpu.VMEM((2, 4, CL, D), BF),
            pltpu.VMEM((4, CL, D), BF),
            pltpu.VMEM((D, D), BF),
            pltpu.VMEM((384, D), BF),
            pltpu.VMEM((D, D), F32),
            pltpu.VMEM((D, 384), F32),
            pltpu.VMEM(block, BF),
            pltpu.VMEM((2, 2, QROWS, D), BF),
            pltpu.VMEM((2, QROWS, D), BF),
            pltpu.VMEM((2, QROWS, D), BF),
            pltpu.VMEM((QROWS, D), BF),
            pltpu.VMEM((QROWS, D), F32),
            pltpu.VMEM(sums.shape, F32),
            pltpu.VMEM((6,) + sums.shape, F32),
        ]
        + rs_scratch(block[2], block[3], False)
        + [
            pltpu.SemaphoreType.DMA((39,)),
            pltpu.SemaphoreType.DMA((39,)),
            pltpu.SemaphoreType.DMA((4,)),
            pltpu.SemaphoreType.DMA((RS_SLOTS,)),
            pltpu.SemaphoreType.DMA((RS_SLOTS,)),
            pltpu.SemaphoreType.DMA((8,)),
        ],
        compiler_params=pltpu.CompilerParams(
            collective_id=collective_id, has_side_effects=True, vmem_limit_bytes=60 << 20
        ),
    )(grp, dkv, n1p, n1c, dkvo, dq, w_q, w_kv, grad_h2, tokens, vec, sums)


GELU_IN = math.sqrt(2.0 / math.pi)


def middle_kernel(
    mixed,
    w_out_g,
    w_up,
    w_down,
    tokens,
    teacher,
    vec,
    b_up,
    final_out,
    grad_h2,
    dw_up,
    dw_down,
    dw_out,
    gm,
    sums,
    wo,
    wu,
    wd,
    h2,
    n2,
    n2t,
    act,
    slope,
    gf,
    gb,
    gbt,
    acc,
    du,
    dd,
    l_sems,
    o_sems,
):
    loads_u = [pltpu.make_async_copy(w_up.at[b], wu.at[b], l_sems.at[b]) for b in range(4)]
    loads_d = [pltpu.make_async_copy(w_down.at[b], wd.at[b], l_sems.at[4 + b]) for b in range(4)]
    for b in range(4):
        loads_u[b].start()
        loads_d[b].start()
    for k in range(2):
        for i in range(2):
            for r in range(4):
                wo[k, 192 * i : 192 * i + 192, 192 * r : 192 * r + 192] = w_out_g[2 * i + k, r]

    @pl.loop(0, 2)
    def _(t):
        r = pl.ds(pl.multiple_of(t * 256, 256), 256)
        hidden = tokens[r].astype(F32) + vec[0:1]
        attended = nn(mixed[0, r], wo[0]) + nn(mixed[1, r], wo[1])
        total = hidden + attended + vec[3:4]
        h2[r] = total
        n2[r] = norm_rows(total, vec[4:5], vec[5:6]).astype(BF)

    n2t[...] = n2[...].T
    acc[...] = jnp.zeros_like(acc)
    for copy in loads_u + loads_d:
        copy.wait()

    @pl.loop(0, 4)
    def _(b):
        @pl.loop(0, 2)
        def _(t):
            r = pl.ds(pl.multiple_of(t * 256, 256), 256)
            pre = nn(n2[r], wu[b]) + b_up[b, 0:1]
            square = pre * pre
            tanh = jnp.tanh(GELU_IN * pre * (1.0 + 0.044715 * square))
            half = 0.5 * (1.0 + tanh)
            low = (pre * half).astype(BF)
            act[b, r] = low
            slope[b, r] = half + (0.5 * GELU_IN) * pre * (1.0 - tanh * tanh) * (
                1.0 + (3.0 * 0.044715) * square
            )
            acc[r] += nt(low, wd[b])

    sums[...] = jnp.zeros_like(sums)

    @pl.loop(0, 2)
    def _(t):
        r = pl.ds(pl.multiple_of(t * 256, 256), 256)
        final = h2[r] + acc[r] + vec[6:7]
        final_out[r] = final.astype(BF)
        diff = final - teacher[r].astype(F32)
        gf[r] = diff
        low = diff.astype(BF)
        gb[r] = low
        sums[6:7] += jnp.sum(low.astype(F32), axis=0, keepdims=True)
        sums[11:12] += jnp.sum(diff * diff, axis=0, keepdims=True)

    gbt[...] = gb[...].T
    acc[...] = jnp.zeros_like(acc)

    @pl.loop(0, 4)
    def _(b):
        dd[b] = nn(gbt[...], act[b]).astype(BF)
        pltpu.make_async_copy(dd.at[b], dw_down.at[b], o_sems.at[b]).start()

        @pl.loop(0, 2)
        def _(t):
            r = pl.ds(pl.multiple_of(t * 256, 256), 256)
            low = (nn(gb[r], wd[b]) * slope[b, r]).astype(BF)
            act[b, r] = low
            sums[pl.ds(7 + b, 1)] += jnp.sum(low.astype(F32), axis=0, keepdims=True)
            acc[r] += nt(low, wu[b])

        du[b] = nn(n2t[...], act[b]).astype(BF)
        pltpu.make_async_copy(du.at[b], dw_up.at[b], o_sems.at[4 + b]).start()

    @pl.loop(0, 2)
    def _(t):
        r = pl.ds(pl.multiple_of(t * 256, 256), 256)
        hidden = h2[r]
        center = jnp.mean(hidden, axis=1, keepdims=True)
        offset = hidden - center
        factor = lax.rsqrt(jnp.mean(offset * offset, axis=1, keepdims=True) + eps)
        unit = offset * factor
        grad = acc[r]
        scaled = grad * vec[4:5]
        first = jnp.mean(scaled, axis=1, keepdims=True)
        second = jnp.mean(scaled * unit, axis=1, keepdims=True)
        total = gf[r] + factor * (scaled - first - unit * second)
        grad_h2[r] = total
        low = total.astype(BF)
        gb[r] = low
        sums[3:4] += jnp.sum(grad * unit, axis=0, keepdims=True)
        sums[4:5] += jnp.sum(grad, axis=0, keepdims=True)
        sums[5:6] += jnp.sum(low.astype(F32), axis=0, keepdims=True)
        gm[0, r] = nt(low, wo[0]).astype(BF)
        gm[1, r] = nt(low, wo[1]).astype(BF)

    for k in range(2):
        whole = tn(mixed[k], gb[...]).astype(BF)
        for i in range(2):
            for r in range(4):
                dw_out[2 * i + k, r] = whole[192 * i : 192 * i + 192, 192 * r : 192 * r + 192]
    for b in range(4):
        pltpu.make_async_copy(dd.at[b], dw_down.at[b], o_sems.at[b]).wait()
        pltpu.make_async_copy(du.at[b], dw_up.at[b], o_sems.at[4 + b]).wait()


def middle(mixed, w_out_g, w_up, w_down, tokens, teacher, vec, b_up):
    any_space = pl.BlockSpec(memory_space=pl.ANY)
    vmem = pl.BlockSpec(memory_space=pltpu.VMEM)
    blocks = (4, D, D)
    return pl.pallas_call(
        middle_kernel,
        name="middle",
        in_specs=[vmem, vmem, any_space, any_space, vmem, vmem, vmem, vmem],
        out_specs=[vmem, vmem, any_space, any_space, vmem, vmem, vmem],
        out_shape=[
            jax.ShapeDtypeStruct((QROWS, D), BF),
            jax.ShapeDtypeStruct((QROWS, D), F32),
            jax.ShapeDtypeStruct(blocks, BF),
            jax.ShapeDtypeStruct(blocks, BF),
            jax.ShapeDtypeStruct((4, 4, 192, 192), BF),
            jax.ShapeDtypeStruct((2, QROWS, 384), BF),
            jax.ShapeDtypeStruct((16, D), F32),
        ],
        scratch_shapes=[
            pltpu.VMEM((2, 384, D), BF),
            pltpu.VMEM(blocks, BF),
            pltpu.VMEM(blocks, BF),
            pltpu.VMEM((QROWS, D), F32),
            pltpu.VMEM((QROWS, D), BF),
            pltpu.VMEM((D, QROWS), BF),
            pltpu.VMEM((4, QROWS, D), BF),
            pltpu.VMEM((4, QROWS, D), F32),
            pltpu.VMEM((QROWS, D), F32),
            pltpu.VMEM((QROWS, D), BF),
            pltpu.VMEM((D, QROWS), BF),
            pltpu.VMEM((QROWS, D), F32),
            pltpu.VMEM(blocks, BF),
            pltpu.VMEM(blocks, BF),
            pltpu.SemaphoreType.DMA((8,)),
            pltpu.SemaphoreType.DMA((8,)),
        ],
        compiler_params=pltpu.CompilerParams(vmem_limit_bytes=60 << 20),
    )(mixed, w_out_g, w_up, w_down, tokens, teacher, vec, b_up)


def norm(hidden, gain, shift):
    center = jnp.mean(hidden, axis=1, keepdims=True)
    offset = hidden - center
    factor = lax.rsqrt(jnp.mean(offset * offset, axis=1, keepdims=True) + eps)
    unit = offset * factor
    return unit * gain + shift, unit, factor


def norm_back(grad, gain, unit, factor):
    grad_unit = grad * gain
    first = jnp.mean(grad_unit, axis=1, keepdims=True)
    second = jnp.mean(grad_unit * unit, axis=1, keepdims=True)
    grad_in = factor * (grad_unit - first - unit * second)
    return grad_in, jnp.sum(grad * unit, axis=0), jnp.sum(grad, axis=0)


def head_layout(blocks):
    chunks = blocks.transpose(1, 0, 2).reshape(D, 6, 3, HD)
    q_list, kv_list = [], []
    for pair in range(3):
        a, b = 2 * pair, 2 * pair + 1
        q_list += [chunks[:, b, 0], chunks[:, a, 0]]
        kv_list += [chunks[:, a, 2], chunks[:, a, 1], chunks[:, b, 1], chunks[:, b, 2]]
    return jnp.concatenate(q_list, axis=1), jnp.concatenate(kv_list, axis=1)


def head_layout_back(grad_q, grad_kv):
    qc = grad_q.reshape(D, 3, 2, HD)
    kc = grad_kv.reshape(D, 3, 4, HD)
    pieces = []
    for pair in range(3):
        pieces += [qc[:, pair, 1], kc[:, pair, 1], kc[:, pair, 0]]
        pieces += [qc[:, pair, 0], kc[:, pair, 2], kc[:, pair, 3]]
    whole = jnp.concatenate(pieces, axis=1)
    return whole.reshape(D, 2, 576).transpose(1, 0, 2)


def on_device(
    tokens,
    teacher,
    pass_embed,
    ln1_gain,
    ln1_bias,
    qkv_weight,
    out_weight,
    out_bias,
    ln2_gain,
    ln2_bias,
    fc1_weight,
    fc1_bias,
    fc2_weight,
    fc2_bias,
    cont_group,
    token_count,
):
    n_dp = lax.axis_size("dp")
    n_gr = lax.axis_size("gr")
    n_gc = lax.axis_size("gc")
    z = lax.axis_index("gr")
    g = lax.axis_index("gc")
    c = g % 2
    y = g // 2
    swap_core = [(i, i ^ 1) for i in range(n_gc)]
    swap_y = [(i, i ^ 2) for i in range(n_gc)]

    packed = jnp.stack(
        [pass_embed, ln1_gain, ln1_bias, out_bias, ln2_gain, ln2_bias, fc2_bias, fc2_bias]
    ).astype(F32)
    if n_dp == 2:
        vec = lax.dynamic_update_slice(jnp.zeros((8, D), F32), packed, (0, z * packed.shape[1]))
        bup = jnp.broadcast_to(fc1_bias.astype(F32), (8, fc1_bias.shape[0]))
        own = jnp.broadcast_to(jnp.pad(cont_group, (0, 120)), (8, 128))
        (
            mixed,
            lse_rows,
            w_out,
            w_up,
            w_down,
            n1_prompt,
            n1_chip,
            q,
            kvo,
            kvp,
            w_q,
            w_kv,
            vectors,
            b_up,
            owners,
        ) = front(
            tokens, vec, bup, own, qkv_weight, [out_weight, fc1_weight, fc2_weight], 1
        )
        n1_chip = n1_chip.reshape(2 * QROWS, D)
        owners = owners[:, 0, :8]
    else:
        vectors = lax.all_gather(packed, "gr", axis=1, tiled=True)
        b_up = lax.all_gather(fc1_bias, "gc", axis=0, tiled=True).astype(F32)
        owners = lax.all_gather(cont_group, "gr", axis=0, tiled=True)
    embed, gain1, shift1, b_out, gain2, shift2, b_down = [vectors[i] for i in range(7)]
    owners = owners.reshape(4, 2, 4)
    mine = lax.dynamic_slice(owners, (2 * y, jnp.maximum(z - 2, 0), 0), (2, 1, 4)).reshape(8)
    own_groups = jnp.repeat(2 * y + jnp.arange(2), 4)
    grp = jnp.where(z < 2, own_groups, mine).astype(jnp.int32)
    z_arr = z.astype(jnp.int32).reshape(1)

    hidden = tokens.astype(F32) + embed
    normed1, unit1, factor1 = norm(hidden, gain1, shift1)
    n1 = normed1.astype(BF)

    if n_dp != 2:
        w_other = lax.ppermute(qkv_weight, "gc", swap_y)
        w_pair = jnp.where(
            y == 0, jnp.stack([qkv_weight, w_other]), jnp.stack([w_other, qkv_weight])
        )
        w_qkv = lax.all_gather(w_pair, "gr", axis=1, tiled=True)
        n1_other = lax.ppermute(n1, "gc", swap_core)
        n1_chip = jnp.where(
            c == 0, jnp.concatenate([n1, n1_other]), jnp.concatenate([n1_other, n1])
        )
        n1_col = lax.all_gather(n1, "gr", axis=0, tiled=True)[:P_SIZE]
        n1_prompt = lax.all_gather(n1_col, "gc", axis=0, tiled=True)
        w_q, w_kv = head_layout(w_qkv)
        kvp = nn(n1_prompt, w_kv).astype(BF)
        kvo = nn(n1_chip, w_kv).astype(BF)
        q = (nn(n1_chip, w_q) * 0.125).astype(BF)
        w_out = lax.all_gather(out_weight, ("gc", "gr"))
        w_up = lax.all_gather(fc1_weight, ("gc", "gr"))
        w_down = lax.all_gather(fc2_weight, ("gc", "gr"))
        mixed_heads, lse = attend(grp, z_arr, q, kvo, kvp)
        lse_rows = lse[:, ::64].reshape(8, CL, 3, 2).transpose(2, 0, 3, 1)
        halves = mixed_heads.reshape(2, QROWS, 384)
        keep = lax.dynamic_index_in_dim(halves, c, 0, keepdims=False)
        give = lax.dynamic_index_in_dim(halves, 1 - c, 0, keepdims=False)
        take = lax.ppermute(give, "gc", swap_core)
        mixed = jnp.where(c == 0, jnp.stack([keep, take]), jnp.stack([take, keep]))
    w_up = w_up.reshape(n_gc, D, FF // n_gc)
    w_down = w_down.reshape(n_gc, D, FF // n_gc)
    if n_dp == 2:
        final, grad_h2, grad_w_up, grad_w_down, grad_w_out, gm, later_sums = middle(
            mixed, w_out, w_up, w_down, tokens, teacher, vectors, b_up
        )
    else:
        w_out = w_out.reshape(2, 2, n_gr, 192, 192).transpose(1, 0, 3, 2, 4).reshape(2, 384, D)

        attended = lax.dot_general(
            mixed, w_out, (((0, 2), (0, 1)), ((), ())), preferred_element_type=F32
        )
        hidden2 = hidden + attended + b_out
        normed2, unit2, factor2 = norm(hidden2, gain2, shift2)
        n2 = normed2.astype(BF)
        pre = lax.dot_general(n2, w_up, (((1,), (1,)), ((), ())), preferred_element_type=F32)
        pre = pre.reshape(QROWS, FF) + b_up
        active, gelu_back = jax.vjp(partial(jax.nn.gelu, approximate=True), pre)
        act = active.astype(BF)
        act_blocks = act.reshape(QROWS, n_gc, FF // n_gc)
        final = (
            hidden2
            + lax.dot_general(
                act_blocks, w_down, (((1, 2), (0, 2)), ((), ())), preferred_element_type=F32
            )
            + b_down
        )
        grad_final = final - teacher.astype(F32)
        squared = jnp.sum(grad_final * grad_final, axis=0)
        gb = grad_final.astype(BF)
        grad_b_down = jnp.sum(gb, axis=0, dtype=F32)
        grad_active = lax.dot_general(
            gb, w_down, (((1,), (1,)), ((), ())), preferred_element_type=F32
        ).reshape(QROWS, FF)
        grad_w_down = jnp.einsum("td,tgf->gdf", gb, act_blocks, preferred_element_type=F32)
        (grad_pre,) = gelu_back(grad_active)
        gp = grad_pre.astype(BF)
        gp_blocks = gp.reshape(QROWS, n_gc, FF // n_gc)
        grad_b_up = jnp.sum(gp, axis=0, dtype=F32)
        grad_w_up = jnp.einsum("td,tgf->gdf", n2, gp_blocks, preferred_element_type=F32)
        grad_n2 = lax.dot_general(
            gp_blocks, w_up, (((1, 2), (0, 2)), ((), ())), preferred_element_type=F32
        )
        back2, grad_gain2, grad_shift2 = norm_back(grad_n2, gain2, unit2, factor2)
        grad_h2 = grad_final + back2
        ga = grad_h2.astype(BF)
        grad_b_out = jnp.sum(ga, axis=0, dtype=F32)
        grad_w_out = jnp.einsum("ctk,tn->ckn", mixed, ga, preferred_element_type=F32)
        gm = jnp.einsum("tn,ckn->ctk", ga, w_out, preferred_element_type=F32).astype(BF)
        grad_w_up = grad_w_up.astype(BF)
        grad_w_down = grad_w_down.astype(BF)
        grad_w_out = (
            grad_w_out.astype(BF)
            .reshape(2, 2, 192, n_gr, 192)
            .transpose(1, 0, 3, 2, 4)
            .reshape(n_gc, n_gr, 192, 192)
        )
    weight_grads = [
        grad_w_down.reshape(n_gc, n_gr, 192, 768),
        grad_w_up.reshape(n_gc, n_gr, 192, 768),
        grad_w_out,
    ]
    if n_dp == 2:
        dq, dkvo, dkv, out_w_down, out_w_up, out_w_out = attend_back_scatter(
            grp, q, lse_rows, kvo, kvp, gm, weight_grads, 3
        )
    else:
        gm_keep = lax.dynamic_index_in_dim(gm, c, 0, keepdims=False)
        gm_give = lax.dynamic_index_in_dim(gm, 1 - c, 0, keepdims=False)
        gm_take = lax.ppermute(gm_give, "gc", swap_core)
        gm_chip = jnp.where(c == 0, jnp.stack([gm_keep, gm_take]), jnp.stack([gm_take, gm_keep]))
        gm_chip = gm_chip.reshape(2 * QROWS, 384)

        def scatter16(blocks):
            part = lax.psum_scatter(
                blocks.reshape(n_gc * n_gr * blocks.shape[2], -1),
                ("gc", "gr"),
                scatter_dimension=0,
                tiled=True,
            )
            return lax.psum(part, "dp").astype(F32)

        out_w_down, out_w_up, out_w_out = [scatter16(grad) for grad in weight_grads]
        dq, dkvo, dkvp = attend_back(grp, z_arr, q, gm_chip, lse_rows, kvo, kvp)
        part_prompt = nt(dkvp, w_kv).astype(BF)

        part_chip = (nt(dq, w_q) + nt(dkvo, w_kv)).reshape(2, QROWS, D)
        grad_kv = tn(n1_prompt, dkvp) + tn(n1_chip, dkvo)
        grad_q = tn(n1_chip, dq)
        grad_qkv = head_layout_back(grad_q, grad_kv)

    if n_dp == 2:
        input_grad, sums, out_w_qkv = tail_exchange(
            grp,
            dkv,
            n1_prompt,
            n1_chip,
            dkvo,
            dq,
            w_q,
            w_kv,
            grad_h2,
            tokens,
            vectors,
            later_sums,
            4,
        )
    else:
        later_sums = jnp.concatenate(
            [
                grad_gain2[None],
                grad_shift2[None],
                grad_b_out[None],
                grad_b_down[None],
                grad_b_up.reshape(4, D),
                squared[None],
                jnp.zeros((4, D), F32),
            ]
        )
        back_prompt = lax.psum_scatter(part_prompt, "gc", scatter_dimension=0, tiled=True)
        back_prompt = lax.psum_scatter(
            jnp.concatenate([back_prompt, jnp.zeros_like(back_prompt)]),
            "gr",
            scatter_dimension=0,
            tiled=True,
        ).astype(F32)
        part_keep = lax.dynamic_index_in_dim(part_chip, c, 0, keepdims=False)
        part_give = lax.dynamic_index_in_dim(part_chip, 1 - c, 0, keepdims=False)
        part_take = lax.ppermute(part_give.astype(BF), "gc", swap_core).astype(F32)
        grad_n1 = part_keep + part_take + back_prompt
        qkv_keep = lax.dynamic_index_in_dim(grad_qkv, y, 0, keepdims=False)
        qkv_give = lax.dynamic_index_in_dim(grad_qkv, 1 - y, 0, keepdims=False)
        qkv_take = lax.ppermute(qkv_give.astype(BF), "gc", swap_y).astype(F32)
        out_w_qkv = lax.psum_scatter(
            (qkv_keep + qkv_take).astype(BF), "gr", scatter_dimension=0, tiled=True
        )
        out_w_qkv = lax.psum(out_w_qkv, "dp").astype(F32)
        back1, grad_gain1, grad_shift1 = norm_back(grad_n1, gain1, unit1, factor1)
        input_grad = grad_h2 + back1
        first_sums = jnp.stack([jnp.sum(input_grad, axis=0), grad_gain1, grad_shift1])
        sums = lax.psum(jnp.concatenate([first_sums, later_sums]), ("dp", "gr", "gc"))
    sums = sums[:12].reshape(12 * D)
    loss = (jnp.sum(sums[11 * D :]) / (D * token_count[0].astype(F32))).reshape(1)
    rows = sums[: 7 * D].reshape(7, n_gr, D // n_gr)
    rows = lax.dynamic_index_in_dim(rows, z, 1, keepdims=False)
    up = lax.dynamic_index_in_dim(
        sums[7 * D : 7 * D + FF].reshape(n_gc, FF // n_gc), g, 0, keepdims=False
    )
    return (
        final.astype(BF),
        loss,
        input_grad,
        rows[0],
        rows[1],
        rows[2],
        out_w_qkv,
        out_w_out,
        rows[5],
        rows[3],
        rows[4],
        out_w_up,
        up,
        out_w_down,
        rows[6],
    )


def solution(mesh):
    rows = P(("dp", "gr", "gc"), None)
    in_specs = (
        rows,
        rows,
        P("gr"),
        P("gr"),
        P("gr"),
        P("gr", "gc"),
        P("gc", "gr"),
        P("gr"),
        P("gr"),
        P("gr"),
        P("gr", "gc"),
        P("gc"),
        P("gr", "gc"),
        P("gr"),
        P(("dp", "gr")),
        P(),
    )
    out_specs = (
        rows,
        P(),
        rows,
        P("gr"),
        P("gr"),
        P("gr"),
        P("gr", "gc"),
        P("gc", "gr"),
        P("gr"),
        P("gr"),
        P("gr"),
        P("gr", "gc"),
        P("gc"),
        P("gr", "gc"),
        P("gr"),
    )
    return jax.shard_map(
        on_device, mesh=mesh, in_specs=in_specs, out_specs=out_specs, check_vma=False
    )
```

```python
from functools import partial
import math

import jax
import jax.numpy as jnp
from jax import lax
from jax.experimental import pallas as pl
from jax.experimental.pallas import tpu as pltpu
from jax.sharding import PartitionSpec as P

D = 768
HD = 64
FF = 3072
P_SIZE = 1024
CL = 128
QROWS = 512
eps = 1e-05
negative = -1e30
BF = jnp.bfloat16
F32 = jnp.float32


def nt(a, b):
    return lax.dot_general(a, b, (((1,), (1,)), ((), ())), preferred_element_type=F32)


def nn(a, b):
    return lax.dot_general(a, b, (((1,), (0,)), ((), ())), preferred_element_type=F32)


def tn(a, b):
    return lax.dot_general(a, b, (((0,), (0,)), ((), ())), preferred_element_type=F32)


def att_fwd_kernel(grp_ref, z_ref, q_ref, kvo_ref, kvp_ref, o_ref, lse_ref):
    j = pl.program_id(1)
    row0 = pl.multiple_of(grp_ref[j] * P_SIZE, P_SIZE)
    z = z_ref[0]
    lane = lax.broadcasted_iota(jnp.int32, (CL, 128), 1)
    low = lane < 64
    zero = jnp.zeros((CL, 128), BF)
    q = q_ref[...]
    q_parts = (jnp.where(low, zero, q), jnp.where(low, q, zero))

    @pl.when(z >= 2)
    def _():
        row = lax.broadcasted_iota(jnp.int32, (CL, CL), 0)
        near_ok = lax.broadcasted_iota(jnp.int32, (CL, CL), 1) <= row
        mixes, sums = [], []
        for h in range(2):
            cols = slice(128 * h, 128 * h + 128)
            kv = kvp_ref[pl.ds(row0, P_SIZE), cols]
            kvo = kvo_ref[:, cols]
            far = nt(q_parts[h], kv)
            near = jnp.where(near_ok, nt(q_parts[h], kvo), negative)
            top = jnp.maximum(
                jnp.max(far, axis=1, keepdims=True), jnp.max(near, axis=1, keepdims=True)
            )
            far = jnp.exp(far - top)
            near = jnp.exp(near - top)
            total = jnp.sum(far, axis=1, keepdims=True) + jnp.sum(near, axis=1, keepdims=True)
            mix = nn(far.astype(BF), kv) + nn(near.astype(BF), kvo)
            mixes.append(mix / total)
            sums.append(jnp.broadcast_to(top + jnp.log(total), (CL, 128)))
        o_ref[...] = jnp.where(low, mixes[0], mixes[1]).astype(BF)
        lse_ref[...] = jnp.where(low, sums[0], sums[1])

    @pl.when(z < 2)
    def _():
        limit = z * QROWS + (j % (QROWS // CL)) * CL
        row = lax.broadcasted_iota(jnp.int32, (CL, P_SIZE), 0)
        key = lax.broadcasted_iota(jnp.int32, (CL, P_SIZE), 1)
        allowed = key - row <= limit
        mixes, sums = [], []
        for h in range(2):
            cols = slice(128 * h, 128 * h + 128)
            kv = kvp_ref[pl.ds(row0, P_SIZE), cols]
            far = jnp.where(allowed, nt(q_parts[h], kv), negative)
            top = jnp.max(far, axis=1, keepdims=True)
            far = jnp.exp(far - top)
            total = jnp.sum(far, axis=1, keepdims=True)
            mix = nn(far.astype(BF), kv)
            mixes.append(mix / total)
            sums.append(jnp.broadcast_to(top + jnp.log(total), (CL, 128)))
        o_ref[...] = jnp.where(low, mixes[0], mixes[1]).astype(BF)
        lse_ref[...] = jnp.where(low, sums[0], sums[1])


def attend(grp, z, q, kvo, kvp):
    rows = q.shape[0]
    pairs = q.shape[1] // 128
    groups_rows = kvp.shape[0]
    return pl.pallas_call(
        att_fwd_kernel,
        name="att_fwd",
        grid_spec=pltpu.PrefetchScalarGridSpec(
            num_scalar_prefetch=2,
            grid=(pairs, rows // CL),
            in_specs=[
                pl.BlockSpec((CL, 128), lambda p, j, *_: (j, p)),
                pl.BlockSpec((CL, 256), lambda p, j, *_: (j, p)),
                pl.BlockSpec((groups_rows, 256), lambda p, j, *_: (0, p)),
            ],
            out_specs=[
                pl.BlockSpec((CL, 128), lambda p, j, *_: (j, p)),
                pl.BlockSpec((CL, 128), lambda p, j, *_: (j, p)),
            ],
        ),
        out_shape=[
            jax.ShapeDtypeStruct((rows, pairs * 128), BF),
            jax.ShapeDtypeStruct((rows, pairs * 128), F32),
        ],
        compiler_params=pltpu.CompilerParams(vmem_limit_bytes=40 << 20),
        cost_estimate=pl.CostEstimate(
            flops=4 * rows * P_SIZE * 128 * pairs * 2,
            bytes_accessed=groups_rows * 512 * pairs,
            transcendentals=rows * P_SIZE * pairs * 2,
        ),
    )(grp, z, q, kvo, kvp)


def att_bwd_kernel(
    grp_ref, z_ref, q_ref, gm_ref, lse_ref, kvo_ref, kvp_ref, dq_ref, dkvo_ref, dkvp_ref, acc
):
    j = pl.program_id(1)
    row0 = pl.multiple_of(grp_ref[j] * P_SIZE, P_SIZE)
    z = z_ref[0]
    low = lax.broadcasted_iota(jnp.int32, (CL, 128), 1) < 64
    zero = jnp.zeros((CL, 128), BF)
    q = q_ref[...]
    gm = gm_ref[...]
    stacks = (
        jnp.concatenate([jnp.where(low, zero, q), jnp.where(low, gm, zero)], axis=0),
        jnp.concatenate([jnp.where(low, q, zero), jnp.where(low, zero, gm)], axis=0),
    )

    @pl.when(j == 0)
    def _():
        acc[...] = jnp.zeros_like(acc)

    @pl.when(z >= 2)
    def _():
        row = lax.broadcasted_iota(jnp.int32, (CL, CL), 0)
        near_ok = row <= lax.broadcasted_iota(jnp.int32, (CL, CL), 1)
        dqs = []
        for h in range(2):
            cols = slice(128 * h, 128 * h + 128)
            kv = kvp_ref[pl.ds(row0, P_SIZE), cols]
            kvo = kvo_ref[:, cols]
            lse = lse_ref[0, 0, h : h + 1, :]
            far = nt(kv, stacks[h])
            near = nt(kvo, stacks[h])
            pf = jnp.exp(far[:, :CL] - lse)
            pn = jnp.where(near_ok, jnp.exp(near[:, :CL] - lse), 0.0)
            df = far[:, CL:]
            dn = near[:, CL:]
            inner = jnp.sum(pf * df, axis=0, keepdims=True) + jnp.sum(
                pn * dn, axis=0, keepdims=True
            )
            sf = (pf * (df - inner)).astype(BF)
            sn = (pn * (dn - inner)).astype(BF)
            acc[pl.ds(row0, P_SIZE), cols] += nn(
                jnp.concatenate([sf, pf.astype(BF)], axis=1), stacks[h]
            )
            dkvo_ref[:, cols] = nn(
                jnp.concatenate([sn, pn.astype(BF)], axis=1), stacks[h]
            ).astype(BF)
            dqs.append(tn(sf, kv) + tn(sn, kvo))
        dq_ref[...] = (jnp.where(low, dqs[1], dqs[0]) * 0.125).astype(BF)

    @pl.when(z < 2)
    def _():
        limit = z * QROWS + (j % (QROWS // CL)) * CL
        key = lax.broadcasted_iota(jnp.int32, (P_SIZE, CL), 0)
        row = lax.broadcasted_iota(jnp.int32, (P_SIZE, CL), 1)
        allowed = key - row <= limit
        dqs = []
        for h in range(2):
            cols = slice(128 * h, 128 * h + 128)
            kv = kvp_ref[pl.ds(row0, P_SIZE), cols]
            lse = lse_ref[0, 0, h : h + 1, :]
            far = nt(kv, stacks[h])
            pf = jnp.where(allowed, jnp.exp(far[:, :CL] - lse), 0.0)
            df = far[:, CL:]
            inner = jnp.sum(pf * df, axis=0, keepdims=True)
            sf = (pf * (df - inner)).astype(BF)
            acc[pl.ds(row0, P_SIZE), cols] += nn(
                jnp.concatenate([sf, pf.astype(BF)], axis=1), stacks[h]
            )
            dqs.append(tn(sf, kv))
        dkvo_ref[...] = jnp.zeros_like(dkvo_ref)
        dq_ref[...] = (jnp.where(low, dqs[1], dqs[0]) * 0.125).astype(BF)

    @pl.when(j == pl.num_programs(1) - 1)
    def _():
        dkvp_ref[...] = acc[...].astype(BF)


def attend_back(grp, z, q, gm, lse, kvo, kvp):
    rows = q.shape[0]
    pairs = q.shape[1] // 128
    groups_rows = kvp.shape[0]
    return pl.pallas_call(
        att_bwd_kernel,
        name="att_bwd",
        grid_spec=pltpu.PrefetchScalarGridSpec(
            num_scalar_prefetch=2,
            grid=(pairs, rows // CL),
            in_specs=[
                pl.BlockSpec((CL, 128), lambda p, j, *_: (j, p)),
                pl.BlockSpec((CL, 128), lambda p, j, *_: (j, p)),
                pl.BlockSpec((1, 1, 2, 128), lambda p, j, *_: (p, j, 0, 0)),
                pl.BlockSpec((CL, 256), lambda p, j, *_: (j, p)),
                pl.BlockSpec((groups_rows, 256), lambda p, j, *_: (0, p)),
            ],
            out_specs=[
                pl.BlockSpec((CL, 128), lambda p, j, *_: (j, p)),
                pl.BlockSpec((CL, 256), lambda p, j, *_: (j, p)),
                pl.BlockSpec((groups_rows, 256), lambda p, j, *_: (0, p)),
            ],
            scratch_shapes=[pltpu.VMEM((groups_rows, 256), F32)],
        ),
        out_shape=[
            jax.ShapeDtypeStruct((rows, pairs * 128), BF),
            jax.ShapeDtypeStruct((rows, pairs * 256), BF),
            jax.ShapeDtypeStruct((groups_rows, pairs * 256), BF),
        ],
        compiler_params=pltpu.CompilerParams(vmem_limit_bytes=48 << 20),
        cost_estimate=pl.CostEstimate(
            flops=10 * rows * P_SIZE * 128 * pairs * 2,
            bytes_accessed=groups_rows * 1024 * pairs,
            transcendentals=rows * P_SIZE * pairs * 2,
        ),
    )(grp, z, q, gm, lse, kvo, kvp)


MESH = pl.DeviceIdType.MESH


def places():
    x = lax.axis_index("dp")
    z = lax.axis_index("gr")
    g = lax.axis_index("gc")
    return x, z, g, g // 2, g % 2


def greet(partners):
    barrier = pltpu.get_barrier_semaphore()
    for partner in partners:
        pl.semaphore_signal(barrier, inc=1, device_id=partner, device_id_type=MESH)
    pl.semaphore_wait(barrier, len(partners))


def all_partners():
    x, z, g, y, c = places()
    by_z = [{"gr": z ^ step} for step in (1, 2, 3)]
    return [{"gc": g ^ 1}, {"gc": g ^ 2}, {"dp": x ^ 1}] + by_z


def send(src, dst, sems, slot, target, send_slot=None):
    return pltpu.make_async_remote_copy(
        src_ref=src,
        dst_ref=dst,
        send_sem=sems[0].at[slot if send_slot is None else send_slot],
        recv_sem=sems[1].at[slot],
        device_id=target,
        device_id_type=MESH,
    )


def add_into(dst, left, right):
    rows = dst.shape[0]
    size = 48 if rows % 48 == 0 else 64

    @pl.loop(0, rows // size)
    def _(i):
        r = pl.ds(pl.multiple_of(i * size, 16), size)
        dst[r] = (left[r].astype(F32) + right[r].astype(F32)).astype(dst.dtype)


RS_SLOTS = 28
RS_ORDER = (3, 2, 1, 0)


def rs_plan(grads, outs, bufs, sems, l_sems, base, paired):
    own, ra, rb0, rb1, rc0, rc1, sc, rd, re = bufs
    x, z, g, y, c = places()
    sib, over_y, over_x = {"gc": g ^ 1}, {"gc": g ^ 2}, {"dp": x ^ 1}
    rows = grads.shape[2]
    q = rows // 4
    mine0 = pl.ds(pl.multiple_of(q * x, 16), q)
    other0 = pl.ds(pl.multiple_of(q * (1 - x), 16), q)
    mine1 = pl.ds(pl.multiple_of(2 * q + q * x, 16), q)
    other1 = pl.ds(pl.multiple_of(2 * q + q * (1 - x), 16), q)
    first = pl.ds(0, 2 * q)
    slot = base * RS_SLOTS

    def load(i, s):
        source = grads.at[2 * i + c, z ^ s] if paired else grads.at[i, z ^ s]
        return pltpu.make_async_copy(source, own.at[i, s], l_sems.at[8 * base + 2 * s + i])

    def hop_a(i, s):
        return send(grads.at[2 * i + 1 - c, z ^ s], ra.at[i, s], sems, slot + 6 * s + i, sib)

    def hop_b0(s):
        return send(own.at[1 - y, s, first], rb0.at[s], sems, slot + 6 * s + 2, over_y)

    def hop_b1(s):
        return send(own.at[:, s, other1], rb1.at[s], sems, slot + 6 * s + 3, over_x)

    def hop_c0(s):
        return send(own.at[y, s, other0], rc0.at[s], sems, slot + 6 * s + 4, over_x)

    def hop_c1(s):
        return send(own.at[1 - y, s, mine1], rc1.at[s], sems, slot + 6 * s + 5, over_y)

    def hop_z(s):
        return send(sc.at[s], rd.at[s - 1], sems, slot + 23 + s, {"gr": z ^ s})

    def hop_d():
        return send(sc.at[0], re, sems, slot + 27, over_x)

    def begin(s):
        for i in range(2):
            load(i, s).start()
            if paired:
                hop_a(i, s).start()

    def after_a(s):
        for i in range(2):
            load(i, s).wait()
            if paired:
                hop_a(i, s).wait()
                add_into(own.at[i, s], own.at[i, s], ra.at[i, s])
        hop_b0(s).start()
        hop_b1(s).start()

    def after_b(s):
        hop_b0(s).wait()
        hop_b1(s).wait()
        add_into(own.at[y, s, first], own.at[y, s, first], rb0.at[s])
        for i in range(2):
            add_into(own.at[i, s, mine1], own.at[i, s, mine1], rb1.at[s, i])
        hop_c0(s).start()
        hop_c1(s).start()

    def after_c(s):
        hop_c0(s).wait()
        hop_c1(s).wait()
        add_into(sc.at[s, pl.ds(0, q)], own.at[y, s, mine0], rc0.at[s])
        add_into(sc.at[s, pl.ds(q, q)], own.at[y, s, mine1], rc1.at[s])
        if s:
            hop_z(s).start()

    def total():
        for s in (1, 2, 3):
            hop_z(s).wait()
        whole = sc[0].astype(F32)
        for i in range(3):
            whole = whole + rd[i].astype(F32)
        sc[0] = whole.astype(BF)
        hop_d().start()

    def finish():
        hop_d().wait()
        outs[mine0] = sc[0, pl.ds(0, q)].astype(F32)
        outs[mine1] = sc[0, pl.ds(q, q)].astype(F32)
        outs[other0] = re[pl.ds(0, q)].astype(F32)
        outs[other1] = re[pl.ds(q, q)].astype(F32)

    return begin, after_a, after_b, after_c, total, finish


def rs_steps(plans):
    order = [(plan, s) for plan in plans for s in RS_ORDER]
    n = len(order)
    steps = [[partial(plan[0], s) for plan, s in order]]
    for i in range(n + 10):
        part = []
        if i < n:
            part.append(partial(order[i][0][1], order[i][1]))
        if 2 <= i < n + 2:
            part.append(partial(order[i - 2][0][2], order[i - 2][1]))
        if 4 <= i < n + 4:
            part.append(partial(order[i - 4][0][3], order[i - 4][1]))
        if 7 <= i < n + 7 and (i - 7) % 4 == 3:
            part.append(plans[(i - 7) // 4][4])
        if 9 <= i < n + 9 and (i - 9) % 4 == 3:
            part.append(plans[(i - 9) // 4][5])
        if part:
            steps.append(part)
    return steps


def rs_scratch(rows, cols, paired):
    q = rows // 4
    return [
        pltpu.VMEM((2, 4, rows, cols), BF),
        pltpu.VMEM((2, 4, rows, cols) if paired else (16, 128), BF),
        pltpu.VMEM((4, 2 * q, cols), BF),
        pltpu.VMEM((4, 2, q, cols), BF),
        pltpu.VMEM((4, q, cols), BF),
        pltpu.VMEM((4, q, cols), BF),
        pltpu.VMEM((4, 2 * q, cols), BF),
        pltpu.VMEM((3, 2 * q, cols), BF),
        pltpu.VMEM((2 * q, cols), BF),
    ]


def att_scatter_kernel(count, grp_ref, q_ref, lse_ref, kvo_ref, kvp_ref, gm, *refs):
    grads = refs[:count]
    dq_ref, dkvo_ref, dkv_ref = refs[count : count + 3]
    outs = refs[count + 3 : 2 * count + 3]
    rest = refs[2 * count + 3 :]
    bufs, (gmx, sem_s, sem_r, l_sems, m_send, m_recv, m_local) = rest[: 9 * count], rest[9 * count :]
    p, j = pl.program_id(0), pl.program_id(1)
    step = p * pl.num_programs(1) + j
    x, z, g, y, c = places()
    hooks = rs_steps(
        [
            rs_plan(grads[k], outs[k], bufs[9 * k : 9 * k + 9], (sem_s, sem_r), l_sems, k, True)
            for k in range(count)
        ]
    )

    def exchange(i):
        cols = pl.ds(128 * i, 128)
        return (
            pltpu.make_async_copy(gm.at[c, :, cols], gmx.at[i, c], m_local.at[i]),
            send(gm.at[1 - c, :, cols], gmx.at[i, c], (m_send, m_recv), i, {"gc": g ^ 1}),
        )

    @pl.when(step == 0)
    def _():
        greet(all_partners())
        for i in range(3):
            for copy in exchange(i):
                copy.start()
        for hook in hooks[0]:
            hook()
        for copy in exchange(0):
            copy.wait()

    for i in (1, 2):

        @pl.when(step == 8 * i)
        def _():
            for copy in exchange(i):
                copy.wait()

    last = len(hooks) - 1
    for when in range(1, 23):
        parts = [h for i in range(1, last) if i * 22 // (last - 1) == when for h in hooks[i]]
        if parts:

            @pl.when(step == when)
            def _():
                for hook in parts:
                    hook()

    group = grp_ref[j]
    low = lax.broadcasted_iota(jnp.int32, (CL, 128), 1) < 64
    zero = jnp.zeros((CL, 128), BF)
    q = q_ref[0]
    gmix = gmx[p, j // 4, pl.ds(pl.multiple_of((j % 4) * CL, CL), CL)]
    stacks = (
        jnp.concatenate([jnp.where(low, zero, q), jnp.where(low, gmix, zero)], axis=0),
        jnp.concatenate([jnp.where(low, q, zero), jnp.where(low, zero, gmix)], axis=0),
    )

    @pl.when(z >= 2)
    def _():
        row = lax.broadcasted_iota(jnp.int32, (CL, CL), 0)
        near_ok = row <= lax.broadcasted_iota(jnp.int32, (CL, CL), 1)
        dqs = []
        for h in range(2):
            cols = slice(128 * h, 128 * h + 128)
            kv = kvp_ref[0, group, :, cols]
            kvo = kvo_ref[0, :, cols]
            lse = lse_ref[0, 0, h : h + 1, :]
            far = nt(kv, stacks[h])
            near = nt(kvo, stacks[h])
            pf = jnp.exp(far[:, :CL] - lse)
            pn = jnp.where(near_ok, jnp.exp(near[:, :CL] - lse), 0.0)
            df = far[:, CL:]
            dn = near[:, CL:]
            inner = jnp.sum(pf * df, axis=0, keepdims=True) + jnp.sum(
                pn * dn, axis=0, keepdims=True
            )
            sf = (pf * (df - inner)).astype(BF)
            sn = (pn * (dn - inner)).astype(BF)
            dkv_ref[0, :, cols] = nn(
                jnp.concatenate([sf, pf.astype(BF)], axis=1), stacks[h]
            ).astype(BF)
            dkvo_ref[:, cols] = nn(
                jnp.concatenate([sn, pn.astype(BF)], axis=1), stacks[h]
            ).astype(BF)
            dqs.append(tn(sf, kv) + tn(sn, kvo))
        dq_ref[...] = (jnp.where(low, dqs[1], dqs[0]) * 0.125).astype(BF)

    @pl.when(z < 2)
    def _():
        limit = z * QROWS + (j % (QROWS // CL)) * CL
        key = lax.broadcasted_iota(jnp.int32, (P_SIZE, CL), 0)
        row = lax.broadcasted_iota(jnp.int32, (P_SIZE, CL), 1)
        allowed = key - row <= limit
        dqs = []
        for h in range(2):
            cols = slice(128 * h, 128 * h + 128)
            kv = kvp_ref[0, group, :, cols]
            lse = lse_ref[0, 0, h : h + 1, :]
            far = nt(kv, stacks[h])
            pf = jnp.where(allowed, jnp.exp(far[:, :CL] - lse), 0.0)
            df = far[:, CL:]
            inner = jnp.sum(pf * df, axis=0, keepdims=True)
            sf = (pf * (df - inner)).astype(BF)
            dkv_ref[0, :, cols] = nn(
                jnp.concatenate([sf, pf.astype(BF)], axis=1), stacks[h]
            ).astype(BF)
            dqs.append(tn(sf, kv))
        dkvo_ref[...] = jnp.zeros_like(dkvo_ref)
        dq_ref[...] = (jnp.where(low, dqs[1], dqs[0]) * 0.125).astype(BF)

    @pl.when(step == 23)
    def _():
        for hook in hooks[last]:
            hook()


def attend_back_scatter(grp, q, lse, kvo, kvp, gm, grads, collective_id):
    rows = q.shape[1]
    count = len(grads)
    any_space = pl.BlockSpec(memory_space=pl.ANY)
    scratch = []
    for grad in grads:
        scratch += rs_scratch(grad.shape[2], grad.shape[3], True)
    slots = RS_SLOTS * count
    return pl.pallas_call(
        partial(att_scatter_kernel, count),
        name="attend_back_scatter",
        grid_spec=pltpu.PrefetchScalarGridSpec(
            num_scalar_prefetch=1,
            grid=(3, rows // CL),
            in_specs=[
                pl.BlockSpec((1, CL, 128), lambda p, j, *_: (p, j, 0)),
                pl.BlockSpec((1, 1, 2, 128), lambda p, j, *_: (p, j, 0, 0)),
                pl.BlockSpec((1, CL, 256), lambda p, j, *_: (p, j, 0)),
                pl.BlockSpec((1, 4, P_SIZE, 256), lambda p, j, *_: (p, 0, 0, 0)),
            ]
            + [any_space] * (count + 1),
            out_specs=[
                pl.BlockSpec((CL, 128), lambda p, j, *_: (j, p)),
                pl.BlockSpec((CL, 256), lambda p, j, *_: (j, p)),
                pl.BlockSpec((1, P_SIZE, 256), lambda p, j, *_: (j, 0, p)),
            ]
            + [pl.BlockSpec(grad.shape[2:], lambda p, j, *_: (0, 0)) for grad in grads],
            scratch_shapes=scratch
            + [
                pltpu.VMEM((3, 2, QROWS, 128), BF),
                pltpu.SemaphoreType.DMA((slots,)),
                pltpu.SemaphoreType.DMA((slots,)),
                pltpu.SemaphoreType.DMA((8 * count,)),
                pltpu.SemaphoreType.DMA((3,)),
                pltpu.SemaphoreType.DMA((3,)),
                pltpu.SemaphoreType.DMA((3,)),
            ],
        ),
        out_shape=[
            jax.ShapeDtypeStruct((rows, 384), BF),
            jax.ShapeDtypeStruct((rows, 768), BF),
            jax.ShapeDtypeStruct((8, P_SIZE, 768), BF),
        ]
        + [jax.ShapeDtypeStruct(grad.shape[2:], F32) for grad in grads],
        compiler_params=pltpu.CompilerParams(
            collective_id=collective_id, has_side_effects=True, vmem_limit_bytes=56 << 20
        ),
    )(grp, q, lse, kvo, kvp, gm, *grads)


def norm_rows(hidden, gain, shift):
    center = jnp.mean(hidden, axis=1, keepdims=True)
    offset = hidden - center
    factor = lax.rsqrt(jnp.mean(offset * offset, axis=1, keepdims=True) + eps)
    return offset * factor * gain + shift


CHUNKS = 4
FRONT = 13
GATHER_SLOTS = 40
SEGMENT = 4


def front_kernel(
    tokens,
    vec,
    bup,
    own,
    wq,
    block0,
    block1,
    block2,
    mixed,
    lse_ref,
    whole0,
    whole1,
    whole2,
    prompts_out,
    chip_out,
    q_out,
    kvo_out,
    kvp_out,
    wq_out,
    wkv_out,
    vec_out,
    bup_out,
    own_out,
    n1,
    vec_in,
    prompts,
    chip,
    wpair,
    q_all,
    kvo_all,
    kvp_all,
    mix,
    own_scalar,
    zs,
    zr,
    ys,
    yr,
    ds,
    dr,
    ws,
    wr,
    ss,
    sr,
    gs,
    gr_,
    ms,
    mr,
    l_sems,
    o_sems,
):
    x, z, g, y, c = places()
    sib, over_y, over_x = {"gc": g ^ 1}, {"gc": g ^ 2}, {"dp": x ^ 1}
    z_sems, y_sems, d_sems, w_sems, s_sems, g_sems = (
        (zs, zr),
        (ys, yr),
        (ds, dr),
        (ws, wr),
        (ss, sr),
        (gs, gr_),
    )
    blocks, wholes = (block0, block1, block2), (whole0, whole1, whole2)
    half_rows = wq.shape[0] // 2
    my_half = pl.ds(pl.multiple_of(x * half_rows, 16), half_rows)
    size = QROWS // CHUNKS
    first_half = jnp.where(z == 0, 0, 1)
    order = (z, z ^ 1, jnp.where(z < 2, 2, 1), jnp.where(z < 2, 3, 0))
    above, below = {"gr": jnp.minimum(z + 1, 3)}, {"gr": jnp.maximum(z - 1, 0)}
    inner = jnp.logical_and(z > 0, z < 3)

    def line(part, sems, base, b):
        return (
            (jnp.logical_and(z < 3, b <= z), send(part, part, sems, base + b, above)),
            (
                jnp.logical_and(z > 0, b >= z),
                send(part, part, sems, base + b, below, base + 4 + b),
            ),
        )

    def pass_on(copies):
        for goes, copy in copies:
            pl.when(goes)(copy.start)

    def passed_on(copies):
        for goes, copy in copies:
            pl.when(goes)(copy.wait_send)

    local_copy = pltpu.make_async_copy

    def small(kind, s):
        if kind == 0:
            return send(vec, vec_in.at[s], s_sems, s, {"gr": z ^ s})
        if kind == 1:
            return send(own, own_out.at[z], s_sems, 3 + s, {"gr": z ^ s})
        return send(bup, bup_out.at[g], s_sems, 6 + s, {"gc": g ^ s})

    def chip_send():
        return send(n1, chip.at[c], s_sems, 10, sib)

    def w_local():
        return local_copy(wq.at[my_half], wpair.at[y, z, my_half], l_sems.at[0])

    def w_line(s):
        return line(wpair.at[y, order[s], my_half], w_sems, 0, order[s])

    def w_gc(s):
        piece = wpair.at[y, order[s], my_half]
        return send(piece, piece, w_sems, 8 + s, over_y)

    def w_dp(s):
        piece = wpair.at[y, order[s], my_half]
        return send(piece, piece, w_sems, 12 + s, over_x)

    def w_dp_far(s):
        piece = wpair.at[1 - y, order[s], my_half]
        return send(piece, piece, w_sems, 16 + s, over_x)

    def chunk(number):
        return jnp.where(number < CHUNKS, first_half, 1 - first_half), number % CHUNKS

    def item(column, number):
        half, k = chunk(number)
        return prompts.at[column, half, pl.ds(pl.multiple_of(k * size, size), size)]

    def up(number):
        half, k = chunk(number)
        ref = item(g, number)
        return send(ref, ref, z_sems, half * CHUNKS + k, {"gr": jnp.minimum(z + 1, 3)})

    def down(number):
        half, k = chunk(number)
        ref = item(g, number)
        return send(
            ref,
            ref,
            z_sems,
            half * CHUNKS + k,
            {"gr": jnp.maximum(z - 1, 0)},
            2 * CHUNKS + k,
        )

    def side(number):
        half, k = chunk(number)
        ref = item(g, number)
        return send(ref, ref, y_sems, half * CHUNKS + k, over_y)

    def core(number, far):
        half, k = chunk(number)
        ref = item(g ^ 2 if far else g, number)
        return send(ref, ref, d_sems, far * 2 * CHUNKS + half * CHUNKS + k, sib)

    def goes_up(number):
        return jnp.logical_and(z < 3, chunk(number)[0] <= z)

    def goes_down(number):
        return jnp.logical_and(z == 1, chunk(number)[0] == 1)

    def forward(number):
        @pl.when(chunk(number)[0] != z)
        def _():
            up(number).wait_recv()

        @pl.when(goes_up(number))
        def _():
            up(number).start()

        @pl.when(goes_down(number))
        def _():
            down(number).start()

        side(number).start()
        core(number, 0).start()

    def across(number):
        side(number).wait_recv()
        core(number, 1).start()

    def plan(a, s):
        block, whole = blocks[a], wholes[a]
        q = block.shape[0] // 4
        half = pl.ds(pl.multiple_of(x * 2 * q, 16), 2 * q)
        qa = pl.ds(pl.multiple_of(x * 2 * q, 16), q)
        qb = pl.ds(pl.multiple_of(x * 2 * q + q, 16), q)
        qc = pl.ds(pl.multiple_of((1 - x) * 2 * q + q, 16), q)
        base = a * GATHER_SLOTS
        mine, far = whole.at[g, order[s]], whole.at[g ^ 2, order[s]]
        o = base + 8 + 8 * s

        def same(part, number, target):
            return lambda: send(part, part, g_sems, o + number, target)

        return {
            "line": lambda: line(mine.at[half], g_sems, base, order[s]),
            "ay": same(mine.at[qa], 0, over_y),
            "ax": same(mine.at[qa], 1, over_x),
            "afx": same(far.at[qa], 2, over_x),
            "bx": same(mine.at[qb], 3, over_x),
            "by": same(mine.at[qb], 4, over_y),
            "bfy": same(mine.at[qc], 5, over_y),
            "bfx": same(far.at[qb], 5, over_x),
            "c1": same(mine, 6, sib),
            "c2": same(far, 7, sib),
        }

    def own_block(a):
        return local_copy(blocks[a], wholes[a].at[g, z], l_sems.at[4 + a])

    def names(s):
        return ("ay", "ax", "afx", "bx", "by", "bfy") if s else ("ay", "afx", "by", "bfx")

    def relay(s):
        @pl.when(inner)
        def _():
            for a in range(3):
                copies = plan(a, s)["line"]()
                copies[0][1].wait_recv()
                pass_on(copies)


    def gather_first(s):
        for a in range(3):
            m = plan(a, s)
            if s:
                pl.when(jnp.logical_not(inner))(m["line"]()[0][1].wait_recv)
                m["bx"]().start()
                m["ax"]().start()
            m["ay"]().start()
            m["by"]().start()

    def gather_second(s):
        for a in range(3):
            m = plan(a, s)
            m["ay"]().wait_recv()
            m["afx"]().start()
            if s:
                m["bx"]().wait_recv()
                m["bfy"]().start()
            else:
                m["by"]().wait_recv()
                m["bfx"]().start()

    def gather_third(s):
        for a in range(3):
            m = plan(a, s)
            for name in ("ax", "afx", "by", "bfy") if s else ("afx", "bfx"):
                m[name]().wait_recv()
            m["c1"]().start()
            m["c2"]().start()

    def out_copies():
        return [
            local_copy(prompts, prompts_out, o_sems.at[0]),
            local_copy(chip, chip_out, o_sems.at[1]),
            local_copy(q_all, q_out, o_sems.at[2]),
            local_copy(kvo_all, kvo_out, o_sems.at[3]),
            local_copy(kvp_all, kvp_out, o_sems.at[4]),
        ]

    def exchange(i):
        cols = pl.ds(128 * i, 128)
        return (
            local_copy(mix.at[i, c], mixed.at[c, :, cols], l_sems.at[7 + i]),
            send(mix.at[i, 1 - c], mixed.at[c, :, cols], (ms, mr), i, sib),
        )

    hooks = {i: [] for i in range(FRONT)}

    def begin():
        greet(all_partners() + [{"gc": g ^ 3}])
        w_local().start()
        for s in (1, 2, 3):
            for kind in range(3):
                small(kind, s).start()
        w_local().wait()
        pass_on(w_line(0))
        own_out[z] = own[...]
        bup_out[g] = bup[...]
        for s in (1, 2, 3):
            small(0, s).wait_recv()
        vec_out[...] = (vec[...] + vec_in[1]) + (vec_in[2] + vec_in[3])

        @pl.loop(0, CHUNKS)
        def _(i):
            rows = pl.ds(pl.multiple_of(i * size, size), size)
            hidden = tokens[rows].astype(F32) + vec_out[0:1]
            n1[rows] = norm_rows(hidden, vec_out[1:2], vec_out[2:3]).astype(BF)

        @pl.when(z < 2)
        def _():
            to = local_copy(n1, prompts.at[g, jnp.minimum(z, 1)], l_sems.at[2])
            to.start()
            to.wait()

    def begin_chip():
        local_copy(n1, chip.at[c], l_sems.at[1]).start()
        chip_send().start()
        w_gc(0).start()
        w_dp(0).start()

    hooks[0] += [begin, partial(forward, 0), begin_chip]
    for i in range(1, 8):
        hooks[i].append(partial(forward, i))
    for i in range(2, 10):
        hooks[i].append(partial(across, i - 2))

    def w_pass(s):
        copies = w_line(s)
        copies[0][1].wait_recv()
        pass_on(copies)
        w_gc(s).start()
        w_dp(s).start()

    def w_across(s):
        w_gc(s).wait_recv()
        w_dp_far(s).start()

    for s in (1, 2, 3):
        hooks[s].append(partial(w_pass, s))
    hooks[2].append(partial(w_across, 0))
    hooks[3] += [partial(w_across, 1)]
    hooks[4] += [partial(w_across, 2), partial(w_across, 3)]

    def assemble():
        for s in range(4):
            w_dp(s).wait_recv()
            w_dp_far(s).wait_recv()
        local_copy(n1, chip.at[c], l_sems.at[1]).wait()
        chip_send().wait_recv()
        for s in (1, 2, 3):
            small(1, s).wait_recv()
        to = local_copy(own_out, own_scalar, l_sems.at[3])
        to.start()
        for head in range(6):
            p, b = head // 2, head % 2
            at_q = 128 * p + (0 if b else 64)
            at_k = 256 * p + (128 if b else 64)
            at_v = 256 * p + (192 if b else 0)
            start = (head % 3) * 192
            for r in range(4):
                rows = slice(192 * r, 192 * r + 192)
                source = wpair.at[head // 3, r]
                wq_out[rows, at_q : at_q + HD] = source[:, start : start + HD]
                wkv_out[rows, at_k : at_k + HD] = source[:, start + HD : start + 2 * HD]
                wkv_out[rows, at_v : at_v + HD] = source[:, start + 2 * HD : start + 3 * HD]
        to.wait()

    hooks[5].append(assemble)

    def project(number):
        core(number, 0).wait_recv()
        core(number, 1).wait_recv()
        half, k = chunk(number)
        w = wkv_out[...]
        rows = jnp.concatenate(
            [
                prompts[i, half, pl.ds(pl.multiple_of(k * size, size), size)]
                for i in range(4)
            ],
            axis=0,
        )
        kv = nn(rows, w).astype(BF)
        to = pl.ds(pl.multiple_of(half * QROWS + k * size, size), size)
        for i in range(4):
            for p in range(3):
                kvp_all[p, i, to] = kv[size * i : size * i + size, 256 * p : 256 * p + 256]
        mine = chip[number // CHUNKS, pl.ds(pl.multiple_of(k * size, size), size)]
        kvo = nn(mine, w).astype(BF)
        queries = (nn(mine, wq_out[...]) * 0.125).astype(BF)
        to = pl.ds(pl.multiple_of(number * size, size), size)
        for p in range(3):
            kvo_all[p, to] = kvo[:, 256 * p : 256 * p + 256]
            q_all[p, to] = queries[:, 128 * p : 128 * p + 128]


    def own_first():
        for a in range(3):
            own_block(a).start()

    def own_down():
        for a in range(3):
            own_block(a).wait()
            goes, copy = plan(a, 0)["line"]()[1]
            pl.when(goes)(copy.start)

    def own_up():
        for a in range(3):
            goes, copy = plan(a, 0)["line"]()[0]
            pl.when(goes)(copy.start)

    hooks[0].append(own_first)
    hooks[1].append(own_down)
    hooks[9].append(own_up)
    hooks[8].append(partial(gather_first, 0))
    hooks[10].append(partial(gather_second, 0))
    between = [[] for _ in range(24 // SEGMENT + 1)]
    last = len(between) - 1
    between[0] += [lambda: [copy.start() for copy in out_copies()], partial(gather_third, 0)]
    hooks[10].append(partial(relay, 1))
    hooks[12].append(partial(relay, 2))
    for slot, stage, s in (
        (0, relay, 3),
        (0, gather_first, 1),
        (1, gather_first, 2),
        (1, gather_second, 1),
        (2, gather_first, 3),
        (2, gather_second, 2),
        (3, gather_third, 1),
        (3, gather_second, 3),
        (4, gather_third, 2),
        (6, gather_third, 3),
    ):
        between[slot].append(partial(stage, s))

    for number in range(FRONT - 8):
        for hook in hooks[number]:
            hook()

    def one_piece(number, carried):
        for i in range(FRONT - 8, FRONT):
            if hooks[i]:

                @pl.when(number == i)
                def _():
                    for hook in hooks[i]:
                        hook()

        project(number - (FRONT - 8))
        return carried

    lax.fori_loop(FRONT - 8, FRONT, one_piece, 0)

    low = lax.broadcasted_iota(jnp.int32, (CL, 128), 1) < 64

    def parts(turn):
        p, j = turn // 8, turn % 8
        shard = 2 * y + j // 4
        group = jnp.where(
            z < 2, shard, own_scalar[shard, 0, jnp.maximum(z - 2, 0) * 4 + j % 4]
        )
        rows_j = pl.ds(pl.multiple_of(j * CL, CL), CL)
        zero = jnp.zeros((CL, 128), BF)
        q = q_all[p, rows_j]
        return p, j, group, rows_j, (jnp.where(low, zero, q), jnp.where(low, q, zero))

    def store(p, j, mixes, sums):
        mix[p, j // 4, pl.ds(pl.multiple_of((j % 4) * CL, CL), CL)] = jnp.where(
            low, mixes[0], mixes[1]
        ).astype(BF)
        flat = jnp.where(low, sums[0], sums[1]).T
        lse_ref[p, j, 0:1] = flat[0:1]
        lse_ref[p, j, 1:2] = flat[64:65]

    def cont_turn(turn, carried):
        p, j, group, rows_j, q_parts = parts(turn)
        row = lax.broadcasted_iota(jnp.int32, (CL, CL), 0)
        near_ok = lax.broadcasted_iota(jnp.int32, (CL, CL), 1) <= row
        mixes, sums = [], []
        for h in range(2):
            cols = slice(128 * h, 128 * h + 128)
            kv = kvp_all[p, group, :, cols]
            kvo = kvo_all[p, rows_j, cols]
            far = nt(q_parts[h], kv)
            near = jnp.where(near_ok, nt(q_parts[h], kvo), negative)
            top = jnp.maximum(
                jnp.max(far, axis=1, keepdims=True), jnp.max(near, axis=1, keepdims=True)
            )
            far = jnp.exp(far - top)
            near = jnp.exp(near - top)
            total = jnp.sum(far, axis=1, keepdims=True) + jnp.sum(near, axis=1, keepdims=True)
            mixes.append((nn(far.astype(BF), kv) + nn(near.astype(BF), kvo)) / total)
            sums.append(jnp.broadcast_to(top + jnp.log(total), (CL, 128)))
        store(p, j, mixes, sums)
        return carried

    def prompt_turn(turn, carried):
        p, j, group, rows_j, q_parts = parts(turn)
        limit = z * QROWS + (j % (QROWS // CL)) * CL
        row = lax.broadcasted_iota(jnp.int32, (CL, P_SIZE), 0)
        key = lax.broadcasted_iota(jnp.int32, (CL, P_SIZE), 1)
        allowed = key - row <= limit
        mixes, sums = [], []
        for h in range(2):
            cols = slice(128 * h, 128 * h + 128)
            kv = kvp_all[p, group, :, cols]
            far = jnp.where(allowed, nt(q_parts[h], kv), negative)
            top = jnp.max(far, axis=1, keepdims=True)
            far = jnp.exp(far - top)
            total = jnp.sum(far, axis=1, keepdims=True)
            mixes.append(nn(far.astype(BF), kv) / total)
            sums.append(jnp.broadcast_to(top + jnp.log(total), (CL, 128)))
        store(p, j, mixes, sums)
        return carried

    def one_turn(turn, carried):
        for segment in range(last):

            @pl.when(turn == segment * SEGMENT)
            def _():
                for hook in between[segment]:
                    hook()

        @pl.when(z >= 2)
        def _():
            cont_turn(turn, 0)

        @pl.when(z < 2)
        def _():
            prompt_turn(turn, 0)

        for i in range(3):

            @pl.when(turn == 8 * i + 7)
            def _():
                for copy in exchange(i):
                    copy.start()

        return carried

    lax.fori_loop(0, 24, one_turn, 0)
    for hook in between[last]:
        hook()

    for number in range(8):
        side(number).wait_send()
        core(number, 0).wait_send()
        core(number, 1).wait_send()

        @pl.when(goes_up(number))
        def _():
            up(number).wait_send()

        @pl.when(goes_down(number))
        def _():
            down(number).wait_send()

    for s in range(4):
        if s:
            small(0, s).wait_send()
            small(1, s).wait_send()
            small(2, s).wait()
        passed_on(w_line(s))
        w_gc(s).wait_send()
        w_dp(s).wait_send()
        w_dp_far(s).wait_send()
    chip_send().wait_send()
    for s in range(4):
        for a in range(3):
            m = plan(a, s)
            passed_on(m["line"]())
            for name in names(s):
                m[name]().wait_send()
            m["c1"]().wait()
            m["c2"]().wait()
    for i in range(3):
        for copy in exchange(i):
            copy.wait()
    for copy in out_copies():
        copy.wait()


def front(tokens, vec, bup, own, wq, blocks, collective_id):
    any_space = pl.BlockSpec(memory_space=pl.ANY)
    vmem = pl.BlockSpec(memory_space=pltpu.VMEM)
    rows = 2 * QROWS

    def dma(count):
        return pltpu.SemaphoreType.DMA((count,))

    slots = 3 * GATHER_SLOTS
    heads = [(3, rows, 128), (3, rows, 256), (3, 4, P_SIZE, 256)]
    return pl.pallas_call(
        front_kernel,
        name="front",
        in_specs=[vmem, vmem, vmem, vmem] + [any_space] * 4,
        out_specs=[any_space, vmem]
        + [any_space] * 8
        + [vmem] * 5,
        out_shape=[
            jax.ShapeDtypeStruct((2, QROWS, 384), BF),
            jax.ShapeDtypeStruct((3, rows // CL, 2, 128), F32),
        ]
        + [jax.ShapeDtypeStruct((4, 4) + block.shape, BF) for block in blocks]
        + [
            jax.ShapeDtypeStruct((4, 2, QROWS, D), BF),
            jax.ShapeDtypeStruct((2, QROWS, D), BF),
        ]
        + [jax.ShapeDtypeStruct(shape, BF) for shape in heads]
        + [
            jax.ShapeDtypeStruct((D, 384), BF),
            jax.ShapeDtypeStruct((D, D), BF),
            jax.ShapeDtypeStruct(vec.shape, F32),
            jax.ShapeDtypeStruct((4,) + bup.shape, F32),
            jax.ShapeDtypeStruct((4,) + own.shape, jnp.int32),
        ],
        scratch_shapes=[
            pltpu.VMEM((QROWS, D), BF),
            pltpu.VMEM((4,) + vec.shape, F32),
            pltpu.VMEM((4, 2, QROWS, D), BF),
            pltpu.VMEM((2, QROWS, D), BF),
            pltpu.VMEM((2, 4) + wq.shape, BF),
        ]
        + [pltpu.VMEM(shape, BF) for shape in heads]
        + [
            pltpu.VMEM((3, 2, QROWS, 128), BF),
            pltpu.SMEM((4,) + own.shape, jnp.int32),
            dma(3 * CHUNKS),
            dma(2 * CHUNKS),
            dma(2 * CHUNKS),
            dma(2 * CHUNKS),
            dma(4 * CHUNKS),
            dma(4 * CHUNKS),
            dma(20),
            dma(20),
            dma(11),
            dma(11),
            dma(slots),
            dma(slots),
            dma(3),
            dma(3),
            dma(10),
            dma(5),
        ],
        compiler_params=pltpu.CompilerParams(
            collective_id=collective_id, has_side_effects=True, vmem_limit_bytes=56 << 20
        ),
    )(tokens, vec, bup, own, wq, *blocks)


def tail_kernel(
    grp,
    dkv,
    n1p,
    n1c,
    dkvo,
    dq,
    w_q,
    w_kv,
    grad_h2,
    tokens,
    vec,
    sums,
    out,
    sums_out,
    dw_out,
    part,
    chip,
    tiles,
    rows_p,
    low,
    wkt,
    wqt,
    dkvw,
    dqw,
    dw,
    ra,
    rb,
    rz,
    take,
    gsum,
    cur,
    sb,
    *rest,
):
    bufs, (sem_s, sem_r, l_sems, w_s, w_r, w_l) = rest[:9], rest[9:]
    sems = (sem_s, sem_r)
    x, z, g, y, c = places()
    sib, over_y, over_x = {"gc": g ^ 1}, {"gc": g ^ 2}, {"dp": x ^ 1}
    down = {"gr": jnp.maximum(z - 1, 0)}
    far = z >= 2
    size = QROWS // CHUNKS
    count = 2 * CHUNKS

    def fetch(t):
        rows = pl.ds(pl.multiple_of(t * size, size), size)
        h, r = t // CHUNKS, pl.ds(pl.multiple_of((t % CHUNKS) * size, size), size)
        slot = t % 2
        return (
            pltpu.make_async_copy(dkv.at[:, rows], tiles.at[slot], l_sems.at[slot]),
            pltpu.make_async_copy(n1p.at[:, h, r], rows_p.at[slot], l_sems.at[2 + slot]),
        )

    for copy in fetch(0):
        copy.start()
    greet(all_partners())
    wkt[...] = w_kv[...].T
    wqt[...] = w_q[...].T
    dkvw[...] = jnp.zeros_like(dkvw)
    dqw[...] = jnp.zeros_like(dqw)

    def at(t):
        return t // CHUNKS, pl.ds(pl.multiple_of((t % CHUNKS) * size, size), size)

    def mine(side, t):
        h, r = at(t)
        return part.at[2 * (1 - y if side == 0 else y) + c, h, r]

    def hop_a(side, t):
        h, r = at(t)
        i = 1 - y if side == 0 else y
        return send(part.at[2 * i + 1 - c, h, r], ra.at[i, h, r], sems, 8 * side + t, sib)

    def hop_y(t):
        h, r = at(t)
        return send(mine(0, t), rb.at[h, r], sems, 16 + t, over_y)

    def hop_z(t):
        h, r = at(t)
        return send(mine(1, t), rz.at[h, r], sems, 24 + t, down)

    hop_chip = send(chip.at[1 - c], take, sems, 32, sib)

    def fold(t, other):
        h, r = at(t)
        add_into(mine(1, t), mine(1, t), other.at[r])

    def stage0(t):
        slot = t % 2
        for copy in fetch(t):
            copy.wait()

        @pl.when(t + 1 < count)
        def _():
            for copy in fetch(t + 1):
                copy.start()

        weights = [
            [jnp.where(grp[j] == i, 1.0, 0.0).astype(F32) for j in range(8)] for i in range(4)
        ]

        @pl.loop(0, size // 16)
        def _(q):
            r = pl.ds(pl.multiple_of(q * 16, 16), 16)
            pieces = [tiles[slot, j, r].astype(F32) for j in range(8)]
            for i in range(4):
                total = weights[i][0] * pieces[0]
                for j in range(1, 8):
                    total = total + weights[i][j] * pieces[j]
                low[i, r] = total.astype(BF)

        whole = low[...].reshape(4 * size, D)
        grads = nn(whole, wkt[...]).astype(BF)
        h, r = at(t)
        for i in range(4):
            part[i, h, r] = grads[size * i : size * i + size]

        @pl.when(far)
        def _():
            hop_a(0, t).start()

        hop_a(1, t).start()
        own = pl.ds(pl.multiple_of(t * size, size), size)
        near, grad_q, rows_c = dkvo[own], dq[own], n1c[own]
        chip[h, r] = (nn(grad_q, wqt[...]) + nn(near, wkt[...])).astype(BF)
        rows = jnp.concatenate([rows_p[slot].reshape(4 * size, D), rows_c], axis=0)
        dkvw[...] += tn(rows, jnp.concatenate([whole, near], axis=0))
        dqw[...] += tn(rows_c, grad_q)

    def stage1(t):
        h, r = at(t)

        @pl.when(far)
        def _():
            hop_a(0, t).wait()
            add_into(mine(0, t), mine(0, t), ra.at[1 - y, h, r])
            hop_y(t).start()

        hop_a(1, t).wait()
        fold(t, ra.at[y, h])

    def stage2(t):
        @pl.when(far)
        def _():
            hop_y(t).wait()
            fold(t, rb.at[t // CHUNKS])

        @pl.when(z == 3)
        def _():
            hop_z(t).start()

    def stage3(t):
        @pl.when(z == 2)
        def _():
            hop_z(t).wait_recv()
            fold(t, rz.at[t // CHUNKS])
            hop_z(t).start()

    def stage4(t):
        @pl.when(z == 1)
        def _():
            hop_z(t).wait_recv()
            fold(t, rz.at[t // CHUNKS])

            @pl.when(t < CHUNKS)
            def _():
                hop_z(t).start()

    def stage5(t):
        @pl.when(jnp.logical_and(z == 0, t < CHUNKS))
        def _():
            hop_z(t).wait_recv()
            fold(t, rz.at[0])

    def stages(t, carried, skip=0):
        todo = list(zip((0, 1, 3, 5, 7, 9), (stage0, stage1, stage2, stage3, stage4, stage5)))
        for lag, stage in todo[skip:]:

            @pl.when(jnp.logical_and(t >= lag, t < count + lag))
            def _():
                stage(t - lag)

        return carried

    lax.fori_loop(0, count, stages, 0)
    hop_chip.start()

    for head in range(6):
        p, b = head // 2, head % 2
        places_in = (
            dqw[:, 128 * p + (0 if b else 64) : 128 * p + (64 if b else 128)],
            dkvw[:, 256 * p + (128 if b else 64) : 256 * p + (192 if b else 128)],
            dkvw[:, 256 * p + (192 if b else 0) : 256 * p + (256 if b else 64)],
        )
        for i, piece in enumerate(places_in):
            at_col = (head % 3) * 192 + HD * i
            for r in range(4):
                dw[head // 3, r, :, at_col : at_col + HD] = piece[192 * r : 192 * r + 192].astype(
                    BF
                )
    begin, after_a, after_b, after_c, total, finish = rs_plan(
        dw, dw_out, bufs, (w_s, w_r), w_l, 0, False
    )
    for s in RS_ORDER:
        begin(s)
    for s in RS_ORDER:
        after_a(s)
    lax.fori_loop(count, count + 3, partial(stages, skip=1), 0)
    for s in RS_ORDER:
        after_b(s)
    lax.fori_loop(count + 3, count + 9, partial(stages, skip=2), 0)
    for s in RS_ORDER:
        after_c(s)

    @pl.loop(0, count)
    def _(t):
        @pl.when(jnp.logical_or(z >= 2, jnp.logical_and(z == 1, t < CHUNKS)))
        def _():
            hop_z(t).wait_send()

    hop_chip.wait()

    cur[...] = sums[...]

    @pl.loop(0, CHUNKS)
    def _(k):
        r = pl.ds(pl.multiple_of(k * size, size), size)
        gsum[r] = chip[c, r].astype(F32) + take[r].astype(F32)

        @pl.when(z < 2)
        def _():
            gsum[r] += part[2 * y + c, jnp.minimum(z, 1), r].astype(F32)

        hidden = tokens[r].astype(F32) + vec[0:1]
        center = jnp.mean(hidden, axis=1, keepdims=True)
        offset = hidden - center
        factor = lax.rsqrt(jnp.mean(offset * offset, axis=1, keepdims=True) + eps)
        unit = offset * factor
        grad = gsum[r]
        scaled = grad * vec[1:2]
        first = jnp.mean(scaled, axis=1, keepdims=True)
        second = jnp.mean(scaled * unit, axis=1, keepdims=True)
        result = grad_h2[r] + factor * (scaled - first - unit * second)
        out[r] = result
        cur[0:1] += jnp.sum(result, axis=0, keepdims=True)
        cur[1:2] += jnp.sum(grad * unit, axis=0, keepdims=True)
        cur[2:3] += jnp.sum(grad, axis=0, keepdims=True)

    for i, target in enumerate((sib, over_y, over_x)):
        hop = send(cur, sb.at[i], sems, 33 + i, target)
        hop.start()
        hop.wait()
        cur[...] += sb[i]
        if i == 1:
            total()
    hops = [send(cur, sb.at[2 + s], sems, 35 + s, {"gr": z ^ s}) for s in (1, 2, 3)]
    for hop in hops:
        hop.start()
    finish()
    for hop in hops:
        hop.wait()
    sums_out[...] = (cur[...] + sb[3]) + (sb[4] + sb[5])


def tail_exchange(
    grp, dkv, n1p, n1c, dkvo, dq, w_q, w_kv, grad_h2, tokens, vec, sums, collective_id
):
    any_space = pl.BlockSpec(memory_space=pl.ANY)
    vmem = pl.BlockSpec(memory_space=pltpu.VMEM)
    block = (2, 4, 192, 576)
    return pl.pallas_call(
        tail_kernel,
        name="tail_exchange",
        in_specs=[pl.BlockSpec(memory_space=pltpu.SMEM), any_space, any_space] + [vmem] * 9,
        out_specs=[vmem, vmem, vmem],
        out_shape=[
            jax.ShapeDtypeStruct((QROWS, D), F32),
            jax.ShapeDtypeStruct(sums.shape, F32),
            jax.ShapeDtypeStruct(block[2:], F32),
        ],
        scratch_shapes=[
            pltpu.VMEM((4, 2, QROWS, D), BF),
            pltpu.VMEM((2, QROWS, D), BF),
            pltpu.VMEM((2, 8, CL, D), BF),
            pltpu.VMEM((2, 4, CL, D), BF),
            pltpu.VMEM((4, CL, D), BF),
            pltpu.VMEM((D, D), BF),
            pltpu.VMEM((384, D), BF),
            pltpu.VMEM((D, D), F32),
            pltpu.VMEM((D, 384), F32),
            pltpu.VMEM(block, BF),
            pltpu.VMEM((2, 2, QROWS, D), BF),
            pltpu.VMEM((2, QROWS, D), BF),
            pltpu.VMEM((2, QROWS, D), BF),
            pltpu.VMEM((QROWS, D), BF),
            pltpu.VMEM((QROWS, D), F32),
            pltpu.VMEM(sums.shape, F32),
            pltpu.VMEM((6,) + sums.shape, F32),
        ]
        + rs_scratch(block[2], block[3], False)
        + [
            pltpu.SemaphoreType.DMA((39,)),
            pltpu.SemaphoreType.DMA((39,)),
            pltpu.SemaphoreType.DMA((4,)),
            pltpu.SemaphoreType.DMA((RS_SLOTS,)),
            pltpu.SemaphoreType.DMA((RS_SLOTS,)),
            pltpu.SemaphoreType.DMA((8,)),
        ],
        compiler_params=pltpu.CompilerParams(
            collective_id=collective_id, has_side_effects=True, vmem_limit_bytes=60 << 20
        ),
    )(grp, dkv, n1p, n1c, dkvo, dq, w_q, w_kv, grad_h2, tokens, vec, sums)


GELU_IN = math.sqrt(2.0 / math.pi)


def middle_kernel(
    mixed,
    w_out_g,
    w_up,
    w_down,
    tokens,
    teacher,
    vec,
    b_up,
    final_out,
    grad_h2,
    dw_up,
    dw_down,
    dw_out,
    gm,
    sums,
    wo,
    wu,
    wd,
    h2,
    n2,
    n2t,
    act,
    slope,
    gf,
    gb,
    gbt,
    acc,
    du,
    dd,
    l_sems,
    o_sems,
):
    loads_u = [pltpu.make_async_copy(w_up.at[b], wu.at[b], l_sems.at[b]) for b in range(4)]
    loads_d = [pltpu.make_async_copy(w_down.at[b], wd.at[b], l_sems.at[4 + b]) for b in range(4)]
    for b in range(4):
        loads_u[b].start()
        loads_d[b].start()
    for k in range(2):
        for i in range(2):
            for r in range(4):
                wo[k, 192 * i : 192 * i + 192, 192 * r : 192 * r + 192] = w_out_g[2 * i + k, r]

    @pl.loop(0, 2)
    def _(t):
        r = pl.ds(pl.multiple_of(t * 256, 256), 256)
        hidden = tokens[r].astype(F32) + vec[0:1]
        attended = nn(mixed[0, r], wo[0]) + nn(mixed[1, r], wo[1])
        total = hidden + attended + vec[3:4]
        h2[r] = total
        n2[r] = norm_rows(total, vec[4:5], vec[5:6]).astype(BF)

    n2t[...] = n2[...].T
    acc[...] = jnp.zeros_like(acc)
    for copy in loads_u + loads_d:
        copy.wait()

    @pl.loop(0, 4)
    def _(b):
        @pl.loop(0, 2)
        def _(t):
            r = pl.ds(pl.multiple_of(t * 256, 256), 256)
            pre = nn(n2[r], wu[b]) + b_up[b, 0:1]
            square = pre * pre
            tanh = jnp.tanh(GELU_IN * pre * (1.0 + 0.044715 * square))
            half = 0.5 * (1.0 + tanh)
            low = (pre * half).astype(BF)
            act[b, r] = low
            slope[b, r] = half + (0.5 * GELU_IN) * pre * (1.0 - tanh * tanh) * (
                1.0 + (3.0 * 0.044715) * square
            )
            acc[r] += nt(low, wd[b])

    sums[...] = jnp.zeros_like(sums)

    @pl.loop(0, 2)
    def _(t):
        r = pl.ds(pl.multiple_of(t * 256, 256), 256)
        final = h2[r] + acc[r] + vec[6:7]
        final_out[r] = final.astype(BF)
        diff = final - teacher[r].astype(F32)
        gf[r] = diff
        low = diff.astype(BF)
        gb[r] = low
        sums[6:7] += jnp.sum(low.astype(F32), axis=0, keepdims=True)
        sums[11:12] += jnp.sum(diff * diff, axis=0, keepdims=True)

    gbt[...] = gb[...].T
    acc[...] = jnp.zeros_like(acc)

    @pl.loop(0, 4)
    def _(b):
        dd[b] = nn(gbt[...], act[b]).astype(BF)
        pltpu.make_async_copy(dd.at[b], dw_down.at[b], o_sems.at[b]).start()

        @pl.loop(0, 2)
        def _(t):
            r = pl.ds(pl.multiple_of(t * 256, 256), 256)
            low = (nn(gb[r], wd[b]) * slope[b, r]).astype(BF)
            act[b, r] = low
            sums[pl.ds(7 + b, 1)] += jnp.sum(low.astype(F32), axis=0, keepdims=True)
            acc[r] += nt(low, wu[b])

        du[b] = nn(n2t[...], act[b]).astype(BF)
        pltpu.make_async_copy(du.at[b], dw_up.at[b], o_sems.at[4 + b]).start()

    @pl.loop(0, 2)
    def _(t):
        r = pl.ds(pl.multiple_of(t * 256, 256), 256)
        hidden = h2[r]
        center = jnp.mean(hidden, axis=1, keepdims=True)
        offset = hidden - center
        factor = lax.rsqrt(jnp.mean(offset * offset, axis=1, keepdims=True) + eps)
        unit = offset * factor
        grad = acc[r]
        scaled = grad * vec[4:5]
        first = jnp.mean(scaled, axis=1, keepdims=True)
        second = jnp.mean(scaled * unit, axis=1, keepdims=True)
        total = gf[r] + factor * (scaled - first - unit * second)
        grad_h2[r] = total
        low = total.astype(BF)
        gb[r] = low
        sums[3:4] += jnp.sum(grad * unit, axis=0, keepdims=True)
        sums[4:5] += jnp.sum(grad, axis=0, keepdims=True)
        sums[5:6] += jnp.sum(low.astype(F32), axis=0, keepdims=True)
        gm[0, r] = nt(low, wo[0]).astype(BF)
        gm[1, r] = nt(low, wo[1]).astype(BF)

    for k in range(2):
        whole = tn(mixed[k], gb[...]).astype(BF)
        for i in range(2):
            for r in range(4):
                dw_out[2 * i + k, r] = whole[192 * i : 192 * i + 192, 192 * r : 192 * r + 192]
    for b in range(4):
        pltpu.make_async_copy(dd.at[b], dw_down.at[b], o_sems.at[b]).wait()
        pltpu.make_async_copy(du.at[b], dw_up.at[b], o_sems.at[4 + b]).wait()


def middle(mixed, w_out_g, w_up, w_down, tokens, teacher, vec, b_up):
    any_space = pl.BlockSpec(memory_space=pl.ANY)
    vmem = pl.BlockSpec(memory_space=pltpu.VMEM)
    blocks = (4, D, D)
    return pl.pallas_call(
        middle_kernel,
        name="middle",
        in_specs=[vmem, vmem, any_space, any_space, vmem, vmem, vmem, vmem],
        out_specs=[vmem, vmem, any_space, any_space, vmem, vmem, vmem],
        out_shape=[
            jax.ShapeDtypeStruct((QROWS, D), BF),
            jax.ShapeDtypeStruct((QROWS, D), F32),
            jax.ShapeDtypeStruct(blocks, BF),
            jax.ShapeDtypeStruct(blocks, BF),
            jax.ShapeDtypeStruct((4, 4, 192, 192), BF),
            jax.ShapeDtypeStruct((2, QROWS, 384), BF),
            jax.ShapeDtypeStruct((16, D), F32),
        ],
        scratch_shapes=[
            pltpu.VMEM((2, 384, D), BF),
            pltpu.VMEM(blocks, BF),
            pltpu.VMEM(blocks, BF),
            pltpu.VMEM((QROWS, D), F32),
            pltpu.VMEM((QROWS, D), BF),
            pltpu.VMEM((D, QROWS), BF),
            pltpu.VMEM((4, QROWS, D), BF),
            pltpu.VMEM((4, QROWS, D), F32),
            pltpu.VMEM((QROWS, D), F32),
            pltpu.VMEM((QROWS, D), BF),
            pltpu.VMEM((D, QROWS), BF),
            pltpu.VMEM((QROWS, D), F32),
            pltpu.VMEM(blocks, BF),
            pltpu.VMEM(blocks, BF),
            pltpu.SemaphoreType.DMA((8,)),
            pltpu.SemaphoreType.DMA((8,)),
        ],
        compiler_params=pltpu.CompilerParams(vmem_limit_bytes=60 << 20),
    )(mixed, w_out_g, w_up, w_down, tokens, teacher, vec, b_up)


def norm(hidden, gain, shift):
    center = jnp.mean(hidden, axis=1, keepdims=True)
    offset = hidden - center
    factor = lax.rsqrt(jnp.mean(offset * offset, axis=1, keepdims=True) + eps)
    unit = offset * factor
    return unit * gain + shift, unit, factor


def norm_back(grad, gain, unit, factor):
    grad_unit = grad * gain
    first = jnp.mean(grad_unit, axis=1, keepdims=True)
    second = jnp.mean(grad_unit * unit, axis=1, keepdims=True)
    grad_in = factor * (grad_unit - first - unit * second)
    return grad_in, jnp.sum(grad * unit, axis=0), jnp.sum(grad, axis=0)


def head_layout(blocks):
    chunks = blocks.transpose(1, 0, 2).reshape(D, 6, 3, HD)
    q_list, kv_list = [], []
    for pair in range(3):
        a, b = 2 * pair, 2 * pair + 1
        q_list += [chunks[:, b, 0], chunks[:, a, 0]]
        kv_list += [chunks[:, a, 2], chunks[:, a, 1], chunks[:, b, 1], chunks[:, b, 2]]
    return jnp.concatenate(q_list, axis=1), jnp.concatenate(kv_list, axis=1)


def head_layout_back(grad_q, grad_kv):
    qc = grad_q.reshape(D, 3, 2, HD)
    kc = grad_kv.reshape(D, 3, 4, HD)
    pieces = []
    for pair in range(3):
        pieces += [qc[:, pair, 1], kc[:, pair, 1], kc[:, pair, 0]]
        pieces += [qc[:, pair, 0], kc[:, pair, 2], kc[:, pair, 3]]
    whole = jnp.concatenate(pieces, axis=1)
    return whole.reshape(D, 2, 576).transpose(1, 0, 2)


def on_device(
    tokens,
    teacher,
    pass_embed,
    ln1_gain,
    ln1_bias,
    qkv_weight,
    out_weight,
    out_bias,
    ln2_gain,
    ln2_bias,
    fc1_weight,
    fc1_bias,
    fc2_weight,
    fc2_bias,
    cont_group,
    token_count,
):
    n_dp = lax.axis_size("dp")
    n_gr = lax.axis_size("gr")
    n_gc = lax.axis_size("gc")
    z = lax.axis_index("gr")
    g = lax.axis_index("gc")
    c = g % 2
    y = g // 2
    swap_core = [(i, i ^ 1) for i in range(n_gc)]
    swap_y = [(i, i ^ 2) for i in range(n_gc)]

    parts = [pass_embed, ln1_gain, ln1_bias, out_bias, ln2_gain, ln2_bias, fc2_bias]
    row = lax.broadcasted_iota(jnp.int32, (8, pass_embed.shape[0]), 0)
    packed = jnp.zeros(row.shape, F32)
    for i, values in enumerate(parts):
        packed = jnp.where(row == i, values.astype(F32)[None], packed)
    if n_dp == 2:
        vec = lax.dynamic_update_slice(jnp.zeros((8, D), F32), packed, (0, z * packed.shape[1]))
        bup = jnp.broadcast_to(fc1_bias.astype(F32), (8, fc1_bias.shape[0]))
        own = jnp.broadcast_to(jnp.pad(cont_group, (0, 120)), (8, 128))
        (
            mixed,
            lse_rows,
            w_out,
            w_up,
            w_down,
            n1_prompt,
            n1_chip,
            q,
            kvo,
            kvp,
            w_q,
            w_kv,
            vectors,
            b_up,
            owners,
        ) = front(
            tokens, vec, bup, own, qkv_weight, [out_weight, fc1_weight, fc2_weight], 1
        )
        n1_chip = n1_chip.reshape(2 * QROWS, D)
        owners = owners[:, 0, :8]
    else:
        vectors = lax.all_gather(packed, "gr", axis=1, tiled=True)
        b_up = lax.all_gather(fc1_bias, "gc", axis=0, tiled=True).astype(F32)
        owners = lax.all_gather(cont_group, "gr", axis=0, tiled=True)
    embed, gain1, shift1, b_out, gain2, shift2, b_down = [vectors[i] for i in range(7)]
    owners = owners.reshape(4, 2, 4)
    mine = lax.dynamic_slice(owners, (2 * y, jnp.maximum(z - 2, 0), 0), (2, 1, 4)).reshape(8)
    own_groups = jnp.repeat(2 * y + jnp.arange(2), 4)
    grp = jnp.where(z < 2, own_groups, mine).astype(jnp.int32)
    z_arr = z.astype(jnp.int32).reshape(1)

    hidden = tokens.astype(F32) + embed
    normed1, unit1, factor1 = norm(hidden, gain1, shift1)
    n1 = normed1.astype(BF)

    if n_dp != 2:
        w_other = lax.ppermute(qkv_weight, "gc", swap_y)
        w_pair = jnp.where(
            y == 0, jnp.stack([qkv_weight, w_other]), jnp.stack([w_other, qkv_weight])
        )
        w_qkv = lax.all_gather(w_pair, "gr", axis=1, tiled=True)
        n1_other = lax.ppermute(n1, "gc", swap_core)
        n1_chip = jnp.where(
            c == 0, jnp.concatenate([n1, n1_other]), jnp.concatenate([n1_other, n1])
        )
        n1_col = lax.all_gather(n1, "gr", axis=0, tiled=True)[:P_SIZE]
        n1_prompt = lax.all_gather(n1_col, "gc", axis=0, tiled=True)
        w_q, w_kv = head_layout(w_qkv)
        kvp = nn(n1_prompt, w_kv).astype(BF)
        kvo = nn(n1_chip, w_kv).astype(BF)
        q = (nn(n1_chip, w_q) * 0.125).astype(BF)
        w_out = lax.all_gather(out_weight, ("gc", "gr"))
        w_up = lax.all_gather(fc1_weight, ("gc", "gr"))
        w_down = lax.all_gather(fc2_weight, ("gc", "gr"))
        mixed_heads, lse = attend(grp, z_arr, q, kvo, kvp)
        lse_rows = lse[:, ::64].reshape(8, CL, 3, 2).transpose(2, 0, 3, 1)
        halves = mixed_heads.reshape(2, QROWS, 384)
        keep = lax.dynamic_index_in_dim(halves, c, 0, keepdims=False)
        give = lax.dynamic_index_in_dim(halves, 1 - c, 0, keepdims=False)
        take = lax.ppermute(give, "gc", swap_core)
        mixed = jnp.where(c == 0, jnp.stack([keep, take]), jnp.stack([take, keep]))
    w_up = w_up.reshape(n_gc, D, FF // n_gc)
    w_down = w_down.reshape(n_gc, D, FF // n_gc)
    if n_dp == 2:
        final, grad_h2, grad_w_up, grad_w_down, grad_w_out, gm, later_sums = middle(
            mixed, w_out, w_up, w_down, tokens, teacher, vectors, b_up
        )
    else:
        w_out = w_out.reshape(2, 2, n_gr, 192, 192).transpose(1, 0, 3, 2, 4).reshape(2, 384, D)

        attended = lax.dot_general(
            mixed, w_out, (((0, 2), (0, 1)), ((), ())), preferred_element_type=F32
        )
        hidden2 = hidden + attended + b_out
        normed2, unit2, factor2 = norm(hidden2, gain2, shift2)
        n2 = normed2.astype(BF)
        pre = lax.dot_general(n2, w_up, (((1,), (1,)), ((), ())), preferred_element_type=F32)
        pre = pre.reshape(QROWS, FF) + b_up
        active, gelu_back = jax.vjp(partial(jax.nn.gelu, approximate=True), pre)
        act = active.astype(BF)
        act_blocks = act.reshape(QROWS, n_gc, FF // n_gc)
        final = (
            hidden2
            + lax.dot_general(
                act_blocks, w_down, (((1, 2), (0, 2)), ((), ())), preferred_element_type=F32
            )
            + b_down
        )
        grad_final = final - teacher.astype(F32)
        squared = jnp.sum(grad_final * grad_final, axis=0)
        gb = grad_final.astype(BF)
        grad_b_down = jnp.sum(gb, axis=0, dtype=F32)
        grad_active = lax.dot_general(
            gb, w_down, (((1,), (1,)), ((), ())), preferred_element_type=F32
        ).reshape(QROWS, FF)
        grad_w_down = jnp.einsum("td,tgf->gdf", gb, act_blocks, preferred_element_type=F32)
        (grad_pre,) = gelu_back(grad_active)
        gp = grad_pre.astype(BF)
        gp_blocks = gp.reshape(QROWS, n_gc, FF // n_gc)
        grad_b_up = jnp.sum(gp, axis=0, dtype=F32)
        grad_w_up = jnp.einsum("td,tgf->gdf", n2, gp_blocks, preferred_element_type=F32)
        grad_n2 = lax.dot_general(
            gp_blocks, w_up, (((1, 2), (0, 2)), ((), ())), preferred_element_type=F32
        )
        back2, grad_gain2, grad_shift2 = norm_back(grad_n2, gain2, unit2, factor2)
        grad_h2 = grad_final + back2
        ga = grad_h2.astype(BF)
        grad_b_out = jnp.sum(ga, axis=0, dtype=F32)
        grad_w_out = jnp.einsum("ctk,tn->ckn", mixed, ga, preferred_element_type=F32)
        gm = jnp.einsum("tn,ckn->ctk", ga, w_out, preferred_element_type=F32).astype(BF)
        grad_w_up = grad_w_up.astype(BF)
        grad_w_down = grad_w_down.astype(BF)
        grad_w_out = (
            grad_w_out.astype(BF)
            .reshape(2, 2, 192, n_gr, 192)
            .transpose(1, 0, 3, 2, 4)
            .reshape(n_gc, n_gr, 192, 192)
        )
    weight_grads = [
        grad_w_down.reshape(n_gc, n_gr, 192, 768),
        grad_w_up.reshape(n_gc, n_gr, 192, 768),
        grad_w_out,
    ]
    if n_dp == 2:
        dq, dkvo, dkv, out_w_down, out_w_up, out_w_out = attend_back_scatter(
            grp, q, lse_rows, kvo, kvp, gm, weight_grads, 3
        )
    else:
        gm_keep = lax.dynamic_index_in_dim(gm, c, 0, keepdims=False)
        gm_give = lax.dynamic_index_in_dim(gm, 1 - c, 0, keepdims=False)
        gm_take = lax.ppermute(gm_give, "gc", swap_core)
        gm_chip = jnp.where(c == 0, jnp.stack([gm_keep, gm_take]), jnp.stack([gm_take, gm_keep]))
        gm_chip = gm_chip.reshape(2 * QROWS, 384)

        def scatter16(blocks):
            part = lax.psum_scatter(
                blocks.reshape(n_gc * n_gr * blocks.shape[2], -1),
                ("gc", "gr"),
                scatter_dimension=0,
                tiled=True,
            )
            return lax.psum(part, "dp").astype(F32)

        out_w_down, out_w_up, out_w_out = [scatter16(grad) for grad in weight_grads]
        dq, dkvo, dkvp = attend_back(grp, z_arr, q, gm_chip, lse_rows, kvo, kvp)
        part_prompt = nt(dkvp, w_kv).astype(BF)

        part_chip = (nt(dq, w_q) + nt(dkvo, w_kv)).reshape(2, QROWS, D)
        grad_kv = tn(n1_prompt, dkvp) + tn(n1_chip, dkvo)
        grad_q = tn(n1_chip, dq)
        grad_qkv = head_layout_back(grad_q, grad_kv)

    if n_dp == 2:
        input_grad, sums, out_w_qkv = tail_exchange(
            grp,
            dkv,
            n1_prompt,
            n1_chip,
            dkvo,
            dq,
            w_q,
            w_kv,
            grad_h2,
            tokens,
            vectors,
            later_sums,
            4,
        )
    else:
        later_sums = jnp.concatenate(
            [
                grad_gain2[None],
                grad_shift2[None],
                grad_b_out[None],
                grad_b_down[None],
                grad_b_up.reshape(4, D),
                squared[None],
                jnp.zeros((4, D), F32),
            ]
        )
        back_prompt = lax.psum_scatter(part_prompt, "gc", scatter_dimension=0, tiled=True)
        back_prompt = lax.psum_scatter(
            jnp.concatenate([back_prompt, jnp.zeros_like(back_prompt)]),
            "gr",
            scatter_dimension=0,
            tiled=True,
        ).astype(F32)
        part_keep = lax.dynamic_index_in_dim(part_chip, c, 0, keepdims=False)
        part_give = lax.dynamic_index_in_dim(part_chip, 1 - c, 0, keepdims=False)
        part_take = lax.ppermute(part_give.astype(BF), "gc", swap_core).astype(F32)
        grad_n1 = part_keep + part_take + back_prompt
        qkv_keep = lax.dynamic_index_in_dim(grad_qkv, y, 0, keepdims=False)
        qkv_give = lax.dynamic_index_in_dim(grad_qkv, 1 - y, 0, keepdims=False)
        qkv_take = lax.ppermute(qkv_give.astype(BF), "gc", swap_y).astype(F32)
        out_w_qkv = lax.psum_scatter(
            (qkv_keep + qkv_take).astype(BF), "gr", scatter_dimension=0, tiled=True
        )
        out_w_qkv = lax.psum(out_w_qkv, "dp").astype(F32)
        back1, grad_gain1, grad_shift1 = norm_back(grad_n1, gain1, unit1, factor1)
        input_grad = grad_h2 + back1
        first_sums = jnp.stack([jnp.sum(input_grad, axis=0), grad_gain1, grad_shift1])
        sums = lax.psum(jnp.concatenate([first_sums, later_sums]), ("dp", "gr", "gc"))
    sums = sums[:12].reshape(12 * D)
    loss = (jnp.sum(sums[11 * D :]) / (D * token_count[0].astype(F32))).reshape(1)
    rows = sums[: 7 * D].reshape(7, n_gr, D // n_gr)
    rows = lax.dynamic_index_in_dim(rows, z, 1, keepdims=False)
    up = lax.dynamic_index_in_dim(
        sums[7 * D : 7 * D + FF].reshape(n_gc, FF // n_gc), g, 0, keepdims=False
    )
    return (
        final.astype(BF),
        loss,
        input_grad,
        rows[0],
        rows[1],
        rows[2],
        out_w_qkv,
        out_w_out,
        rows[5],
        rows[3],
        rows[4],
        out_w_up,
        up,
        out_w_down,
        rows[6],
    )


def solution(mesh):
    rows = P(("dp", "gr", "gc"), None)
    in_specs = (
        rows,
        rows,
        P("gr"),
        P("gr"),
        P("gr"),
        P("gr", "gc"),
        P("gc", "gr"),
        P("gr"),
        P("gr"),
        P("gr"),
        P("gr", "gc"),
        P("gc"),
        P("gr", "gc"),
        P("gr"),
        P(("dp", "gr")),
        P(),
    )
    out_specs = (
        rows,
        P(),
        rows,
        P("gr"),
        P("gr"),
        P("gr"),
        P("gr", "gc"),
        P("gc", "gr"),
        P("gr"),
        P("gr"),
        P("gr"),
        P("gr", "gc"),
        P("gc"),
        P("gr", "gc"),
        P("gr"),
    )
    return jax.shard_map(
        on_device, mesh=mesh, in_specs=in_specs, out_specs=out_specs, check_vma=False
    )
```

```python
from functools import partial
import math

import jax
import jax.numpy as jnp
from jax import lax
from jax.experimental import pallas as pl
from jax.experimental.pallas import tpu as pltpu
from jax.sharding import PartitionSpec as P

D = 768
HD = 64
FF = 3072
P_SIZE = 1024
CL = 128
QROWS = 512
eps = 1e-05
negative = -1e30
BF = jnp.bfloat16
F32 = jnp.float32


def nt(a, b):
    return lax.dot_general(a, b, (((1,), (1,)), ((), ())), preferred_element_type=F32)


def nn(a, b):
    return lax.dot_general(a, b, (((1,), (0,)), ((), ())), preferred_element_type=F32)


def tn(a, b):
    return lax.dot_general(a, b, (((0,), (0,)), ((), ())), preferred_element_type=F32)


def att_fwd_kernel(grp_ref, z_ref, q_ref, kvo_ref, kvp_ref, o_ref, lse_ref):
    j = pl.program_id(1)
    row0 = pl.multiple_of(grp_ref[j] * P_SIZE, P_SIZE)
    z = z_ref[0]
    lane = lax.broadcasted_iota(jnp.int32, (CL, 128), 1)
    low = lane < 64
    zero = jnp.zeros((CL, 128), BF)
    q = q_ref[...]
    q_parts = (jnp.where(low, zero, q), jnp.where(low, q, zero))

    @pl.when(z >= 2)
    def _():
        row = lax.broadcasted_iota(jnp.int32, (CL, CL), 0)
        near_ok = lax.broadcasted_iota(jnp.int32, (CL, CL), 1) <= row
        mixes, sums = [], []
        for h in range(2):
            cols = slice(128 * h, 128 * h + 128)
            kv = kvp_ref[pl.ds(row0, P_SIZE), cols]
            kvo = kvo_ref[:, cols]
            far = nt(q_parts[h], kv)
            near = jnp.where(near_ok, nt(q_parts[h], kvo), negative)
            top = jnp.maximum(
                jnp.max(far, axis=1, keepdims=True), jnp.max(near, axis=1, keepdims=True)
            )
            far = jnp.exp(far - top)
            near = jnp.exp(near - top)
            total = jnp.sum(far, axis=1, keepdims=True) + jnp.sum(near, axis=1, keepdims=True)
            mix = nn(far.astype(BF), kv) + nn(near.astype(BF), kvo)
            mixes.append(mix / total)
            sums.append(jnp.broadcast_to(top + jnp.log(total), (CL, 128)))
        o_ref[...] = jnp.where(low, mixes[0], mixes[1]).astype(BF)
        lse_ref[...] = jnp.where(low, sums[0], sums[1])

    @pl.when(z < 2)
    def _():
        limit = z * QROWS + (j % (QROWS // CL)) * CL
        row = lax.broadcasted_iota(jnp.int32, (CL, P_SIZE), 0)
        key = lax.broadcasted_iota(jnp.int32, (CL, P_SIZE), 1)
        allowed = key - row <= limit
        mixes, sums = [], []
        for h in range(2):
            cols = slice(128 * h, 128 * h + 128)
            kv = kvp_ref[pl.ds(row0, P_SIZE), cols]
            far = jnp.where(allowed, nt(q_parts[h], kv), negative)
            top = jnp.max(far, axis=1, keepdims=True)
            far = jnp.exp(far - top)
            total = jnp.sum(far, axis=1, keepdims=True)
            mix = nn(far.astype(BF), kv)
            mixes.append(mix / total)
            sums.append(jnp.broadcast_to(top + jnp.log(total), (CL, 128)))
        o_ref[...] = jnp.where(low, mixes[0], mixes[1]).astype(BF)
        lse_ref[...] = jnp.where(low, sums[0], sums[1])


def attend(grp, z, q, kvo, kvp):
    rows = q.shape[0]
    pairs = q.shape[1] // 128
    groups_rows = kvp.shape[0]
    return pl.pallas_call(
        att_fwd_kernel,
        name="att_fwd",
        grid_spec=pltpu.PrefetchScalarGridSpec(
            num_scalar_prefetch=2,
            grid=(pairs, rows // CL),
            in_specs=[
                pl.BlockSpec((CL, 128), lambda p, j, *_: (j, p)),
                pl.BlockSpec((CL, 256), lambda p, j, *_: (j, p)),
                pl.BlockSpec((groups_rows, 256), lambda p, j, *_: (0, p)),
            ],
            out_specs=[
                pl.BlockSpec((CL, 128), lambda p, j, *_: (j, p)),
                pl.BlockSpec((CL, 128), lambda p, j, *_: (j, p)),
            ],
        ),
        out_shape=[
            jax.ShapeDtypeStruct((rows, pairs * 128), BF),
            jax.ShapeDtypeStruct((rows, pairs * 128), F32),
        ],
        compiler_params=pltpu.CompilerParams(vmem_limit_bytes=40 << 20),
        cost_estimate=pl.CostEstimate(
            flops=4 * rows * P_SIZE * 128 * pairs * 2,
            bytes_accessed=groups_rows * 512 * pairs,
            transcendentals=rows * P_SIZE * pairs * 2,
        ),
    )(grp, z, q, kvo, kvp)


def att_bwd_kernel(
    grp_ref, z_ref, q_ref, gm_ref, lse_ref, kvo_ref, kvp_ref, dq_ref, dkvo_ref, dkvp_ref, acc
):
    j = pl.program_id(1)
    row0 = pl.multiple_of(grp_ref[j] * P_SIZE, P_SIZE)
    z = z_ref[0]
    low = lax.broadcasted_iota(jnp.int32, (CL, 128), 1) < 64
    zero = jnp.zeros((CL, 128), BF)
    q = q_ref[...]
    gm = gm_ref[...]
    stacks = (
        jnp.concatenate([jnp.where(low, zero, q), jnp.where(low, gm, zero)], axis=0),
        jnp.concatenate([jnp.where(low, q, zero), jnp.where(low, zero, gm)], axis=0),
    )

    @pl.when(j == 0)
    def _():
        acc[...] = jnp.zeros_like(acc)

    @pl.when(z >= 2)
    def _():
        row = lax.broadcasted_iota(jnp.int32, (CL, CL), 0)
        near_ok = row <= lax.broadcasted_iota(jnp.int32, (CL, CL), 1)
        dqs = []
        for h in range(2):
            cols = slice(128 * h, 128 * h + 128)
            kv = kvp_ref[pl.ds(row0, P_SIZE), cols]
            kvo = kvo_ref[:, cols]
            lse = lse_ref[0, 0, h : h + 1, :]
            far = nt(kv, stacks[h])
            near = nt(kvo, stacks[h])
            pf = jnp.exp(far[:, :CL] - lse)
            pn = jnp.where(near_ok, jnp.exp(near[:, :CL] - lse), 0.0)
            df = far[:, CL:]
            dn = near[:, CL:]
            inner = jnp.sum(pf * df, axis=0, keepdims=True) + jnp.sum(
                pn * dn, axis=0, keepdims=True
            )
            sf = (pf * (df - inner)).astype(BF)
            sn = (pn * (dn - inner)).astype(BF)
            acc[pl.ds(row0, P_SIZE), cols] += nn(
                jnp.concatenate([sf, pf.astype(BF)], axis=1), stacks[h]
            )
            dkvo_ref[:, cols] = nn(
                jnp.concatenate([sn, pn.astype(BF)], axis=1), stacks[h]
            ).astype(BF)
            dqs.append(tn(sf, kv) + tn(sn, kvo))
        dq_ref[...] = (jnp.where(low, dqs[1], dqs[0]) * 0.125).astype(BF)

    @pl.when(z < 2)
    def _():
        limit = z * QROWS + (j % (QROWS // CL)) * CL
        key = lax.broadcasted_iota(jnp.int32, (P_SIZE, CL), 0)
        row = lax.broadcasted_iota(jnp.int32, (P_SIZE, CL), 1)
        allowed = key - row <= limit
        dqs = []
        for h in range(2):
            cols = slice(128 * h, 128 * h + 128)
            kv = kvp_ref[pl.ds(row0, P_SIZE), cols]
            lse = lse_ref[0, 0, h : h + 1, :]
            far = nt(kv, stacks[h])
            pf = jnp.where(allowed, jnp.exp(far[:, :CL] - lse), 0.0)
            df = far[:, CL:]
            inner = jnp.sum(pf * df, axis=0, keepdims=True)
            sf = (pf * (df - inner)).astype(BF)
            acc[pl.ds(row0, P_SIZE), cols] += nn(
                jnp.concatenate([sf, pf.astype(BF)], axis=1), stacks[h]
            )
            dqs.append(tn(sf, kv))
        dkvo_ref[...] = jnp.zeros_like(dkvo_ref)
        dq_ref[...] = (jnp.where(low, dqs[1], dqs[0]) * 0.125).astype(BF)

    @pl.when(j == pl.num_programs(1) - 1)
    def _():
        dkvp_ref[...] = acc[...].astype(BF)


def attend_back(grp, z, q, gm, lse, kvo, kvp):
    rows = q.shape[0]
    pairs = q.shape[1] // 128
    groups_rows = kvp.shape[0]
    return pl.pallas_call(
        att_bwd_kernel,
        name="att_bwd",
        grid_spec=pltpu.PrefetchScalarGridSpec(
            num_scalar_prefetch=2,
            grid=(pairs, rows // CL),
            in_specs=[
                pl.BlockSpec((CL, 128), lambda p, j, *_: (j, p)),
                pl.BlockSpec((CL, 128), lambda p, j, *_: (j, p)),
                pl.BlockSpec((1, 1, 2, 128), lambda p, j, *_: (p, j, 0, 0)),
                pl.BlockSpec((CL, 256), lambda p, j, *_: (j, p)),
                pl.BlockSpec((groups_rows, 256), lambda p, j, *_: (0, p)),
            ],
            out_specs=[
                pl.BlockSpec((CL, 128), lambda p, j, *_: (j, p)),
                pl.BlockSpec((CL, 256), lambda p, j, *_: (j, p)),
                pl.BlockSpec((groups_rows, 256), lambda p, j, *_: (0, p)),
            ],
            scratch_shapes=[pltpu.VMEM((groups_rows, 256), F32)],
        ),
        out_shape=[
            jax.ShapeDtypeStruct((rows, pairs * 128), BF),
            jax.ShapeDtypeStruct((rows, pairs * 256), BF),
            jax.ShapeDtypeStruct((groups_rows, pairs * 256), BF),
        ],
        compiler_params=pltpu.CompilerParams(vmem_limit_bytes=48 << 20),
        cost_estimate=pl.CostEstimate(
            flops=10 * rows * P_SIZE * 128 * pairs * 2,
            bytes_accessed=groups_rows * 1024 * pairs,
            transcendentals=rows * P_SIZE * pairs * 2,
        ),
    )(grp, z, q, gm, lse, kvo, kvp)


MESH = pl.DeviceIdType.MESH


def places():
    x = lax.axis_index("dp")
    z = lax.axis_index("gr")
    g = lax.axis_index("gc")
    return x, z, g, g // 2, g % 2


def greet(partners):
    barrier = pltpu.get_barrier_semaphore()
    for partner in partners:
        pl.semaphore_signal(barrier, inc=1, device_id=partner, device_id_type=MESH)
    pl.semaphore_wait(barrier, len(partners))


def all_partners():
    x, z, g, y, c = places()
    by_z = [{"gr": z ^ step} for step in (1, 2, 3)]
    return [{"gc": g ^ 1}, {"gc": g ^ 2}, {"dp": x ^ 1}] + by_z


def send(src, dst, sems, slot, target, send_slot=None):
    return pltpu.make_async_remote_copy(
        src_ref=src,
        dst_ref=dst,
        send_sem=sems[0].at[slot if send_slot is None else send_slot],
        recv_sem=sems[1].at[slot],
        device_id=target,
        device_id_type=MESH,
    )


def add_into(dst, left, right):
    rows = dst.shape[0]
    size = 48 if rows % 48 == 0 else 64

    @pl.loop(0, rows // size)
    def _(i):
        r = pl.ds(pl.multiple_of(i * size, 16), size)
        dst[r] = (left[r].astype(F32) + right[r].astype(F32)).astype(dst.dtype)


RS_SLOTS = 28
RS_ORDER = (3, 2, 1, 0)
PACE = 26


def rs_plan(grads, outs, bufs, sems, l_sems, base, paired):
    own, ra, rb0, rb1, rc0, rc1, sc, rd, re = bufs
    x, z, g, y, c = places()
    sib, over_y, over_x = {"gc": g ^ 1}, {"gc": g ^ 2}, {"dp": x ^ 1}
    rows = grads.shape[2]
    q = rows // 4
    mine0 = pl.ds(pl.multiple_of(q * x, 16), q)
    other0 = pl.ds(pl.multiple_of(q * (1 - x), 16), q)
    mine1 = pl.ds(pl.multiple_of(2 * q + q * x, 16), q)
    other1 = pl.ds(pl.multiple_of(2 * q + q * (1 - x), 16), q)
    first = pl.ds(0, 2 * q)
    slot = base * RS_SLOTS

    def load(i, s):
        source = grads.at[2 * i + c, z ^ s] if paired else grads.at[i, z ^ s]
        return pltpu.make_async_copy(source, own.at[i, s], l_sems.at[8 * base + 2 * s + i])

    def hop_a(i, s):
        return send(grads.at[2 * i + 1 - c, z ^ s], ra.at[i, s], sems, slot + 6 * s + i, sib)

    def hop_b0(s):
        return send(own.at[1 - y, s, first], rb0.at[s], sems, slot + 6 * s + 2, over_y)

    def hop_b1(s):
        return send(own.at[:, s, other1], rb1.at[s], sems, slot + 6 * s + 3, over_x)

    def hop_c0(s):
        return send(own.at[y, s, other0], rc0.at[s], sems, slot + 6 * s + 4, over_x)

    def hop_c1(s):
        return send(own.at[1 - y, s, mine1], rc1.at[s], sems, slot + 6 * s + 5, over_y)

    def hop_z(s):
        return send(sc.at[s], rd.at[s - 1], sems, slot + 23 + s, {"gr": z ^ s})

    def hop_d():
        return send(sc.at[0], re, sems, slot + 27, over_x)

    def begin(s):
        for i in range(2):
            load(i, s).start()
            if paired:
                hop_a(i, s).start()

    def after_a(s):
        for i in range(2):
            load(i, s).wait()
            if paired:
                hop_a(i, s).wait()
                add_into(own.at[i, s], own.at[i, s], ra.at[i, s])
        hop_b0(s).start()
        hop_b1(s).start()

    def after_b(s):
        hop_b0(s).wait()
        hop_b1(s).wait()
        add_into(own.at[y, s, first], own.at[y, s, first], rb0.at[s])
        for i in range(2):
            add_into(own.at[i, s, mine1], own.at[i, s, mine1], rb1.at[s, i])
        hop_c0(s).start()
        hop_c1(s).start()

    def after_c(s):
        hop_c0(s).wait()
        hop_c1(s).wait()
        add_into(sc.at[s, pl.ds(0, q)], own.at[y, s, mine0], rc0.at[s])
        add_into(sc.at[s, pl.ds(q, q)], own.at[y, s, mine1], rc1.at[s])
        if s:
            hop_z(s).start()

    def total():
        for s in (1, 2, 3):
            hop_z(s).wait()
        whole = sc[0].astype(F32)
        for i in range(3):
            whole = whole + rd[i].astype(F32)
        sc[0] = whole.astype(BF)
        hop_d().start()

    def finish():
        hop_d().wait()
        outs[mine0] = sc[0, pl.ds(0, q)].astype(F32)
        outs[mine1] = sc[0, pl.ds(q, q)].astype(F32)
        outs[other0] = re[pl.ds(0, q)].astype(F32)
        outs[other1] = re[pl.ds(q, q)].astype(F32)

    return begin, after_a, after_b, after_c, total, finish


def rs_steps(plans):
    order = [(plan, s) for plan in plans for s in RS_ORDER]
    n = len(order)
    steps = [[partial(plan[0], s) for plan, s in order]]
    for i in range(n + 10):
        part = []
        if i < n:
            part.append(partial(order[i][0][1], order[i][1]))
        if 2 <= i < n + 2:
            part.append(partial(order[i - 2][0][2], order[i - 2][1]))
        if 4 <= i < n + 4:
            part.append(partial(order[i - 4][0][3], order[i - 4][1]))
        if 7 <= i < n + 7 and (i - 7) % 4 == 3:
            part.append(plans[(i - 7) // 4][4])
        if 9 <= i < n + 9 and (i - 9) % 4 == 3:
            part.append(plans[(i - 9) // 4][5])
        if part:
            steps.append(part)
    return steps


def rs_scratch(rows, cols, paired):
    q = rows // 4
    return [
        pltpu.VMEM((2, 4, rows, cols), BF),
        pltpu.VMEM((2, 4, rows, cols) if paired else (16, 128), BF),
        pltpu.VMEM((4, 2 * q, cols), BF),
        pltpu.VMEM((4, 2, q, cols), BF),
        pltpu.VMEM((4, q, cols), BF),
        pltpu.VMEM((4, q, cols), BF),
        pltpu.VMEM((4, 2 * q, cols), BF),
        pltpu.VMEM((3, 2 * q, cols), BF),
        pltpu.VMEM((2 * q, cols), BF),
    ]


def att_scatter_kernel(count, grp_ref, q_ref, lse_ref, kvo_ref, kvp_ref, gm, *refs):
    grads = refs[:count]
    dq_ref, dkvo_ref, dkv_ref = refs[count : count + 3]
    outs = refs[count + 3 : 2 * count + 3]
    rest = refs[2 * count + 3 :]
    bufs, (gmx, sem_s, sem_r, l_sems, m_send, m_recv, m_local) = rest[: 9 * count], rest[9 * count :]
    p, j = pl.program_id(0), pl.program_id(1)
    step = p * pl.num_programs(1) + j
    x, z, g, y, c = places()
    hooks = rs_steps(
        [
            rs_plan(grads[k], outs[k], bufs[9 * k : 9 * k + 9], (sem_s, sem_r), l_sems, k, True)
            for k in range(count)
        ]
    )

    def exchange(i):
        cols = pl.ds(128 * i, 128)
        return (
            pltpu.make_async_copy(gm.at[c, :, cols], gmx.at[i, c], m_local.at[i]),
            send(gm.at[1 - c, :, cols], gmx.at[i, c], (m_send, m_recv), i, {"gc": g ^ 1}),
        )

    @pl.when(step == 0)
    def _():
        greet(all_partners())
        for i in range(3):
            for copy in exchange(i):
                copy.start()
        for hook in hooks[0]:
            hook()
        for copy in exchange(0):
            copy.wait()

    for i in (1, 2):

        @pl.when(step == 8 * i)
        def _():
            for copy in exchange(i):
                copy.wait()

    last = len(hooks) - 1
    for when in range(1, 23):
        parts = [h for i in range(1, last) if max(1, i * PACE // (last - 1)) == when for h in hooks[i]]
        if parts:

            @pl.when(step == when)
            def _():
                for hook in parts:
                    hook()

    group = grp_ref[j]
    low = lax.broadcasted_iota(jnp.int32, (CL, 128), 1) < 64
    zero = jnp.zeros((CL, 128), BF)
    q = q_ref[0]
    gmix = gmx[p, j // 4, pl.ds(pl.multiple_of((j % 4) * CL, CL), CL)]
    stacks = (
        jnp.concatenate([jnp.where(low, zero, q), jnp.where(low, gmix, zero)], axis=0),
        jnp.concatenate([jnp.where(low, q, zero), jnp.where(low, zero, gmix)], axis=0),
    )

    @pl.when(z >= 2)
    def _():
        row = lax.broadcasted_iota(jnp.int32, (CL, CL), 0)
        near_ok = row <= lax.broadcasted_iota(jnp.int32, (CL, CL), 1)
        dqs = []
        for h in range(2):
            cols = slice(128 * h, 128 * h + 128)
            kv = kvp_ref[0, group, :, cols]
            kvo = kvo_ref[0, :, cols]
            lse = lse_ref[0, 0, h : h + 1, :]
            far = nt(kv, stacks[h])
            near = nt(kvo, stacks[h])
            pf = jnp.exp(far[:, :CL] - lse)
            pn = jnp.where(near_ok, jnp.exp(near[:, :CL] - lse), 0.0)
            df = far[:, CL:]
            dn = near[:, CL:]
            inner = jnp.sum(pf * df, axis=0, keepdims=True) + jnp.sum(
                pn * dn, axis=0, keepdims=True
            )
            sf = (pf * (df - inner)).astype(BF)
            sn = (pn * (dn - inner)).astype(BF)
            dkv_ref[0, :, cols] = nn(
                jnp.concatenate([sf, pf.astype(BF)], axis=1), stacks[h]
            ).astype(BF)
            dkvo_ref[:, cols] = nn(
                jnp.concatenate([sn, pn.astype(BF)], axis=1), stacks[h]
            ).astype(BF)
            dqs.append(tn(sf, kv) + tn(sn, kvo))
        dq_ref[...] = (jnp.where(low, dqs[1], dqs[0]) * 0.125).astype(BF)

    @pl.when(z < 2)
    def _():
        limit = z * QROWS + (j % (QROWS // CL)) * CL
        key = lax.broadcasted_iota(jnp.int32, (P_SIZE, CL), 0)
        row = lax.broadcasted_iota(jnp.int32, (P_SIZE, CL), 1)
        allowed = key - row <= limit
        dqs = []
        for h in range(2):
            cols = slice(128 * h, 128 * h + 128)
            kv = kvp_ref[0, group, :, cols]
            lse = lse_ref[0, 0, h : h + 1, :]
            far = nt(kv, stacks[h])
            pf = jnp.where(allowed, jnp.exp(far[:, :CL] - lse), 0.0)
            df = far[:, CL:]
            inner = jnp.sum(pf * df, axis=0, keepdims=True)
            sf = (pf * (df - inner)).astype(BF)
            dkv_ref[0, :, cols] = nn(
                jnp.concatenate([sf, pf.astype(BF)], axis=1), stacks[h]
            ).astype(BF)
            dqs.append(tn(sf, kv))
        dkvo_ref[...] = jnp.zeros_like(dkvo_ref)
        dq_ref[...] = (jnp.where(low, dqs[1], dqs[0]) * 0.125).astype(BF)

    @pl.when(step == 23)
    def _():
        for i in range(1, last + 1):
            if i == last or i * PACE // (last - 1) > 22:
                for hook in hooks[i]:
                    hook()


def attend_back_scatter(grp, q, lse, kvo, kvp, gm, grads, collective_id):
    rows = q.shape[1]
    count = len(grads)
    any_space = pl.BlockSpec(memory_space=pl.ANY)
    scratch = []
    for grad in grads:
        scratch += rs_scratch(grad.shape[2], grad.shape[3], True)
    slots = RS_SLOTS * count
    return pl.pallas_call(
        partial(att_scatter_kernel, count),
        name="attend_back_scatter",
        grid_spec=pltpu.PrefetchScalarGridSpec(
            num_scalar_prefetch=1,
            grid=(3, rows // CL),
            in_specs=[
                pl.BlockSpec((1, CL, 128), lambda p, j, *_: (p, j, 0)),
                pl.BlockSpec((1, 1, 2, 128), lambda p, j, *_: (p, j, 0, 0)),
                pl.BlockSpec((1, CL, 256), lambda p, j, *_: (p, j, 0)),
                pl.BlockSpec((1, 4, P_SIZE, 256), lambda p, j, *_: (p, 0, 0, 0)),
            ]
            + [any_space] * (count + 1),
            out_specs=[
                pl.BlockSpec((CL, 128), lambda p, j, *_: (j, p)),
                pl.BlockSpec((CL, 256), lambda p, j, *_: (j, p)),
                pl.BlockSpec((1, P_SIZE, 256), lambda p, j, *_: (j, 0, p)),
            ]
            + [pl.BlockSpec(grad.shape[2:], lambda p, j, *_: (0, 0)) for grad in grads],
            scratch_shapes=scratch
            + [
                pltpu.VMEM((3, 2, QROWS, 128), BF),
                pltpu.SemaphoreType.DMA((slots,)),
                pltpu.SemaphoreType.DMA((slots,)),
                pltpu.SemaphoreType.DMA((8 * count,)),
                pltpu.SemaphoreType.DMA((3,)),
                pltpu.SemaphoreType.DMA((3,)),
                pltpu.SemaphoreType.DMA((3,)),
            ],
        ),
        out_shape=[
            jax.ShapeDtypeStruct((rows, 384), BF),
            jax.ShapeDtypeStruct((rows, 768), BF),
            jax.ShapeDtypeStruct((8, P_SIZE, 768), BF),
        ]
        + [jax.ShapeDtypeStruct(grad.shape[2:], F32) for grad in grads],
        compiler_params=pltpu.CompilerParams(
            collective_id=collective_id, has_side_effects=True, vmem_limit_bytes=56 << 20
        ),
    )(grp, q, lse, kvo, kvp, gm, *grads)


def norm_rows(hidden, gain, shift):
    center = jnp.mean(hidden, axis=1, keepdims=True)
    offset = hidden - center
    factor = lax.rsqrt(jnp.mean(offset * offset, axis=1, keepdims=True) + eps)
    return offset * factor * gain + shift


CHUNKS = 4
FRONT = 13
GATHER_SLOTS = 40
SEGMENT = 4


def front_kernel(
    tokens,
    vec,
    bup,
    own,
    wq,
    block0,
    block1,
    block2,
    mixed,
    lse_ref,
    whole0,
    whole1,
    whole2,
    prompts_out,
    chip_out,
    q_out,
    kvo_out,
    kvp_out,
    wq_out,
    wkv_out,
    vec_out,
    bup_out,
    own_out,
    n1,
    vec_in,
    prompts,
    chip,
    wpair,
    q_all,
    kvo_all,
    kvp_all,
    mix,
    own_scalar,
    zs,
    zr,
    ys,
    yr,
    ds,
    dr,
    ws,
    wr,
    ss,
    sr,
    gs,
    gr_,
    ms,
    mr,
    l_sems,
    o_sems,
):
    x, z, g, y, c = places()
    sib, over_y, over_x = {"gc": g ^ 1}, {"gc": g ^ 2}, {"dp": x ^ 1}
    z_sems, y_sems, d_sems, w_sems, s_sems, g_sems = (
        (zs, zr),
        (ys, yr),
        (ds, dr),
        (ws, wr),
        (ss, sr),
        (gs, gr_),
    )
    blocks, wholes = (block0, block1, block2), (whole0, whole1, whole2)
    half_rows = wq.shape[0] // 2
    my_half = pl.ds(pl.multiple_of(x * half_rows, 16), half_rows)
    size = QROWS // CHUNKS
    first_half = jnp.where(z == 0, 0, 1)
    order = (z, z ^ 1, jnp.where(z < 2, 2, 1), jnp.where(z < 2, 3, 0))
    above, below = {"gr": jnp.minimum(z + 1, 3)}, {"gr": jnp.maximum(z - 1, 0)}
    inner = jnp.logical_and(z > 0, z < 3)

    def line(part, sems, base, b):
        return (
            (jnp.logical_and(z < 3, b <= z), send(part, part, sems, base + b, above)),
            (
                jnp.logical_and(z > 0, b >= z),
                send(part, part, sems, base + b, below, base + 4 + b),
            ),
        )

    def pass_on(copies):
        for goes, copy in copies:
            pl.when(goes)(copy.start)

    def passed_on(copies):
        for goes, copy in copies:
            pl.when(goes)(copy.wait_send)

    local_copy = pltpu.make_async_copy

    def small(kind, s):
        if kind == 0:
            return send(vec, vec_in.at[s], s_sems, s, {"gr": z ^ s})
        if kind == 1:
            return send(own, own_out.at[z], s_sems, 3 + s, {"gr": z ^ s})
        return send(bup, bup_out.at[g], s_sems, 6 + s, {"gc": g ^ s})

    def chip_send():
        return send(n1, chip.at[c], s_sems, 10, sib)

    def w_local():
        return local_copy(wq.at[my_half], wpair.at[y, z, my_half], l_sems.at[0])

    def w_line(s):
        return line(wpair.at[y, order[s], my_half], w_sems, 0, order[s])

    def w_gc(s):
        piece = wpair.at[y, order[s], my_half]
        return send(piece, piece, w_sems, 8 + s, over_y)

    def w_dp(s):
        piece = wpair.at[y, order[s], my_half]
        return send(piece, piece, w_sems, 12 + s, over_x)

    def w_dp_far(s):
        piece = wpair.at[1 - y, order[s], my_half]
        return send(piece, piece, w_sems, 16 + s, over_x)

    def chunk(number):
        return jnp.where(number < CHUNKS, first_half, 1 - first_half), number % CHUNKS

    def item(column, number):
        half, k = chunk(number)
        return prompts.at[column, half, pl.ds(pl.multiple_of(k * size, size), size)]

    def up(number):
        half, k = chunk(number)
        ref = item(g, number)
        return send(ref, ref, z_sems, half * CHUNKS + k, {"gr": jnp.minimum(z + 1, 3)})

    def down(number):
        half, k = chunk(number)
        ref = item(g, number)
        return send(
            ref,
            ref,
            z_sems,
            half * CHUNKS + k,
            {"gr": jnp.maximum(z - 1, 0)},
            2 * CHUNKS + k,
        )

    def side(number):
        half, k = chunk(number)
        ref = item(g, number)
        return send(ref, ref, y_sems, half * CHUNKS + k, over_y)

    def core(number, far):
        half, k = chunk(number)
        ref = item(g ^ 2 if far else g, number)
        return send(ref, ref, d_sems, far * 2 * CHUNKS + half * CHUNKS + k, sib)

    def goes_up(number):
        return jnp.logical_and(z < 3, chunk(number)[0] <= z)

    def goes_down(number):
        return jnp.logical_and(z == 1, chunk(number)[0] == 1)

    def forward(number):
        @pl.when(chunk(number)[0] != z)
        def _():
            up(number).wait_recv()

        @pl.when(goes_up(number))
        def _():
            up(number).start()

        @pl.when(goes_down(number))
        def _():
            down(number).start()

        side(number).start()
        core(number, 0).start()

    def across(number):
        side(number).wait_recv()
        core(number, 1).start()

    def plan(a, s):
        block, whole = blocks[a], wholes[a]
        q = block.shape[0] // 4
        half = pl.ds(pl.multiple_of(x * 2 * q, 16), 2 * q)
        qa = pl.ds(pl.multiple_of(x * 2 * q, 16), q)
        qb = pl.ds(pl.multiple_of(x * 2 * q + q, 16), q)
        qc = pl.ds(pl.multiple_of((1 - x) * 2 * q + q, 16), q)
        base = a * GATHER_SLOTS
        mine, far = whole.at[g, order[s]], whole.at[g ^ 2, order[s]]
        o = base + 8 + 8 * s

        def same(part, number, target):
            return lambda: send(part, part, g_sems, o + number, target)

        return {
            "line": lambda: line(mine.at[half], g_sems, base, order[s]),
            "ay": same(mine.at[qa], 0, over_y),
            "ax": same(mine.at[qa], 1, over_x),
            "afx": same(far.at[qa], 2, over_x),
            "bx": same(mine.at[qb], 3, over_x),
            "by": same(mine.at[qb], 4, over_y),
            "bfy": same(mine.at[qc], 5, over_y),
            "bfx": same(far.at[qb], 5, over_x),
            "c1": same(mine, 6, sib),
            "c2": same(far, 7, sib),
        }

    def own_block(a):
        return local_copy(blocks[a], wholes[a].at[g, z], l_sems.at[4 + a])

    def names(s):
        return ("ay", "ax", "afx", "bx", "by", "bfy") if s else ("ay", "afx", "by", "bfx")

    def relay(s):
        @pl.when(inner)
        def _():
            for a in range(3):
                copies = plan(a, s)["line"]()
                copies[0][1].wait_recv()
                pass_on(copies)


    def gather_first(s):
        for a in range(3):
            m = plan(a, s)
            if s:
                pl.when(jnp.logical_not(inner))(m["line"]()[0][1].wait_recv)
                m["bx"]().start()
                m["ax"]().start()
            m["ay"]().start()
            m["by"]().start()

    def gather_second(s):
        for a in range(3):
            m = plan(a, s)
            m["ay"]().wait_recv()
            m["afx"]().start()
            if s:
                m["bx"]().wait_recv()
                m["bfy"]().start()
            else:
                m["by"]().wait_recv()
                m["bfx"]().start()

    def gather_third(s):
        for a in range(3):
            m = plan(a, s)
            for name in ("ax", "afx", "by", "bfy") if s else ("afx", "bfx"):
                m[name]().wait_recv()
            m["c1"]().start()
            m["c2"]().start()

    def out_copies():
        return [
            local_copy(prompts, prompts_out, o_sems.at[0]),
            local_copy(chip, chip_out, o_sems.at[1]),
            local_copy(q_all, q_out, o_sems.at[2]),
            local_copy(kvo_all, kvo_out, o_sems.at[3]),
            local_copy(kvp_all, kvp_out, o_sems.at[4]),
        ]

    def exchange(i):
        cols = pl.ds(128 * i, 128)
        return (
            local_copy(mix.at[i, c], mixed.at[c, :, cols], l_sems.at[7 + i]),
            send(mix.at[i, 1 - c], mixed.at[c, :, cols], (ms, mr), i, sib),
        )

    hooks = {i: [] for i in range(FRONT)}

    def begin():
        greet(all_partners() + [{"gc": g ^ 3}])
        w_local().start()
        for s in (1, 2, 3):
            for kind in range(3):
                small(kind, s).start()
        w_local().wait()
        pass_on(w_line(0))
        own_out[z] = own[...]
        bup_out[g] = bup[...]
        for s in (1, 2, 3):
            small(0, s).wait_recv()
        vec_out[...] = (vec[...] + vec_in[1]) + (vec_in[2] + vec_in[3])

        @pl.loop(0, CHUNKS)
        def _(i):
            rows = pl.ds(pl.multiple_of(i * size, size), size)
            hidden = tokens[rows].astype(F32) + vec_out[0:1]
            n1[rows] = norm_rows(hidden, vec_out[1:2], vec_out[2:3]).astype(BF)

        @pl.when(z < 2)
        def _():
            to = local_copy(n1, prompts.at[g, jnp.minimum(z, 1)], l_sems.at[2])
            to.start()
            to.wait()

    def begin_chip():
        local_copy(n1, chip.at[c], l_sems.at[1]).start()
        chip_send().start()
        w_gc(0).start()
        w_dp(0).start()

    hooks[0] += [begin, partial(forward, 0), begin_chip]
    for i in range(1, 8):
        hooks[i].append(partial(forward, i))
    for i in range(2, 10):
        hooks[i].append(partial(across, i - 2))

    def w_pass(s):
        copies = w_line(s)
        copies[0][1].wait_recv()
        pass_on(copies)
        w_gc(s).start()
        w_dp(s).start()

    def w_across(s):
        w_gc(s).wait_recv()
        w_dp_far(s).start()

    for s in (1, 2, 3):
        hooks[s].append(partial(w_pass, s))
    hooks[2].append(partial(w_across, 0))
    hooks[3] += [partial(w_across, 1)]
    hooks[4] += [partial(w_across, 2), partial(w_across, 3)]

    def assemble():
        for s in range(4):
            w_dp(s).wait_recv()
            w_dp_far(s).wait_recv()
        local_copy(n1, chip.at[c], l_sems.at[1]).wait()
        chip_send().wait_recv()
        for s in (1, 2, 3):
            small(1, s).wait_recv()
        to = local_copy(own_out, own_scalar, l_sems.at[3])
        to.start()
        for head in range(6):
            p, b = head // 2, head % 2
            at_q = 128 * p + (0 if b else 64)
            at_k = 256 * p + (128 if b else 64)
            at_v = 256 * p + (192 if b else 0)
            start = (head % 3) * 192
            for r in range(4):
                rows = slice(192 * r, 192 * r + 192)
                source = wpair.at[head // 3, r]
                wq_out[rows, at_q : at_q + HD] = source[:, start : start + HD]
                wkv_out[rows, at_k : at_k + HD] = source[:, start + HD : start + 2 * HD]
                wkv_out[rows, at_v : at_v + HD] = source[:, start + 2 * HD : start + 3 * HD]
        to.wait()

    hooks[5].append(assemble)

    def project(number):
        core(number, 0).wait_recv()
        core(number, 1).wait_recv()
        half, k = chunk(number)
        w = wkv_out[...]
        rows = jnp.concatenate(
            [
                prompts[i, half, pl.ds(pl.multiple_of(k * size, size), size)]
                for i in range(4)
            ],
            axis=0,
        )
        kv = nn(rows, w).astype(BF)
        to = pl.ds(pl.multiple_of(half * QROWS + k * size, size), size)
        for i in range(4):
            for p in range(3):
                kvp_all[p, i, to] = kv[size * i : size * i + size, 256 * p : 256 * p + 256]
        mine = chip[number // CHUNKS, pl.ds(pl.multiple_of(k * size, size), size)]
        kvo = nn(mine, w).astype(BF)
        queries = (nn(mine, wq_out[...]) * 0.125).astype(BF)
        to = pl.ds(pl.multiple_of(number * size, size), size)
        for p in range(3):
            kvo_all[p, to] = kvo[:, 256 * p : 256 * p + 256]
            q_all[p, to] = queries[:, 128 * p : 128 * p + 128]


    def own_first():
        for a in range(3):
            own_block(a).start()

    def own_down():
        for a in range(3):
            own_block(a).wait()
            goes, copy = plan(a, 0)["line"]()[1]
            pl.when(goes)(copy.start)

    def own_up():
        for a in range(3):
            goes, copy = plan(a, 0)["line"]()[0]
            pl.when(goes)(copy.start)

    hooks[0].append(own_first)
    hooks[1].append(own_down)
    hooks[9].append(own_up)
    hooks[8].append(partial(gather_first, 0))
    hooks[10].append(partial(gather_second, 0))
    between = [[] for _ in range(24 // SEGMENT + 1)]
    last = len(between) - 1
    between[0] += [lambda: [copy.start() for copy in out_copies()], partial(gather_third, 0)]
    hooks[10].append(partial(relay, 1))
    hooks[12].append(partial(relay, 2))
    for slot, stage, s in (
        (0, relay, 3),
        (0, gather_first, 1),
        (1, gather_first, 2),
        (1, gather_second, 1),
        (2, gather_first, 3),
        (2, gather_second, 2),
        (3, gather_third, 1),
        (3, gather_second, 3),
        (4, gather_third, 2),
        (6, gather_third, 3),
    ):
        between[slot].append(partial(stage, s))

    for number in range(FRONT - 8):
        for hook in hooks[number]:
            hook()

    def one_piece(number, carried):
        for i in range(FRONT - 8, FRONT):
            if hooks[i]:

                @pl.when(number == i)
                def _():
                    for hook in hooks[i]:
                        hook()

        project(number - (FRONT - 8))
        return carried

    lax.fori_loop(FRONT - 8, FRONT, one_piece, 0)

    low = lax.broadcasted_iota(jnp.int32, (CL, 128), 1) < 64

    def parts(turn):
        p, j = turn // 8, turn % 8
        shard = 2 * y + j // 4
        group = jnp.where(
            z < 2, shard, own_scalar[shard, 0, jnp.maximum(z - 2, 0) * 4 + j % 4]
        )
        rows_j = pl.ds(pl.multiple_of(j * CL, CL), CL)
        zero = jnp.zeros((CL, 128), BF)
        q = q_all[p, rows_j]
        return p, j, group, rows_j, (jnp.where(low, zero, q), jnp.where(low, q, zero))

    def store(p, j, mixes, sums):
        mix[p, j // 4, pl.ds(pl.multiple_of((j % 4) * CL, CL), CL)] = jnp.where(
            low, mixes[0], mixes[1]
        ).astype(BF)
        flat = jnp.where(low, sums[0], sums[1]).T
        lse_ref[p, j, 0:1] = flat[0:1]
        lse_ref[p, j, 1:2] = flat[64:65]

    def cont_turn(turn, carried):
        p, j, group, rows_j, q_parts = parts(turn)
        row = lax.broadcasted_iota(jnp.int32, (CL, CL), 0)
        near_ok = lax.broadcasted_iota(jnp.int32, (CL, CL), 1) <= row
        mixes, sums = [], []
        for h in range(2):
            cols = slice(128 * h, 128 * h + 128)
            kv = kvp_all[p, group, :, cols]
            kvo = kvo_all[p, rows_j, cols]
            far = nt(q_parts[h], kv)
            near = jnp.where(near_ok, nt(q_parts[h], kvo), negative)
            top = jnp.maximum(
                jnp.max(far, axis=1, keepdims=True), jnp.max(near, axis=1, keepdims=True)
            )
            far = jnp.exp(far - top)
            near = jnp.exp(near - top)
            total = jnp.sum(far, axis=1, keepdims=True) + jnp.sum(near, axis=1, keepdims=True)
            mixes.append((nn(far.astype(BF), kv) + nn(near.astype(BF), kvo)) / total)
            sums.append(jnp.broadcast_to(top + jnp.log(total), (CL, 128)))
        store(p, j, mixes, sums)
        return carried

    def prompt_turn(turn, carried):
        p, j, group, rows_j, q_parts = parts(turn)
        limit = z * QROWS + (j % (QROWS // CL)) * CL
        row = lax.broadcasted_iota(jnp.int32, (CL, P_SIZE), 0)
        key = lax.broadcasted_iota(jnp.int32, (CL, P_SIZE), 1)
        allowed = key - row <= limit
        mixes, sums = [], []
        for h in range(2):
            cols = slice(128 * h, 128 * h + 128)
            kv = kvp_all[p, group, :, cols]
            far = jnp.where(allowed, nt(q_parts[h], kv), negative)
            top = jnp.max(far, axis=1, keepdims=True)
            far = jnp.exp(far - top)
            total = jnp.sum(far, axis=1, keepdims=True)
            mixes.append(nn(far.astype(BF), kv) / total)
            sums.append(jnp.broadcast_to(top + jnp.log(total), (CL, 128)))
        store(p, j, mixes, sums)
        return carried

    def one_turn(turn, carried):
        for segment in range(last):

            @pl.when(turn == segment * SEGMENT)
            def _():
                for hook in between[segment]:
                    hook()

        @pl.when(z >= 2)
        def _():
            cont_turn(turn, 0)

        @pl.when(z < 2)
        def _():
            prompt_turn(turn, 0)

        for i in range(3):

            @pl.when(turn == 8 * i + 7)
            def _():
                for copy in exchange(i):
                    copy.start()

        return carried

    lax.fori_loop(0, 24, one_turn, 0)
    for hook in between[last]:
        hook()

    for number in range(8):
        side(number).wait_send()
        core(number, 0).wait_send()
        core(number, 1).wait_send()

        @pl.when(goes_up(number))
        def _():
            up(number).wait_send()

        @pl.when(goes_down(number))
        def _():
            down(number).wait_send()

    for s in range(4):
        if s:
            small(0, s).wait_send()
            small(1, s).wait_send()
            small(2, s).wait()
        passed_on(w_line(s))
        w_gc(s).wait_send()
        w_dp(s).wait_send()
        w_dp_far(s).wait_send()
    chip_send().wait_send()
    for s in range(4):
        for a in range(3):
            m = plan(a, s)
            passed_on(m["line"]())
            for name in names(s):
                m[name]().wait_send()
            m["c1"]().wait()
            m["c2"]().wait()
    for i in range(3):
        for copy in exchange(i):
            copy.wait()
    for copy in out_copies():
        copy.wait()


def front(tokens, vectors, bias, own, wq, blocks, collective_id):
    def body(tokens_ref, *refs):
        parts, bias_ref = refs[:7], refs[7]
        rest, vec, bup = refs[8:-2], refs[-2], refs[-1]
        z = lax.axis_index("gr")
        width = bias_ref.shape[0] // 4
        vec[...] = jnp.zeros_like(vec)
        for k in range(4):

            @pl.when(z == k)
            def _():
                for i, part in enumerate(parts):
                    vec[i : i + 1, width * k : width * k + width] = (
                        part[...].astype(F32).reshape(1, width)
                    )

        bup[0:1] = bias_ref[...].astype(F32).reshape(1, 4 * width)
        front_kernel(tokens_ref, vec, bup, *rest)

    any_space = pl.BlockSpec(memory_space=pl.ANY)
    vmem = pl.BlockSpec(memory_space=pltpu.VMEM)
    rows = 2 * QROWS

    def dma(count):
        return pltpu.SemaphoreType.DMA((count,))

    slots = 3 * GATHER_SLOTS
    heads = [(3, rows, 128), (3, rows, 256), (3, 4, P_SIZE, 256)]
    return pl.pallas_call(
        body,
        name="front",
        in_specs=[vmem] * 10 + [any_space] * 4,
        out_specs=[any_space, vmem]
        + [any_space] * 8
        + [vmem] * 5,
        out_shape=[
            jax.ShapeDtypeStruct((2, QROWS, 384), BF),
            jax.ShapeDtypeStruct((3, rows // CL, 2, 128), F32),
        ]
        + [jax.ShapeDtypeStruct((4, 4) + block.shape, BF) for block in blocks]
        + [
            jax.ShapeDtypeStruct((4, 2, QROWS, D), BF),
            jax.ShapeDtypeStruct((2, QROWS, D), BF),
        ]
        + [jax.ShapeDtypeStruct(shape, BF) for shape in heads]
        + [
            jax.ShapeDtypeStruct((D, 384), BF),
            jax.ShapeDtypeStruct((D, D), BF),
            jax.ShapeDtypeStruct((8, D), F32),
            jax.ShapeDtypeStruct((4, 8, D), F32),
            jax.ShapeDtypeStruct((4,) + own.shape, jnp.int32),
        ],
        scratch_shapes=[
            pltpu.VMEM((QROWS, D), BF),
            pltpu.VMEM((4, 8, D), F32),
            pltpu.VMEM((4, 2, QROWS, D), BF),
            pltpu.VMEM((2, QROWS, D), BF),
            pltpu.VMEM((2, 4) + wq.shape, BF),
        ]
        + [pltpu.VMEM(shape, BF) for shape in heads]
        + [
            pltpu.VMEM((3, 2, QROWS, 128), BF),
            pltpu.SMEM((4,) + own.shape, jnp.int32),
            dma(3 * CHUNKS),
            dma(2 * CHUNKS),
            dma(2 * CHUNKS),
            dma(2 * CHUNKS),
            dma(4 * CHUNKS),
            dma(4 * CHUNKS),
            dma(20),
            dma(20),
            dma(11),
            dma(11),
            dma(slots),
            dma(slots),
            dma(3),
            dma(3),
            dma(10),
            dma(5),
            pltpu.VMEM((8, D), F32),
            pltpu.VMEM((8, D), F32),
        ],
        compiler_params=pltpu.CompilerParams(
            collective_id=collective_id, has_side_effects=True, vmem_limit_bytes=56 << 20
        ),
    )(tokens, *vectors, bias, own, wq, *blocks)


def tail_kernel(
    grp,
    dkv,
    n1p,
    n1c,
    dkvo,
    dq,
    w_q,
    w_kv,
    grad_h2,
    tokens,
    vec,
    sums,
    out,
    sums_out,
    dw_out,
    part,
    chip,
    tiles,
    rows_p,
    low,
    wkt,
    wqt,
    dkvw,
    dqw,
    dw,
    ra,
    rb,
    rz,
    take,
    gsum,
    cur,
    sb,
    *rest,
):
    bufs, (sem_s, sem_r, l_sems, w_s, w_r, w_l) = rest[:9], rest[9:]
    sems = (sem_s, sem_r)
    x, z, g, y, c = places()
    sib, over_y, over_x = {"gc": g ^ 1}, {"gc": g ^ 2}, {"dp": x ^ 1}
    down = {"gr": jnp.maximum(z - 1, 0)}
    far = z >= 2
    size = QROWS // CHUNKS
    count = 2 * CHUNKS

    def fetch(t):
        rows = pl.ds(pl.multiple_of(t * size, size), size)
        h, r = t // CHUNKS, pl.ds(pl.multiple_of((t % CHUNKS) * size, size), size)
        slot = t % 2
        return (
            pltpu.make_async_copy(dkv.at[:, rows], tiles.at[slot], l_sems.at[slot]),
            pltpu.make_async_copy(n1p.at[:, h, r], rows_p.at[slot], l_sems.at[2 + slot]),
        )

    for copy in fetch(0):
        copy.start()
    greet(all_partners())
    wkt[...] = w_kv[...].T
    wqt[...] = w_q[...].T
    dkvw[...] = jnp.zeros_like(dkvw)
    dqw[...] = jnp.zeros_like(dqw)

    def at(t):
        return t // CHUNKS, pl.ds(pl.multiple_of((t % CHUNKS) * size, size), size)

    def mine(side, t):
        h, r = at(t)
        return part.at[2 * (1 - y if side == 0 else y) + c, h, r]

    def hop_a(side, t):
        h, r = at(t)
        i = 1 - y if side == 0 else y
        return send(part.at[2 * i + 1 - c, h, r], ra.at[i, h, r], sems, 8 * side + t, sib)

    def hop_y(t):
        h, r = at(t)
        return send(mine(0, t), rb.at[h, r], sems, 16 + t, over_y)

    def hop_z(t):
        h, r = at(t)
        return send(mine(1, t), rz.at[h, r], sems, 24 + t, down)

    hop_chip = send(chip.at[1 - c], take, sems, 32, sib)

    def fold(t, other):
        h, r = at(t)
        add_into(mine(1, t), mine(1, t), other.at[r])

    def stage0(t):
        slot = t % 2
        for copy in fetch(t):
            copy.wait()

        @pl.when(t + 1 < count)
        def _():
            for copy in fetch(t + 1):
                copy.start()

        weights = [
            [jnp.where(grp[j] == i, 1.0, 0.0).astype(F32) for j in range(8)] for i in range(4)
        ]

        @pl.loop(0, size // 16)
        def _(q):
            r = pl.ds(pl.multiple_of(q * 16, 16), 16)
            pieces = [tiles[slot, j, r].astype(F32) for j in range(8)]
            for i in range(4):
                total = weights[i][0] * pieces[0]
                for j in range(1, 8):
                    total = total + weights[i][j] * pieces[j]
                low[i, r] = total.astype(BF)

        whole = low[...].reshape(4 * size, D)
        grads = nn(whole, wkt[...]).astype(BF)
        h, r = at(t)
        for i in range(4):
            part[i, h, r] = grads[size * i : size * i + size]

        @pl.when(far)
        def _():
            hop_a(0, t).start()

        hop_a(1, t).start()
        own = pl.ds(pl.multiple_of(t * size, size), size)
        near, grad_q, rows_c = dkvo[own], dq[own], n1c[own]
        chip[h, r] = (nn(grad_q, wqt[...]) + nn(near, wkt[...])).astype(BF)
        rows = jnp.concatenate([rows_p[slot].reshape(4 * size, D), rows_c], axis=0)
        dkvw[...] += tn(rows, jnp.concatenate([whole, near], axis=0))
        dqw[...] += tn(rows_c, grad_q)

    def stage1(t):
        h, r = at(t)

        @pl.when(far)
        def _():
            hop_a(0, t).wait()
            add_into(mine(0, t), mine(0, t), ra.at[1 - y, h, r])
            hop_y(t).start()

        hop_a(1, t).wait()
        fold(t, ra.at[y, h])

    def stage2(t):
        @pl.when(far)
        def _():
            hop_y(t).wait()
            fold(t, rb.at[t // CHUNKS])

        @pl.when(z == 3)
        def _():
            hop_z(t).start()

    def stage3(t):
        @pl.when(z == 2)
        def _():
            hop_z(t).wait_recv()
            fold(t, rz.at[t // CHUNKS])
            hop_z(t).start()

    def stage4(t):
        @pl.when(z == 1)
        def _():
            hop_z(t).wait_recv()
            fold(t, rz.at[t // CHUNKS])

            @pl.when(t < CHUNKS)
            def _():
                hop_z(t).start()

    def stage5(t):
        @pl.when(jnp.logical_and(z == 0, t < CHUNKS))
        def _():
            hop_z(t).wait_recv()
            fold(t, rz.at[0])

    def stages(t, carried, skip=0):
        todo = list(zip((0, 1, 3, 5, 7, 9), (stage0, stage1, stage2, stage3, stage4, stage5)))
        for lag, stage in todo[skip:]:

            @pl.when(jnp.logical_and(t >= lag, t < count + lag))
            def _():
                stage(t - lag)

        return carried

    lax.fori_loop(0, count, stages, 0)
    hop_chip.start()

    for head in range(6):
        p, b = head // 2, head % 2
        places_in = (
            dqw[:, 128 * p + (0 if b else 64) : 128 * p + (64 if b else 128)],
            dkvw[:, 256 * p + (128 if b else 64) : 256 * p + (192 if b else 128)],
            dkvw[:, 256 * p + (192 if b else 0) : 256 * p + (256 if b else 64)],
        )
        for i, piece in enumerate(places_in):
            at_col = (head % 3) * 192 + HD * i
            for r in range(4):
                dw[head // 3, r, :, at_col : at_col + HD] = piece[192 * r : 192 * r + 192].astype(
                    BF
                )
    begin, after_a, after_b, after_c, total, finish = rs_plan(
        dw, dw_out, bufs, (w_s, w_r), w_l, 0, False
    )
    for s in RS_ORDER:
        begin(s)
    for s in RS_ORDER:
        after_a(s)
    lax.fori_loop(count, count + 3, partial(stages, skip=1), 0)
    for s in RS_ORDER:
        after_b(s)
    lax.fori_loop(count + 3, count + 9, partial(stages, skip=2), 0)
    for s in RS_ORDER:
        after_c(s)

    @pl.loop(0, count)
    def _(t):
        @pl.when(jnp.logical_or(z >= 2, jnp.logical_and(z == 1, t < CHUNKS)))
        def _():
            hop_z(t).wait_send()

    hop_chip.wait()

    cur[...] = sums[...]

    @pl.loop(0, CHUNKS)
    def _(k):
        r = pl.ds(pl.multiple_of(k * size, size), size)
        gsum[r] = chip[c, r].astype(F32) + take[r].astype(F32)

        @pl.when(z < 2)
        def _():
            gsum[r] += part[2 * y + c, jnp.minimum(z, 1), r].astype(F32)

        hidden = tokens[r].astype(F32) + vec[0:1]
        center = jnp.mean(hidden, axis=1, keepdims=True)
        offset = hidden - center
        factor = lax.rsqrt(jnp.mean(offset * offset, axis=1, keepdims=True) + eps)
        unit = offset * factor
        grad = gsum[r]
        scaled = grad * vec[1:2]
        first = jnp.mean(scaled, axis=1, keepdims=True)
        second = jnp.mean(scaled * unit, axis=1, keepdims=True)
        result = grad_h2[r] + factor * (scaled - first - unit * second)
        out[r] = result
        cur[0:1] += jnp.sum(result, axis=0, keepdims=True)
        cur[1:2] += jnp.sum(grad * unit, axis=0, keepdims=True)
        cur[2:3] += jnp.sum(grad, axis=0, keepdims=True)

    for i, target in enumerate((sib, over_y, over_x)):
        hop = send(cur, sb.at[i], sems, 33 + i, target)
        hop.start()
        hop.wait()
        cur[...] += sb[i]
        if i == 1:
            total()
    hops = [send(cur, sb.at[2 + s], sems, 35 + s, {"gr": z ^ s}) for s in (1, 2, 3)]
    for hop in hops:
        hop.start()
    finish()
    for hop in hops:
        hop.wait()
    sums_out[...] = (cur[...] + sb[3]) + (sb[4] + sb[5])


def tail_exchange(
    grp, dkv, n1p, n1c, dkvo, dq, w_q, w_kv, grad_h2, tokens, vec, sums, collective_id
):
    any_space = pl.BlockSpec(memory_space=pl.ANY)
    vmem = pl.BlockSpec(memory_space=pltpu.VMEM)
    block = (2, 4, 192, 576)
    return pl.pallas_call(
        tail_kernel,
        name="tail_exchange",
        in_specs=[pl.BlockSpec(memory_space=pltpu.SMEM), any_space, any_space] + [vmem] * 9,
        out_specs=[vmem, vmem, vmem],
        out_shape=[
            jax.ShapeDtypeStruct((QROWS, D), F32),
            jax.ShapeDtypeStruct(sums.shape, F32),
            jax.ShapeDtypeStruct(block[2:], F32),
        ],
        scratch_shapes=[
            pltpu.VMEM((4, 2, QROWS, D), BF),
            pltpu.VMEM((2, QROWS, D), BF),
            pltpu.VMEM((2, 8, CL, D), BF),
            pltpu.VMEM((2, 4, CL, D), BF),
            pltpu.VMEM((4, CL, D), BF),
            pltpu.VMEM((D, D), BF),
            pltpu.VMEM((384, D), BF),
            pltpu.VMEM((D, D), F32),
            pltpu.VMEM((D, 384), F32),
            pltpu.VMEM(block, BF),
            pltpu.VMEM((2, 2, QROWS, D), BF),
            pltpu.VMEM((2, QROWS, D), BF),
            pltpu.VMEM((2, QROWS, D), BF),
            pltpu.VMEM((QROWS, D), BF),
            pltpu.VMEM((QROWS, D), F32),
            pltpu.VMEM(sums.shape, F32),
            pltpu.VMEM((6,) + sums.shape, F32),
        ]
        + rs_scratch(block[2], block[3], False)
        + [
            pltpu.SemaphoreType.DMA((39,)),
            pltpu.SemaphoreType.DMA((39,)),
            pltpu.SemaphoreType.DMA((4,)),
            pltpu.SemaphoreType.DMA((RS_SLOTS,)),
            pltpu.SemaphoreType.DMA((RS_SLOTS,)),
            pltpu.SemaphoreType.DMA((8,)),
        ],
        compiler_params=pltpu.CompilerParams(
            collective_id=collective_id, has_side_effects=True, vmem_limit_bytes=60 << 20
        ),
    )(grp, dkv, n1p, n1c, dkvo, dq, w_q, w_kv, grad_h2, tokens, vec, sums)


GELU_IN = math.sqrt(2.0 / math.pi)


def middle_kernel(
    mixed,
    w_out_g,
    w_up,
    w_down,
    tokens,
    teacher,
    vec,
    b_up,
    final_out,
    grad_h2,
    dw_up,
    dw_down,
    dw_out,
    gm,
    sums,
    wo,
    wu,
    wd,
    h2,
    n2,
    n2t,
    act,
    slope,
    gf,
    gb,
    gbt,
    acc,
    du,
    dd,
    l_sems,
    o_sems,
):
    loads_u = [pltpu.make_async_copy(w_up.at[b], wu.at[b], l_sems.at[b]) for b in range(4)]
    loads_d = [pltpu.make_async_copy(w_down.at[b], wd.at[b], l_sems.at[4 + b]) for b in range(4)]
    for b in range(4):
        loads_u[b].start()
        loads_d[b].start()
    for k in range(2):
        for i in range(2):
            for r in range(4):
                wo[k, 192 * i : 192 * i + 192, 192 * r : 192 * r + 192] = w_out_g[2 * i + k, r]

    @pl.loop(0, 2)
    def _(t):
        r = pl.ds(pl.multiple_of(t * 256, 256), 256)
        hidden = tokens[r].astype(F32) + vec[0:1]
        attended = nn(mixed[0, r], wo[0]) + nn(mixed[1, r], wo[1])
        total = hidden + attended + vec[3:4]
        h2[r] = total
        n2[r] = norm_rows(total, vec[4:5], vec[5:6]).astype(BF)

    n2t[...] = n2[...].T
    acc[...] = jnp.zeros_like(acc)
    for copy in loads_u + loads_d:
        copy.wait()

    @pl.loop(0, 4)
    def _(b):
        @pl.loop(0, 1)
        def _(t):
            r = pl.ds(pl.multiple_of(t * QROWS, QROWS), QROWS)
            pre = nn(n2[r], wu[b]) + b_up[b, 0:1]
            square = pre * pre
            tanh = jnp.tanh(GELU_IN * pre * (1.0 + 0.044715 * square))
            half = 0.5 * (1.0 + tanh)
            low = (pre * half).astype(BF)
            act[b, r] = low
            slope[b, r] = half + (0.5 * GELU_IN) * pre * (1.0 - tanh * tanh) * (
                1.0 + (3.0 * 0.044715) * square
            )
            acc[r] += nt(low, wd[b])

    sums[...] = jnp.zeros_like(sums)

    @pl.loop(0, 2)
    def _(t):
        r = pl.ds(pl.multiple_of(t * 256, 256), 256)
        final = h2[r] + acc[r] + vec[6:7]
        final_out[r] = final.astype(BF)
        diff = final - teacher[r].astype(F32)
        gf[r] = diff
        low = diff.astype(BF)
        gb[r] = low
        sums[6:7] += jnp.sum(low.astype(F32), axis=0, keepdims=True)
        sums[11:12] += jnp.sum(diff * diff, axis=0, keepdims=True)

    gbt[...] = gb[...].T
    acc[...] = jnp.zeros_like(acc)

    @pl.loop(0, 4)
    def _(b):
        dd[b] = nn(gbt[...], act[b]).astype(BF)
        pltpu.make_async_copy(dd.at[b], dw_down.at[b], o_sems.at[b]).start()

        @pl.loop(0, 1)
        def _(t):
            r = pl.ds(pl.multiple_of(t * QROWS, QROWS), QROWS)
            low = (nn(gb[r], wd[b]) * slope[b, r]).astype(BF)
            act[b, r] = low
            sums[pl.ds(7 + b, 1)] += jnp.sum(low.astype(F32), axis=0, keepdims=True)
            acc[r] += nt(low, wu[b])

        du[b] = nn(n2t[...], act[b]).astype(BF)
        pltpu.make_async_copy(du.at[b], dw_up.at[b], o_sems.at[4 + b]).start()

    @pl.loop(0, 2)
    def _(t):
        r = pl.ds(pl.multiple_of(t * 256, 256), 256)
        hidden = h2[r]
        center = jnp.mean(hidden, axis=1, keepdims=True)
        offset = hidden - center
        factor = lax.rsqrt(jnp.mean(offset * offset, axis=1, keepdims=True) + eps)
        unit = offset * factor
        grad = acc[r]
        scaled = grad * vec[4:5]
        first = jnp.mean(scaled, axis=1, keepdims=True)
        second = jnp.mean(scaled * unit, axis=1, keepdims=True)
        total = gf[r] + factor * (scaled - first - unit * second)
        grad_h2[r] = total
        low = total.astype(BF)
        gb[r] = low
        sums[3:4] += jnp.sum(grad * unit, axis=0, keepdims=True)
        sums[4:5] += jnp.sum(grad, axis=0, keepdims=True)
        sums[5:6] += jnp.sum(low.astype(F32), axis=0, keepdims=True)
        gm[0, r] = nt(low, wo[0]).astype(BF)
        gm[1, r] = nt(low, wo[1]).astype(BF)

    for k in range(2):
        whole = tn(mixed[k], gb[...]).astype(BF)
        for i in range(2):
            for r in range(4):
                dw_out[2 * i + k, r] = whole[192 * i : 192 * i + 192, 192 * r : 192 * r + 192]
    for b in range(4):
        pltpu.make_async_copy(dd.at[b], dw_down.at[b], o_sems.at[b]).wait()
        pltpu.make_async_copy(du.at[b], dw_up.at[b], o_sems.at[4 + b]).wait()


def middle(mixed, w_out_g, w_up, w_down, tokens, teacher, vec, b_up):
    any_space = pl.BlockSpec(memory_space=pl.ANY)
    vmem = pl.BlockSpec(memory_space=pltpu.VMEM)
    blocks = (4, D, D)
    return pl.pallas_call(
        middle_kernel,
        name="middle",
        in_specs=[vmem, vmem, any_space, any_space, vmem, vmem, vmem, vmem],
        out_specs=[vmem, vmem, any_space, any_space, vmem, vmem, vmem],
        out_shape=[
            jax.ShapeDtypeStruct((QROWS, D), BF),
            jax.ShapeDtypeStruct((QROWS, D), F32),
            jax.ShapeDtypeStruct(blocks, BF),
            jax.ShapeDtypeStruct(blocks, BF),
            jax.ShapeDtypeStruct((4, 4, 192, 192), BF),
            jax.ShapeDtypeStruct((2, QROWS, 384), BF),
            jax.ShapeDtypeStruct((16, D), F32),
        ],
        scratch_shapes=[
            pltpu.VMEM((2, 384, D), BF),
            pltpu.VMEM(blocks, BF),
            pltpu.VMEM(blocks, BF),
            pltpu.VMEM((QROWS, D), F32),
            pltpu.VMEM((QROWS, D), BF),
            pltpu.VMEM((D, QROWS), BF),
            pltpu.VMEM((4, QROWS, D), BF),
            pltpu.VMEM((4, QROWS, D), F32),
            pltpu.VMEM((QROWS, D), F32),
            pltpu.VMEM((QROWS, D), BF),
            pltpu.VMEM((D, QROWS), BF),
            pltpu.VMEM((QROWS, D), F32),
            pltpu.VMEM(blocks, BF),
            pltpu.VMEM(blocks, BF),
            pltpu.SemaphoreType.DMA((8,)),
            pltpu.SemaphoreType.DMA((8,)),
        ],
        compiler_params=pltpu.CompilerParams(vmem_limit_bytes=60 << 20),
    )(mixed, w_out_g, w_up, w_down, tokens, teacher, vec, b_up)


def norm(hidden, gain, shift):
    center = jnp.mean(hidden, axis=1, keepdims=True)
    offset = hidden - center
    factor = lax.rsqrt(jnp.mean(offset * offset, axis=1, keepdims=True) + eps)
    unit = offset * factor
    return unit * gain + shift, unit, factor


def norm_back(grad, gain, unit, factor):
    grad_unit = grad * gain
    first = jnp.mean(grad_unit, axis=1, keepdims=True)
    second = jnp.mean(grad_unit * unit, axis=1, keepdims=True)
    grad_in = factor * (grad_unit - first - unit * second)
    return grad_in, jnp.sum(grad * unit, axis=0), jnp.sum(grad, axis=0)


def head_layout(blocks):
    chunks = blocks.transpose(1, 0, 2).reshape(D, 6, 3, HD)
    q_list, kv_list = [], []
    for pair in range(3):
        a, b = 2 * pair, 2 * pair + 1
        q_list += [chunks[:, b, 0], chunks[:, a, 0]]
        kv_list += [chunks[:, a, 2], chunks[:, a, 1], chunks[:, b, 1], chunks[:, b, 2]]
    return jnp.concatenate(q_list, axis=1), jnp.concatenate(kv_list, axis=1)


def head_layout_back(grad_q, grad_kv):
    qc = grad_q.reshape(D, 3, 2, HD)
    kc = grad_kv.reshape(D, 3, 4, HD)
    pieces = []
    for pair in range(3):
        pieces += [qc[:, pair, 1], kc[:, pair, 1], kc[:, pair, 0]]
        pieces += [qc[:, pair, 0], kc[:, pair, 2], kc[:, pair, 3]]
    whole = jnp.concatenate(pieces, axis=1)
    return whole.reshape(D, 2, 576).transpose(1, 0, 2)


def on_device(
    tokens,
    teacher,
    pass_embed,
    ln1_gain,
    ln1_bias,
    qkv_weight,
    out_weight,
    out_bias,
    ln2_gain,
    ln2_bias,
    fc1_weight,
    fc1_bias,
    fc2_weight,
    fc2_bias,
    cont_group,
    token_count,
):
    n_dp = lax.axis_size("dp")
    n_gr = lax.axis_size("gr")
    n_gc = lax.axis_size("gc")
    z = lax.axis_index("gr")
    g = lax.axis_index("gc")
    c = g % 2
    y = g // 2
    swap_core = [(i, i ^ 1) for i in range(n_gc)]
    swap_y = [(i, i ^ 2) for i in range(n_gc)]

    parts = [pass_embed, ln1_gain, ln1_bias, out_bias, ln2_gain, ln2_bias, fc2_bias]
    if n_dp == 2:
        own = jnp.broadcast_to(jnp.pad(cont_group, (0, 120)), (8, 128))
        (
            mixed,
            lse_rows,
            w_out,
            w_up,
            w_down,
            n1_prompt,
            n1_chip,
            q,
            kvo,
            kvp,
            w_q,
            w_kv,
            vectors,
            b_up,
            owners,
        ) = front(
            tokens, parts, fc1_bias, own, qkv_weight, [out_weight, fc1_weight, fc2_weight], 1
        )
        n1_chip = n1_chip.reshape(2 * QROWS, D)
        owners = owners[:, 0, :8]
    else:
        vectors = lax.all_gather(jnp.stack(parts).astype(F32), "gr", axis=1, tiled=True)
        b_up = lax.all_gather(fc1_bias, "gc", axis=0, tiled=True).astype(F32)
        owners = lax.all_gather(cont_group, "gr", axis=0, tiled=True)
    embed, gain1, shift1, b_out, gain2, shift2, b_down = [vectors[i] for i in range(7)]
    owners = owners.reshape(4, 2, 4)
    mine = lax.dynamic_slice(owners, (2 * y, jnp.maximum(z - 2, 0), 0), (2, 1, 4)).reshape(8)
    own_groups = jnp.repeat(2 * y + jnp.arange(2), 4)
    grp = jnp.where(z < 2, own_groups, mine).astype(jnp.int32)
    z_arr = z.astype(jnp.int32).reshape(1)

    hidden = tokens.astype(F32) + embed
    normed1, unit1, factor1 = norm(hidden, gain1, shift1)
    n1 = normed1.astype(BF)

    if n_dp != 2:
        w_other = lax.ppermute(qkv_weight, "gc", swap_y)
        w_pair = jnp.where(
            y == 0, jnp.stack([qkv_weight, w_other]), jnp.stack([w_other, qkv_weight])
        )
        w_qkv = lax.all_gather(w_pair, "gr", axis=1, tiled=True)
        n1_other = lax.ppermute(n1, "gc", swap_core)
        n1_chip = jnp.where(
            c == 0, jnp.concatenate([n1, n1_other]), jnp.concatenate([n1_other, n1])
        )
        n1_col = lax.all_gather(n1, "gr", axis=0, tiled=True)[:P_SIZE]
        n1_prompt = lax.all_gather(n1_col, "gc", axis=0, tiled=True)
        w_q, w_kv = head_layout(w_qkv)
        kvp = nn(n1_prompt, w_kv).astype(BF)
        kvo = nn(n1_chip, w_kv).astype(BF)
        q = (nn(n1_chip, w_q) * 0.125).astype(BF)
        w_out = lax.all_gather(out_weight, ("gc", "gr"))
        w_up = lax.all_gather(fc1_weight, ("gc", "gr"))
        w_down = lax.all_gather(fc2_weight, ("gc", "gr"))
        mixed_heads, lse = attend(grp, z_arr, q, kvo, kvp)
        lse_rows = lse[:, ::64].reshape(8, CL, 3, 2).transpose(2, 0, 3, 1)
        halves = mixed_heads.reshape(2, QROWS, 384)
        keep = lax.dynamic_index_in_dim(halves, c, 0, keepdims=False)
        give = lax.dynamic_index_in_dim(halves, 1 - c, 0, keepdims=False)
        take = lax.ppermute(give, "gc", swap_core)
        mixed = jnp.where(c == 0, jnp.stack([keep, take]), jnp.stack([take, keep]))
    w_up = w_up.reshape(n_gc, D, FF // n_gc)
    w_down = w_down.reshape(n_gc, D, FF // n_gc)
    if n_dp == 2:
        final, grad_h2, grad_w_up, grad_w_down, grad_w_out, gm, later_sums = middle(
            mixed, w_out, w_up, w_down, tokens, teacher, vectors, b_up
        )
    else:
        w_out = w_out.reshape(2, 2, n_gr, 192, 192).transpose(1, 0, 3, 2, 4).reshape(2, 384, D)

        attended = lax.dot_general(
            mixed, w_out, (((0, 2), (0, 1)), ((), ())), preferred_element_type=F32
        )
        hidden2 = hidden + attended + b_out
        normed2, unit2, factor2 = norm(hidden2, gain2, shift2)
        n2 = normed2.astype(BF)
        pre = lax.dot_general(n2, w_up, (((1,), (1,)), ((), ())), preferred_element_type=F32)
        pre = pre.reshape(QROWS, FF) + b_up
        active, gelu_back = jax.vjp(partial(jax.nn.gelu, approximate=True), pre)
        act = active.astype(BF)
        act_blocks = act.reshape(QROWS, n_gc, FF // n_gc)
        final = (
            hidden2
            + lax.dot_general(
                act_blocks, w_down, (((1, 2), (0, 2)), ((), ())), preferred_element_type=F32
            )
            + b_down
        )
        grad_final = final - teacher.astype(F32)
        squared = jnp.sum(grad_final * grad_final, axis=0)
        gb = grad_final.astype(BF)
        grad_b_down = jnp.sum(gb, axis=0, dtype=F32)
        grad_active = lax.dot_general(
            gb, w_down, (((1,), (1,)), ((), ())), preferred_element_type=F32
        ).reshape(QROWS, FF)
        grad_w_down = jnp.einsum("td,tgf->gdf", gb, act_blocks, preferred_element_type=F32)
        (grad_pre,) = gelu_back(grad_active)
        gp = grad_pre.astype(BF)
        gp_blocks = gp.reshape(QROWS, n_gc, FF // n_gc)
        grad_b_up = jnp.sum(gp, axis=0, dtype=F32)
        grad_w_up = jnp.einsum("td,tgf->gdf", n2, gp_blocks, preferred_element_type=F32)
        grad_n2 = lax.dot_general(
            gp_blocks, w_up, (((1, 2), (0, 2)), ((), ())), preferred_element_type=F32
        )
        back2, grad_gain2, grad_shift2 = norm_back(grad_n2, gain2, unit2, factor2)
        grad_h2 = grad_final + back2
        ga = grad_h2.astype(BF)
        grad_b_out = jnp.sum(ga, axis=0, dtype=F32)
        grad_w_out = jnp.einsum("ctk,tn->ckn", mixed, ga, preferred_element_type=F32)
        gm = jnp.einsum("tn,ckn->ctk", ga, w_out, preferred_element_type=F32).astype(BF)
        grad_w_up = grad_w_up.astype(BF)
        grad_w_down = grad_w_down.astype(BF)
        grad_w_out = (
            grad_w_out.astype(BF)
            .reshape(2, 2, 192, n_gr, 192)
            .transpose(1, 0, 3, 2, 4)
            .reshape(n_gc, n_gr, 192, 192)
        )
    weight_grads = [
        grad_w_down.reshape(n_gc, n_gr, 192, 768),
        grad_w_up.reshape(n_gc, n_gr, 192, 768),
        grad_w_out,
    ]
    if n_dp == 2:
        dq, dkvo, dkv, out_w_down, out_w_up, out_w_out = attend_back_scatter(
            grp, q, lse_rows, kvo, kvp, gm, weight_grads, 3
        )
    else:
        gm_keep = lax.dynamic_index_in_dim(gm, c, 0, keepdims=False)
        gm_give = lax.dynamic_index_in_dim(gm, 1 - c, 0, keepdims=False)
        gm_take = lax.ppermute(gm_give, "gc", swap_core)
        gm_chip = jnp.where(c == 0, jnp.stack([gm_keep, gm_take]), jnp.stack([gm_take, gm_keep]))
        gm_chip = gm_chip.reshape(2 * QROWS, 384)

        def scatter16(blocks):
            part = lax.psum_scatter(
                blocks.reshape(n_gc * n_gr * blocks.shape[2], -1),
                ("gc", "gr"),
                scatter_dimension=0,
                tiled=True,
            )
            return lax.psum(part, "dp").astype(F32)

        out_w_down, out_w_up, out_w_out = [scatter16(grad) for grad in weight_grads]
        dq, dkvo, dkvp = attend_back(grp, z_arr, q, gm_chip, lse_rows, kvo, kvp)
        part_prompt = nt(dkvp, w_kv).astype(BF)

        part_chip = (nt(dq, w_q) + nt(dkvo, w_kv)).reshape(2, QROWS, D)
        grad_kv = tn(n1_prompt, dkvp) + tn(n1_chip, dkvo)
        grad_q = tn(n1_chip, dq)
        grad_qkv = head_layout_back(grad_q, grad_kv)

    if n_dp == 2:
        input_grad, sums, out_w_qkv = tail_exchange(
            grp,
            dkv,
            n1_prompt,
            n1_chip,
            dkvo,
            dq,
            w_q,
            w_kv,
            grad_h2,
            tokens,
            vectors,
            later_sums,
            4,
        )
    else:
        later_sums = jnp.concatenate(
            [
                grad_gain2[None],
                grad_shift2[None],
                grad_b_out[None],
                grad_b_down[None],
                grad_b_up.reshape(4, D),
                squared[None],
                jnp.zeros((4, D), F32),
            ]
        )
        back_prompt = lax.psum_scatter(part_prompt, "gc", scatter_dimension=0, tiled=True)
        back_prompt = lax.psum_scatter(
            jnp.concatenate([back_prompt, jnp.zeros_like(back_prompt)]),
            "gr",
            scatter_dimension=0,
            tiled=True,
        ).astype(F32)
        part_keep = lax.dynamic_index_in_dim(part_chip, c, 0, keepdims=False)
        part_give = lax.dynamic_index_in_dim(part_chip, 1 - c, 0, keepdims=False)
        part_take = lax.ppermute(part_give.astype(BF), "gc", swap_core).astype(F32)
        grad_n1 = part_keep + part_take + back_prompt
        qkv_keep = lax.dynamic_index_in_dim(grad_qkv, y, 0, keepdims=False)
        qkv_give = lax.dynamic_index_in_dim(grad_qkv, 1 - y, 0, keepdims=False)
        qkv_take = lax.ppermute(qkv_give.astype(BF), "gc", swap_y).astype(F32)
        out_w_qkv = lax.psum_scatter(
            (qkv_keep + qkv_take).astype(BF), "gr", scatter_dimension=0, tiled=True
        )
        out_w_qkv = lax.psum(out_w_qkv, "dp").astype(F32)
        back1, grad_gain1, grad_shift1 = norm_back(grad_n1, gain1, unit1, factor1)
        input_grad = grad_h2 + back1
        first_sums = jnp.stack([jnp.sum(input_grad, axis=0), grad_gain1, grad_shift1])
        sums = lax.psum(jnp.concatenate([first_sums, later_sums]), ("dp", "gr", "gc"))
    sums = sums[:12].reshape(12 * D)
    loss = (jnp.sum(sums[11 * D :]) / (D * token_count[0].astype(F32))).reshape(1)
    rows = sums[: 7 * D].reshape(7, n_gr, D // n_gr)
    rows = lax.dynamic_index_in_dim(rows, z, 1, keepdims=False)
    up = lax.dynamic_index_in_dim(
        sums[7 * D : 7 * D + FF].reshape(n_gc, FF // n_gc), g, 0, keepdims=False
    )
    return (
        final.astype(BF),
        loss,
        input_grad,
        rows[0],
        rows[1],
        rows[2],
        out_w_qkv,
        out_w_out,
        rows[5],
        rows[3],
        rows[4],
        out_w_up,
        up,
        out_w_down,
        rows[6],
    )


def solution(mesh):
    rows = P(("dp", "gr", "gc"), None)
    in_specs = (
        rows,
        rows,
        P("gr"),
        P("gr"),
        P("gr"),
        P("gr", "gc"),
        P("gc", "gr"),
        P("gr"),
        P("gr"),
        P("gr"),
        P("gr", "gc"),
        P("gc"),
        P("gr", "gc"),
        P("gr"),
        P(("dp", "gr")),
        P(),
    )
    out_specs = (
        rows,
        P(),
        rows,
        P("gr"),
        P("gr"),
        P("gr"),
        P("gr", "gc"),
        P("gc", "gr"),
        P("gr"),
        P("gr"),
        P("gr"),
        P("gr", "gc"),
        P("gc"),
        P("gr", "gc"),
        P("gr"),
    )
    return jax.shard_map(
        on_device, mesh=mesh, in_specs=in_specs, out_specs=out_specs, check_vma=False
    )
```

```python
from functools import partial
import math

import jax
import jax.numpy as jnp
from jax import lax
from jax.experimental import pallas as pl
from jax.experimental.pallas import tpu as pltpu
from jax.sharding import PartitionSpec as P

D = 768
HD = 64
FF = 3072
P_SIZE = 1024
CL = 128
QROWS = 512
eps = 1e-05
negative = -1e30
BF = jnp.bfloat16
F32 = jnp.float32


def nt(a, b):
    return lax.dot_general(a, b, (((1,), (1,)), ((), ())), preferred_element_type=F32)


def nn(a, b):
    return lax.dot_general(a, b, (((1,), (0,)), ((), ())), preferred_element_type=F32)


def tn(a, b):
    return lax.dot_general(a, b, (((0,), (0,)), ((), ())), preferred_element_type=F32)


def att_fwd_kernel(grp_ref, z_ref, q_ref, kvo_ref, kvp_ref, o_ref, lse_ref):
    j = pl.program_id(1)
    row0 = pl.multiple_of(grp_ref[j] * P_SIZE, P_SIZE)
    z = z_ref[0]
    lane = lax.broadcasted_iota(jnp.int32, (CL, 128), 1)
    low = lane < 64
    zero = jnp.zeros((CL, 128), BF)
    q = q_ref[...]
    q_parts = (jnp.where(low, zero, q), jnp.where(low, q, zero))

    @pl.when(z >= 2)
    def _():
        row = lax.broadcasted_iota(jnp.int32, (CL, CL), 0)
        near_ok = lax.broadcasted_iota(jnp.int32, (CL, CL), 1) <= row
        mixes, sums = [], []
        for h in range(2):
            cols = slice(128 * h, 128 * h + 128)
            kv = kvp_ref[pl.ds(row0, P_SIZE), cols]
            kvo = kvo_ref[:, cols]
            far = nt(q_parts[h], kv)
            near = jnp.where(near_ok, nt(q_parts[h], kvo), negative)
            top = jnp.maximum(
                jnp.max(far, axis=1, keepdims=True), jnp.max(near, axis=1, keepdims=True)
            )
            far = jnp.exp(far - top)
            near = jnp.exp(near - top)
            total = jnp.sum(far, axis=1, keepdims=True) + jnp.sum(near, axis=1, keepdims=True)
            mix = nn(far.astype(BF), kv) + nn(near.astype(BF), kvo)
            mixes.append(mix / total)
            sums.append(jnp.broadcast_to(top + jnp.log(total), (CL, 128)))
        o_ref[...] = jnp.where(low, mixes[0], mixes[1]).astype(BF)
        lse_ref[...] = jnp.where(low, sums[0], sums[1])

    @pl.when(z < 2)
    def _():
        limit = z * QROWS + (j % (QROWS // CL)) * CL
        row = lax.broadcasted_iota(jnp.int32, (CL, P_SIZE), 0)
        key = lax.broadcasted_iota(jnp.int32, (CL, P_SIZE), 1)
        allowed = key - row <= limit
        mixes, sums = [], []
        for h in range(2):
            cols = slice(128 * h, 128 * h + 128)
            kv = kvp_ref[pl.ds(row0, P_SIZE), cols]
            far = jnp.where(allowed, nt(q_parts[h], kv), negative)
            top = jnp.max(far, axis=1, keepdims=True)
            far = jnp.exp(far - top)
            total = jnp.sum(far, axis=1, keepdims=True)
            mix = nn(far.astype(BF), kv)
            mixes.append(mix / total)
            sums.append(jnp.broadcast_to(top + jnp.log(total), (CL, 128)))
        o_ref[...] = jnp.where(low, mixes[0], mixes[1]).astype(BF)
        lse_ref[...] = jnp.where(low, sums[0], sums[1])


def attend(grp, z, q, kvo, kvp):
    rows = q.shape[0]
    pairs = q.shape[1] // 128
    groups_rows = kvp.shape[0]
    return pl.pallas_call(
        att_fwd_kernel,
        name="att_fwd",
        grid_spec=pltpu.PrefetchScalarGridSpec(
            num_scalar_prefetch=2,
            grid=(pairs, rows // CL),
            in_specs=[
                pl.BlockSpec((CL, 128), lambda p, j, *_: (j, p)),
                pl.BlockSpec((CL, 256), lambda p, j, *_: (j, p)),
                pl.BlockSpec((groups_rows, 256), lambda p, j, *_: (0, p)),
            ],
            out_specs=[
                pl.BlockSpec((CL, 128), lambda p, j, *_: (j, p)),
                pl.BlockSpec((CL, 128), lambda p, j, *_: (j, p)),
            ],
        ),
        out_shape=[
            jax.ShapeDtypeStruct((rows, pairs * 128), BF),
            jax.ShapeDtypeStruct((rows, pairs * 128), F32),
        ],
        compiler_params=pltpu.CompilerParams(vmem_limit_bytes=40 << 20),
        cost_estimate=pl.CostEstimate(
            flops=4 * rows * P_SIZE * 128 * pairs * 2,
            bytes_accessed=groups_rows * 512 * pairs,
            transcendentals=rows * P_SIZE * pairs * 2,
        ),
    )(grp, z, q, kvo, kvp)


def att_bwd_kernel(
    grp_ref, z_ref, q_ref, gm_ref, lse_ref, kvo_ref, kvp_ref, dq_ref, dkvo_ref, dkvp_ref, acc
):
    j = pl.program_id(1)
    row0 = pl.multiple_of(grp_ref[j] * P_SIZE, P_SIZE)
    z = z_ref[0]
    low = lax.broadcasted_iota(jnp.int32, (CL, 128), 1) < 64
    zero = jnp.zeros((CL, 128), BF)
    q = q_ref[...]
    gm = gm_ref[...]
    stacks = (
        jnp.concatenate([jnp.where(low, zero, q), jnp.where(low, gm, zero)], axis=0),
        jnp.concatenate([jnp.where(low, q, zero), jnp.where(low, zero, gm)], axis=0),
    )

    @pl.when(j == 0)
    def _():
        acc[...] = jnp.zeros_like(acc)

    @pl.when(z >= 2)
    def _():
        row = lax.broadcasted_iota(jnp.int32, (CL, CL), 0)
        near_ok = row <= lax.broadcasted_iota(jnp.int32, (CL, CL), 1)
        dqs = []
        for h in range(2):
            cols = slice(128 * h, 128 * h + 128)
            kv = kvp_ref[pl.ds(row0, P_SIZE), cols]
            kvo = kvo_ref[:, cols]
            lse = lse_ref[0, 0, h : h + 1, :]
            far = nt(kv, stacks[h])
            near = nt(kvo, stacks[h])
            pf = jnp.exp(far[:, :CL] - lse)
            pn = jnp.where(near_ok, jnp.exp(near[:, :CL] - lse), 0.0)
            df = far[:, CL:]
            dn = near[:, CL:]
            inner = jnp.sum(pf * df, axis=0, keepdims=True) + jnp.sum(
                pn * dn, axis=0, keepdims=True
            )
            sf = (pf * (df - inner)).astype(BF)
            sn = (pn * (dn - inner)).astype(BF)
            acc[pl.ds(row0, P_SIZE), cols] += nn(
                jnp.concatenate([sf, pf.astype(BF)], axis=1), stacks[h]
            )
            dkvo_ref[:, cols] = nn(
                jnp.concatenate([sn, pn.astype(BF)], axis=1), stacks[h]
            ).astype(BF)
            dqs.append(tn(sf, kv) + tn(sn, kvo))
        dq_ref[...] = (jnp.where(low, dqs[1], dqs[0]) * 0.125).astype(BF)

    @pl.when(z < 2)
    def _():
        limit = z * QROWS + (j % (QROWS // CL)) * CL
        key = lax.broadcasted_iota(jnp.int32, (P_SIZE, CL), 0)
        row = lax.broadcasted_iota(jnp.int32, (P_SIZE, CL), 1)
        allowed = key - row <= limit
        dqs = []
        for h in range(2):
            cols = slice(128 * h, 128 * h + 128)
            kv = kvp_ref[pl.ds(row0, P_SIZE), cols]
            lse = lse_ref[0, 0, h : h + 1, :]
            far = nt(kv, stacks[h])
            pf = jnp.where(allowed, jnp.exp(far[:, :CL] - lse), 0.0)
            df = far[:, CL:]
            inner = jnp.sum(pf * df, axis=0, keepdims=True)
            sf = (pf * (df - inner)).astype(BF)
            acc[pl.ds(row0, P_SIZE), cols] += nn(
                jnp.concatenate([sf, pf.astype(BF)], axis=1), stacks[h]
            )
            dqs.append(tn(sf, kv))
        dkvo_ref[...] = jnp.zeros_like(dkvo_ref)
        dq_ref[...] = (jnp.where(low, dqs[1], dqs[0]) * 0.125).astype(BF)

    @pl.when(j == pl.num_programs(1) - 1)
    def _():
        dkvp_ref[...] = acc[...].astype(BF)


def attend_back(grp, z, q, gm, lse, kvo, kvp):
    rows = q.shape[0]
    pairs = q.shape[1] // 128
    groups_rows = kvp.shape[0]
    return pl.pallas_call(
        att_bwd_kernel,
        name="att_bwd",
        grid_spec=pltpu.PrefetchScalarGridSpec(
            num_scalar_prefetch=2,
            grid=(pairs, rows // CL),
            in_specs=[
                pl.BlockSpec((CL, 128), lambda p, j, *_: (j, p)),
                pl.BlockSpec((CL, 128), lambda p, j, *_: (j, p)),
                pl.BlockSpec((1, 1, 2, 128), lambda p, j, *_: (p, j, 0, 0)),
                pl.BlockSpec((CL, 256), lambda p, j, *_: (j, p)),
                pl.BlockSpec((groups_rows, 256), lambda p, j, *_: (0, p)),
            ],
            out_specs=[
                pl.BlockSpec((CL, 128), lambda p, j, *_: (j, p)),
                pl.BlockSpec((CL, 256), lambda p, j, *_: (j, p)),
                pl.BlockSpec((groups_rows, 256), lambda p, j, *_: (0, p)),
            ],
            scratch_shapes=[pltpu.VMEM((groups_rows, 256), F32)],
        ),
        out_shape=[
            jax.ShapeDtypeStruct((rows, pairs * 128), BF),
            jax.ShapeDtypeStruct((rows, pairs * 256), BF),
            jax.ShapeDtypeStruct((groups_rows, pairs * 256), BF),
        ],
        compiler_params=pltpu.CompilerParams(vmem_limit_bytes=48 << 20),
        cost_estimate=pl.CostEstimate(
            flops=10 * rows * P_SIZE * 128 * pairs * 2,
            bytes_accessed=groups_rows * 1024 * pairs,
            transcendentals=rows * P_SIZE * pairs * 2,
        ),
    )(grp, z, q, gm, lse, kvo, kvp)


MESH = pl.DeviceIdType.MESH


def places():
    x = lax.axis_index("dp")
    z = lax.axis_index("gr")
    g = lax.axis_index("gc")
    return x, z, g, g // 2, g % 2


def greet(partners):
    barrier = pltpu.get_barrier_semaphore()
    for partner in partners:
        pl.semaphore_signal(barrier, inc=1, device_id=partner, device_id_type=MESH)
    pl.semaphore_wait(barrier, len(partners))


def all_partners():
    x, z, g, y, c = places()
    by_z = [{"gr": z ^ step} for step in (1, 2, 3)]
    return [{"gc": g ^ 1}, {"gc": g ^ 2}, {"dp": x ^ 1}] + by_z


def send(src, dst, sems, slot, target, send_slot=None):
    return pltpu.make_async_remote_copy(
        src_ref=src,
        dst_ref=dst,
        send_sem=sems[0].at[slot if send_slot is None else send_slot],
        recv_sem=sems[1].at[slot],
        device_id=target,
        device_id_type=MESH,
    )


def add_into(dst, left, right):
    rows = dst.shape[0]
    size = 48 if rows % 48 == 0 else 64

    @pl.loop(0, rows // size)
    def _(i):
        r = pl.ds(pl.multiple_of(i * size, 16), size)
        dst[r] = (left[r].astype(F32) + right[r].astype(F32)).astype(dst.dtype)


RS_SLOTS = 28
RS_ORDER = (3, 2, 1, 0)
PACE = 26


def rs_plan(grads, outs, bufs, sems, l_sems, base, paired):
    own, ra, rb0, rb1, rc0, rc1, sc, rd, re = bufs
    x, z, g, y, c = places()
    sib, over_y, over_x = {"gc": g ^ 1}, {"gc": g ^ 2}, {"dp": x ^ 1}
    rows = grads.shape[2]
    q = rows // 4
    mine0 = pl.ds(pl.multiple_of(q * x, 16), q)
    other0 = pl.ds(pl.multiple_of(q * (1 - x), 16), q)
    mine1 = pl.ds(pl.multiple_of(2 * q + q * x, 16), q)
    other1 = pl.ds(pl.multiple_of(2 * q + q * (1 - x), 16), q)
    first = pl.ds(0, 2 * q)
    slot = base * RS_SLOTS

    def load(i, s):
        source = grads.at[2 * i + c, z ^ s] if paired else grads.at[i, z ^ s]
        return pltpu.make_async_copy(source, own.at[i, s], l_sems.at[8 * base + 2 * s + i])

    def hop_a(i, s):
        return send(grads.at[2 * i + 1 - c, z ^ s], ra.at[i, s], sems, slot + 6 * s + i, sib)

    def hop_b0(s):
        return send(own.at[1 - y, s, first], rb0.at[s], sems, slot + 6 * s + 2, over_y)

    def hop_b1(s):
        return send(own.at[:, s, other1], rb1.at[s], sems, slot + 6 * s + 3, over_x)

    def hop_c0(s):
        return send(own.at[y, s, other0], rc0.at[s], sems, slot + 6 * s + 4, over_x)

    def hop_c1(s):
        return send(own.at[1 - y, s, mine1], rc1.at[s], sems, slot + 6 * s + 5, over_y)

    def hop_z(s):
        return send(sc.at[s], rd.at[s - 1], sems, slot + 23 + s, {"gr": z ^ s})

    def hop_d():
        return send(sc.at[0], re, sems, slot + 27, over_x)

    def begin(s):
        for i in range(2):
            load(i, s).start()
            if paired:
                hop_a(i, s).start()

    def after_a(s):
        for i in range(2):
            load(i, s).wait()
            if paired:
                hop_a(i, s).wait()
                add_into(own.at[i, s], own.at[i, s], ra.at[i, s])
        hop_b0(s).start()
        hop_b1(s).start()

    def after_b(s):
        hop_b0(s).wait()
        hop_b1(s).wait()
        add_into(own.at[y, s, first], own.at[y, s, first], rb0.at[s])
        for i in range(2):
            add_into(own.at[i, s, mine1], own.at[i, s, mine1], rb1.at[s, i])
        hop_c0(s).start()
        hop_c1(s).start()

    def after_c(s):
        hop_c0(s).wait()
        hop_c1(s).wait()
        add_into(sc.at[s, pl.ds(0, q)], own.at[y, s, mine0], rc0.at[s])
        add_into(sc.at[s, pl.ds(q, q)], own.at[y, s, mine1], rc1.at[s])
        if s:
            hop_z(s).start()

    def total():
        for s in (1, 2, 3):
            hop_z(s).wait()
        whole = sc[0].astype(F32)
        for i in range(3):
            whole = whole + rd[i].astype(F32)
        sc[0] = whole.astype(BF)
        hop_d().start()

    def finish():
        hop_d().wait()
        outs[mine0] = sc[0, pl.ds(0, q)].astype(F32)
        outs[mine1] = sc[0, pl.ds(q, q)].astype(F32)
        outs[other0] = re[pl.ds(0, q)].astype(F32)
        outs[other1] = re[pl.ds(q, q)].astype(F32)

    return begin, after_a, after_b, after_c, total, finish


def rs_steps(plans):
    order = [(plan, s) for plan in plans for s in RS_ORDER]
    n = len(order)
    steps = [[partial(plan[0], s) for plan, s in order]]
    for i in range(n + 10):
        part = []
        if i < n:
            part.append(partial(order[i][0][1], order[i][1]))
        if 2 <= i < n + 2:
            part.append(partial(order[i - 2][0][2], order[i - 2][1]))
        if 4 <= i < n + 4:
            part.append(partial(order[i - 4][0][3], order[i - 4][1]))
        if 7 <= i < n + 7 and (i - 7) % 4 == 3:
            part.append(plans[(i - 7) // 4][4])
        if 9 <= i < n + 9 and (i - 9) % 4 == 3:
            part.append(plans[(i - 9) // 4][5])
        if part:
            steps.append(part)
    return steps


def rs_scratch(rows, cols, paired):
    q = rows // 4
    return [
        pltpu.VMEM((2, 4, rows, cols), BF),
        pltpu.VMEM((2, 4, rows, cols) if paired else (16, 128), BF),
        pltpu.VMEM((4, 2 * q, cols), BF),
        pltpu.VMEM((4, 2, q, cols), BF),
        pltpu.VMEM((4, q, cols), BF),
        pltpu.VMEM((4, q, cols), BF),
        pltpu.VMEM((4, 2 * q, cols), BF),
        pltpu.VMEM((3, 2 * q, cols), BF),
        pltpu.VMEM((2 * q, cols), BF),
    ]


def att_scatter_kernel(count, grp_ref, q_ref, lse_ref, kvo_ref, kvp_ref, gm, *refs):
    grads = refs[:count]
    dq_ref, dkvo_ref, dkv_ref = refs[count : count + 3]
    outs = refs[count + 3 : 2 * count + 3]
    rest = refs[2 * count + 3 :]
    bufs, (gmx, sem_s, sem_r, l_sems, m_send, m_recv, m_local) = rest[: 9 * count], rest[9 * count :]
    p, j = pl.program_id(0), pl.program_id(1)
    step = p * pl.num_programs(1) + j
    x, z, g, y, c = places()
    hooks = rs_steps(
        [
            rs_plan(grads[k], outs[k], bufs[9 * k : 9 * k + 9], (sem_s, sem_r), l_sems, k, True)
            for k in range(count)
        ]
    )

    def exchange(i):
        cols = pl.ds(128 * i, 128)
        return (
            pltpu.make_async_copy(gm.at[c, :, cols], gmx.at[i, c], m_local.at[i]),
            send(gm.at[1 - c, :, cols], gmx.at[i, c], (m_send, m_recv), i, {"gc": g ^ 1}),
        )

    @pl.when(step == 0)
    def _():
        greet(all_partners())
        for i in range(3):
            for copy in exchange(i):
                copy.start()
        for hook in hooks[0]:
            hook()
        for copy in exchange(0):
            copy.wait()

    for i in (1, 2):

        @pl.when(step == 8 * i)
        def _():
            for copy in exchange(i):
                copy.wait()

    last = len(hooks) - 1
    for when in range(1, 23):
        parts = [h for i in range(1, last) if max(1, i * PACE // (last - 1)) == when for h in hooks[i]]
        if parts:

            @pl.when(step == when)
            def _():
                for hook in parts:
                    hook()

    group = grp_ref[j]
    low = lax.broadcasted_iota(jnp.int32, (CL, 128), 1) < 64
    zero = jnp.zeros((CL, 128), BF)
    q = q_ref[0]
    gmix = gmx[p, j // 4, pl.ds(pl.multiple_of((j % 4) * CL, CL), CL)]
    stacks = (
        jnp.concatenate([jnp.where(low, zero, q), jnp.where(low, gmix, zero)], axis=0),
        jnp.concatenate([jnp.where(low, q, zero), jnp.where(low, zero, gmix)], axis=0),
    )

    @pl.when(z >= 2)
    def _():
        row = lax.broadcasted_iota(jnp.int32, (CL, CL), 0)
        near_ok = row <= lax.broadcasted_iota(jnp.int32, (CL, CL), 1)
        dqs = []
        for h in range(2):
            cols = slice(128 * h, 128 * h + 128)
            kv = kvp_ref[0, group, :, cols]
            kvo = kvo_ref[0, :, cols]
            lse = lse_ref[0, 0, h : h + 1, :]
            far = nt(kv, stacks[h])
            near = nt(kvo, stacks[h])
            pf = jnp.exp(far[:, :CL] - lse)
            pn = jnp.where(near_ok, jnp.exp(near[:, :CL] - lse), 0.0)
            df = far[:, CL:]
            dn = near[:, CL:]
            inner = jnp.sum(pf * df, axis=0, keepdims=True) + jnp.sum(
                pn * dn, axis=0, keepdims=True
            )
            sf = (pf * (df - inner)).astype(BF)
            sn = (pn * (dn - inner)).astype(BF)
            dkv_ref[0, :, cols] = nn(
                jnp.concatenate([sf, pf.astype(BF)], axis=1), stacks[h]
            ).astype(BF)
            dkvo_ref[:, cols] = nn(
                jnp.concatenate([sn, pn.astype(BF)], axis=1), stacks[h]
            ).astype(BF)
            dqs.append(tn(sf, kv) + tn(sn, kvo))
        dq_ref[...] = (jnp.where(low, dqs[1], dqs[0]) * 0.125).astype(BF)

    @pl.when(z < 2)
    def _():
        limit = z * QROWS + (j % (QROWS // CL)) * CL
        key = lax.broadcasted_iota(jnp.int32, (P_SIZE, CL), 0)
        row = lax.broadcasted_iota(jnp.int32, (P_SIZE, CL), 1)
        allowed = key - row <= limit
        dqs = []
        for h in range(2):
            cols = slice(128 * h, 128 * h + 128)
            kv = kvp_ref[0, group, :, cols]
            lse = lse_ref[0, 0, h : h + 1, :]
            far = nt(kv, stacks[h])
            pf = jnp.where(allowed, jnp.exp(far[:, :CL] - lse), 0.0)
            df = far[:, CL:]
            inner = jnp.sum(pf * df, axis=0, keepdims=True)
            sf = (pf * (df - inner)).astype(BF)
            dkv_ref[0, :, cols] = nn(
                jnp.concatenate([sf, pf.astype(BF)], axis=1), stacks[h]
            ).astype(BF)
            dqs.append(tn(sf, kv))
        dkvo_ref[...] = jnp.zeros_like(dkvo_ref)
        dq_ref[...] = (jnp.where(low, dqs[1], dqs[0]) * 0.125).astype(BF)

    @pl.when(step == 23)
    def _():
        for i in range(1, last + 1):
            if i == last or i * PACE // (last - 1) > 22:
                for hook in hooks[i]:
                    hook()


def attend_back_scatter(grp, q, lse, kvo, kvp, gm, grads, collective_id):
    rows = q.shape[1]
    count = len(grads)
    any_space = pl.BlockSpec(memory_space=pl.ANY)
    scratch = []
    for grad in grads:
        scratch += rs_scratch(grad.shape[2], grad.shape[3], True)
    slots = RS_SLOTS * count
    return pl.pallas_call(
        partial(att_scatter_kernel, count),
        name="attend_back_scatter",
        grid_spec=pltpu.PrefetchScalarGridSpec(
            num_scalar_prefetch=1,
            grid=(3, rows // CL),
            in_specs=[
                pl.BlockSpec((1, CL, 128), lambda p, j, *_: (p, j, 0)),
                pl.BlockSpec((1, 1, 2, 128), lambda p, j, *_: (p, j, 0, 0)),
                pl.BlockSpec((1, CL, 256), lambda p, j, *_: (p, j, 0)),
                pl.BlockSpec((1, 4, P_SIZE, 256), lambda p, j, *_: (p, 0, 0, 0)),
            ]
            + [any_space] * (count + 1),
            out_specs=[
                pl.BlockSpec((CL, 128), lambda p, j, *_: (j, p)),
                pl.BlockSpec((CL, 256), lambda p, j, *_: (j, p)),
                pl.BlockSpec((1, P_SIZE, 256), lambda p, j, *_: (j, 0, p)),
            ]
            + [pl.BlockSpec(grad.shape[2:], lambda p, j, *_: (0, 0)) for grad in grads],
            scratch_shapes=scratch
            + [
                pltpu.VMEM((3, 2, QROWS, 128), BF),
                pltpu.SemaphoreType.DMA((slots,)),
                pltpu.SemaphoreType.DMA((slots,)),
                pltpu.SemaphoreType.DMA((8 * count,)),
                pltpu.SemaphoreType.DMA((3,)),
                pltpu.SemaphoreType.DMA((3,)),
                pltpu.SemaphoreType.DMA((3,)),
            ],
        ),
        out_shape=[
            jax.ShapeDtypeStruct((rows, 384), BF),
            jax.ShapeDtypeStruct((rows, 768), BF),
            jax.ShapeDtypeStruct((8, P_SIZE, 768), BF),
        ]
        + [jax.ShapeDtypeStruct(grad.shape[2:], F32) for grad in grads],
        compiler_params=pltpu.CompilerParams(
            collective_id=collective_id, has_side_effects=True, vmem_limit_bytes=56 << 20
        ),
    )(grp, q, lse, kvo, kvp, gm, *grads)


def norm_rows(hidden, gain, shift):
    center = jnp.mean(hidden, axis=1, keepdims=True)
    offset = hidden - center
    factor = lax.rsqrt(jnp.mean(offset * offset, axis=1, keepdims=True) + eps)
    return offset * factor * gain + shift


CHUNKS = 4
PIECES = 4
FRONT = 5 + 2 * PIECES
GATHER_SLOTS = 40
SEGMENT = 4


def front_kernel(
    tokens,
    vec,
    bup,
    own,
    wq,
    block0,
    block1,
    block2,
    mixed,
    lse_ref,
    whole0,
    whole1,
    whole2,
    prompts_out,
    chip_out,
    q_out,
    kvo_out,
    kvp_out,
    wq_out,
    wkv_out,
    vec_out,
    bup_out,
    own_out,
    n1,
    vec_in,
    prompts,
    chip,
    wpair,
    q_all,
    kvo_all,
    kvp_all,
    mix,
    own_scalar,
    zs,
    zr,
    ys,
    yr,
    ds,
    dr,
    ws,
    wr,
    ss,
    sr,
    gs,
    gr_,
    ms,
    mr,
    l_sems,
    o_sems,
):
    x, z, g, y, c = places()
    sib, over_y, over_x = {"gc": g ^ 1}, {"gc": g ^ 2}, {"dp": x ^ 1}
    z_sems, y_sems, d_sems, w_sems, s_sems, g_sems = (
        (zs, zr),
        (ys, yr),
        (ds, dr),
        (ws, wr),
        (ss, sr),
        (gs, gr_),
    )
    blocks, wholes = (block0, block1, block2), (whole0, whole1, whole2)
    half_rows = wq.shape[0] // 2
    my_half = pl.ds(pl.multiple_of(x * half_rows, 16), half_rows)
    size = QROWS // PIECES
    first_half = jnp.where(z == 0, 0, 1)
    order = (z, z ^ 1, jnp.where(z < 2, 2, 1), jnp.where(z < 2, 3, 0))
    above, below = {"gr": jnp.minimum(z + 1, 3)}, {"gr": jnp.maximum(z - 1, 0)}
    inner = jnp.logical_and(z > 0, z < 3)

    def line(part, sems, base, b):
        return (
            (jnp.logical_and(z < 3, b <= z), send(part, part, sems, base + b, above)),
            (
                jnp.logical_and(z > 0, b >= z),
                send(part, part, sems, base + b, below, base + 4 + b),
            ),
        )

    def pass_on(copies):
        for goes, copy in copies:
            pl.when(goes)(copy.start)

    def passed_on(copies):
        for goes, copy in copies:
            pl.when(goes)(copy.wait_send)

    local_copy = pltpu.make_async_copy

    def small(kind, s):
        if kind == 0:
            return send(vec, vec_in.at[s], s_sems, s, {"gr": z ^ s})
        if kind == 1:
            return send(own, own_out.at[z], s_sems, 3 + s, {"gr": z ^ s})
        return send(bup, bup_out.at[g], s_sems, 6 + s, {"gc": g ^ s})

    def chip_send():
        return send(n1, chip.at[c], s_sems, 10, sib)

    def w_local():
        return local_copy(wq.at[my_half], wpair.at[y, z, my_half], l_sems.at[0])

    def w_line(s):
        return line(wpair.at[y, order[s], my_half], w_sems, 0, order[s])

    def w_gc(s):
        piece = wpair.at[y, order[s], my_half]
        return send(piece, piece, w_sems, 8 + s, over_y)

    def w_dp(s):
        piece = wpair.at[y, order[s], my_half]
        return send(piece, piece, w_sems, 12 + s, over_x)

    def w_dp_far(s):
        piece = wpair.at[1 - y, order[s], my_half]
        return send(piece, piece, w_sems, 16 + s, over_x)

    def chunk(number):
        return jnp.where(number < PIECES, first_half, 1 - first_half), number % PIECES

    def item(column, number):
        half, k = chunk(number)
        return prompts.at[column, half, pl.ds(pl.multiple_of(k * size, size), size)]

    def up(number):
        half, k = chunk(number)
        ref = item(g, number)
        return send(ref, ref, z_sems, half * PIECES + k, {"gr": jnp.minimum(z + 1, 3)})

    def down(number):
        half, k = chunk(number)
        ref = item(g, number)
        return send(
            ref,
            ref,
            z_sems,
            half * PIECES + k,
            {"gr": jnp.maximum(z - 1, 0)},
            2 * PIECES + k,
        )

    def side(number):
        half, k = chunk(number)
        ref = item(g, number)
        return send(ref, ref, y_sems, half * PIECES + k, over_y)

    def core(number, far):
        half, k = chunk(number)
        ref = item(g ^ 2 if far else g, number)
        return send(ref, ref, d_sems, far * 2 * PIECES + half * PIECES + k, sib)

    def goes_up(number):
        return jnp.logical_and(z < 3, chunk(number)[0] <= z)

    def goes_down(number):
        return jnp.logical_and(z == 1, chunk(number)[0] == 1)

    def forward(number):
        @pl.when(chunk(number)[0] != z)
        def _():
            up(number).wait_recv()

        @pl.when(goes_up(number))
        def _():
            up(number).start()

        @pl.when(goes_down(number))
        def _():
            down(number).start()

        side(number).start()
        core(number, 0).start()

    def across(number):
        side(number).wait_recv()
        core(number, 1).start()

    def plan(a, s):
        block, whole = blocks[a], wholes[a]
        q = block.shape[0] // 4
        half = pl.ds(pl.multiple_of(x * 2 * q, 16), 2 * q)
        qa = pl.ds(pl.multiple_of(x * 2 * q, 16), q)
        qb = pl.ds(pl.multiple_of(x * 2 * q + q, 16), q)
        qc = pl.ds(pl.multiple_of((1 - x) * 2 * q + q, 16), q)
        base = a * GATHER_SLOTS
        mine, far = whole.at[g, order[s]], whole.at[g ^ 2, order[s]]
        o = base + 8 + 8 * s

        def same(part, number, target):
            return lambda: send(part, part, g_sems, o + number, target)

        return {
            "line": lambda: line(mine.at[half], g_sems, base, order[s]),
            "ay": same(mine.at[qa], 0, over_y),
            "ax": same(mine.at[qa], 1, over_x),
            "afx": same(far.at[qa], 2, over_x),
            "bx": same(mine.at[qb], 3, over_x),
            "by": same(mine.at[qb], 4, over_y),
            "bfy": same(mine.at[qc], 5, over_y),
            "bfx": same(far.at[qb], 5, over_x),
            "c1": same(mine, 6, sib),
            "c2": same(far, 7, sib),
        }

    def own_block(a):
        return local_copy(blocks[a], wholes[a].at[g, z], l_sems.at[4 + a])

    def names(s):
        return ("ay", "ax", "afx", "bx", "by", "bfy") if s else ("ay", "afx", "by", "bfx")

    def relay(s):
        @pl.when(inner)
        def _():
            for a in range(3):
                copies = plan(a, s)["line"]()
                copies[0][1].wait_recv()
                pass_on(copies)


    def gather_first(s):
        for a in range(3):
            m = plan(a, s)
            if s:
                pl.when(jnp.logical_not(inner))(m["line"]()[0][1].wait_recv)
                m["bx"]().start()
                m["ax"]().start()
            m["ay"]().start()
            m["by"]().start()

    def gather_second(s):
        for a in range(3):
            m = plan(a, s)
            m["ay"]().wait_recv()
            m["afx"]().start()
            if s:
                m["bx"]().wait_recv()
                m["bfy"]().start()
            else:
                m["by"]().wait_recv()
                m["bfx"]().start()

    def gather_third(s):
        for a in range(3):
            m = plan(a, s)
            for name in ("ax", "afx", "by", "bfy") if s else ("afx", "bfx"):
                m[name]().wait_recv()
            m["c1"]().start()
            m["c2"]().start()

    def out_copies():
        return [
            local_copy(prompts, prompts_out, o_sems.at[0]),
            local_copy(chip, chip_out, o_sems.at[1]),
            local_copy(q_all, q_out, o_sems.at[2]),
            local_copy(kvo_all, kvo_out, o_sems.at[3]),
            local_copy(kvp_all, kvp_out, o_sems.at[4]),
        ]

    def exchange(i):
        cols = pl.ds(128 * i, 128)
        return (
            local_copy(mix.at[i, c], mixed.at[c, :, cols], l_sems.at[7 + i]),
            send(mix.at[i, 1 - c], mixed.at[c, :, cols], (ms, mr), i, sib),
        )

    hooks = {i: [] for i in range(FRONT)}

    def begin():
        greet(all_partners() + [{"gc": g ^ 3}])
        w_local().start()
        for s in (1, 2, 3):
            for kind in range(3):
                small(kind, s).start()
        w_local().wait()
        pass_on(w_line(0))
        own_out[z] = own[...]
        bup_out[g] = bup[...]
        for s in (1, 2, 3):
            small(0, s).wait_recv()
        vec_out[...] = (vec[...] + vec_in[1]) + (vec_in[2] + vec_in[3])

        @pl.loop(0, PIECES)
        def _(i):
            rows = pl.ds(pl.multiple_of(i * size, size), size)
            hidden = tokens[rows].astype(F32) + vec_out[0:1]
            n1[rows] = norm_rows(hidden, vec_out[1:2], vec_out[2:3]).astype(BF)

        @pl.when(z < 2)
        def _():
            to = local_copy(n1, prompts.at[g, jnp.minimum(z, 1)], l_sems.at[2])
            to.start()
            to.wait()

    def begin_chip():
        local_copy(n1, chip.at[c], l_sems.at[1]).start()
        chip_send().start()
        w_gc(0).start()
        w_dp(0).start()

    hooks[0] += [begin, partial(forward, 0), begin_chip]
    for i in range(1, 2 * PIECES):
        hooks[i].append(partial(forward, i))
    for i in range(2, 2 * PIECES + 2):
        hooks[i].append(partial(across, i - 2))

    def w_pass(s):
        copies = w_line(s)
        copies[0][1].wait_recv()
        pass_on(copies)
        w_gc(s).start()
        w_dp(s).start()

    def w_across(s):
        w_gc(s).wait_recv()
        w_dp_far(s).start()

    for s in (1, 2, 3):
        hooks[s].append(partial(w_pass, s))
    hooks[2].append(partial(w_across, 0))
    hooks[3] += [partial(w_across, 1)]
    hooks[4] += [partial(w_across, 2), partial(w_across, 3)]

    def assemble():
        for s in range(4):
            w_dp(s).wait_recv()
            w_dp_far(s).wait_recv()
        local_copy(n1, chip.at[c], l_sems.at[1]).wait()
        chip_send().wait_recv()
        for s in (1, 2, 3):
            small(1, s).wait_recv()
        to = local_copy(own_out, own_scalar, l_sems.at[3])
        to.start()
        for head in range(6):
            p, b = head // 2, head % 2
            at_q = 128 * p + (0 if b else 64)
            at_k = 256 * p + (128 if b else 64)
            at_v = 256 * p + (192 if b else 0)
            start = (head % 3) * 192
            for r in range(4):
                rows = slice(192 * r, 192 * r + 192)
                source = wpair.at[head // 3, r]
                wq_out[rows, at_q : at_q + HD] = source[:, start : start + HD]
                wkv_out[rows, at_k : at_k + HD] = source[:, start + HD : start + 2 * HD]
                wkv_out[rows, at_v : at_v + HD] = source[:, start + 2 * HD : start + 3 * HD]
        to.wait()

    hooks[5].append(assemble)

    def project(number):
        core(number, 0).wait_recv()
        core(number, 1).wait_recv()
        half, k = chunk(number)
        w = wkv_out[...]
        rows = jnp.concatenate(
            [
                prompts[i, half, pl.ds(pl.multiple_of(k * size, size), size)]
                for i in range(4)
            ],
            axis=0,
        )
        kv = nn(rows, w).astype(BF)
        to = pl.ds(pl.multiple_of(half * QROWS + k * size, size), size)
        for i in range(4):
            for p in range(3):
                kvp_all[p, i, to] = kv[size * i : size * i + size, 256 * p : 256 * p + 256]
        mine = chip[number // PIECES, pl.ds(pl.multiple_of(k * size, size), size)]
        kvo = nn(mine, w).astype(BF)
        queries = (nn(mine, wq_out[...]) * 0.125).astype(BF)
        to = pl.ds(pl.multiple_of(number * size, size), size)
        for p in range(3):
            kvo_all[p, to] = kvo[:, 256 * p : 256 * p + 256]
            q_all[p, to] = queries[:, 128 * p : 128 * p + 128]


    def own_first():
        for a in range(3):
            own_block(a).start()

    def own_down():
        for a in range(3):
            own_block(a).wait()
            goes, copy = plan(a, 0)["line"]()[1]
            pl.when(goes)(copy.start)

    def own_up():
        for a in range(3):
            goes, copy = plan(a, 0)["line"]()[0]
            pl.when(goes)(copy.start)

    hooks[0].append(own_first)
    hooks[1].append(own_down)
    hooks[8].append(own_up)
    hooks[7].append(partial(gather_first, 0))
    hooks[9].append(partial(gather_second, 0))
    between = [[] for _ in range(24 // SEGMENT + 1)]
    last = len(between) - 1
    between[0] += [lambda: [copy.start() for copy in out_copies()], partial(gather_third, 0)]
    hooks[9].append(partial(relay, 1))
    hooks[11].append(partial(relay, 2))
    for slot, stage, s in (
        (0, relay, 3),
        (0, gather_first, 1),
        (1, gather_first, 2),
        (1, gather_second, 1),
        (2, gather_first, 3),
        (2, gather_second, 2),
        (3, gather_third, 1),
        (3, gather_second, 3),
        (4, gather_third, 2),
        (6, gather_third, 3),
    ):
        between[slot].append(partial(stage, s))

    for number in range(FRONT - 2 * PIECES):
        for hook in hooks[number]:
            hook()

    def one_piece(number, carried):
        for i in range(FRONT - 2 * PIECES, FRONT):
            if hooks[i]:

                @pl.when(number == i)
                def _():
                    for hook in hooks[i]:
                        hook()

        project(number - (FRONT - 2 * PIECES))
        return carried

    lax.fori_loop(FRONT - 2 * PIECES, FRONT, one_piece, 0)

    low = lax.broadcasted_iota(jnp.int32, (CL, 128), 1) < 64

    def parts(turn):
        p, j = turn // 8, turn % 8
        shard = 2 * y + j // 4
        group = jnp.where(
            z < 2, shard, own_scalar[shard, 0, jnp.maximum(z - 2, 0) * 4 + j % 4]
        )
        rows_j = pl.ds(pl.multiple_of(j * CL, CL), CL)
        zero = jnp.zeros((CL, 128), BF)
        q = q_all[p, rows_j]
        return p, j, group, rows_j, (jnp.where(low, zero, q), jnp.where(low, q, zero))

    def store(p, j, mixes, sums):
        mix[p, j // 4, pl.ds(pl.multiple_of((j % 4) * CL, CL), CL)] = jnp.where(
            low, mixes[0], mixes[1]
        ).astype(BF)
        flat = jnp.where(low, sums[0], sums[1]).T
        lse_ref[p, j, 0:1] = flat[0:1]
        lse_ref[p, j, 1:2] = flat[64:65]

    def cont_turn(turn, carried):
        p, j, group, rows_j, q_parts = parts(turn)
        row = lax.broadcasted_iota(jnp.int32, (CL, CL), 0)
        near_ok = lax.broadcasted_iota(jnp.int32, (CL, CL), 1) <= row
        mixes, sums = [], []
        for h in range(2):
            cols = slice(128 * h, 128 * h + 128)
            kv = kvp_all[p, group, :, cols]
            kvo = kvo_all[p, rows_j, cols]
            far = nt(q_parts[h], kv)
            near = jnp.where(near_ok, nt(q_parts[h], kvo), negative)
            top = jnp.maximum(
                jnp.max(far, axis=1, keepdims=True), jnp.max(near, axis=1, keepdims=True)
            )
            far = jnp.exp(far - top)
            near = jnp.exp(near - top)
            total = jnp.sum(far, axis=1, keepdims=True) + jnp.sum(near, axis=1, keepdims=True)
            mixes.append((nn(far.astype(BF), kv) + nn(near.astype(BF), kvo)) / total)
            sums.append(jnp.broadcast_to(top + jnp.log(total), (CL, 128)))
        store(p, j, mixes, sums)
        return carried

    def prompt_turn(turn, carried):
        p, j, group, rows_j, q_parts = parts(turn)
        limit = z * QROWS + (j % (QROWS // CL)) * CL
        row = lax.broadcasted_iota(jnp.int32, (CL, P_SIZE), 0)
        key = lax.broadcasted_iota(jnp.int32, (CL, P_SIZE), 1)
        allowed = key - row <= limit
        mixes, sums = [], []
        for h in range(2):
            cols = slice(128 * h, 128 * h + 128)
            kv = kvp_all[p, group, :, cols]
            far = jnp.where(allowed, nt(q_parts[h], kv), negative)
            top = jnp.max(far, axis=1, keepdims=True)
            far = jnp.exp(far - top)
            total = jnp.sum(far, axis=1, keepdims=True)
            mixes.append(nn(far.astype(BF), kv) / total)
            sums.append(jnp.broadcast_to(top + jnp.log(total), (CL, 128)))
        store(p, j, mixes, sums)
        return carried

    def one_turn(turn, carried):
        for segment in range(last):

            @pl.when(turn == segment * SEGMENT)
            def _():
                for hook in between[segment]:
                    hook()

        @pl.when(z >= 2)
        def _():
            cont_turn(turn, 0)

        @pl.when(z < 2)
        def _():
            prompt_turn(turn, 0)

        for i in range(3):

            @pl.when(turn == 8 * i + 7)
            def _():
                for copy in exchange(i):
                    copy.start()

        return carried

    lax.fori_loop(0, 24, one_turn, 0)
    for hook in between[last]:
        hook()

    for number in range(2 * PIECES):
        side(number).wait_send()
        core(number, 0).wait_send()
        core(number, 1).wait_send()

        @pl.when(goes_up(number))
        def _():
            up(number).wait_send()

        @pl.when(goes_down(number))
        def _():
            down(number).wait_send()

    for s in range(4):
        if s:
            small(0, s).wait_send()
            small(1, s).wait_send()
            small(2, s).wait()
        passed_on(w_line(s))
        w_gc(s).wait_send()
        w_dp(s).wait_send()
        w_dp_far(s).wait_send()
    chip_send().wait_send()
    for s in range(4):
        for a in range(3):
            m = plan(a, s)
            passed_on(m["line"]())
            for name in names(s):
                m[name]().wait_send()
            m["c1"]().wait()
            m["c2"]().wait()
    for i in range(3):
        for copy in exchange(i):
            copy.wait()
    for copy in out_copies():
        copy.wait()


def front(tokens, vectors, bias, own, wq, blocks, collective_id):
    def body(tokens_ref, *refs):
        parts, bias_ref = refs[:7], refs[7]
        rest, vec, bup = refs[8:-2], refs[-2], refs[-1]
        z = lax.axis_index("gr")
        width = bias_ref.shape[0] // 4
        vec[...] = jnp.zeros_like(vec)
        for k in range(4):

            @pl.when(z == k)
            def _():
                for i, part in enumerate(parts):
                    vec[i : i + 1, width * k : width * k + width] = (
                        part[...].astype(F32).reshape(1, width)
                    )

        bup[0:1] = bias_ref[...].astype(F32).reshape(1, 4 * width)
        front_kernel(tokens_ref, vec, bup, *rest)

    any_space = pl.BlockSpec(memory_space=pl.ANY)
    vmem = pl.BlockSpec(memory_space=pltpu.VMEM)
    rows = 2 * QROWS

    def dma(count):
        return pltpu.SemaphoreType.DMA((count,))

    slots = 3 * GATHER_SLOTS
    heads = [(3, rows, 128), (3, rows, 256), (3, 4, P_SIZE, 256)]
    return pl.pallas_call(
        body,
        name="front",
        in_specs=[vmem] * 10 + [any_space] * 4,
        out_specs=[any_space, vmem]
        + [any_space] * 8
        + [vmem] * 5,
        out_shape=[
            jax.ShapeDtypeStruct((2, QROWS, 384), BF),
            jax.ShapeDtypeStruct((3, rows // CL, 2, 128), F32),
        ]
        + [jax.ShapeDtypeStruct((4, 4) + block.shape, BF) for block in blocks]
        + [
            jax.ShapeDtypeStruct((4, 2, QROWS, D), BF),
            jax.ShapeDtypeStruct((2, QROWS, D), BF),
        ]
        + [jax.ShapeDtypeStruct(shape, BF) for shape in heads]
        + [
            jax.ShapeDtypeStruct((D, 384), BF),
            jax.ShapeDtypeStruct((D, D), BF),
            jax.ShapeDtypeStruct((8, D), F32),
            jax.ShapeDtypeStruct((4, 8, D), F32),
            jax.ShapeDtypeStruct((4,) + own.shape, jnp.int32),
        ],
        scratch_shapes=[
            pltpu.VMEM((QROWS, D), BF),
            pltpu.VMEM((4, 8, D), F32),
            pltpu.VMEM((4, 2, QROWS, D), BF),
            pltpu.VMEM((2, QROWS, D), BF),
            pltpu.VMEM((2, 4) + wq.shape, BF),
        ]
        + [pltpu.VMEM(shape, BF) for shape in heads]
        + [
            pltpu.VMEM((3, 2, QROWS, 128), BF),
            pltpu.SMEM((4,) + own.shape, jnp.int32),
            dma(3 * PIECES),
            dma(2 * PIECES),
            dma(2 * PIECES),
            dma(2 * PIECES),
            dma(4 * PIECES),
            dma(4 * PIECES),
            dma(20),
            dma(20),
            dma(11),
            dma(11),
            dma(slots),
            dma(slots),
            dma(3),
            dma(3),
            dma(10),
            dma(5),
            pltpu.VMEM((8, D), F32),
            pltpu.VMEM((8, D), F32),
        ],
        compiler_params=pltpu.CompilerParams(
            collective_id=collective_id, has_side_effects=True, vmem_limit_bytes=56 << 20
        ),
    )(tokens, *vectors, bias, own, wq, *blocks)


def tail_kernel(
    grp,
    dkv,
    n1p,
    n1c,
    dkvo,
    dq,
    w_q,
    w_kv,
    grad_h2,
    tokens,
    vec,
    sums,
    out,
    sums_out,
    dw_out,
    part,
    chip,
    tiles,
    rows_p,
    low,
    wkt,
    wqt,
    dkvw,
    dqw,
    dw,
    ra,
    rb,
    rz,
    take,
    gsum,
    cur,
    sb,
    *rest,
):
    bufs, (sem_s, sem_r, l_sems, w_s, w_r, w_l) = rest[:9], rest[9:]
    sems = (sem_s, sem_r)
    x, z, g, y, c = places()
    sib, over_y, over_x = {"gc": g ^ 1}, {"gc": g ^ 2}, {"dp": x ^ 1}
    down = {"gr": jnp.maximum(z - 1, 0)}
    far = z >= 2
    size = QROWS // CHUNKS
    count = 2 * CHUNKS

    def fetch(t):
        rows = pl.ds(pl.multiple_of(t * size, size), size)
        h, r = t // CHUNKS, pl.ds(pl.multiple_of((t % CHUNKS) * size, size), size)
        slot = t % 2
        return (
            pltpu.make_async_copy(dkv.at[:, rows], tiles.at[slot], l_sems.at[slot]),
            pltpu.make_async_copy(n1p.at[:, h, r], rows_p.at[slot], l_sems.at[2 + slot]),
        )

    for copy in fetch(0):
        copy.start()
    greet(all_partners())
    wkt[...] = w_kv[...].T
    wqt[...] = w_q[...].T
    dkvw[...] = jnp.zeros_like(dkvw)
    dqw[...] = jnp.zeros_like(dqw)

    def at(t):
        return t // CHUNKS, pl.ds(pl.multiple_of((t % CHUNKS) * size, size), size)

    def mine(side, t):
        h, r = at(t)
        return part.at[2 * (1 - y if side == 0 else y) + c, h, r]

    def hop_a(side, t):
        h, r = at(t)
        i = 1 - y if side == 0 else y
        return send(part.at[2 * i + 1 - c, h, r], ra.at[i, h, r], sems, 8 * side + t, sib)

    def hop_y(t):
        h, r = at(t)
        return send(mine(0, t), rb.at[h, r], sems, 16 + t, over_y)

    def hop_z(t):
        h, r = at(t)
        return send(mine(1, t), rz.at[h, r], sems, 24 + t, down)

    hop_chip = send(chip.at[1 - c], take, sems, 32, sib)

    def fold(t, other):
        h, r = at(t)
        add_into(mine(1, t), mine(1, t), other.at[r])

    def stage0(t):
        slot = t % 2
        for copy in fetch(t):
            copy.wait()

        @pl.when(t + 1 < count)
        def _():
            for copy in fetch(t + 1):
                copy.start()

        weights = [
            [jnp.where(grp[j] == i, 1.0, 0.0).astype(F32) for j in range(8)] for i in range(4)
        ]

        @pl.loop(0, size // 16)
        def _(q):
            r = pl.ds(pl.multiple_of(q * 16, 16), 16)
            pieces = [tiles[slot, j, r].astype(F32) for j in range(8)]
            for i in range(4):
                total = weights[i][0] * pieces[0]
                for j in range(1, 8):
                    total = total + weights[i][j] * pieces[j]
                low[i, r] = total.astype(BF)

        whole = low[...].reshape(4 * size, D)
        grads = nn(whole, wkt[...]).astype(BF)
        h, r = at(t)
        for i in range(4):
            part[i, h, r] = grads[size * i : size * i + size]

        @pl.when(far)
        def _():
            hop_a(0, t).start()

        hop_a(1, t).start()
        own = pl.ds(pl.multiple_of(t * size, size), size)
        near, grad_q, rows_c = dkvo[own], dq[own], n1c[own]
        chip[h, r] = (nn(grad_q, wqt[...]) + nn(near, wkt[...])).astype(BF)
        rows = jnp.concatenate([rows_p[slot].reshape(4 * size, D), rows_c], axis=0)
        dkvw[...] += tn(rows, jnp.concatenate([whole, near], axis=0))
        dqw[...] += tn(rows_c, grad_q)

    def stage1(t):
        h, r = at(t)

        @pl.when(far)
        def _():
            hop_a(0, t).wait()
            add_into(mine(0, t), mine(0, t), ra.at[1 - y, h, r])
            hop_y(t).start()

        hop_a(1, t).wait()
        fold(t, ra.at[y, h])

    def stage2(t):
        @pl.when(far)
        def _():
            hop_y(t).wait()
            fold(t, rb.at[t // CHUNKS])

        @pl.when(z == 3)
        def _():
            hop_z(t).start()

    def stage3(t):
        @pl.when(z == 2)
        def _():
            hop_z(t).wait_recv()
            fold(t, rz.at[t // CHUNKS])
            hop_z(t).start()

    def stage4(t):
        @pl.when(z == 1)
        def _():
            hop_z(t).wait_recv()
            fold(t, rz.at[t // CHUNKS])

            @pl.when(t < CHUNKS)
            def _():
                hop_z(t).start()

    def stage5(t):
        @pl.when(jnp.logical_and(z == 0, t < CHUNKS))
        def _():
            hop_z(t).wait_recv()
            fold(t, rz.at[0])

    def stages(t, carried, skip=0):
        todo = list(zip((0, 1, 3, 5, 7, 9), (stage0, stage1, stage2, stage3, stage4, stage5)))
        for lag, stage in todo[skip:]:

            @pl.when(jnp.logical_and(t >= lag, t < count + lag))
            def _():
                stage(t - lag)

        return carried

    lax.fori_loop(0, count, stages, 0)
    hop_chip.start()

    for head in range(6):
        p, b = head // 2, head % 2
        places_in = (
            dqw[:, 128 * p + (0 if b else 64) : 128 * p + (64 if b else 128)],
            dkvw[:, 256 * p + (128 if b else 64) : 256 * p + (192 if b else 128)],
            dkvw[:, 256 * p + (192 if b else 0) : 256 * p + (256 if b else 64)],
        )
        for i, piece in enumerate(places_in):
            at_col = (head % 3) * 192 + HD * i
            for r in range(4):
                dw[head // 3, r, :, at_col : at_col + HD] = piece[192 * r : 192 * r + 192].astype(
                    BF
                )
    begin, after_a, after_b, after_c, total, finish = rs_plan(
        dw, dw_out, bufs, (w_s, w_r), w_l, 0, False
    )
    for s in RS_ORDER:
        begin(s)
    for s in RS_ORDER:
        after_a(s)
    lax.fori_loop(count, count + 2, partial(stages, skip=1), 0)
    for s in RS_ORDER:
        after_b(s)
    lax.fori_loop(count + 2, count + 3, partial(stages, skip=2), 0)
    lax.fori_loop(count + 3, count + 6, partial(stages, skip=2), 0)
    for s in RS_ORDER:
        after_c(s)
    lax.fori_loop(count + 6, count + 9, partial(stages, skip=3), 0)

    @pl.loop(0, count)
    def _(t):
        @pl.when(jnp.logical_or(z >= 2, jnp.logical_and(z == 1, t < CHUNKS)))
        def _():
            hop_z(t).wait_send()

    hop_chip.wait()

    cur[...] = sums[...]

    @pl.loop(0, CHUNKS)
    def _(k):
        r = pl.ds(pl.multiple_of(k * size, size), size)
        gsum[r] = chip[c, r].astype(F32) + take[r].astype(F32)

        @pl.when(z < 2)
        def _():
            gsum[r] += part[2 * y + c, jnp.minimum(z, 1), r].astype(F32)

        hidden = tokens[r].astype(F32) + vec[0:1]
        center = jnp.mean(hidden, axis=1, keepdims=True)
        offset = hidden - center
        factor = lax.rsqrt(jnp.mean(offset * offset, axis=1, keepdims=True) + eps)
        unit = offset * factor
        grad = gsum[r]
        scaled = grad * vec[1:2]
        first = jnp.mean(scaled, axis=1, keepdims=True)
        second = jnp.mean(scaled * unit, axis=1, keepdims=True)
        result = grad_h2[r] + factor * (scaled - first - unit * second)
        out[r] = result
        cur[0:1] += jnp.sum(result, axis=0, keepdims=True)
        cur[1:2] += jnp.sum(grad * unit, axis=0, keepdims=True)
        cur[2:3] += jnp.sum(grad, axis=0, keepdims=True)

    for i, target in enumerate((sib, over_y, over_x)):
        hop = send(cur, sb.at[i], sems, 33 + i, target)
        hop.start()
        hop.wait()
        cur[...] += sb[i]
        if i == 1:
            total()
    hops = [send(cur, sb.at[2 + s], sems, 35 + s, {"gr": z ^ s}) for s in (1, 2, 3)]
    for hop in hops:
        hop.start()
    finish()
    for hop in hops:
        hop.wait()
    sums_out[...] = (cur[...] + sb[3]) + (sb[4] + sb[5])


def tail_exchange(
    grp, dkv, n1p, n1c, dkvo, dq, w_q, w_kv, grad_h2, tokens, vec, sums, collective_id
):
    any_space = pl.BlockSpec(memory_space=pl.ANY)
    vmem = pl.BlockSpec(memory_space=pltpu.VMEM)
    block = (2, 4, 192, 576)
    return pl.pallas_call(
        tail_kernel,
        name="tail_exchange",
        in_specs=[pl.BlockSpec(memory_space=pltpu.SMEM), any_space, any_space] + [vmem] * 9,
        out_specs=[vmem, vmem, vmem],
        out_shape=[
            jax.ShapeDtypeStruct((QROWS, D), F32),
            jax.ShapeDtypeStruct(sums.shape, F32),
            jax.ShapeDtypeStruct(block[2:], F32),
        ],
        scratch_shapes=[
            pltpu.VMEM((4, 2, QROWS, D), BF),
            pltpu.VMEM((2, QROWS, D), BF),
            pltpu.VMEM((2, 8, CL, D), BF),
            pltpu.VMEM((2, 4, CL, D), BF),
            pltpu.VMEM((4, CL, D), BF),
            pltpu.VMEM((D, D), BF),
            pltpu.VMEM((384, D), BF),
            pltpu.VMEM((D, D), F32),
            pltpu.VMEM((D, 384), F32),
            pltpu.VMEM(block, BF),
            pltpu.VMEM((2, 2, QROWS, D), BF),
            pltpu.VMEM((2, QROWS, D), BF),
            pltpu.VMEM((2, QROWS, D), BF),
            pltpu.VMEM((QROWS, D), BF),
            pltpu.VMEM((QROWS, D), F32),
            pltpu.VMEM(sums.shape, F32),
            pltpu.VMEM((6,) + sums.shape, F32),
        ]
        + rs_scratch(block[2], block[3], False)
        + [
            pltpu.SemaphoreType.DMA((39,)),
            pltpu.SemaphoreType.DMA((39,)),
            pltpu.SemaphoreType.DMA((4,)),
            pltpu.SemaphoreType.DMA((RS_SLOTS,)),
            pltpu.SemaphoreType.DMA((RS_SLOTS,)),
            pltpu.SemaphoreType.DMA((8,)),
        ],
        compiler_params=pltpu.CompilerParams(
            collective_id=collective_id, has_side_effects=True, vmem_limit_bytes=60 << 20
        ),
    )(grp, dkv, n1p, n1c, dkvo, dq, w_q, w_kv, grad_h2, tokens, vec, sums)


GELU_IN = math.sqrt(2.0 / math.pi)


def middle_kernel(
    mixed,
    w_out_g,
    w_up,
    w_down,
    tokens,
    teacher,
    vec,
    b_up,
    final_out,
    grad_h2,
    dw_up,
    dw_down,
    dw_out,
    gm,
    sums,
    wo,
    wu,
    wd,
    h2,
    n2,
    n2t,
    act,
    slope,
    gf,
    gb,
    gbt,
    acc,
    du,
    dd,
    l_sems,
    o_sems,
):
    loads_u = [pltpu.make_async_copy(w_up.at[b], wu.at[b], l_sems.at[b]) for b in range(4)]
    loads_d = [pltpu.make_async_copy(w_down.at[b], wd.at[b], l_sems.at[4 + b]) for b in range(4)]
    for b in range(4):
        loads_u[b].start()
        loads_d[b].start()
    for k in range(2):
        for i in range(2):
            for r in range(4):
                wo[k, 192 * i : 192 * i + 192, 192 * r : 192 * r + 192] = w_out_g[2 * i + k, r]

    @pl.loop(0, 1)
    def _(t):
        r = pl.ds(pl.multiple_of(t * QROWS, QROWS), QROWS)
        hidden = tokens[r].astype(F32) + vec[0:1]
        attended = nn(mixed[0, r], wo[0]) + nn(mixed[1, r], wo[1])
        total = hidden + attended + vec[3:4]
        h2[r] = total
        n2[r] = norm_rows(total, vec[4:5], vec[5:6]).astype(BF)

    n2t[...] = n2[...].T
    acc[...] = jnp.zeros_like(acc)
    for copy in loads_u + loads_d:
        copy.wait()

    @pl.loop(0, 4)
    def _(b):
        @pl.loop(0, 1)
        def _(t):
            r = pl.ds(pl.multiple_of(t * QROWS, QROWS), QROWS)
            pre = nn(n2[r], wu[b]) + b_up[b, 0:1]
            square = pre * pre
            tanh = jnp.tanh(GELU_IN * pre * (1.0 + 0.044715 * square))
            half = 0.5 * (1.0 + tanh)
            low = (pre * half).astype(BF)
            act[b, r] = low
            slope[b, r] = half + (0.5 * GELU_IN) * pre * (1.0 - tanh * tanh) * (
                1.0 + (3.0 * 0.044715) * square
            )
            acc[r] += nt(low, wd[b])

    sums[...] = jnp.zeros_like(sums)

    @pl.loop(0, 1)
    def _(t):
        r = pl.ds(pl.multiple_of(t * QROWS, QROWS), QROWS)
        final = h2[r] + acc[r] + vec[6:7]
        final_out[r] = final.astype(BF)
        diff = final - teacher[r].astype(F32)
        gf[r] = diff
        low = diff.astype(BF)
        gb[r] = low
        sums[6:7] += jnp.sum(low.astype(F32), axis=0, keepdims=True)
        sums[11:12] += jnp.sum(diff * diff, axis=0, keepdims=True)

    gbt[...] = gb[...].T
    acc[...] = jnp.zeros_like(acc)

    @pl.loop(0, 4)
    def _(b):
        dd[b] = nn(gbt[...], act[b]).astype(BF)
        pltpu.make_async_copy(dd.at[b], dw_down.at[b], o_sems.at[b]).start()

        @pl.loop(0, 1)
        def _(t):
            r = pl.ds(pl.multiple_of(t * QROWS, QROWS), QROWS)
            low = (nn(gb[r], wd[b]) * slope[b, r]).astype(BF)
            act[b, r] = low
            sums[pl.ds(7 + b, 1)] += jnp.sum(low.astype(F32), axis=0, keepdims=True)
            acc[r] += nt(low, wu[b])

        du[b] = nn(n2t[...], act[b]).astype(BF)
        pltpu.make_async_copy(du.at[b], dw_up.at[b], o_sems.at[4 + b]).start()

    @pl.loop(0, 1)
    def _(t):
        r = pl.ds(pl.multiple_of(t * QROWS, QROWS), QROWS)
        hidden = h2[r]
        center = jnp.mean(hidden, axis=1, keepdims=True)
        offset = hidden - center
        factor = lax.rsqrt(jnp.mean(offset * offset, axis=1, keepdims=True) + eps)
        unit = offset * factor
        grad = acc[r]
        scaled = grad * vec[4:5]
        first = jnp.mean(scaled, axis=1, keepdims=True)
        second = jnp.mean(scaled * unit, axis=1, keepdims=True)
        total = gf[r] + factor * (scaled - first - unit * second)
        grad_h2[r] = total
        low = total.astype(BF)
        gb[r] = low
        sums[3:4] += jnp.sum(grad * unit, axis=0, keepdims=True)
        sums[4:5] += jnp.sum(grad, axis=0, keepdims=True)
        sums[5:6] += jnp.sum(low.astype(F32), axis=0, keepdims=True)
        gm[0, r] = nt(low, wo[0]).astype(BF)
        gm[1, r] = nt(low, wo[1]).astype(BF)

    for k in range(2):
        whole = tn(mixed[k], gb[...]).astype(BF)
        for i in range(2):
            for r in range(4):
                dw_out[2 * i + k, r] = whole[192 * i : 192 * i + 192, 192 * r : 192 * r + 192]
    for b in range(4):
        pltpu.make_async_copy(dd.at[b], dw_down.at[b], o_sems.at[b]).wait()
        pltpu.make_async_copy(du.at[b], dw_up.at[b], o_sems.at[4 + b]).wait()


def middle(mixed, w_out_g, w_up, w_down, tokens, teacher, vec, b_up):
    any_space = pl.BlockSpec(memory_space=pl.ANY)
    vmem = pl.BlockSpec(memory_space=pltpu.VMEM)
    blocks = (4, D, D)
    return pl.pallas_call(
        middle_kernel,
        name="middle",
        in_specs=[vmem, vmem, any_space, any_space, vmem, vmem, vmem, vmem],
        out_specs=[vmem, vmem, any_space, any_space, vmem, vmem, vmem],
        out_shape=[
            jax.ShapeDtypeStruct((QROWS, D), BF),
            jax.ShapeDtypeStruct((QROWS, D), F32),
            jax.ShapeDtypeStruct(blocks, BF),
            jax.ShapeDtypeStruct(blocks, BF),
            jax.ShapeDtypeStruct((4, 4, 192, 192), BF),
            jax.ShapeDtypeStruct((2, QROWS, 384), BF),
            jax.ShapeDtypeStruct((16, D), F32),
        ],
        scratch_shapes=[
            pltpu.VMEM((2, 384, D), BF),
            pltpu.VMEM(blocks, BF),
            pltpu.VMEM(blocks, BF),
            pltpu.VMEM((QROWS, D), F32),
            pltpu.VMEM((QROWS, D), BF),
            pltpu.VMEM((D, QROWS), BF),
            pltpu.VMEM((4, QROWS, D), BF),
            pltpu.VMEM((4, QROWS, D), F32),
            pltpu.VMEM((QROWS, D), F32),
            pltpu.VMEM((QROWS, D), BF),
            pltpu.VMEM((D, QROWS), BF),
            pltpu.VMEM((QROWS, D), F32),
            pltpu.VMEM(blocks, BF),
            pltpu.VMEM(blocks, BF),
            pltpu.SemaphoreType.DMA((8,)),
            pltpu.SemaphoreType.DMA((8,)),
        ],
        compiler_params=pltpu.CompilerParams(vmem_limit_bytes=60 << 20),
    )(mixed, w_out_g, w_up, w_down, tokens, teacher, vec, b_up)


def norm(hidden, gain, shift):
    center = jnp.mean(hidden, axis=1, keepdims=True)
    offset = hidden - center
    factor = lax.rsqrt(jnp.mean(offset * offset, axis=1, keepdims=True) + eps)
    unit = offset * factor
    return unit * gain + shift, unit, factor


def norm_back(grad, gain, unit, factor):
    grad_unit = grad * gain
    first = jnp.mean(grad_unit, axis=1, keepdims=True)
    second = jnp.mean(grad_unit * unit, axis=1, keepdims=True)
    grad_in = factor * (grad_unit - first - unit * second)
    return grad_in, jnp.sum(grad * unit, axis=0), jnp.sum(grad, axis=0)


def head_layout(blocks):
    chunks = blocks.transpose(1, 0, 2).reshape(D, 6, 3, HD)
    q_list, kv_list = [], []
    for pair in range(3):
        a, b = 2 * pair, 2 * pair + 1
        q_list += [chunks[:, b, 0], chunks[:, a, 0]]
        kv_list += [chunks[:, a, 2], chunks[:, a, 1], chunks[:, b, 1], chunks[:, b, 2]]
    return jnp.concatenate(q_list, axis=1), jnp.concatenate(kv_list, axis=1)


def head_layout_back(grad_q, grad_kv):
    qc = grad_q.reshape(D, 3, 2, HD)
    kc = grad_kv.reshape(D, 3, 4, HD)
    pieces = []
    for pair in range(3):
        pieces += [qc[:, pair, 1], kc[:, pair, 1], kc[:, pair, 0]]
        pieces += [qc[:, pair, 0], kc[:, pair, 2], kc[:, pair, 3]]
    whole = jnp.concatenate(pieces, axis=1)
    return whole.reshape(D, 2, 576).transpose(1, 0, 2)


def on_device(
    tokens,
    teacher,
    pass_embed,
    ln1_gain,
    ln1_bias,
    qkv_weight,
    out_weight,
    out_bias,
    ln2_gain,
    ln2_bias,
    fc1_weight,
    fc1_bias,
    fc2_weight,
    fc2_bias,
    cont_group,
    token_count,
):
    n_dp = lax.axis_size("dp")
    n_gr = lax.axis_size("gr")
    n_gc = lax.axis_size("gc")
    z = lax.axis_index("gr")
    g = lax.axis_index("gc")
    c = g % 2
    y = g // 2
    swap_core = [(i, i ^ 1) for i in range(n_gc)]
    swap_y = [(i, i ^ 2) for i in range(n_gc)]

    parts = [pass_embed, ln1_gain, ln1_bias, out_bias, ln2_gain, ln2_bias, fc2_bias]
    if n_dp == 2:
        own = jnp.broadcast_to(jnp.pad(cont_group, (0, 120)), (8, 128))
        (
            mixed,
            lse_rows,
            w_out,
            w_up,
            w_down,
            n1_prompt,
            n1_chip,
            q,
            kvo,
            kvp,
            w_q,
            w_kv,
            vectors,
            b_up,
            owners,
        ) = front(
            tokens, parts, fc1_bias, own, qkv_weight, [out_weight, fc1_weight, fc2_weight], 1
        )
        n1_chip = n1_chip.reshape(2 * QROWS, D)
        owners = owners[:, 0, :8]
    else:
        vectors = lax.all_gather(jnp.stack(parts).astype(F32), "gr", axis=1, tiled=True)
        b_up = lax.all_gather(fc1_bias, "gc", axis=0, tiled=True).astype(F32)
        owners = lax.all_gather(cont_group, "gr", axis=0, tiled=True)
    embed, gain1, shift1, b_out, gain2, shift2, b_down = [vectors[i] for i in range(7)]
    owners = owners.reshape(4, 2, 4)
    mine = lax.dynamic_slice(owners, (2 * y, jnp.maximum(z - 2, 0), 0), (2, 1, 4)).reshape(8)
    own_groups = jnp.repeat(2 * y + jnp.arange(2), 4)
    grp = jnp.where(z < 2, own_groups, mine).astype(jnp.int32)
    z_arr = z.astype(jnp.int32).reshape(1)

    hidden = tokens.astype(F32) + embed
    normed1, unit1, factor1 = norm(hidden, gain1, shift1)
    n1 = normed1.astype(BF)

    if n_dp != 2:
        w_other = lax.ppermute(qkv_weight, "gc", swap_y)
        w_pair = jnp.where(
            y == 0, jnp.stack([qkv_weight, w_other]), jnp.stack([w_other, qkv_weight])
        )
        w_qkv = lax.all_gather(w_pair, "gr", axis=1, tiled=True)
        n1_other = lax.ppermute(n1, "gc", swap_core)
        n1_chip = jnp.where(
            c == 0, jnp.concatenate([n1, n1_other]), jnp.concatenate([n1_other, n1])
        )
        n1_col = lax.all_gather(n1, "gr", axis=0, tiled=True)[:P_SIZE]
        n1_prompt = lax.all_gather(n1_col, "gc", axis=0, tiled=True)
        w_q, w_kv = head_layout(w_qkv)
        kvp = nn(n1_prompt, w_kv).astype(BF)
        kvo = nn(n1_chip, w_kv).astype(BF)
        q = (nn(n1_chip, w_q) * 0.125).astype(BF)
        w_out = lax.all_gather(out_weight, ("gc", "gr"))
        w_up = lax.all_gather(fc1_weight, ("gc", "gr"))
        w_down = lax.all_gather(fc2_weight, ("gc", "gr"))
        mixed_heads, lse = attend(grp, z_arr, q, kvo, kvp)
        lse_rows = lse[:, ::64].reshape(8, CL, 3, 2).transpose(2, 0, 3, 1)
        halves = mixed_heads.reshape(2, QROWS, 384)
        keep = lax.dynamic_index_in_dim(halves, c, 0, keepdims=False)
        give = lax.dynamic_index_in_dim(halves, 1 - c, 0, keepdims=False)
        take = lax.ppermute(give, "gc", swap_core)
        mixed = jnp.where(c == 0, jnp.stack([keep, take]), jnp.stack([take, keep]))
    w_up = w_up.reshape(n_gc, D, FF // n_gc)
    w_down = w_down.reshape(n_gc, D, FF // n_gc)
    if n_dp == 2:
        final, grad_h2, grad_w_up, grad_w_down, grad_w_out, gm, later_sums = middle(
            mixed, w_out, w_up, w_down, tokens, teacher, vectors, b_up
        )
    else:
        w_out = w_out.reshape(2, 2, n_gr, 192, 192).transpose(1, 0, 3, 2, 4).reshape(2, 384, D)

        attended = lax.dot_general(
            mixed, w_out, (((0, 2), (0, 1)), ((), ())), preferred_element_type=F32
        )
        hidden2 = hidden + attended + b_out
        normed2, unit2, factor2 = norm(hidden2, gain2, shift2)
        n2 = normed2.astype(BF)
        pre = lax.dot_general(n2, w_up, (((1,), (1,)), ((), ())), preferred_element_type=F32)
        pre = pre.reshape(QROWS, FF) + b_up
        active, gelu_back = jax.vjp(partial(jax.nn.gelu, approximate=True), pre)
        act = active.astype(BF)
        act_blocks = act.reshape(QROWS, n_gc, FF // n_gc)
        final = (
            hidden2
            + lax.dot_general(
                act_blocks, w_down, (((1, 2), (0, 2)), ((), ())), preferred_element_type=F32
            )
            + b_down
        )
        grad_final = final - teacher.astype(F32)
        squared = jnp.sum(grad_final * grad_final, axis=0)
        gb = grad_final.astype(BF)
        grad_b_down = jnp.sum(gb, axis=0, dtype=F32)
        grad_active = lax.dot_general(
            gb, w_down, (((1,), (1,)), ((), ())), preferred_element_type=F32
        ).reshape(QROWS, FF)
        grad_w_down = jnp.einsum("td,tgf->gdf", gb, act_blocks, preferred_element_type=F32)
        (grad_pre,) = gelu_back(grad_active)
        gp = grad_pre.astype(BF)
        gp_blocks = gp.reshape(QROWS, n_gc, FF // n_gc)
        grad_b_up = jnp.sum(gp, axis=0, dtype=F32)
        grad_w_up = jnp.einsum("td,tgf->gdf", n2, gp_blocks, preferred_element_type=F32)
        grad_n2 = lax.dot_general(
            gp_blocks, w_up, (((1, 2), (0, 2)), ((), ())), preferred_element_type=F32
        )
        back2, grad_gain2, grad_shift2 = norm_back(grad_n2, gain2, unit2, factor2)
        grad_h2 = grad_final + back2
        ga = grad_h2.astype(BF)
        grad_b_out = jnp.sum(ga, axis=0, dtype=F32)
        grad_w_out = jnp.einsum("ctk,tn->ckn", mixed, ga, preferred_element_type=F32)
        gm = jnp.einsum("tn,ckn->ctk", ga, w_out, preferred_element_type=F32).astype(BF)
        grad_w_up = grad_w_up.astype(BF)
        grad_w_down = grad_w_down.astype(BF)
        grad_w_out = (
            grad_w_out.astype(BF)
            .reshape(2, 2, 192, n_gr, 192)
            .transpose(1, 0, 3, 2, 4)
            .reshape(n_gc, n_gr, 192, 192)
        )
    weight_grads = [
        grad_w_down.reshape(n_gc, n_gr, 192, 768),
        grad_w_up.reshape(n_gc, n_gr, 192, 768),
        grad_w_out,
    ]
    if n_dp == 2:
        dq, dkvo, dkv, out_w_down, out_w_up, out_w_out = attend_back_scatter(
            grp, q, lse_rows, kvo, kvp, gm, weight_grads, 3
        )
    else:
        gm_keep = lax.dynamic_index_in_dim(gm, c, 0, keepdims=False)
        gm_give = lax.dynamic_index_in_dim(gm, 1 - c, 0, keepdims=False)
        gm_take = lax.ppermute(gm_give, "gc", swap_core)
        gm_chip = jnp.where(c == 0, jnp.stack([gm_keep, gm_take]), jnp.stack([gm_take, gm_keep]))
        gm_chip = gm_chip.reshape(2 * QROWS, 384)

        def scatter16(blocks):
            part = lax.psum_scatter(
                blocks.reshape(n_gc * n_gr * blocks.shape[2], -1),
                ("gc", "gr"),
                scatter_dimension=0,
                tiled=True,
            )
            return lax.psum(part, "dp").astype(F32)

        out_w_down, out_w_up, out_w_out = [scatter16(grad) for grad in weight_grads]
        dq, dkvo, dkvp = attend_back(grp, z_arr, q, gm_chip, lse_rows, kvo, kvp)
        part_prompt = nt(dkvp, w_kv).astype(BF)

        part_chip = (nt(dq, w_q) + nt(dkvo, w_kv)).reshape(2, QROWS, D)
        grad_kv = tn(n1_prompt, dkvp) + tn(n1_chip, dkvo)
        grad_q = tn(n1_chip, dq)
        grad_qkv = head_layout_back(grad_q, grad_kv)

    if n_dp == 2:
        input_grad, sums, out_w_qkv = tail_exchange(
            grp,
            dkv,
            n1_prompt,
            n1_chip,
            dkvo,
            dq,
            w_q,
            w_kv,
            grad_h2,
            tokens,
            vectors,
            later_sums,
            4,
        )
    else:
        later_sums = jnp.concatenate(
            [
                grad_gain2[None],
                grad_shift2[None],
                grad_b_out[None],
                grad_b_down[None],
                grad_b_up.reshape(4, D),
                squared[None],
                jnp.zeros((4, D), F32),
            ]
        )
        back_prompt = lax.psum_scatter(part_prompt, "gc", scatter_dimension=0, tiled=True)
        back_prompt = lax.psum_scatter(
            jnp.concatenate([back_prompt, jnp.zeros_like(back_prompt)]),
            "gr",
            scatter_dimension=0,
            tiled=True,
        ).astype(F32)
        part_keep = lax.dynamic_index_in_dim(part_chip, c, 0, keepdims=False)
        part_give = lax.dynamic_index_in_dim(part_chip, 1 - c, 0, keepdims=False)
        part_take = lax.ppermute(part_give.astype(BF), "gc", swap_core).astype(F32)
        grad_n1 = part_keep + part_take + back_prompt
        qkv_keep = lax.dynamic_index_in_dim(grad_qkv, y, 0, keepdims=False)
        qkv_give = lax.dynamic_index_in_dim(grad_qkv, 1 - y, 0, keepdims=False)
        qkv_take = lax.ppermute(qkv_give.astype(BF), "gc", swap_y).astype(F32)
        out_w_qkv = lax.psum_scatter(
            (qkv_keep + qkv_take).astype(BF), "gr", scatter_dimension=0, tiled=True
        )
        out_w_qkv = lax.psum(out_w_qkv, "dp").astype(F32)
        back1, grad_gain1, grad_shift1 = norm_back(grad_n1, gain1, unit1, factor1)
        input_grad = grad_h2 + back1
        first_sums = jnp.stack([jnp.sum(input_grad, axis=0), grad_gain1, grad_shift1])
        sums = lax.psum(jnp.concatenate([first_sums, later_sums]), ("dp", "gr", "gc"))
    sums = sums[:12].reshape(12 * D)
    loss = (jnp.sum(sums[11 * D :]) / (D * token_count[0].astype(F32))).reshape(1)
    rows = sums[: 7 * D].reshape(7, n_gr, D // n_gr)
    rows = lax.dynamic_index_in_dim(rows, z, 1, keepdims=False)
    up = lax.dynamic_index_in_dim(
        sums[7 * D : 7 * D + FF].reshape(n_gc, FF // n_gc), g, 0, keepdims=False
    )
    return (
        final.astype(BF),
        loss,
        input_grad,
        rows[0],
        rows[1],
        rows[2],
        out_w_qkv,
        out_w_out,
        rows[5],
        rows[3],
        rows[4],
        out_w_up,
        up,
        out_w_down,
        rows[6],
    )


def solution(mesh):
    rows = P(("dp", "gr", "gc"), None)
    in_specs = (
        rows,
        rows,
        P("gr"),
        P("gr"),
        P("gr"),
        P("gr", "gc"),
        P("gc", "gr"),
        P("gr"),
        P("gr"),
        P("gr"),
        P("gr", "gc"),
        P("gc"),
        P("gr", "gc"),
        P("gr"),
        P(("dp", "gr")),
        P(),
    )
    out_specs = (
        rows,
        P(),
        rows,
        P("gr"),
        P("gr"),
        P("gr"),
        P("gr", "gc"),
        P("gc", "gr"),
        P("gr"),
        P("gr"),
        P("gr"),
        P("gr", "gc"),
        P("gc"),
        P("gr", "gc"),
        P("gr"),
    )
    return jax.shard_map(
        on_device, mesh=mesh, in_specs=in_specs, out_specs=out_specs, check_vma=False
    )
```

```python
from functools import partial
import math

import jax
import jax.numpy as jnp
from jax import lax
from jax.experimental import pallas as pl
from jax.experimental.pallas import tpu as pltpu
from jax.sharding import PartitionSpec as P

D = 768
HD = 64
FF = 3072
P_SIZE = 1024
CL = 128
QROWS = 512
eps = 1e-05
negative = -1e30
BF = jnp.bfloat16
F32 = jnp.float32


def nt(a, b):
    return lax.dot_general(a, b, (((1,), (1,)), ((), ())), preferred_element_type=F32)


def nn(a, b):
    return lax.dot_general(a, b, (((1,), (0,)), ((), ())), preferred_element_type=F32)


def tn(a, b):
    return lax.dot_general(a, b, (((0,), (0,)), ((), ())), preferred_element_type=F32)


def att_fwd_kernel(grp_ref, z_ref, q_ref, kvo_ref, kvp_ref, o_ref, lse_ref):
    j = pl.program_id(1)
    row0 = pl.multiple_of(grp_ref[j] * P_SIZE, P_SIZE)
    z = z_ref[0]
    lane = lax.broadcasted_iota(jnp.int32, (CL, 128), 1)
    low = lane < 64
    zero = jnp.zeros((CL, 128), BF)
    q = q_ref[...]
    q_parts = (jnp.where(low, zero, q), jnp.where(low, q, zero))

    @pl.when(z >= 2)
    def _():
        row = lax.broadcasted_iota(jnp.int32, (CL, CL), 0)
        near_ok = lax.broadcasted_iota(jnp.int32, (CL, CL), 1) <= row
        mixes, sums = [], []
        for h in range(2):
            cols = slice(128 * h, 128 * h + 128)
            kv = kvp_ref[pl.ds(row0, P_SIZE), cols]
            kvo = kvo_ref[:, cols]
            far = nt(q_parts[h], kv)
            near = jnp.where(near_ok, nt(q_parts[h], kvo), negative)
            top = jnp.maximum(
                jnp.max(far, axis=1, keepdims=True), jnp.max(near, axis=1, keepdims=True)
            )
            far = jnp.exp(far - top)
            near = jnp.exp(near - top)
            total = jnp.sum(far, axis=1, keepdims=True) + jnp.sum(near, axis=1, keepdims=True)
            mix = nn(far.astype(BF), kv) + nn(near.astype(BF), kvo)
            mixes.append(mix / total)
            sums.append(jnp.broadcast_to(top + jnp.log(total), (CL, 128)))
        o_ref[...] = jnp.where(low, mixes[0], mixes[1]).astype(BF)
        lse_ref[...] = jnp.where(low, sums[0], sums[1])

    @pl.when(z < 2)
    def _():
        limit = z * QROWS + (j % (QROWS // CL)) * CL
        row = lax.broadcasted_iota(jnp.int32, (CL, P_SIZE), 0)
        key = lax.broadcasted_iota(jnp.int32, (CL, P_SIZE), 1)
        allowed = key - row <= limit
        mixes, sums = [], []
        for h in range(2):
            cols = slice(128 * h, 128 * h + 128)
            kv = kvp_ref[pl.ds(row0, P_SIZE), cols]
            far = jnp.where(allowed, nt(q_parts[h], kv), negative)
            top = jnp.max(far, axis=1, keepdims=True)
            far = jnp.exp(far - top)
            total = jnp.sum(far, axis=1, keepdims=True)
            mix = nn(far.astype(BF), kv)
            mixes.append(mix / total)
            sums.append(jnp.broadcast_to(top + jnp.log(total), (CL, 128)))
        o_ref[...] = jnp.where(low, mixes[0], mixes[1]).astype(BF)
        lse_ref[...] = jnp.where(low, sums[0], sums[1])


def attend(grp, z, q, kvo, kvp):
    rows = q.shape[0]
    pairs = q.shape[1] // 128
    groups_rows = kvp.shape[0]
    return pl.pallas_call(
        att_fwd_kernel,
        name="att_fwd",
        grid_spec=pltpu.PrefetchScalarGridSpec(
            num_scalar_prefetch=2,
            grid=(pairs, rows // CL),
            in_specs=[
                pl.BlockSpec((CL, 128), lambda p, j, *_: (j, p)),
                pl.BlockSpec((CL, 256), lambda p, j, *_: (j, p)),
                pl.BlockSpec((groups_rows, 256), lambda p, j, *_: (0, p)),
            ],
            out_specs=[
                pl.BlockSpec((CL, 128), lambda p, j, *_: (j, p)),
                pl.BlockSpec((CL, 128), lambda p, j, *_: (j, p)),
            ],
        ),
        out_shape=[
            jax.ShapeDtypeStruct((rows, pairs * 128), BF),
            jax.ShapeDtypeStruct((rows, pairs * 128), F32),
        ],
        compiler_params=pltpu.CompilerParams(vmem_limit_bytes=40 << 20),
        cost_estimate=pl.CostEstimate(
            flops=4 * rows * P_SIZE * 128 * pairs * 2,
            bytes_accessed=groups_rows * 512 * pairs,
            transcendentals=rows * P_SIZE * pairs * 2,
        ),
    )(grp, z, q, kvo, kvp)


def att_bwd_kernel(
    grp_ref, z_ref, q_ref, gm_ref, lse_ref, kvo_ref, kvp_ref, dq_ref, dkvo_ref, dkvp_ref, acc
):
    j = pl.program_id(1)
    row0 = pl.multiple_of(grp_ref[j] * P_SIZE, P_SIZE)
    z = z_ref[0]
    low = lax.broadcasted_iota(jnp.int32, (CL, 128), 1) < 64
    zero = jnp.zeros((CL, 128), BF)
    q = q_ref[...]
    gm = gm_ref[...]
    stacks = (
        jnp.concatenate([jnp.where(low, zero, q), jnp.where(low, gm, zero)], axis=0),
        jnp.concatenate([jnp.where(low, q, zero), jnp.where(low, zero, gm)], axis=0),
    )

    @pl.when(j == 0)
    def _():
        acc[...] = jnp.zeros_like(acc)

    @pl.when(z >= 2)
    def _():
        row = lax.broadcasted_iota(jnp.int32, (CL, CL), 0)
        near_ok = row <= lax.broadcasted_iota(jnp.int32, (CL, CL), 1)
        dqs = []
        for h in range(2):
            cols = slice(128 * h, 128 * h + 128)
            kv = kvp_ref[pl.ds(row0, P_SIZE), cols]
            kvo = kvo_ref[:, cols]
            lse = lse_ref[0, 0, h : h + 1, :]
            far = nt(kv, stacks[h])
            near = nt(kvo, stacks[h])
            pf = jnp.exp(far[:, :CL] - lse)
            pn = jnp.where(near_ok, jnp.exp(near[:, :CL] - lse), 0.0)
            df = far[:, CL:]
            dn = near[:, CL:]
            inner = jnp.sum(pf * df, axis=0, keepdims=True) + jnp.sum(
                pn * dn, axis=0, keepdims=True
            )
            sf = (pf * (df - inner)).astype(BF)
            sn = (pn * (dn - inner)).astype(BF)
            acc[pl.ds(row0, P_SIZE), cols] += nn(
                jnp.concatenate([sf, pf.astype(BF)], axis=1), stacks[h]
            )
            dkvo_ref[:, cols] = nn(
                jnp.concatenate([sn, pn.astype(BF)], axis=1), stacks[h]
            ).astype(BF)
            dqs.append(tn(sf, kv) + tn(sn, kvo))
        dq_ref[...] = (jnp.where(low, dqs[1], dqs[0]) * 0.125).astype(BF)

    @pl.when(z < 2)
    def _():
        limit = z * QROWS + (j % (QROWS // CL)) * CL
        key = lax.broadcasted_iota(jnp.int32, (P_SIZE, CL), 0)
        row = lax.broadcasted_iota(jnp.int32, (P_SIZE, CL), 1)
        allowed = key - row <= limit
        dqs = []
        for h in range(2):
            cols = slice(128 * h, 128 * h + 128)
            kv = kvp_ref[pl.ds(row0, P_SIZE), cols]
            lse = lse_ref[0, 0, h : h + 1, :]
            far = nt(kv, stacks[h])
            pf = jnp.where(allowed, jnp.exp(far[:, :CL] - lse), 0.0)
            df = far[:, CL:]
            inner = jnp.sum(pf * df, axis=0, keepdims=True)
            sf = (pf * (df - inner)).astype(BF)
            acc[pl.ds(row0, P_SIZE), cols] += nn(
                jnp.concatenate([sf, pf.astype(BF)], axis=1), stacks[h]
            )
            dqs.append(tn(sf, kv))
        dkvo_ref[...] = jnp.zeros_like(dkvo_ref)
        dq_ref[...] = (jnp.where(low, dqs[1], dqs[0]) * 0.125).astype(BF)

    @pl.when(j == pl.num_programs(1) - 1)
    def _():
        dkvp_ref[...] = acc[...].astype(BF)


def attend_back(grp, z, q, gm, lse, kvo, kvp):
    rows = q.shape[0]
    pairs = q.shape[1] // 128
    groups_rows = kvp.shape[0]
    return pl.pallas_call(
        att_bwd_kernel,
        name="att_bwd",
        grid_spec=pltpu.PrefetchScalarGridSpec(
            num_scalar_prefetch=2,
            grid=(pairs, rows // CL),
            in_specs=[
                pl.BlockSpec((CL, 128), lambda p, j, *_: (j, p)),
                pl.BlockSpec((CL, 128), lambda p, j, *_: (j, p)),
                pl.BlockSpec((1, 1, 2, 128), lambda p, j, *_: (p, j, 0, 0)),
                pl.BlockSpec((CL, 256), lambda p, j, *_: (j, p)),
                pl.BlockSpec((groups_rows, 256), lambda p, j, *_: (0, p)),
            ],
            out_specs=[
                pl.BlockSpec((CL, 128), lambda p, j, *_: (j, p)),
                pl.BlockSpec((CL, 256), lambda p, j, *_: (j, p)),
                pl.BlockSpec((groups_rows, 256), lambda p, j, *_: (0, p)),
            ],
            scratch_shapes=[pltpu.VMEM((groups_rows, 256), F32)],
        ),
        out_shape=[
            jax.ShapeDtypeStruct((rows, pairs * 128), BF),
            jax.ShapeDtypeStruct((rows, pairs * 256), BF),
            jax.ShapeDtypeStruct((groups_rows, pairs * 256), BF),
        ],
        compiler_params=pltpu.CompilerParams(vmem_limit_bytes=48 << 20),
        cost_estimate=pl.CostEstimate(
            flops=10 * rows * P_SIZE * 128 * pairs * 2,
            bytes_accessed=groups_rows * 1024 * pairs,
            transcendentals=rows * P_SIZE * pairs * 2,
        ),
    )(grp, z, q, gm, lse, kvo, kvp)


MESH = pl.DeviceIdType.MESH


def places():
    x = lax.axis_index("dp")
    z = lax.axis_index("gr")
    g = lax.axis_index("gc")
    return x, z, g, g // 2, g % 2


def greet(partners, meanwhile=None):
    barrier = pltpu.get_barrier_semaphore()
    for partner in partners:
        pl.semaphore_signal(barrier, inc=1, device_id=partner, device_id_type=MESH)
    if meanwhile is not None:
        meanwhile()
    pl.semaphore_wait(barrier, len(partners))


def all_partners():
    x, z, g, y, c = places()
    by_z = [{"gr": z ^ step} for step in (1, 2, 3)]
    return [{"gc": g ^ 1}, {"gc": g ^ 2}, {"dp": x ^ 1}] + by_z


def send(src, dst, sems, slot, target, send_slot=None):
    return pltpu.make_async_remote_copy(
        src_ref=src,
        dst_ref=dst,
        send_sem=sems[0].at[slot if send_slot is None else send_slot],
        recv_sem=sems[1].at[slot],
        device_id=target,
        device_id_type=MESH,
    )


def add_into(dst, left, right):
    rows = dst.shape[0]
    size = 48 if rows % 48 == 0 else 64

    @pl.loop(0, rows // size)
    def _(i):
        r = pl.ds(pl.multiple_of(i * size, 16), size)
        dst[r] = (left[r].astype(F32) + right[r].astype(F32)).astype(dst.dtype)


RS_SLOTS = 28
RS_ORDER = (3, 2, 1, 0)
PACE = 26


def rs_plan(grads, outs, bufs, sems, l_sems, base, paired):
    own, ra, rb0, rb1, rc0, rc1, sc, rd, re = bufs
    x, z, g, y, c = places()
    sib, over_y, over_x = {"gc": g ^ 1}, {"gc": g ^ 2}, {"dp": x ^ 1}
    rows = grads.shape[2]
    q = rows // 4
    mine0 = pl.ds(pl.multiple_of(q * x, 16), q)
    other0 = pl.ds(pl.multiple_of(q * (1 - x), 16), q)
    mine1 = pl.ds(pl.multiple_of(2 * q + q * x, 16), q)
    other1 = pl.ds(pl.multiple_of(2 * q + q * (1 - x), 16), q)
    first = pl.ds(0, 2 * q)
    slot = base * RS_SLOTS

    def load(i, s):
        source = grads.at[2 * i + c, z ^ s] if paired else grads.at[i, z ^ s]
        return pltpu.make_async_copy(source, own.at[i, s], l_sems.at[8 * base + 2 * s + i])

    def hop_a(i, s):
        return send(grads.at[2 * i + 1 - c, z ^ s], ra.at[i, s], sems, slot + 6 * s + i, sib)

    def hop_b0(s):
        return send(own.at[1 - y, s, first], rb0.at[s], sems, slot + 6 * s + 2, over_y)

    def hop_b1(s):
        return send(own.at[:, s, other1], rb1.at[s], sems, slot + 6 * s + 3, over_x)

    def hop_c0(s):
        return send(own.at[y, s, other0], rc0.at[s], sems, slot + 6 * s + 4, over_x)

    def hop_c1(s):
        return send(own.at[1 - y, s, mine1], rc1.at[s], sems, slot + 6 * s + 5, over_y)

    def hop_z(s):
        return send(sc.at[s], rd.at[s - 1], sems, slot + 23 + s, {"gr": z ^ s})

    def hop_d():
        return send(sc.at[0], re, sems, slot + 27, over_x)

    def begin(s):
        for i in range(2):
            load(i, s).start()
            if paired:
                hop_a(i, s).start()

    def after_a(s):
        for i in range(2):
            load(i, s).wait()
            if paired:
                hop_a(i, s).wait()
                add_into(own.at[i, s], own.at[i, s], ra.at[i, s])
        hop_b0(s).start()
        hop_b1(s).start()

    def after_b(s):
        hop_b0(s).wait()
        hop_b1(s).wait()
        add_into(own.at[y, s, first], own.at[y, s, first], rb0.at[s])
        for i in range(2):
            add_into(own.at[i, s, mine1], own.at[i, s, mine1], rb1.at[s, i])
        hop_c0(s).start()
        hop_c1(s).start()

    def after_c(s):
        hop_c0(s).wait()
        hop_c1(s).wait()
        add_into(sc.at[s, pl.ds(0, q)], own.at[y, s, mine0], rc0.at[s])
        add_into(sc.at[s, pl.ds(q, q)], own.at[y, s, mine1], rc1.at[s])
        if s:
            hop_z(s).start()

    def total():
        for s in (1, 2, 3):
            hop_z(s).wait()
        whole = sc[0].astype(F32)
        for i in range(3):
            whole = whole + rd[i].astype(F32)
        sc[0] = whole.astype(BF)
        hop_d().start()

    def finish():
        hop_d().wait()
        outs[mine0] = sc[0, pl.ds(0, q)].astype(F32)
        outs[mine1] = sc[0, pl.ds(q, q)].astype(F32)
        outs[other0] = re[pl.ds(0, q)].astype(F32)
        outs[other1] = re[pl.ds(q, q)].astype(F32)

    return begin, after_a, after_b, after_c, total, finish


def rs_steps(plans):
    order = [(plan, s) for plan in plans for s in RS_ORDER]
    n = len(order)
    steps = [[partial(plan[0], s) for plan, s in order]]
    for i in range(n + 10):
        part = []
        if i < n:
            part.append(partial(order[i][0][1], order[i][1]))
        if 2 <= i < n + 2:
            part.append(partial(order[i - 2][0][2], order[i - 2][1]))
        if 4 <= i < n + 4:
            part.append(partial(order[i - 4][0][3], order[i - 4][1]))
        if 7 <= i < n + 7 and (i - 7) % 4 == 3:
            part.append(plans[(i - 7) // 4][4])
        if 9 <= i < n + 9 and (i - 9) % 4 == 3:
            part.append(plans[(i - 9) // 4][5])
        if part:
            steps.append(part)
    return steps


def rs_scratch(rows, cols, paired):
    q = rows // 4
    return [
        pltpu.VMEM((2, 4, rows, cols), BF),
        pltpu.VMEM((2, 4, rows, cols) if paired else (16, 128), BF),
        pltpu.VMEM((4, 2 * q, cols), BF),
        pltpu.VMEM((4, 2, q, cols), BF),
        pltpu.VMEM((4, q, cols), BF),
        pltpu.VMEM((4, q, cols), BF),
        pltpu.VMEM((4, 2 * q, cols), BF),
        pltpu.VMEM((3, 2 * q, cols), BF),
        pltpu.VMEM((2 * q, cols), BF),
    ]


def att_scatter_kernel(count, grp_ref, q_ref, lse_ref, kvo_ref, kvp_ref, gm, *refs):
    grads = refs[:count]
    dq_ref, dkvo_ref, dkv_ref = refs[count : count + 3]
    outs = refs[count + 3 : 2 * count + 3]
    rest = refs[2 * count + 3 :]
    bufs, (gmx, sem_s, sem_r, l_sems, m_send, m_recv, m_local) = rest[: 9 * count], rest[9 * count :]
    p, j = pl.program_id(0), pl.program_id(1)
    step = p * pl.num_programs(1) + j
    x, z, g, y, c = places()
    hooks = rs_steps(
        [
            rs_plan(grads[k], outs[k], bufs[9 * k : 9 * k + 9], (sem_s, sem_r), l_sems, k, True)
            for k in range(count)
        ]
    )

    def exchange(i):
        cols = pl.ds(128 * i, 128)
        return (
            pltpu.make_async_copy(gm.at[c, :, cols], gmx.at[i, c], m_local.at[i]),
            send(gm.at[1 - c, :, cols], gmx.at[i, c], (m_send, m_recv), i, {"gc": g ^ 1}),
        )

    @pl.when(step == 0)
    def _():
        greet(all_partners())
        for i in range(3):
            for copy in exchange(i):
                copy.start()
        for hook in hooks[0]:
            hook()
        for copy in exchange(0):
            copy.wait()

    for i in (1, 2):

        @pl.when(step == 8 * i)
        def _():
            for copy in exchange(i):
                copy.wait()

    last = len(hooks) - 1
    for when in range(1, 23):
        parts = [h for i in range(1, last) if max(1, i * PACE // (last - 1)) == when for h in hooks[i]]
        if parts:

            @pl.when(step == when)
            def _():
                for hook in parts:
                    hook()

    group = grp_ref[j]
    low = lax.broadcasted_iota(jnp.int32, (CL, 128), 1) < 64
    zero = jnp.zeros((CL, 128), BF)
    q = q_ref[0]
    gmix = gmx[p, j // 4, pl.ds(pl.multiple_of((j % 4) * CL, CL), CL)]
    stacks = (
        jnp.concatenate([jnp.where(low, zero, q), jnp.where(low, gmix, zero)], axis=0),
        jnp.concatenate([jnp.where(low, q, zero), jnp.where(low, zero, gmix)], axis=0),
    )

    @pl.when(z >= 2)
    def _():
        row = lax.broadcasted_iota(jnp.int32, (CL, CL), 0)
        near_ok = row <= lax.broadcasted_iota(jnp.int32, (CL, CL), 1)
        dqs = []
        for h in range(2):
            cols = slice(128 * h, 128 * h + 128)
            kv = kvp_ref[0, group, :, cols]
            kvo = kvo_ref[0, :, cols]
            lse = lse_ref[0, 0, h : h + 1, :]
            far = nt(kv, stacks[h])
            near = nt(kvo, stacks[h])
            pf = jnp.exp(far[:, :CL] - lse)
            pn = jnp.where(near_ok, jnp.exp(near[:, :CL] - lse), 0.0)
            df = far[:, CL:]
            dn = near[:, CL:]
            inner = jnp.sum(pf * df, axis=0, keepdims=True) + jnp.sum(
                pn * dn, axis=0, keepdims=True
            )
            sf = (pf * (df - inner)).astype(BF)
            sn = (pn * (dn - inner)).astype(BF)
            dkv_ref[0, :, cols] = nn(
                jnp.concatenate([sf, pf.astype(BF)], axis=1), stacks[h]
            ).astype(BF)
            dkvo_ref[:, cols] = nn(
                jnp.concatenate([sn, pn.astype(BF)], axis=1), stacks[h]
            ).astype(BF)
            dqs.append(tn(sf, kv) + tn(sn, kvo))
        dq_ref[...] = (jnp.where(low, dqs[1], dqs[0]) * 0.125).astype(BF)

    @pl.when(z < 2)
    def _():
        limit = z * QROWS + (j % (QROWS // CL)) * CL
        key = lax.broadcasted_iota(jnp.int32, (P_SIZE, CL), 0)
        row = lax.broadcasted_iota(jnp.int32, (P_SIZE, CL), 1)
        allowed = key - row <= limit
        dqs = []
        for h in range(2):
            cols = slice(128 * h, 128 * h + 128)
            kv = kvp_ref[0, group, :, cols]
            lse = lse_ref[0, 0, h : h + 1, :]
            far = nt(kv, stacks[h])
            pf = jnp.where(allowed, jnp.exp(far[:, :CL] - lse), 0.0)
            df = far[:, CL:]
            inner = jnp.sum(pf * df, axis=0, keepdims=True)
            sf = (pf * (df - inner)).astype(BF)
            dkv_ref[0, :, cols] = nn(
                jnp.concatenate([sf, pf.astype(BF)], axis=1), stacks[h]
            ).astype(BF)
            dqs.append(tn(sf, kv))
        dkvo_ref[...] = jnp.zeros_like(dkvo_ref)
        dq_ref[...] = (jnp.where(low, dqs[1], dqs[0]) * 0.125).astype(BF)

    @pl.when(step == 23)
    def _():
        for i in range(1, last + 1):
            if i == last or i * PACE // (last - 1) > 22:
                for hook in hooks[i]:
                    hook()


def attend_back_scatter(grp, q, lse, kvo, kvp, gm, grads, collective_id):
    rows = q.shape[1]
    count = len(grads)
    any_space = pl.BlockSpec(memory_space=pl.ANY)
    scratch = []
    for grad in grads:
        scratch += rs_scratch(grad.shape[2], grad.shape[3], True)
    slots = RS_SLOTS * count
    return pl.pallas_call(
        partial(att_scatter_kernel, count),
        name="attend_back_scatter",
        grid_spec=pltpu.PrefetchScalarGridSpec(
            num_scalar_prefetch=1,
            grid=(3, rows // CL),
            in_specs=[
                pl.BlockSpec((1, CL, 128), lambda p, j, *_: (p, j, 0)),
                pl.BlockSpec((1, 1, 2, 128), lambda p, j, *_: (p, j, 0, 0)),
                pl.BlockSpec((1, CL, 256), lambda p, j, *_: (p, j, 0)),
                pl.BlockSpec((1, 4, P_SIZE, 256), lambda p, j, *_: (p, 0, 0, 0)),
            ]
            + [any_space] * (count + 1),
            out_specs=[
                pl.BlockSpec((CL, 128), lambda p, j, *_: (j, p)),
                pl.BlockSpec((CL, 256), lambda p, j, *_: (j, p)),
                pl.BlockSpec((1, P_SIZE, 256), lambda p, j, *_: (j, 0, p)),
            ]
            + [pl.BlockSpec(grad.shape[2:], lambda p, j, *_: (0, 0)) for grad in grads],
            scratch_shapes=scratch
            + [
                pltpu.VMEM((3, 2, QROWS, 128), BF),
                pltpu.SemaphoreType.DMA((slots,)),
                pltpu.SemaphoreType.DMA((slots,)),
                pltpu.SemaphoreType.DMA((8 * count,)),
                pltpu.SemaphoreType.DMA((3,)),
                pltpu.SemaphoreType.DMA((3,)),
                pltpu.SemaphoreType.DMA((3,)),
            ],
        ),
        out_shape=[
            jax.ShapeDtypeStruct((rows, 384), BF),
            jax.ShapeDtypeStruct((rows, 768), BF),
            jax.ShapeDtypeStruct((8, P_SIZE, 768), BF),
        ]
        + [jax.ShapeDtypeStruct(grad.shape[2:], F32) for grad in grads],
        compiler_params=pltpu.CompilerParams(
            collective_id=collective_id, has_side_effects=True, vmem_limit_bytes=56 << 20
        ),
    )(grp, q, lse, kvo, kvp, gm, *grads)


def norm_rows(hidden, gain, shift):
    center = jnp.mean(hidden, axis=1, keepdims=True)
    offset = hidden - center
    factor = lax.rsqrt(jnp.mean(offset * offset, axis=1, keepdims=True) + eps)
    return offset * factor * gain + shift


CHUNKS = 4
PIECES = 4
FRONT = 5 + 2 * PIECES
GATHER_SLOTS = 40
SEGMENT = 4


def front_kernel(
    tokens,
    vec,
    bup,
    own,
    wq,
    block0,
    block1,
    block2,
    mixed,
    lse_ref,
    whole0,
    whole1,
    whole2,
    prompts_out,
    chip_out,
    q_out,
    kvo_out,
    kvp_out,
    wq_out,
    wkv_out,
    vec_out,
    bup_out,
    own_out,
    n1,
    vec_in,
    prompts,
    chip,
    wpair,
    q_all,
    kvo_all,
    kvp_all,
    mix,
    own_scalar,
    zs,
    zr,
    ys,
    yr,
    ds,
    dr,
    ws,
    wr,
    ss,
    sr,
    gs,
    gr_,
    ms,
    mr,
    l_sems,
    o_sems,
):
    x, z, g, y, c = places()
    sib, over_y, over_x = {"gc": g ^ 1}, {"gc": g ^ 2}, {"dp": x ^ 1}
    z_sems, y_sems, d_sems, w_sems, s_sems, g_sems = (
        (zs, zr),
        (ys, yr),
        (ds, dr),
        (ws, wr),
        (ss, sr),
        (gs, gr_),
    )
    blocks, wholes = (block0, block1, block2), (whole0, whole1, whole2)
    half_rows = wq.shape[0] // 2
    my_half = pl.ds(pl.multiple_of(x * half_rows, 16), half_rows)
    size = QROWS // PIECES
    first_half = jnp.where(z == 0, 0, 1)
    order = (z, z ^ 1, jnp.where(z < 2, 2, 1), jnp.where(z < 2, 3, 0))
    above, below = {"gr": jnp.minimum(z + 1, 3)}, {"gr": jnp.maximum(z - 1, 0)}
    inner = jnp.logical_and(z > 0, z < 3)

    def line(part, sems, base, b):
        return (
            (jnp.logical_and(z < 3, b <= z), send(part, part, sems, base + b, above)),
            (
                jnp.logical_and(z > 0, b >= z),
                send(part, part, sems, base + b, below, base + 4 + b),
            ),
        )

    def pass_on(copies):
        for goes, copy in copies:
            pl.when(goes)(copy.start)

    def passed_on(copies):
        for goes, copy in copies:
            pl.when(goes)(copy.wait_send)

    local_copy = pltpu.make_async_copy

    def small(kind, s):
        if kind == 0:
            return send(vec, vec_in.at[s], s_sems, s, {"gr": z ^ s})
        if kind == 1:
            return send(own, own_out.at[z], s_sems, 3 + s, {"gr": z ^ s})
        return send(bup, bup_out.at[g], s_sems, 6 + s, {"gc": g ^ s})

    def chip_send():
        return send(n1, chip.at[c], s_sems, 10, sib)

    def w_local():
        return local_copy(wq.at[my_half], wpair.at[y, z, my_half], l_sems.at[0])

    def w_line(s):
        return line(wpair.at[y, order[s], my_half], w_sems, 0, order[s])

    def w_gc(s):
        piece = wpair.at[y, order[s], my_half]
        return send(piece, piece, w_sems, 8 + s, over_y)

    def w_dp(s):
        piece = wpair.at[y, order[s], my_half]
        return send(piece, piece, w_sems, 12 + s, over_x)

    def w_dp_far(s):
        piece = wpair.at[1 - y, order[s], my_half]
        return send(piece, piece, w_sems, 16 + s, over_x)

    def chunk(number):
        return jnp.where(number < PIECES, first_half, 1 - first_half), number % PIECES

    def item(column, number):
        half, k = chunk(number)
        return prompts.at[column, half, pl.ds(pl.multiple_of(k * size, size), size)]

    def up(number):
        half, k = chunk(number)
        ref = item(g, number)
        return send(ref, ref, z_sems, half * PIECES + k, {"gr": jnp.minimum(z + 1, 3)})

    def down(number):
        half, k = chunk(number)
        ref = item(g, number)
        return send(
            ref,
            ref,
            z_sems,
            half * PIECES + k,
            {"gr": jnp.maximum(z - 1, 0)},
            2 * PIECES + k,
        )

    def side(number):
        half, k = chunk(number)
        ref = item(g, number)
        return send(ref, ref, y_sems, half * PIECES + k, over_y)

    def core(number, far):
        half, k = chunk(number)
        ref = item(g ^ 2 if far else g, number)
        return send(ref, ref, d_sems, far * 2 * PIECES + half * PIECES + k, sib)

    def goes_up(number):
        return jnp.logical_and(z < 3, chunk(number)[0] <= z)

    def goes_down(number):
        return jnp.logical_and(z == 1, chunk(number)[0] == 1)

    def forward(number):
        @pl.when(chunk(number)[0] != z)
        def _():
            up(number).wait_recv()

        @pl.when(goes_up(number))
        def _():
            up(number).start()

        @pl.when(goes_down(number))
        def _():
            down(number).start()

        side(number).start()
        core(number, 0).start()

    def across(number):
        side(number).wait_recv()
        core(number, 1).start()

    def plan(a, s):
        block, whole = blocks[a], wholes[a]
        q = block.shape[0] // 4
        half = pl.ds(pl.multiple_of(x * 2 * q, 16), 2 * q)
        qa = pl.ds(pl.multiple_of(x * 2 * q, 16), q)
        qb = pl.ds(pl.multiple_of(x * 2 * q + q, 16), q)
        qc = pl.ds(pl.multiple_of((1 - x) * 2 * q + q, 16), q)
        base = a * GATHER_SLOTS
        mine, far = whole.at[g, order[s]], whole.at[g ^ 2, order[s]]
        o = base + 8 + 8 * s

        def same(part, number, target):
            return lambda: send(part, part, g_sems, o + number, target)

        return {
            "line": lambda: line(mine.at[half], g_sems, base, order[s]),
            "ay": same(mine.at[qa], 0, over_y),
            "ax": same(mine.at[qa], 1, over_x),
            "afx": same(far.at[qa], 2, over_x),
            "bx": same(mine.at[qb], 3, over_x),
            "by": same(mine.at[qb], 4, over_y),
            "bfy": same(mine.at[qc], 5, over_y),
            "bfx": same(far.at[qb], 5, over_x),
            "c1": same(mine, 6, sib),
            "c2": same(far, 7, sib),
        }

    def own_block(a):
        return local_copy(blocks[a], wholes[a].at[g, z], l_sems.at[4 + a])

    def names(s):
        return ("ay", "ax", "afx", "bx", "by", "bfy") if s else ("ay", "afx", "by", "bfx")

    def relay(s):
        @pl.when(inner)
        def _():
            for a in range(3):
                copies = plan(a, s)["line"]()
                copies[0][1].wait_recv()
                pass_on(copies)


    def gather_first(s):
        for a in range(3):
            m = plan(a, s)
            if s:
                pl.when(jnp.logical_not(inner))(m["line"]()[0][1].wait_recv)
                m["bx"]().start()
                m["ax"]().start()
            m["ay"]().start()
            m["by"]().start()

    def gather_second(s):
        for a in range(3):
            m = plan(a, s)
            m["ay"]().wait_recv()
            m["afx"]().start()
            if s:
                m["bx"]().wait_recv()
                m["bfy"]().start()
            else:
                m["by"]().wait_recv()
                m["bfx"]().start()

    def gather_third(s):
        for a in range(3):
            m = plan(a, s)
            for name in ("ax", "afx", "by", "bfy") if s else ("afx", "bfx"):
                m[name]().wait_recv()
            m["c1"]().start()
            m["c2"]().start()

    def out_copies():
        return [
            local_copy(prompts, prompts_out, o_sems.at[0]),
            local_copy(chip, chip_out, o_sems.at[1]),
            local_copy(q_all, q_out, o_sems.at[2]),
            local_copy(kvo_all, kvo_out, o_sems.at[3]),
            local_copy(kvp_all, kvp_out, o_sems.at[4]),
        ]

    def exchange(i):
        cols = pl.ds(128 * i, 128)
        return (
            local_copy(mix.at[i, c], mixed.at[c, :, cols], l_sems.at[7 + i]),
            send(mix.at[i, 1 - c], mixed.at[c, :, cols], (ms, mr), i, sib),
        )

    hooks = {i: [] for i in range(FRONT)}

    def begin():
        greet(all_partners() + [{"gc": g ^ 3}])
        w_local().start()
        for s in (1, 2, 3):
            for kind in range(3):
                small(kind, s).start()
        w_local().wait()
        pass_on(w_line(0))
        own_out[z] = own[...]
        bup_out[g] = bup[...]
        for s in (1, 2, 3):
            small(0, s).wait_recv()
        vec_out[...] = (vec[...] + vec_in[1]) + (vec_in[2] + vec_in[3])

        @pl.loop(0, PIECES)
        def _(i):
            rows = pl.ds(pl.multiple_of(i * size, size), size)
            hidden = tokens[rows].astype(F32) + vec_out[0:1]
            n1[rows] = norm_rows(hidden, vec_out[1:2], vec_out[2:3]).astype(BF)

        @pl.when(z < 2)
        def _():
            to = local_copy(n1, prompts.at[g, jnp.minimum(z, 1)], l_sems.at[2])
            to.start()
            to.wait()

    def begin_chip():
        local_copy(n1, chip.at[c], l_sems.at[1]).start()
        chip_send().start()
        w_gc(0).start()
        w_dp(0).start()

    hooks[0] += [begin, partial(forward, 0), begin_chip]
    for i in range(1, 2 * PIECES):
        hooks[i].append(partial(forward, i))
    for i in range(2, 2 * PIECES + 2):
        hooks[i].append(partial(across, i - 2))

    def w_pass(s):
        copies = w_line(s)
        copies[0][1].wait_recv()
        pass_on(copies)
        w_gc(s).start()
        w_dp(s).start()

    def w_across(s):
        w_gc(s).wait_recv()
        w_dp_far(s).start()

    for s in (1, 2, 3):
        hooks[s].append(partial(w_pass, s))
    hooks[2].append(partial(w_across, 0))
    hooks[3] += [partial(w_across, 1)]
    hooks[4] += [partial(w_across, 2), partial(w_across, 3)]

    def assemble():
        for s in range(4):
            w_dp(s).wait_recv()
            w_dp_far(s).wait_recv()
        local_copy(n1, chip.at[c], l_sems.at[1]).wait()
        chip_send().wait_recv()
        for s in (1, 2, 3):
            small(1, s).wait_recv()
        to = local_copy(own_out, own_scalar, l_sems.at[3])
        to.start()
        for head in range(6):
            p, b = head // 2, head % 2
            at_q = 128 * p + (0 if b else 64)
            at_k = 256 * p + (128 if b else 64)
            at_v = 256 * p + (192 if b else 0)
            start = (head % 3) * 192
            for r in range(4):
                rows = slice(192 * r, 192 * r + 192)
                source = wpair.at[head // 3, r]
                wq_out[rows, at_q : at_q + HD] = source[:, start : start + HD]
                wkv_out[rows, at_k : at_k + HD] = source[:, start + HD : start + 2 * HD]
                wkv_out[rows, at_v : at_v + HD] = source[:, start + 2 * HD : start + 3 * HD]
        to.wait()

    hooks[5].append(assemble)

    def project(number):
        core(number, 0).wait_recv()
        core(number, 1).wait_recv()
        half, k = chunk(number)
        w = wkv_out[...]
        rows = jnp.concatenate(
            [
                prompts[i, half, pl.ds(pl.multiple_of(k * size, size), size)]
                for i in range(4)
            ],
            axis=0,
        )
        kv = nn(rows, w).astype(BF)
        to = pl.ds(pl.multiple_of(half * QROWS + k * size, size), size)
        for i in range(4):
            for p in range(3):
                kvp_all[p, i, to] = kv[size * i : size * i + size, 256 * p : 256 * p + 256]
        mine = chip[number // PIECES, pl.ds(pl.multiple_of(k * size, size), size)]
        kvo = nn(mine, w).astype(BF)
        queries = (nn(mine, wq_out[...]) * 0.125).astype(BF)
        to = pl.ds(pl.multiple_of(number * size, size), size)
        for p in range(3):
            kvo_all[p, to] = kvo[:, 256 * p : 256 * p + 256]
            q_all[p, to] = queries[:, 128 * p : 128 * p + 128]


    def own_first():
        for a in range(3):
            own_block(a).start()

    def own_down():
        for a in range(3):
            own_block(a).wait()
            goes, copy = plan(a, 0)["line"]()[1]
            pl.when(goes)(copy.start)

    def own_up():
        for a in range(3):
            goes, copy = plan(a, 0)["line"]()[0]
            pl.when(goes)(copy.start)

    hooks[0].append(own_first)
    hooks[1].append(own_down)
    hooks[8].append(own_up)
    hooks[7].append(partial(gather_first, 0))
    hooks[9].append(partial(gather_second, 0))
    between = [[] for _ in range(24 // SEGMENT + 1)]
    last = len(between) - 1
    between[0] += [lambda: [copy.start() for copy in out_copies()], partial(gather_third, 0)]
    hooks[9].append(partial(relay, 1))
    hooks[11].append(partial(relay, 2))
    for slot, stage, s in (
        (0, relay, 3),
        (0, gather_first, 1),
        (1, gather_first, 2),
        (1, gather_second, 1),
        (2, gather_first, 3),
        (2, gather_second, 2),
        (3, gather_third, 1),
        (3, gather_second, 3),
        (4, gather_third, 2),
        (6, gather_third, 3),
    ):
        between[slot].append(partial(stage, s))

    for number in range(FRONT - 2 * PIECES):
        for hook in hooks[number]:
            hook()

    def one_piece(number, carried):
        for i in range(FRONT - 2 * PIECES, FRONT):
            if hooks[i]:

                @pl.when(number == i)
                def _():
                    for hook in hooks[i]:
                        hook()

        project(number - (FRONT - 2 * PIECES))
        return carried

    lax.fori_loop(FRONT - 2 * PIECES, FRONT, one_piece, 0)

    low = lax.broadcasted_iota(jnp.int32, (CL, 128), 1) < 64

    def parts(turn):
        p, j = turn // 8, turn % 8
        shard = 2 * y + j // 4
        group = jnp.where(
            z < 2, shard, own_scalar[shard, 0, jnp.maximum(z - 2, 0) * 4 + j % 4]
        )
        rows_j = pl.ds(pl.multiple_of(j * CL, CL), CL)
        zero = jnp.zeros((CL, 128), BF)
        q = q_all[p, rows_j]
        return p, j, group, rows_j, (jnp.where(low, zero, q), jnp.where(low, q, zero))

    def store(p, j, mixes, sums):
        mix[p, j // 4, pl.ds(pl.multiple_of((j % 4) * CL, CL), CL)] = jnp.where(
            low, mixes[0], mixes[1]
        ).astype(BF)
        flat = jnp.where(low, sums[0], sums[1]).T
        lse_ref[p, j, 0:1] = flat[0:1]
        lse_ref[p, j, 1:2] = flat[64:65]

    def cont_turn(turn, carried):
        p, j, group, rows_j, q_parts = parts(turn)
        row = lax.broadcasted_iota(jnp.int32, (CL, CL), 0)
        near_ok = lax.broadcasted_iota(jnp.int32, (CL, CL), 1) <= row
        mixes, sums = [], []
        for h in range(2):
            cols = slice(128 * h, 128 * h + 128)
            kv = kvp_all[p, group, :, cols]
            kvo = kvo_all[p, rows_j, cols]
            far = nt(q_parts[h], kv)
            near = jnp.where(near_ok, nt(q_parts[h], kvo), negative)
            top = jnp.maximum(
                jnp.max(far, axis=1, keepdims=True), jnp.max(near, axis=1, keepdims=True)
            )
            far = jnp.exp(far - top)
            near = jnp.exp(near - top)
            total = jnp.sum(far, axis=1, keepdims=True) + jnp.sum(near, axis=1, keepdims=True)
            mixes.append((nn(far.astype(BF), kv) + nn(near.astype(BF), kvo)) / total)
            sums.append(jnp.broadcast_to(top + jnp.log(total), (CL, 128)))
        store(p, j, mixes, sums)
        return carried

    def prompt_turn(turn, carried):
        p, j, group, rows_j, q_parts = parts(turn)
        limit = z * QROWS + (j % (QROWS // CL)) * CL
        row = lax.broadcasted_iota(jnp.int32, (CL, P_SIZE), 0)
        key = lax.broadcasted_iota(jnp.int32, (CL, P_SIZE), 1)
        allowed = key - row <= limit
        mixes, sums = [], []
        for h in range(2):
            cols = slice(128 * h, 128 * h + 128)
            kv = kvp_all[p, group, :, cols]
            far = jnp.where(allowed, nt(q_parts[h], kv), negative)
            top = jnp.max(far, axis=1, keepdims=True)
            far = jnp.exp(far - top)
            total = jnp.sum(far, axis=1, keepdims=True)
            mixes.append(nn(far.astype(BF), kv) / total)
            sums.append(jnp.broadcast_to(top + jnp.log(total), (CL, 128)))
        store(p, j, mixes, sums)
        return carried

    def one_turn(turn, carried):
        for segment in range(last):

            @pl.when(turn == segment * SEGMENT)
            def _():
                for hook in between[segment]:
                    hook()

        @pl.when(z >= 2)
        def _():
            cont_turn(turn, 0)

        @pl.when(z < 2)
        def _():
            prompt_turn(turn, 0)

        for i in range(3):

            @pl.when(turn == 8 * i + 7)
            def _():
                for copy in exchange(i):
                    copy.start()

        return carried

    lax.fori_loop(0, 24, one_turn, 0)
    for hook in between[last]:
        hook()

    for number in range(2 * PIECES):
        side(number).wait_send()
        core(number, 0).wait_send()
        core(number, 1).wait_send()

        @pl.when(goes_up(number))
        def _():
            up(number).wait_send()

        @pl.when(goes_down(number))
        def _():
            down(number).wait_send()

    for s in range(4):
        if s:
            small(0, s).wait_send()
            small(1, s).wait_send()
            small(2, s).wait()
        passed_on(w_line(s))
        w_gc(s).wait_send()
        w_dp(s).wait_send()
        w_dp_far(s).wait_send()
    chip_send().wait_send()
    for s in range(4):
        for a in range(3):
            m = plan(a, s)
            passed_on(m["line"]())
            for name in names(s):
                m[name]().wait_send()
            m["c1"]().wait()
            m["c2"]().wait()
    for i in range(3):
        for copy in exchange(i):
            copy.wait()
    for copy in out_copies():
        copy.wait()


def front(tokens, vectors, bias, own, wq, blocks, collective_id):
    def body(tokens_ref, *refs):
        parts, bias_ref = refs[:7], refs[7]
        rest, vec, bup = refs[8:-2], refs[-2], refs[-1]
        z = lax.axis_index("gr")
        width = bias_ref.shape[0] // 4
        vec[...] = jnp.zeros_like(vec)
        for k in range(4):

            @pl.when(z == k)
            def _():
                for i, part in enumerate(parts):
                    vec[i : i + 1, width * k : width * k + width] = (
                        part[...].astype(F32).reshape(1, width)
                    )

        bup[0:1] = bias_ref[...].astype(F32).reshape(1, 4 * width)
        front_kernel(tokens_ref, vec, bup, *rest)

    any_space = pl.BlockSpec(memory_space=pl.ANY)
    vmem = pl.BlockSpec(memory_space=pltpu.VMEM)
    rows = 2 * QROWS

    def dma(count):
        return pltpu.SemaphoreType.DMA((count,))

    slots = 3 * GATHER_SLOTS
    heads = [(3, rows, 128), (3, rows, 256), (3, 4, P_SIZE, 256)]
    return pl.pallas_call(
        body,
        name="front",
        in_specs=[vmem] * 10 + [any_space] * 4,
        out_specs=[any_space, vmem]
        + [any_space] * 8
        + [vmem] * 5,
        out_shape=[
            jax.ShapeDtypeStruct((2, QROWS, 384), BF),
            jax.ShapeDtypeStruct((3, rows // CL, 2, 128), F32),
        ]
        + [jax.ShapeDtypeStruct((4, 4) + block.shape, BF) for block in blocks]
        + [
            jax.ShapeDtypeStruct((4, 2, QROWS, D), BF),
            jax.ShapeDtypeStruct((2, QROWS, D), BF),
        ]
        + [jax.ShapeDtypeStruct(shape, BF) for shape in heads]
        + [
            jax.ShapeDtypeStruct((D, 384), BF),
            jax.ShapeDtypeStruct((D, D), BF),
            jax.ShapeDtypeStruct((8, D), F32),
            jax.ShapeDtypeStruct((4, 8, D), F32),
            jax.ShapeDtypeStruct((4,) + own.shape, jnp.int32),
        ],
        scratch_shapes=[
            pltpu.VMEM((QROWS, D), BF),
            pltpu.VMEM((4, 8, D), F32),
            pltpu.VMEM((4, 2, QROWS, D), BF),
            pltpu.VMEM((2, QROWS, D), BF),
            pltpu.VMEM((2, 4) + wq.shape, BF),
        ]
        + [pltpu.VMEM(shape, BF) for shape in heads]
        + [
            pltpu.VMEM((3, 2, QROWS, 128), BF),
            pltpu.SMEM((4,) + own.shape, jnp.int32),
            dma(3 * PIECES),
            dma(2 * PIECES),
            dma(2 * PIECES),
            dma(2 * PIECES),
            dma(4 * PIECES),
            dma(4 * PIECES),
            dma(20),
            dma(20),
            dma(11),
            dma(11),
            dma(slots),
            dma(slots),
            dma(3),
            dma(3),
            dma(10),
            dma(5),
            pltpu.VMEM((8, D), F32),
            pltpu.VMEM((8, D), F32),
        ],
        compiler_params=pltpu.CompilerParams(
            collective_id=collective_id, has_side_effects=True, vmem_limit_bytes=56 << 20
        ),
    )(tokens, *vectors, bias, own, wq, *blocks)


def tail_kernel(
    grp,
    dkv,
    n1p,
    n1c,
    dkvo,
    dq,
    w_q,
    w_kv,
    grad_h2,
    tokens,
    vec,
    sums,
    out,
    sums_out,
    dw_out,
    part,
    chip,
    tiles,
    rows_p,
    low,
    wkt,
    wqt,
    dkvw,
    dqw,
    dw,
    ra,
    rb,
    rz,
    take,
    gsum,
    cur,
    sb,
    *rest,
):
    bufs, (sem_s, sem_r, l_sems, w_s, w_r, w_l) = rest[:9], rest[9:]
    sems = (sem_s, sem_r)
    x, z, g, y, c = places()
    sib, over_y, over_x = {"gc": g ^ 1}, {"gc": g ^ 2}, {"dp": x ^ 1}
    down = {"gr": jnp.maximum(z - 1, 0)}
    far = z >= 2
    size = QROWS // CHUNKS
    count = 2 * CHUNKS

    def fetch(t):
        rows = pl.ds(pl.multiple_of(t * size, size), size)
        h, r = t // CHUNKS, pl.ds(pl.multiple_of((t % CHUNKS) * size, size), size)
        slot = t % 2
        return (
            pltpu.make_async_copy(dkv.at[:, rows], tiles.at[slot], l_sems.at[slot]),
            pltpu.make_async_copy(n1p.at[:, h, r], rows_p.at[slot], l_sems.at[2 + slot]),
        )

    for copy in fetch(0):
        copy.start()

    def prepare():
        wkt[...] = w_kv[...].T
        wqt[...] = w_q[...].T
        dkvw[...] = jnp.zeros_like(dkvw)
        dqw[...] = jnp.zeros_like(dqw)

    greet(all_partners(), prepare)

    def at(t):
        return t // CHUNKS, pl.ds(pl.multiple_of((t % CHUNKS) * size, size), size)

    def mine(side, t):
        h, r = at(t)
        return part.at[2 * (1 - y if side == 0 else y) + c, h, r]

    def hop_a(side, t):
        h, r = at(t)
        i = 1 - y if side == 0 else y
        return send(part.at[2 * i + 1 - c, h, r], ra.at[i, h, r], sems, 8 * side + t, sib)

    def hop_y(t):
        h, r = at(t)
        return send(mine(0, t), rb.at[h, r], sems, 16 + t, over_y)

    def hop_z(t):
        h, r = at(t)
        return send(mine(1, t), rz.at[h, r], sems, 24 + t, down)

    hop_chip = send(chip.at[1 - c], take, sems, 32, sib)

    def fold(t, other):
        h, r = at(t)
        add_into(mine(1, t), mine(1, t), other.at[r])

    def stage0(t):
        slot = t % 2
        for copy in fetch(t):
            copy.wait()

        @pl.when(t + 1 < count)
        def _():
            for copy in fetch(t + 1):
                copy.start()

        weights = [
            [jnp.where(grp[j] == i, 1.0, 0.0).astype(F32) for j in range(8)] for i in range(4)
        ]

        @pl.loop(0, size // 16)
        def _(q):
            r = pl.ds(pl.multiple_of(q * 16, 16), 16)
            pieces = [tiles[slot, j, r].astype(F32) for j in range(8)]
            for i in range(4):
                total = weights[i][0] * pieces[0]
                for j in range(1, 8):
                    total = total + weights[i][j] * pieces[j]
                low[i, r] = total.astype(BF)

        whole = low[...].reshape(4 * size, D)
        grads = nn(whole, wkt[...]).astype(BF)
        h, r = at(t)
        for i in range(4):
            part[i, h, r] = grads[size * i : size * i + size]

        @pl.when(far)
        def _():
            hop_a(0, t).start()

        hop_a(1, t).start()
        own = pl.ds(pl.multiple_of(t * size, size), size)
        near, grad_q, rows_c = dkvo[own], dq[own], n1c[own]
        chip[h, r] = (nn(grad_q, wqt[...]) + nn(near, wkt[...])).astype(BF)
        rows = jnp.concatenate([rows_p[slot].reshape(4 * size, D), rows_c], axis=0)
        dkvw[...] += tn(rows, jnp.concatenate([whole, near], axis=0))
        dqw[...] += tn(rows_c, grad_q)

    def stage1(t):
        h, r = at(t)

        @pl.when(far)
        def _():
            hop_a(0, t).wait()
            add_into(mine(0, t), mine(0, t), ra.at[1 - y, h, r])
            hop_y(t).start()

        hop_a(1, t).wait()
        fold(t, ra.at[y, h])

    def stage2(t):
        @pl.when(far)
        def _():
            hop_y(t).wait()
            fold(t, rb.at[t // CHUNKS])

        @pl.when(z == 3)
        def _():
            hop_z(t).start()

    def stage3(t):
        @pl.when(z == 2)
        def _():
            hop_z(t).wait_recv()
            fold(t, rz.at[t // CHUNKS])
            hop_z(t).start()

    def stage4(t):
        @pl.when(z == 1)
        def _():
            hop_z(t).wait_recv()
            fold(t, rz.at[t // CHUNKS])

            @pl.when(t < CHUNKS)
            def _():
                hop_z(t).start()

    def stage5(t):
        @pl.when(jnp.logical_and(z == 0, t < CHUNKS))
        def _():
            hop_z(t).wait_recv()
            fold(t, rz.at[0])

    def stages(t, carried, skip=0):
        todo = list(zip((0, 1, 3, 5, 7, 9), (stage0, stage1, stage2, stage3, stage4, stage5)))
        for lag, stage in todo[skip:]:

            @pl.when(jnp.logical_and(t >= lag, t < count + lag))
            def _():
                stage(t - lag)

        return carried

    lax.fori_loop(0, count, stages, 0)
    hop_chip.start()

    for head in range(6):
        p, b = head // 2, head % 2
        places_in = (
            dqw[:, 128 * p + (0 if b else 64) : 128 * p + (64 if b else 128)],
            dkvw[:, 256 * p + (128 if b else 64) : 256 * p + (192 if b else 128)],
            dkvw[:, 256 * p + (192 if b else 0) : 256 * p + (256 if b else 64)],
        )
        for i, piece in enumerate(places_in):
            at_col = (head % 3) * 192 + HD * i
            for r in range(4):
                dw[head // 3, r, :, at_col : at_col + HD] = piece[192 * r : 192 * r + 192].astype(
                    BF
                )
    begin, after_a, after_b, after_c, total, finish = rs_plan(
        dw, dw_out, bufs, (w_s, w_r), w_l, 0, False
    )
    for s in RS_ORDER:
        begin(s)
    for s in RS_ORDER:
        after_a(s)
    lax.fori_loop(count, count + 2, partial(stages, skip=1), 0)
    for s in RS_ORDER:
        after_b(s)
    lax.fori_loop(count + 2, count + 3, partial(stages, skip=2), 0)
    lax.fori_loop(count + 3, count + 6, partial(stages, skip=2), 0)
    for s in RS_ORDER:
        after_c(s)
    lax.fori_loop(count + 6, count + 9, partial(stages, skip=3), 0)

    @pl.loop(0, count)
    def _(t):
        @pl.when(jnp.logical_or(z >= 2, jnp.logical_and(z == 1, t < CHUNKS)))
        def _():
            hop_z(t).wait_send()

    hop_chip.wait()

    cur[...] = sums[...]

    @pl.loop(0, CHUNKS)
    def _(k):
        r = pl.ds(pl.multiple_of(k * size, size), size)
        gsum[r] = chip[c, r].astype(F32) + take[r].astype(F32)

        @pl.when(z < 2)
        def _():
            gsum[r] += part[2 * y + c, jnp.minimum(z, 1), r].astype(F32)

        hidden = tokens[r].astype(F32) + vec[0:1]
        center = jnp.mean(hidden, axis=1, keepdims=True)
        offset = hidden - center
        factor = lax.rsqrt(jnp.mean(offset * offset, axis=1, keepdims=True) + eps)
        unit = offset * factor
        grad = gsum[r]
        scaled = grad * vec[1:2]
        first = jnp.mean(scaled, axis=1, keepdims=True)
        second = jnp.mean(scaled * unit, axis=1, keepdims=True)
        result = grad_h2[r] + factor * (scaled - first - unit * second)
        out[r] = result
        cur[0:1] += jnp.sum(result, axis=0, keepdims=True)
        cur[1:2] += jnp.sum(grad * unit, axis=0, keepdims=True)
        cur[2:3] += jnp.sum(grad, axis=0, keepdims=True)

    for i, target in enumerate((sib, over_y, over_x)):
        hop = send(cur, sb.at[i], sems, 33 + i, target)
        hop.start()
        hop.wait()
        cur[...] += sb[i]
        if i == 1:
            total()
    hops = [send(cur, sb.at[2 + s], sems, 35 + s, {"gr": z ^ s}) for s in (1, 2, 3)]
    for hop in hops:
        hop.start()
    finish()
    for hop in hops:
        hop.wait()
    sums_out[...] = (cur[...] + sb[3]) + (sb[4] + sb[5])


def tail_exchange(
    grp, dkv, n1p, n1c, dkvo, dq, w_q, w_kv, grad_h2, tokens, vec, sums, collective_id
):
    any_space = pl.BlockSpec(memory_space=pl.ANY)
    vmem = pl.BlockSpec(memory_space=pltpu.VMEM)
    block = (2, 4, 192, 576)
    return pl.pallas_call(
        tail_kernel,
        name="tail_exchange",
        in_specs=[pl.BlockSpec(memory_space=pltpu.SMEM), any_space, any_space] + [vmem] * 9,
        out_specs=[vmem, vmem, vmem],
        out_shape=[
            jax.ShapeDtypeStruct((QROWS, D), F32),
            jax.ShapeDtypeStruct(sums.shape, F32),
            jax.ShapeDtypeStruct(block[2:], F32),
        ],
        scratch_shapes=[
            pltpu.VMEM((4, 2, QROWS, D), BF),
            pltpu.VMEM((2, QROWS, D), BF),
            pltpu.VMEM((2, 8, CL, D), BF),
            pltpu.VMEM((2, 4, CL, D), BF),
            pltpu.VMEM((4, CL, D), BF),
            pltpu.VMEM((D, D), BF),
            pltpu.VMEM((384, D), BF),
            pltpu.VMEM((D, D), F32),
            pltpu.VMEM((D, 384), F32),
            pltpu.VMEM(block, BF),
            pltpu.VMEM((2, 2, QROWS, D), BF),
            pltpu.VMEM((2, QROWS, D), BF),
            pltpu.VMEM((2, QROWS, D), BF),
            pltpu.VMEM((QROWS, D), BF),
            pltpu.VMEM((QROWS, D), F32),
            pltpu.VMEM(sums.shape, F32),
            pltpu.VMEM((6,) + sums.shape, F32),
        ]
        + rs_scratch(block[2], block[3], False)
        + [
            pltpu.SemaphoreType.DMA((39,)),
            pltpu.SemaphoreType.DMA((39,)),
            pltpu.SemaphoreType.DMA((4,)),
            pltpu.SemaphoreType.DMA((RS_SLOTS,)),
            pltpu.SemaphoreType.DMA((RS_SLOTS,)),
            pltpu.SemaphoreType.DMA((8,)),
        ],
        compiler_params=pltpu.CompilerParams(
            collective_id=collective_id, has_side_effects=True, vmem_limit_bytes=60 << 20
        ),
    )(grp, dkv, n1p, n1c, dkvo, dq, w_q, w_kv, grad_h2, tokens, vec, sums)


GELU_IN = math.sqrt(2.0 / math.pi)


def middle_kernel(
    mixed,
    w_out_g,
    w_up,
    w_down,
    tokens,
    teacher,
    vec,
    b_up,
    final_out,
    grad_h2,
    dw_up,
    dw_down,
    dw_out,
    gm,
    sums,
    wo,
    wu,
    wd,
    h2,
    n2,
    n2t,
    act,
    slope,
    gf,
    gb,
    gbt,
    acc,
    du,
    dd,
    l_sems,
    o_sems,
):
    loads_u = [pltpu.make_async_copy(w_up.at[b], wu.at[b], l_sems.at[b]) for b in range(4)]
    loads_d = [pltpu.make_async_copy(w_down.at[b], wd.at[b], l_sems.at[4 + b]) for b in range(4)]
    for b in range(4):
        loads_u[b].start()
        loads_d[b].start()
    for k in range(2):
        for i in range(2):
            for r in range(4):
                wo[k, 192 * i : 192 * i + 192, 192 * r : 192 * r + 192] = w_out_g[2 * i + k, r]

    @pl.loop(0, 1)
    def _(t):
        r = pl.ds(pl.multiple_of(t * QROWS, QROWS), QROWS)
        hidden = tokens[r].astype(F32) + vec[0:1]
        attended = nn(mixed[0, r], wo[0]) + nn(mixed[1, r], wo[1])
        total = hidden + attended + vec[3:4]
        h2[r] = total
        n2[r] = norm_rows(total, vec[4:5], vec[5:6]).astype(BF)

    n2t[...] = n2[...].T
    acc[...] = jnp.zeros_like(acc)
    for copy in loads_u + loads_d:
        copy.wait()

    @pl.loop(0, 4)
    def _(b):
        @pl.loop(0, 1)
        def _(t):
            r = pl.ds(pl.multiple_of(t * QROWS, QROWS), QROWS)
            pre = nn(n2[r], wu[b]) + b_up[b, 0:1]
            square = pre * pre
            tanh = jnp.tanh(GELU_IN * pre * (1.0 + 0.044715 * square))
            half = 0.5 * (1.0 + tanh)
            low = (pre * half).astype(BF)
            act[b, r] = low
            slope[b, r] = half + (0.5 * GELU_IN) * pre * (1.0 - tanh * tanh) * (
                1.0 + (3.0 * 0.044715) * square
            )
            acc[r] += nt(low, wd[b])

    sums[...] = jnp.zeros_like(sums)

    @pl.loop(0, 1)
    def _(t):
        r = pl.ds(pl.multiple_of(t * QROWS, QROWS), QROWS)
        final = h2[r] + acc[r] + vec[6:7]
        final_out[r] = final.astype(BF)
        diff = final - teacher[r].astype(F32)
        gf[r] = diff
        low = diff.astype(BF)
        gb[r] = low
        sums[6:7] += jnp.sum(low.astype(F32), axis=0, keepdims=True)
        sums[11:12] += jnp.sum(diff * diff, axis=0, keepdims=True)

    gbt[...] = gb[...].T
    acc[...] = jnp.zeros_like(acc)

    @pl.loop(0, 4)
    def _(b):
        dd[b] = nn(gbt[...], act[b]).astype(BF)
        pltpu.make_async_copy(dd.at[b], dw_down.at[b], o_sems.at[b]).start()

        @pl.loop(0, 1)
        def _(t):
            r = pl.ds(pl.multiple_of(t * QROWS, QROWS), QROWS)
            low = (nn(gb[r], wd[b]) * slope[b, r]).astype(BF)
            act[b, r] = low
            sums[pl.ds(7 + b, 1)] += jnp.sum(low.astype(F32), axis=0, keepdims=True)
            acc[r] += nt(low, wu[b])

        du[b] = nn(n2t[...], act[b]).astype(BF)
        pltpu.make_async_copy(du.at[b], dw_up.at[b], o_sems.at[4 + b]).start()

    @pl.loop(0, 1)
    def _(t):
        r = pl.ds(pl.multiple_of(t * QROWS, QROWS), QROWS)
        hidden = h2[r]
        center = jnp.mean(hidden, axis=1, keepdims=True)
        offset = hidden - center
        factor = lax.rsqrt(jnp.mean(offset * offset, axis=1, keepdims=True) + eps)
        unit = offset * factor
        grad = acc[r]
        scaled = grad * vec[4:5]
        first = jnp.mean(scaled, axis=1, keepdims=True)
        second = jnp.mean(scaled * unit, axis=1, keepdims=True)
        total = gf[r] + factor * (scaled - first - unit * second)
        grad_h2[r] = total
        low = total.astype(BF)
        gb[r] = low
        sums[3:4] += jnp.sum(grad * unit, axis=0, keepdims=True)
        sums[4:5] += jnp.sum(grad, axis=0, keepdims=True)
        sums[5:6] += jnp.sum(low.astype(F32), axis=0, keepdims=True)
        gm[0, r] = nt(low, wo[0]).astype(BF)
        gm[1, r] = nt(low, wo[1]).astype(BF)

    for k in range(2):
        whole = tn(mixed[k], gb[...]).astype(BF)
        for i in range(2):
            for r in range(4):
                dw_out[2 * i + k, r] = whole[192 * i : 192 * i + 192, 192 * r : 192 * r + 192]
    for b in range(4):
        pltpu.make_async_copy(dd.at[b], dw_down.at[b], o_sems.at[b]).wait()
        pltpu.make_async_copy(du.at[b], dw_up.at[b], o_sems.at[4 + b]).wait()


def middle(mixed, w_out_g, w_up, w_down, tokens, teacher, vec, b_up):
    any_space = pl.BlockSpec(memory_space=pl.ANY)
    vmem = pl.BlockSpec(memory_space=pltpu.VMEM)
    blocks = (4, D, D)
    return pl.pallas_call(
        middle_kernel,
        name="middle",
        in_specs=[vmem, vmem, any_space, any_space, vmem, vmem, vmem, vmem],
        out_specs=[vmem, vmem, any_space, any_space, vmem, vmem, vmem],
        out_shape=[
            jax.ShapeDtypeStruct((QROWS, D), BF),
            jax.ShapeDtypeStruct((QROWS, D), F32),
            jax.ShapeDtypeStruct(blocks, BF),
            jax.ShapeDtypeStruct(blocks, BF),
            jax.ShapeDtypeStruct((4, 4, 192, 192), BF),
            jax.ShapeDtypeStruct((2, QROWS, 384), BF),
            jax.ShapeDtypeStruct((16, D), F32),
        ],
        scratch_shapes=[
            pltpu.VMEM((2, 384, D), BF),
            pltpu.VMEM(blocks, BF),
            pltpu.VMEM(blocks, BF),
            pltpu.VMEM((QROWS, D), F32),
            pltpu.VMEM((QROWS, D), BF),
            pltpu.VMEM((D, QROWS), BF),
            pltpu.VMEM((4, QROWS, D), BF),
            pltpu.VMEM((4, QROWS, D), F32),
            pltpu.VMEM((QROWS, D), F32),
            pltpu.VMEM((QROWS, D), BF),
            pltpu.VMEM((D, QROWS), BF),
            pltpu.VMEM((QROWS, D), F32),
            pltpu.VMEM(blocks, BF),
            pltpu.VMEM(blocks, BF),
            pltpu.SemaphoreType.DMA((8,)),
            pltpu.SemaphoreType.DMA((8,)),
        ],
        compiler_params=pltpu.CompilerParams(vmem_limit_bytes=60 << 20),
    )(mixed, w_out_g, w_up, w_down, tokens, teacher, vec, b_up)


def norm(hidden, gain, shift):
    center = jnp.mean(hidden, axis=1, keepdims=True)
    offset = hidden - center
    factor = lax.rsqrt(jnp.mean(offset * offset, axis=1, keepdims=True) + eps)
    unit = offset * factor
    return unit * gain + shift, unit, factor


def norm_back(grad, gain, unit, factor):
    grad_unit = grad * gain
    first = jnp.mean(grad_unit, axis=1, keepdims=True)
    second = jnp.mean(grad_unit * unit, axis=1, keepdims=True)
    grad_in = factor * (grad_unit - first - unit * second)
    return grad_in, jnp.sum(grad * unit, axis=0), jnp.sum(grad, axis=0)


def head_layout(blocks):
    chunks = blocks.transpose(1, 0, 2).reshape(D, 6, 3, HD)
    q_list, kv_list = [], []
    for pair in range(3):
        a, b = 2 * pair, 2 * pair + 1
        q_list += [chunks[:, b, 0], chunks[:, a, 0]]
        kv_list += [chunks[:, a, 2], chunks[:, a, 1], chunks[:, b, 1], chunks[:, b, 2]]
    return jnp.concatenate(q_list, axis=1), jnp.concatenate(kv_list, axis=1)


def head_layout_back(grad_q, grad_kv):
    qc = grad_q.reshape(D, 3, 2, HD)
    kc = grad_kv.reshape(D, 3, 4, HD)
    pieces = []
    for pair in range(3):
        pieces += [qc[:, pair, 1], kc[:, pair, 1], kc[:, pair, 0]]
        pieces += [qc[:, pair, 0], kc[:, pair, 2], kc[:, pair, 3]]
    whole = jnp.concatenate(pieces, axis=1)
    return whole.reshape(D, 2, 576).transpose(1, 0, 2)


def on_device(
    tokens,
    teacher,
    pass_embed,
    ln1_gain,
    ln1_bias,
    qkv_weight,
    out_weight,
    out_bias,
    ln2_gain,
    ln2_bias,
    fc1_weight,
    fc1_bias,
    fc2_weight,
    fc2_bias,
    cont_group,
    token_count,
):
    n_dp = lax.axis_size("dp")
    n_gr = lax.axis_size("gr")
    n_gc = lax.axis_size("gc")
    z = lax.axis_index("gr")
    g = lax.axis_index("gc")
    c = g % 2
    y = g // 2
    swap_core = [(i, i ^ 1) for i in range(n_gc)]
    swap_y = [(i, i ^ 2) for i in range(n_gc)]

    parts = [pass_embed, ln1_gain, ln1_bias, out_bias, ln2_gain, ln2_bias, fc2_bias]
    if n_dp == 2:
        own = jnp.broadcast_to(jnp.pad(cont_group, (0, 120)), (8, 128))
        (
            mixed,
            lse_rows,
            w_out,
            w_up,
            w_down,
            n1_prompt,
            n1_chip,
            q,
            kvo,
            kvp,
            w_q,
            w_kv,
            vectors,
            b_up,
            owners,
        ) = front(
            tokens, parts, fc1_bias, own, qkv_weight, [out_weight, fc1_weight, fc2_weight], 1
        )
        n1_chip = n1_chip.reshape(2 * QROWS, D)
        owners = owners[:, 0, :8]
    else:
        vectors = lax.all_gather(jnp.stack(parts).astype(F32), "gr", axis=1, tiled=True)
        b_up = lax.all_gather(fc1_bias, "gc", axis=0, tiled=True).astype(F32)
        owners = lax.all_gather(cont_group, "gr", axis=0, tiled=True)
    embed, gain1, shift1, b_out, gain2, shift2, b_down = [vectors[i] for i in range(7)]
    owners = owners.reshape(4, 2, 4)
    mine = lax.dynamic_slice(owners, (2 * y, jnp.maximum(z - 2, 0), 0), (2, 1, 4)).reshape(8)
    own_groups = jnp.repeat(2 * y + jnp.arange(2), 4)
    grp = jnp.where(z < 2, own_groups, mine).astype(jnp.int32)
    z_arr = z.astype(jnp.int32).reshape(1)

    hidden = tokens.astype(F32) + embed
    normed1, unit1, factor1 = norm(hidden, gain1, shift1)
    n1 = normed1.astype(BF)

    if n_dp != 2:
        w_other = lax.ppermute(qkv_weight, "gc", swap_y)
        w_pair = jnp.where(
            y == 0, jnp.stack([qkv_weight, w_other]), jnp.stack([w_other, qkv_weight])
        )
        w_qkv = lax.all_gather(w_pair, "gr", axis=1, tiled=True)
        n1_other = lax.ppermute(n1, "gc", swap_core)
        n1_chip = jnp.where(
            c == 0, jnp.concatenate([n1, n1_other]), jnp.concatenate([n1_other, n1])
        )
        n1_col = lax.all_gather(n1, "gr", axis=0, tiled=True)[:P_SIZE]
        n1_prompt = lax.all_gather(n1_col, "gc", axis=0, tiled=True)
        w_q, w_kv = head_layout(w_qkv)
        kvp = nn(n1_prompt, w_kv).astype(BF)
        kvo = nn(n1_chip, w_kv).astype(BF)
        q = (nn(n1_chip, w_q) * 0.125).astype(BF)
        w_out = lax.all_gather(out_weight, ("gc", "gr"))
        w_up = lax.all_gather(fc1_weight, ("gc", "gr"))
        w_down = lax.all_gather(fc2_weight, ("gc", "gr"))
        mixed_heads, lse = attend(grp, z_arr, q, kvo, kvp)
        lse_rows = lse[:, ::64].reshape(8, CL, 3, 2).transpose(2, 0, 3, 1)
        halves = mixed_heads.reshape(2, QROWS, 384)
        keep = lax.dynamic_index_in_dim(halves, c, 0, keepdims=False)
        give = lax.dynamic_index_in_dim(halves, 1 - c, 0, keepdims=False)
        take = lax.ppermute(give, "gc", swap_core)
        mixed = jnp.where(c == 0, jnp.stack([keep, take]), jnp.stack([take, keep]))
    w_up = w_up.reshape(n_gc, D, FF // n_gc)
    w_down = w_down.reshape(n_gc, D, FF // n_gc)
    if n_dp == 2:
        final, grad_h2, grad_w_up, grad_w_down, grad_w_out, gm, later_sums = middle(
            mixed, w_out, w_up, w_down, tokens, teacher, vectors, b_up
        )
    else:
        w_out = w_out.reshape(2, 2, n_gr, 192, 192).transpose(1, 0, 3, 2, 4).reshape(2, 384, D)

        attended = lax.dot_general(
            mixed, w_out, (((0, 2), (0, 1)), ((), ())), preferred_element_type=F32
        )
        hidden2 = hidden + attended + b_out
        normed2, unit2, factor2 = norm(hidden2, gain2, shift2)
        n2 = normed2.astype(BF)
        pre = lax.dot_general(n2, w_up, (((1,), (1,)), ((), ())), preferred_element_type=F32)
        pre = pre.reshape(QROWS, FF) + b_up
        active, gelu_back = jax.vjp(partial(jax.nn.gelu, approximate=True), pre)
        act = active.astype(BF)
        act_blocks = act.reshape(QROWS, n_gc, FF // n_gc)
        final = (
            hidden2
            + lax.dot_general(
                act_blocks, w_down, (((1, 2), (0, 2)), ((), ())), preferred_element_type=F32
            )
            + b_down
        )
        grad_final = final - teacher.astype(F32)
        squared = jnp.sum(grad_final * grad_final, axis=0)
        gb = grad_final.astype(BF)
        grad_b_down = jnp.sum(gb, axis=0, dtype=F32)
        grad_active = lax.dot_general(
            gb, w_down, (((1,), (1,)), ((), ())), preferred_element_type=F32
        ).reshape(QROWS, FF)
        grad_w_down = jnp.einsum("td,tgf->gdf", gb, act_blocks, preferred_element_type=F32)
        (grad_pre,) = gelu_back(grad_active)
        gp = grad_pre.astype(BF)
        gp_blocks = gp.reshape(QROWS, n_gc, FF // n_gc)
        grad_b_up = jnp.sum(gp, axis=0, dtype=F32)
        grad_w_up = jnp.einsum("td,tgf->gdf", n2, gp_blocks, preferred_element_type=F32)
        grad_n2 = lax.dot_general(
            gp_blocks, w_up, (((1, 2), (0, 2)), ((), ())), preferred_element_type=F32
        )
        back2, grad_gain2, grad_shift2 = norm_back(grad_n2, gain2, unit2, factor2)
        grad_h2 = grad_final + back2
        ga = grad_h2.astype(BF)
        grad_b_out = jnp.sum(ga, axis=0, dtype=F32)
        grad_w_out = jnp.einsum("ctk,tn->ckn", mixed, ga, preferred_element_type=F32)
        gm = jnp.einsum("tn,ckn->ctk", ga, w_out, preferred_element_type=F32).astype(BF)
        grad_w_up = grad_w_up.astype(BF)
        grad_w_down = grad_w_down.astype(BF)
        grad_w_out = (
            grad_w_out.astype(BF)
            .reshape(2, 2, 192, n_gr, 192)
            .transpose(1, 0, 3, 2, 4)
            .reshape(n_gc, n_gr, 192, 192)
        )
    weight_grads = [
        grad_w_down.reshape(n_gc, n_gr, 192, 768),
        grad_w_up.reshape(n_gc, n_gr, 192, 768),
        grad_w_out,
    ]
    if n_dp == 2:
        dq, dkvo, dkv, out_w_down, out_w_up, out_w_out = attend_back_scatter(
            grp, q, lse_rows, kvo, kvp, gm, weight_grads, 3
        )
    else:
        gm_keep = lax.dynamic_index_in_dim(gm, c, 0, keepdims=False)
        gm_give = lax.dynamic_index_in_dim(gm, 1 - c, 0, keepdims=False)
        gm_take = lax.ppermute(gm_give, "gc", swap_core)
        gm_chip = jnp.where(c == 0, jnp.stack([gm_keep, gm_take]), jnp.stack([gm_take, gm_keep]))
        gm_chip = gm_chip.reshape(2 * QROWS, 384)

        def scatter16(blocks):
            part = lax.psum_scatter(
                blocks.reshape(n_gc * n_gr * blocks.shape[2], -1),
                ("gc", "gr"),
                scatter_dimension=0,
                tiled=True,
            )
            return lax.psum(part, "dp").astype(F32)

        out_w_down, out_w_up, out_w_out = [scatter16(grad) for grad in weight_grads]
        dq, dkvo, dkvp = attend_back(grp, z_arr, q, gm_chip, lse_rows, kvo, kvp)
        part_prompt = nt(dkvp, w_kv).astype(BF)

        part_chip = (nt(dq, w_q) + nt(dkvo, w_kv)).reshape(2, QROWS, D)
        grad_kv = tn(n1_prompt, dkvp) + tn(n1_chip, dkvo)
        grad_q = tn(n1_chip, dq)
        grad_qkv = head_layout_back(grad_q, grad_kv)

    if n_dp == 2:
        input_grad, sums, out_w_qkv = tail_exchange(
            grp,
            dkv,
            n1_prompt,
            n1_chip,
            dkvo,
            dq,
            w_q,
            w_kv,
            grad_h2,
            tokens,
            vectors,
            later_sums,
            4,
        )
    else:
        later_sums = jnp.concatenate(
            [
                grad_gain2[None],
                grad_shift2[None],
                grad_b_out[None],
                grad_b_down[None],
                grad_b_up.reshape(4, D),
                squared[None],
                jnp.zeros((4, D), F32),
            ]
        )
        back_prompt = lax.psum_scatter(part_prompt, "gc", scatter_dimension=0, tiled=True)
        back_prompt = lax.psum_scatter(
            jnp.concatenate([back_prompt, jnp.zeros_like(back_prompt)]),
            "gr",
            scatter_dimension=0,
            tiled=True,
        ).astype(F32)
        part_keep = lax.dynamic_index_in_dim(part_chip, c, 0, keepdims=False)
        part_give = lax.dynamic_index_in_dim(part_chip, 1 - c, 0, keepdims=False)
        part_take = lax.ppermute(part_give.astype(BF), "gc", swap_core).astype(F32)
        grad_n1 = part_keep + part_take + back_prompt
        qkv_keep = lax.dynamic_index_in_dim(grad_qkv, y, 0, keepdims=False)
        qkv_give = lax.dynamic_index_in_dim(grad_qkv, 1 - y, 0, keepdims=False)
        qkv_take = lax.ppermute(qkv_give.astype(BF), "gc", swap_y).astype(F32)
        out_w_qkv = lax.psum_scatter(
            (qkv_keep + qkv_take).astype(BF), "gr", scatter_dimension=0, tiled=True
        )
        out_w_qkv = lax.psum(out_w_qkv, "dp").astype(F32)
        back1, grad_gain1, grad_shift1 = norm_back(grad_n1, gain1, unit1, factor1)
        input_grad = grad_h2 + back1
        first_sums = jnp.stack([jnp.sum(input_grad, axis=0), grad_gain1, grad_shift1])
        sums = lax.psum(jnp.concatenate([first_sums, later_sums]), ("dp", "gr", "gc"))
    sums = sums[:12].reshape(12 * D)
    loss = (jnp.sum(sums[11 * D :]) / (D * token_count[0].astype(F32))).reshape(1)
    rows = sums[: 7 * D].reshape(7, n_gr, D // n_gr)
    rows = lax.dynamic_index_in_dim(rows, z, 1, keepdims=False)
    up = lax.dynamic_index_in_dim(
        sums[7 * D : 7 * D + FF].reshape(n_gc, FF // n_gc), g, 0, keepdims=False
    )
    return (
        final.astype(BF),
        loss,
        input_grad,
        rows[0],
        rows[1],
        rows[2],
        out_w_qkv,
        out_w_out,
        rows[5],
        rows[3],
        rows[4],
        out_w_up,
        up,
        out_w_down,
        rows[6],
    )


def solution(mesh):
    rows = P(("dp", "gr", "gc"), None)
    in_specs = (
        rows,
        rows,
        P("gr"),
        P("gr"),
        P("gr"),
        P("gr", "gc"),
        P("gc", "gr"),
        P("gr"),
        P("gr"),
        P("gr"),
        P("gr", "gc"),
        P("gc"),
        P("gr", "gc"),
        P("gr"),
        P(("dp", "gr")),
        P(),
    )
    out_specs = (
        rows,
        P(),
        rows,
        P("gr"),
        P("gr"),
        P("gr"),
        P("gr", "gc"),
        P("gc", "gr"),
        P("gr"),
        P("gr"),
        P("gr"),
        P("gr", "gc"),
        P("gc"),
        P("gr", "gc"),
        P("gr"),
    )
    return jax.shard_map(
        on_device, mesh=mesh, in_specs=in_specs, out_specs=out_specs, check_vma=False
    )
```
